32 devices in a mesh: fsdp: 32 (over z, y, x, core).
Axes of the slice: x: 2, y: 2, z: 4, core: 2. Of those that a mesh axis runs over, the one named last changes fastest.
Arguments:
- tokens: bfloat16 [2, 8192, 1024], P(None, 'fsdp'), may hold values from -6 to 6
- condition: bfloat16 [2, 8192], P(None, 'fsdp'), may hold values from -6 to 6
- attend: bfloat16 [3145728], P('fsdp'), may hold values from -0.1875 to 0.1875
- project: bfloat16 [1048576], P('fsdp'), may hold values from -0.25 to 0.25
- expand: bfloat16 [4194304], P('fsdp'), may hold values from -0.1875 to 0.1875
- contract: bfloat16 [4194304], P('fsdp'), may hold values from -0.1875 to 0.1875
- modulate: bfloat16 [6291456], P('fsdp'), may hold values from -0.1875 to 0.1875
- biases: bfloat16 [14336], P('fsdp'), may hold values from -2 to 2
- cotangent: bfloat16 [2, 8192, 1024], P(None, 'fsdp'), may hold values from -6 to 6
Outputs:
- output: bfloat16 [2, 8192, 1024], P(None, 'fsdp')
- grad_tokens: float32 [2, 8192, 1024], P(None, 'fsdp')
- grad_condition: float32 [2, 8192], P(None, 'fsdp')
- grad_attend: float32 [3145728], P('fsdp')
- grad_project: float32 [1048576], P('fsdp')
- expand_gradient: float32 [4194304], P('fsdp')
- grad_contract: float32 [4194304], P('fsdp')
- grad_modulate: float32 [6291456], P('fsdp')
- grad_biases: float32 [14336], P('fsdp')
The draws below stay inside these ranges and needn't reach their ends.
All inputs are finite; a program needn't handle non-finite values.
Results may differ from the reference program's by a relative error of at most 0.011.
Values may be sent and summed in bfloat16 or wider, within the bound.
A program may use at most 384 MiB of HBM per device.

```python
import jax
import jax.numpy as jnp
from jax import lax

D = 1024
HEADS = 16
HEAD = 64
FF = 4096
MICRO = 2
LATENT = 1024
TOKENS_MB = 8192
LATENTS = 8


def shard_levels(stream_key, shape, pieces, low, largest):
    loudness = 1.0
    for position, blocks in pieces:
        heights = jax.random.uniform(jax.random.fold_in(jax.random.fold_in(stream_key, 6), position), (blocks,), jnp.float32, low / len(pieces), largest / len(pieces))
        loudness = loudness * jnp.repeat(jnp.exp(heights), shape[position] // blocks).reshape((-1,) + (1,) * (len(shape) - 1 - position))
    return loudness


def centred(stream_key, dims, deviation, bound, shards=(), kind=jnp.bfloat16):
    factor_of = shard_levels(stream_key, dims, shards, -0.22, 0.18) if shards else 1.0
    entries = jax.random.normal(stream_key, dims, jnp.float32) * deviation * factor_of
    return jnp.minimum(jnp.maximum(entries, -bound), bound).astype(kind)


def setup_inputs(seed: int = 0) -> dict:
    splits = jax.random.split(jax.random.key(seed), 10)
    tokens = centred(splits[0], (MICRO, TOKENS_MB, D), 1.0, 6.0, ((1, 32),))
    condition = centred(splits[1], (MICRO, LATENTS * D), 1.0, 6.0, ((1, 32),))
    attend = centred(splits[2], (3 * D * D,), D ** -0.5, 0.1875, ((0, 32),))
    project = centred(splits[3], (D * D,), (max(D // 2, 2)) ** -0.5, 0.25, ((0, 32),))
    expand = centred(splits[4], (D * FF,), D ** -0.5, 0.1875, ((0, 32),))
    contract = centred(splits[5], (FF * D,), (max(FF // 4, 2)) ** -0.5, 0.1875, ((0, 32),))
    modulate = centred(splits[6], (6 * D * D,), D ** -0.5, 0.1875, ((0, 32),))
    biases = centred(splits[7], (10 * D + FF,), 0.3, 2.0, ((0, 32),))
    cotangent = centred(splits[8], (MICRO, TOKENS_MB, D), 1.0, 6.0, ((1, 32),))
    return dict(tokens=tokens, condition=condition, attend=attend, project=project, expand=expand, contract=contract, modulate=modulate, biases=biases, cotangent=cotangent)


epsilon = 1e-06
highest = lax.Precision.HIGHEST

@jax.custom_vjp
def low(v):
    return lax.optimization_barrier(v.astype(jnp.bfloat16)).astype(jnp.float32)

@jax.custom_vjp
def low_back(v):
    return v

def low_keep(v):
    return (low(v), None)

def low_pass(kept, grad):
    return (grad,)

def back_keep(v):
    return (v, None)

def back_low(kept, grad):
    return (low(grad),)
low.defvjp(low_keep, low_pass)
low_back.defvjp(back_keep, back_low)

def normalize(values):
    center = values - lax.optimization_barrier(jnp.mean(values, axis=-1, keepdims=True))
    spread = lax.optimization_barrier(jnp.mean(center * center, axis=-1, keepdims=True))
    return center * lax.rsqrt(spread + epsilon)

def matmul(left, right):
    return jnp.dot(left, right, precision=highest, preferred_element_type=jnp.float32)

def attend_head(parts):
    query_head, key_head, value_head = parts
    scores = low_back(matmul(query_head, key_head.T) * HEAD ** (-0.5))
    chances = low(jax.nn.softmax(scores, axis=-1))
    return matmul(chances, value_head)

def block_forward(inputs, condition, attend, project, expand, contract, modulate, biases):
    bias_query = biases[0:D]
    bias_value = biases[D:2 * D]
    bias_project = biases[2 * D:3 * D]
    bias_expand = biases[3 * D:3 * D + FF]
    bias_contract = biases[3 * D + FF:4 * D + FF]
    bias_modulate = biases[4 * D + FF:]
    cond_act = low(jax.nn.silu(condition))
    modulation = matmul(cond_act[None, :], modulate)[0] + bias_modulate
    blocks = [modulation[part * D:(part + 1) * D] for part in range(6)]
    offsets_one, factors_one, gates_one, offsets_two, factors_two, gates_two = blocks
    first_low = low(normalize(inputs) * (1.0 + factors_one) + offsets_one)
    bias_row = jnp.concatenate([bias_query, jnp.zeros((D,), jnp.float32), bias_value])
    projected = low(low_back(matmul(first_low, attend) + bias_row))
    heads_in = projected.reshape(LATENT, 3, HEADS, HEAD).transpose(1, 2, 0, 3)
    blended = lax.map(jax.checkpoint(attend_head), (heads_in[0], heads_in[1], heads_in[2]))
    blended = low(low_back(blended.transpose(1, 0, 2).reshape(LATENT, D)))
    attended = low_back(matmul(blended, project) + bias_project)
    middle = inputs + gates_one * attended
    second_half = low(normalize(middle) * (1.0 + factors_two) + offsets_two)
    hidden = low_back(matmul(second_half, expand) + bias_expand)
    activation_reduced = low(jax.nn.gelu(hidden, approximate=True))
    branch = low_back(matmul(activation_reduced, contract) + bias_contract)
    return middle + gates_two * branch

def reference(tokens, condition, attend, project, expand, contract, modulate, biases, cotangent):
    weights = (attend.astype(jnp.float32).reshape(D, 3 * D), project.astype(jnp.float32).reshape(D, D), expand.astype(jnp.float32).reshape(D, FF), contract.astype(jnp.float32).reshape(FF, D), modulate.astype(jnp.float32).reshape(D, 6 * D), biases.astype(jnp.float32))
    latent_total = MICRO * LATENTS
    token_blocks = tokens.astype(jnp.float32).reshape(latent_total, LATENT, D)
    cond_rows = condition.astype(jnp.float32).reshape(latent_total, D)
    back_blocks = cotangent.astype(jnp.float32).reshape(latent_total, LATENT, D)

    def step(totals, item):
        block_in, cond_row, block_back = item
        result, pullback = jax.vjp(block_forward, block_in, cond_row, *weights)
        grads = pullback(block_back)
        totals = tuple((total + grad for total, grad in zip(totals, grads[2:])))
        return (totals, (result.astype(jnp.bfloat16), grads[0], grads[1]))
    start = tuple((jnp.zeros_like(weight) for weight in weights))
    totals, (results, grad_tokens, grad_condition) = lax.scan(step, start, (token_blocks, cond_rows, back_blocks))
    return (results.reshape(MICRO, TOKENS_MB, D), grad_tokens.reshape(MICRO, TOKENS_MB, D), grad_condition.reshape(MICRO, LATENTS * D), totals[0].reshape(-1), totals[1].reshape(-1), totals[2].reshape(-1), totals[3].reshape(-1), totals[4].reshape(-1), totals[5])
```

```python
import functools

import jax
import jax.numpy as jnp
from jax import lax
from jax.experimental import pallas as pl
from jax.experimental.pallas import tpu as pltpu
from jax.sharding import PartitionSpec as P

D = 1024
HEADS = 16
HEAD = 64
FF = 4096
GROUP = 4
OWN = D // GROUP
SCALE = HEAD**-0.5
LANES = 128
MICROS = 2

epsilon = 1e-06
highest = lax.Precision.HIGHEST
MESH = pl.DeviceIdType.MESH
MIB = 1 << 20


def silu(values):
    return values / (1.0 + jnp.exp(-values))


class Links:
    def __init__(self, planes, send_sem, recv_sem, local_sem=None):
        me = lax.axis_index("fsdp")
        self.planes = planes
        self.c = me % 2
        self.x = (me // 2) % 2
        self.y = (me // 4) % 2
        self.z = me // 8
        self.core = me + 1 - 2 * self.c
        self.beside = me + 2 - 4 * self.x
        self.across = me + 4 - 8 * self.y
        self.place = me % 8
        self.send_sem, self.recv_sem, self.local_sem = send_sem, recv_sem, local_sem
        self.used = 0
        self.local_used = 0
        self.pending = []

    def plane(self, step):
        return (self.z + step) % self.planes

    def plane_device(self, step):
        return self.plane(step) * 8 + self.place

    def partners(self):
        return [self.core, self.beside, self.across] + [
            self.plane_device(step) for step in range(1, self.planes)
        ]

    def greet(self, partners):
        barrier = pltpu.get_barrier_semaphore()
        for partner in partners:
            pl.semaphore_signal(barrier, inc=1, device_id=(partner,), device_id_type=MESH)
        pl.semaphore_wait(barrier, len(partners))

    def send(self, source, target, device):
        copy = pltpu.make_async_remote_copy(
            src_ref=source,
            dst_ref=target,
            send_sem=self.send_sem.at[self.used],
            recv_sem=self.recv_sem.at[self.used],
            device_id=(device,),
            device_id_type=MESH,
        )
        self.used += 1
        copy.start()
        self.pending.append(copy)
        return copy

    def local(self, source, target):
        copy = pltpu.make_async_copy(source, target, self.local_sem.at[self.local_used])
        self.local_used += 1
        copy.start()
        return copy

    def finish_sends(self):
        for copy in self.pending:
            copy.wait_send()
        self.pending = []


def arrived(copies):
    for copy in copies:
        copy.wait_recv()


ANY = pl.BlockSpec(memory_space=pl.ANY)
VMEM = pl.BlockSpec(memory_space=pltpu.VMEM)


def remote_call(body, name, collective_id, outs, in_specs, out_specs, scratch, sems, local_sems, vmem):
    return pl.pallas_call(
        body,
        out_shape=outs,
        in_specs=in_specs,
        out_specs=out_specs,
        scratch_shapes=[
            pltpu.SemaphoreType.DMA((sems,)),
            pltpu.SemaphoreType.DMA((sems,)),
            pltpu.SemaphoreType.DMA((max(local_sems, 1),)),
            *scratch,
        ],
        compiler_params=pltpu.CompilerParams(
            collective_id=collective_id, has_side_effects=True, vmem_limit_bytes=vmem
        ),
        name=name,
    )


def small_gather_body(planes, own_ref, out_ref, send_sem, recv_sem, local_sem):
    links = Links(planes, send_sem, recv_sem)
    links.greet(links.partners())
    z, y, x, c = links.z, links.y, links.x, links.c
    out_ref[z, y, x, c] = own_ref[...]
    spread(links, out_ref)
    links.finish_sends()


def spread(links, out_ref):
    z, y, x, c = links.z, links.y, links.x, links.c
    block = out_ref.at[z, y, x, c]
    arrived([links.send(block, block, links.plane_device(s)) for s in range(1, links.planes)])
    block = out_ref.at[:, y, x, c]
    arrived([links.send(block, block, links.across)])
    block = out_ref.at[:, :, x, c]
    arrived([links.send(block, block, links.beside)])
    block = out_ref.at[:, :, :, c]
    arrived([links.send(block, block, links.core)])


def small_gather(own, planes, collective_id):
    return remote_call(
        functools.partial(small_gather_body, planes),
        "small_gather",
        collective_id,
        jax.ShapeDtypeStruct((planes, 2, 2, 2, *own.shape), own.dtype),
        [VMEM],
        VMEM,
        [],
        planes + 2,
        0,
        40 * MIB,
    )(own)


class WeightGather:
    def __init__(self, links, shard, full, parts):
        self.links, self.shard, self.full = links, shard, full
        width = shard.shape[-1] // parts
        self.columns = [pl.ds(part * width, width) for part in range(parts)]
        z, y, x, c = links.z, links.y, links.x, links.c
        self.own = links.local(shard, full.at[z, y, x, c])
        self.own_there = False


def gather_first(weight, part):
    links, columns = weight.links, weight.columns[part]
    source = weight.shard.at[:, columns]
    target = weight.full.at[links.z, links.y, links.x, links.c, :, columns]
    return [links.send(source, target, links.plane_device(s)) for s in range(1, links.planes)]


def gather_second(weight, part, late):
    links, columns = weight.links, weight.columns[part]
    if not weight.own_there:
        weight.own.wait()
        weight.own_there = True
    block = weight.full.at[:, links.y, links.x, links.c, :, columns]
    late.append(links.send(block, block, links.core))
    return [links.send(block, block, links.beside if part % 2 == 0 else links.across)]


def gather_third(weight, part, late):
    links, columns = weight.links, weight.columns[part]
    y, x, c = links.y, links.x, links.c
    if part % 2 == 0:
        fresh = weight.full.at[:, y, 1 - x, c, :, columns]
        block, device = weight.full.at[:, y, :, c, :, columns], links.across
    else:
        fresh = weight.full.at[:, 1 - y, x, c, :, columns]
        block, device = weight.full.at[:, :, x, c, :, columns], links.beside
    late.append(links.send(fresh, fresh, links.core))
    return [links.send(block, block, device)]


def gather_fourth(weight, part, late):
    links, columns = weight.links, weight.columns[part]
    y, x, c = links.y, links.x, links.c
    if part % 2 == 0:
        fresh = weight.full.at[:, 1 - y, :, c, :, columns]
    else:
        fresh = weight.full.at[:, :, 1 - x, c, :, columns]
    late.append(links.send(fresh, fresh, links.core))


def gather_steps(pieces):
    count = len(pieces)
    late = []
    first, second, third = {}, {}, {}
    for k in range(min(2, count)):
        first[k] = gather_first(*pieces[k])
    yield
    for k in range(count + 4):
        if k < count:
            if k + 2 < count:
                first[k + 2] = gather_first(*pieces[k + 2])
            arrived(first.pop(k))
            second[k] = gather_second(*pieces[k], late)
        if 0 <= k - 2 < count:
            arrived(second.pop(k - 2))
            third[k - 2] = gather_third(*pieces[k - 2], late)
        if 0 <= k - 4 < count:
            arrived(third.pop(k - 4))
            gather_fourth(*pieces[k - 4], late)
        yield
    arrived(late)


def gather_body(
    planes,
    tokens,
    attend,
    project,
    expand,
    contract,
    partial,
    tokens_out,
    attend_out,
    project_out,
    expand_out,
    contract_out,
    modulation_out,
    send_sem,
    recv_sem,
    local_sem,
    attend_held,
    sum_core,
    sum_beside,
    sum_across,
    sum_planes,
    total,
):
    links = Links(planes, send_sem, recv_sem, local_sem)
    links.greet(links.partners())
    z, y, x, c = links.z, links.y, links.x, links.c

    weights = [
        WeightGather(links, project, project_out, 2),
        WeightGather(links, expand, expand_out, 4),
        WeightGather(links, contract, contract_out, 4),
    ]
    pieces = [(w, part) for w in weights for part in range(len(w.columns))]

    own_slice = links.local(attend.at[x, c], attend_out.at[z, y, x, c])
    to_core = links.send(attend.at[x, 1 - c], attend_out.at[z, y, x, c], links.core)
    held = links.send(attend.at[1 - x, 1 - c], attend_held, links.core)
    to_beside = links.send(attend.at[1 - x, c], attend_out.at[z, y, x, c], links.beside)
    own_tokens = links.local(tokens, tokens_out.at[:, x, c])
    tokens_core = links.send(tokens, tokens_out.at[:, x, c], links.core)
    tokens_beside = links.send(tokens, tokens_out.at[:, x, c], links.beside)
    step = links.send(partial.at[:, :, :, 1 - c], sum_core, links.core)

    arrived([held])
    held_beside = links.send(attend_held, attend_out.at[z, y, x, 1 - c], links.beside)
    steps = gather_steps(pieces)
    next(steps)

    arrived([step])
    sum_core[...] = sum_core[...] + partial[:, :, :, c]
    step = links.send(sum_core.at[:, :, 1 - x], sum_beside, links.beside)

    own_slice.wait()
    arrived([to_core, to_beside, held_beside])
    half = attend_out.shape[-1] // 2
    over_planes = []
    for part in range(2):
        block = attend_out.at[z, y, :, :, :, pl.ds(part * half, half)]
        over_planes.append(
            [links.send(block, block, links.plane_device(s)) for s in range(1, planes)]
        )

    arrived([step])
    sum_beside[...] = sum_beside[...] + sum_core[:, :, x]
    step = links.send(sum_beside.at[:, 1 - y], sum_across, links.across)

    over_y = []
    for part in range(2):
        arrived(over_planes[part])
        block = attend_out.at[:, y, :, :, :, pl.ds(part * half, half)]
        over_y.append(links.send(block, block, links.across))

    arrived([step])
    sum_across[...] = sum_across[...] + sum_beside[:, y]
    step = [
        links.send(sum_across.at[links.plane(s)], sum_planes.at[s - 1], links.plane_device(s))
        for s in range(1, planes)
    ]
    next(steps)

    arrived(step)
    result = sum_across[z]
    for s in range(1, planes):
        result = result + sum_planes[s - 1]
    total[...] = result
    modulation_out[x, c] = result
    step = [
        links.send(total, modulation_out.at[x, c], links.core),
        links.send(total, modulation_out.at[x, c], links.beside),
    ]
    next(steps)
    arrived(step)
    step = links.send(modulation_out.at[1 - x, c], modulation_out.at[1 - x, c], links.core)

    arrived([tokens_beside])
    fresh = tokens_out.at[:, 1 - x, c]
    tokens_late = links.send(fresh, fresh, links.core)

    for _ in steps:
        pass
    arrived([step, tokens_core, tokens_late, *over_y])
    own_tokens.wait()
    links.finish_sends()


def gather_all(tokens, attend, project, expand, contract, partial, planes):
    grid = (planes, 2, 2, 2)
    rows = partial.shape[-2]

    def full(shard):
        return jax.ShapeDtypeStruct((*grid, *shard.shape[-2:]), shard.dtype)

    return remote_call(
        functools.partial(gather_body, planes),
        "gather_all",
        1,
        (
            jax.ShapeDtypeStruct((tokens.shape[0], 2, 2, *tokens.shape[1:]), tokens.dtype),
            full(attend),
            full(project),
            full(expand),
            full(contract),
            jax.ShapeDtypeStruct((2, 2, rows, LANES), jnp.float32),
        ),
        [ANY] * 5 + [VMEM],
        (ANY,) * 5 + (VMEM,),
        [
            pltpu.VMEM((attend.shape[-2], attend.shape[-1]), attend.dtype),
            pltpu.VMEM((planes, 2, 2, rows, LANES), jnp.float32),
            pltpu.VMEM((planes, 2, rows, LANES), jnp.float32),
            pltpu.VMEM((planes, rows, LANES), jnp.float32),
            pltpu.VMEM((planes - 1, rows, LANES), jnp.float32),
            pltpu.VMEM((rows, LANES), jnp.float32),
        ],
        20 + 13 * (planes - 1) + 10 * 5,
        8,
        40 * MIB,
    )(tokens, attend, project, expand, contract, partial)


def attention_body(qkv_ref, out_ref, log_ref):
    rows = 256
    for head in range(OWN // HEAD):
        at = head * HEAD
        keys = qkv_ref[0, :, OWN + at : OWN + at + HEAD]
        values_t = qkv_ref[0, :, 2 * OWN + at : 2 * OWN + at + HEAD].T

        @pl.loop(0, qkv_ref.shape[1] // rows)
        def _(block):
            here = pl.ds(pl.multiple_of(block * rows, rows), rows)
            queries = qkv_ref[0, here, at : at + HEAD] * SCALE
            scores = lax.dot_general(
                keys, queries, (((1,), (1,)), ((), ())), preferred_element_type=jnp.float32
            )
            top = jnp.max(scores, axis=0, keepdims=True)
            weights = jnp.exp(scores - top)
            totals = jnp.sum(weights, axis=0, keepdims=True)
            blended = jnp.dot(
                values_t, weights.astype(jnp.bfloat16), preferred_element_type=jnp.float32
            )
            out_ref[0, here, at : at + HEAD] = (blended / totals).T.astype(jnp.bfloat16)
            log_ref[0, head, block] = top + jnp.log(totals)


def attention(qkv):
    micros, rows, _ = qkv.shape
    heads = OWN // HEAD
    blocks = rows // 256
    return pl.pallas_call(
        attention_body,
        grid=(micros,),
        out_shape=(
            jax.ShapeDtypeStruct((micros, rows, OWN), jnp.bfloat16),
            jax.ShapeDtypeStruct((micros, heads, blocks, 1, 256), jnp.float32),
        ),
        in_specs=[pl.BlockSpec((1, rows, 3 * OWN), lambda m: (m, 0, 0))],
        out_specs=(
            pl.BlockSpec((1, rows, OWN), lambda m: (m, 0, 0)),
            pl.BlockSpec((1, heads, blocks, 1, 256), lambda m: (m, 0, 0, 0, 0)),
        ),
        compiler_params=pltpu.CompilerParams(vmem_limit_bytes=48 * MIB),
        name="attention",
    )(qkv)


def attention_back_body(qkv_ref, blended_ref, grad_ref, log_ref, out_ref, key_sum, value_sum):
    rows = 256
    for head in range(OWN // HEAD):
        at = head * HEAD
        keys = qkv_ref[0, :, OWN + at : OWN + at + HEAD]
        keys_t = keys.T
        values = qkv_ref[0, :, 2 * OWN + at : 2 * OWN + at + HEAD]
        key_sum[...] = jnp.zeros_like(key_sum)
        value_sum[...] = jnp.zeros_like(value_sum)

        @pl.loop(0, qkv_ref.shape[1] // rows)
        def _(block):
            here = pl.ds(pl.multiple_of(block * rows, rows), rows)
            queries = qkv_ref[0, here, at : at + HEAD] * SCALE
            grads = grad_ref[0, here, at : at + HEAD]
            blended = blended_ref[0, here, at : at + HEAD]
            row_terms = jnp.sum(
                (grads.astype(jnp.float32) * blended.astype(jnp.float32)).T, axis=0, keepdims=True
            )
            scores = lax.dot_general(
                keys, queries, (((1,), (1,)), ((), ())), preferred_element_type=jnp.float32
            )
            chances = jnp.exp(scores - log_ref[0, head, block])
            grad_chances = lax.dot_general(
                values, grads, (((1,), (1,)), ((), ())), preferred_element_type=jnp.float32
            )
            grad_scores = (chances * (grad_chances - row_terms)).astype(jnp.bfloat16)
            value_sum[...] += jnp.dot(
                chances.astype(jnp.bfloat16), grads, preferred_element_type=jnp.float32
            )
            key_sum[...] += jnp.dot(grad_scores, queries, preferred_element_type=jnp.float32)
            grad_queries = jnp.dot(keys_t, grad_scores, preferred_element_type=jnp.float32)
            out_ref[0, here, at : at + HEAD] = (grad_queries.T * SCALE).astype(jnp.bfloat16)

        out_ref[0, :, OWN + at : OWN + at + HEAD] = key_sum[...].astype(jnp.bfloat16)
        out_ref[0, :, 2 * OWN + at : 2 * OWN + at + HEAD] = value_sum[...].astype(jnp.bfloat16)


def attention_back(qkv, blended, grads, logs):
    micros, rows, _ = qkv.shape
    heads = OWN // HEAD
    blocks = rows // 256
    wide = pl.BlockSpec((1, rows, 3 * OWN), lambda m: (m, 0, 0))
    narrow = pl.BlockSpec((1, rows, OWN), lambda m: (m, 0, 0))
    return pl.pallas_call(
        attention_back_body,
        grid=(micros,),
        out_shape=jax.ShapeDtypeStruct((micros, rows, 3 * OWN), jnp.bfloat16),
        in_specs=[
            wide,
            narrow,
            narrow,
            pl.BlockSpec((1, heads, blocks, 1, 256), lambda m: (m, 0, 0, 0, 0)),
        ],
        out_specs=wide,
        scratch_shapes=[pltpu.VMEM((rows, HEAD), jnp.float32)] * 2,
        compiler_params=pltpu.CompilerParams(vmem_limit_bytes=48 * MIB),
        name="attention_back",
    )(qkv, blended, grads, logs)


def heads_to_tokens_body(blended, out, send_sem, recv_sem, local_sem):
    links = Links(1, send_sem, recv_sem, local_sem)
    x, c = links.x, links.c
    corner = links.beside + 1 - 2 * c
    links.greet([links.core, links.beside, corner])
    target = out.at[:, :, pl.ds(pl.multiple_of((2 * x + c) * OWN, OWN), OWN)]
    own = links.local(blended.at[:, x, c], target)
    copies = [
        links.send(blended.at[:, 1 - x, 1 - c], target, corner),
        links.send(blended.at[:, 1 - x, c], target, links.beside),
        links.send(blended.at[:, x, 1 - c], target, links.core),
    ]
    arrived(copies)
    own.wait()
    links.finish_sends()


def heads_to_tokens(blended):
    micros, rows, _ = blended.shape
    own_rows = rows // GROUP
    return remote_call(
        heads_to_tokens_body,
        "heads_to_tokens",
        2,
        jax.ShapeDtypeStruct((micros, own_rows, D), blended.dtype),
        [ANY],
        ANY,
        [],
        3,
        1,
        40 * MIB,
    )(blended.reshape(micros, 2, 2, own_rows, OWN))


def tokens_to_heads_body(grads, out, send_sem, recv_sem, local_sem):
    links = Links(1, send_sem, recv_sem, local_sem)
    x, c = links.x, links.c
    corner = links.beside + 1 - 2 * c
    links.greet([links.core, links.beside, corner])

    def columns(to_x, to_c):
        return grads.at[:, :, pl.ds(pl.multiple_of((2 * to_x + to_c) * OWN, OWN), OWN)]

    target = out.at[:, x, c]
    own = links.local(columns(x, c), target)
    copies = [
        links.send(columns(1 - x, 1 - c), target, corner),
        links.send(columns(1 - x, c), target, links.beside),
        links.send(columns(x, 1 - c), target, links.core),
    ]
    arrived(copies)
    own.wait()
    links.finish_sends()


def tokens_to_heads(grads):
    micros, own_rows, _ = grads.shape
    return remote_call(
        tokens_to_heads_body,
        "tokens_to_heads",
        3,
        jax.ShapeDtypeStruct((micros, 2, 2, own_rows, OWN), grads.dtype),
        [ANY],
        ANY,
        [],
        3,
        1,
        40 * MIB,
    )(grads).reshape(micros, GROUP * own_rows, OWN)


def token_sums_body(partial, out, send_sem, recv_sem, local_sem, from_core, own, from_beside):
    links = Links(1, send_sem, recv_sem, local_sem)
    x, c = links.x, links.c
    links.greet([links.core, links.beside])
    far = links.send(partial.at[:, 1 - x, 1 - c], from_core.at[0], links.core)
    near = links.send(partial.at[:, x, 1 - c], from_core.at[1], links.core)
    loads = [
        links.local(partial.at[:, 1 - x, c], own.at[0]),
        links.local(partial.at[:, x, c], own.at[1]),
    ]
    micros = out.shape[0]
    loads[0].wait()
    arrived([far])
    passed = []
    for m in range(micros):
        own[0, m] = (
            own[0, m].astype(jnp.float32) + from_core[0, m].astype(jnp.float32)
        ).astype(jnp.bfloat16)
        passed.append(links.send(own.at[0, m], from_beside.at[m], links.beside))
    loads[1].wait()
    arrived([near])
    for m in range(micros):
        out[m] = own[1, m].astype(jnp.float32) + from_core[1, m].astype(jnp.float32)
    for m in range(micros):
        arrived([passed[m]])
        out[m] += from_beside[m].astype(jnp.float32)
    links.finish_sends()


def token_sums(partial):
    micros, rows, width = partial.shape
    own_rows = rows // GROUP
    held = pltpu.VMEM((2, micros, own_rows, width), partial.dtype)
    return remote_call(
        token_sums_body,
        "token_sums",
        4,
        jax.ShapeDtypeStruct((micros, own_rows, width), jnp.float32),
        [ANY],
        VMEM,
        [held, held, pltpu.VMEM((micros, own_rows, width), partial.dtype)],
        4,
        2,
        40 * MIB,
    )(partial.reshape(micros, 2, 2, own_rows, width))


def small_sums_body(planes, partial, out, send_sem, recv_sem, local_sem, from_core, from_beside):
    links = Links(planes, send_sem, recv_sem)
    links.greet(links.partners())
    z, y, x, c = links.z, links.y, links.x, links.c
    arrived([links.send(partial.at[:, 1 - c], from_core, links.core)])
    from_core[...] = from_core[...] + partial[:, c]
    arrived([links.send(from_core.at[1 - x], from_beside, links.beside)])
    out[z, y, x, c] = from_core[x] + from_beside[...]
    spread(links, out)
    links.finish_sends()


def small_sums(partial, planes):
    block = partial.shape[2:]
    return remote_call(
        functools.partial(small_sums_body, planes),
        "small_sums",
        5,
        jax.ShapeDtypeStruct((planes, 2, 2, 2, *block), jnp.float32),
        [VMEM],
        VMEM,
        [pltpu.VMEM((2, *block), jnp.float32), pltpu.VMEM(block, jnp.float32)],
        planes + 4,
        0,
        40 * MIB,
    )(partial)


class SumPiece:
    def __init__(self, links, grads, out, columns, part, scratch):
        self.links, self.grads, self.out = links, grads, out
        self.columns, self.part = columns, part
        self.own, self.first, self.second, self.third, self.fourth = scratch


def add_blocks(target, left, right, count):
    @pl.loop(0, count)
    def _(i):
        target(i)[...] = (
            left(i)[...].astype(jnp.float32) + right(i)[...].astype(jnp.float32)
        ).astype(jnp.bfloat16)


def sum_first(piece):
    links = piece.links
    c = links.c
    source = piece.grads.at[:, :, :, 1 - c, :, piece.columns]
    sent = links.send(source, piece.first, links.core)
    loaded = links.local(piece.grads.at[:, :, :, c, :, piece.columns], piece.own)
    return sent, loaded


def sum_second(piece, before):
    links = piece.links
    x, y, planes = links.x, links.y, links.planes
    sent, loaded = before
    loaded.wait()
    arrived([sent])
    own, first = piece.own, piece.first
    turn = piece.part % 2 == 0
    for order in range(2):

        def at(ref):
            def block(i):
                z, other = i // 2, i % 2
                if turn:
                    return ref.at[z, other, (1 - x) if order == 0 else x]
                return ref.at[z, (1 - y) if order == 0 else y, other]

            return block

        add_blocks(at(own), at(own), at(first), planes * 2)
        if order == 0:
            source = own.at[:, :, 1 - x] if turn else own.at[:, 1 - y]
            copy = links.send(source, piece.second, links.beside if turn else links.across)
    return copy


def sum_third(piece, before):
    links = piece.links
    x, y, planes = links.x, links.y, links.planes
    arrived([before])
    own, second = piece.own, piece.second
    turn = piece.part % 2 == 0
    for order in range(2):
        if turn:
            away = (1 - y) if order == 0 else y

            def kept(i):
                return own.at[i, away, x]

        else:
            away = (1 - x) if order == 0 else x

            def kept(i):
                return own.at[i, y, away]

        def came(i):
            return second.at[i, away]

        add_blocks(came, kept, came, planes)
        if order == 0:
            copy = links.send(
                second.at[:, away], piece.third, links.across if turn else links.beside
            )
    return copy


def sum_fourth(piece, before):
    links = piece.links
    x, y, z, planes = links.x, links.y, links.z, links.planes
    arrived([before])
    second, third = piece.second, piece.third
    stay = y if piece.part % 2 == 0 else x

    def kept(i):
        return second.at[i, stay]

    def came(i):
        return third.at[i]

    add_blocks(came, kept, came, planes)
    return [
        links.send(third.at[links.plane(s)], piece.fourth.at[s - 1], links.plane_device(s))
        for s in range(1, planes)
    ]


def sum_last(piece, before):
    links = piece.links
    arrived(before)
    result = piece.third[links.z].astype(jnp.float32)
    for s in range(1, links.planes):
        result = result + piece.fourth[s - 1].astype(jnp.float32)
    piece.out[:, piece.columns] = result


def sum_steps(pieces):
    count = len(pieces)
    stages = (sum_second, sum_third, sum_fourth, sum_last)
    state = {}
    for k in range(count + 5):
        if k < count:
            state[k] = sum_first(pieces[k])
        yield
        for stage, run in enumerate(stages):
            j = k - 1 - stage
            if 0 <= j < count:
                state[j] = run(pieces[j], state[j])
        yield


def sums_body(planes, plan, attend, *refs):
    links_sems, scratch = refs[2 * len(plan) + 1 :][:3], refs[2 * len(plan) + 4 :]
    grads, attend_out, outs = refs[: len(plan)], refs[len(plan)], refs[len(plan) + 1 :][: len(plan)]
    links = Links(planes, *links_sems)
    links.greet(links.partners())
    z, y, x, c = links.z, links.y, links.x, links.c
    attend_own, attend_across, attend_planes, attend_sum, attend_held = scratch[:5]
    scratch = scratch[5:]
    pieces = []
    used = 0
    for parts, grad, out in zip(plan, grads, outs):
        width = grad.shape[-1] // parts
        for part in range(parts):
            pieces.append(
                SumPiece(links, grad, out, pl.ds(part * width, width), part, scratch[used : used + 5])
            )
            used += 5

    step = links.send(attend.at[:, 1 - y], attend_across, links.across)
    loaded = links.local(attend.at[:, y], attend_own)
    steps = sum_steps(pieces)
    next(steps)
    next(steps)
    loaded.wait()
    arrived([step])
    for i in range(2):

        def block(ref):
            return lambda k: ref.at[k // 2, i, k % 2]

        add_blocks(block(attend_own), block(attend_own), block(attend_across), planes * 2)
    over = [
        links.send(attend_own.at[links.plane(s)], attend_planes.at[s - 1], links.plane_device(s))
        for s in range(1, planes)
    ]
    next(steps)
    next(steps)
    arrived(over)
    for i in range(2):
        for j in range(2):
            result = attend_own[z, i, j].astype(jnp.float32)
            for s in range(1, planes):
                result = result + attend_planes[s - 1, i, j].astype(jnp.float32)
            attend_sum[i, j] = result
    beside = links.send(attend_sum.at[1 - x], attend_held, links.beside)
    near = links.send(attend_sum.at[x, 1 - c], attend_out.at[x, c], links.core)
    attend_out[x, c] = attend_sum[x, c]
    next(steps)
    next(steps)
    arrived([beside])
    attend_out[1 - x, c] = attend_held[c]
    far = links.send(attend_held.at[1 - c], attend_out.at[1 - x, c], links.core)
    for _ in steps:
        pass
    arrived([near, far])
    links.finish_sends()


def weight_sums(attend, weights, plan, planes):
    def piece_scratch(grad, parts):
        rows, width = grad.shape[-2], grad.shape[-1] // parts
        return [
            pltpu.VMEM((planes, 2, 2, rows, width), jnp.bfloat16),
            pltpu.VMEM((planes, 2, 2, rows, width), jnp.bfloat16),
            pltpu.VMEM((planes, 2, rows, width), jnp.bfloat16),
            pltpu.VMEM((planes, rows, width), jnp.bfloat16),
            pltpu.VMEM((planes - 1, rows, width), jnp.bfloat16),
        ]

    rows, width = attend.shape[-2:]
    scratch = [
        pltpu.VMEM((planes, 2, 2, rows, width), jnp.bfloat16),
        pltpu.VMEM((planes, 2, 2, rows, width), jnp.bfloat16),
        pltpu.VMEM((planes - 1, 2, 2, rows, width), jnp.bfloat16),
        pltpu.VMEM((2, 2, rows, width), jnp.float32),
        pltpu.VMEM((2, rows, width), jnp.float32),
    ]
    for grad, parts in zip(weights, plan):
        for _ in range(parts):
            scratch += piece_scratch(grad, parts)
    return remote_call(
        functools.partial(sums_body, planes, plan),
        "weight_sums",
        6,
        (
            jax.ShapeDtypeStruct((2, 2, rows, width), jnp.float32),
            *(jax.ShapeDtypeStruct(grad.shape[-2:], jnp.float32) for grad in weights),
        ),
        [ANY] * (1 + len(weights)),
        (VMEM,) * (1 + len(weights)),
        scratch,
        8 + planes + sum(plan) * (2 + planes),
        2 + sum(plan),
        60 * MIB,
    )(attend, *weights)


def normalize(values):
    center = values - jnp.mean(values, axis=-1, keepdims=True)
    spread_of = jnp.mean(center * center, axis=-1, keepdims=True)
    scale = lax.rsqrt(spread_of + epsilon)
    return center * scale, scale


def norm_back(grads, normed, scale, factors):
    inner = grads * (1.0 + factors)
    return scale * (
        inner
        - jnp.mean(inner, axis=-1, keepdims=True)
        - normed * jnp.mean(inner * normed, axis=-1, keepdims=True)
    )


def einsum(spec, left, right):
    return jnp.einsum(spec, left, right, preferred_element_type=jnp.float32)


def per_device(tokens, condition, attend, project, expand, contract, modulate, biases, cotangent):
    devices = lax.axis_size("fsdp")
    planes = devices // 8
    latents = devices // GROUP
    me = lax.axis_index("fsdp")
    quarter, latent = me % GROUP, me // GROUP
    micros, own_rows, _ = tokens.shape
    latent_rows = own_rows * GROUP
    rows = D // devices
    grid = (planes, 2, 2, 2)

    held = jnp.concatenate([condition.reshape(-1), biases]).astype(jnp.float32)
    held = jnp.pad(held, (0, -held.size % (8 * LANES)))
    small = small_gather(held.reshape(-1, LANES), planes, 0).reshape(devices, -1)
    conditions = small[:, : condition.size].reshape(latents, GROUP, micros, -1)
    conditions = conditions.transpose(2, 0, 1, 3).reshape(micros * latents, D)
    cond_act = silu(conditions).astype(jnp.bfloat16)
    bias_all = small[:, condition.size : condition.size + biases.size].reshape(-1)
    bias_query = bias_all[0:D]
    bias_value = bias_all[D : 2 * D]
    bias_project = bias_all[2 * D : 3 * D]
    bias_expand = bias_all[3 * D : 3 * D + FF]
    bias_contract = bias_all[3 * D + FF : 4 * D + FF]
    bias_modulate = bias_all[4 * D + FF :]

    modulate_rows = modulate.reshape(rows, 6 * D)
    cond_own = lax.dynamic_slice_in_dim(cond_act, me * rows, rows, axis=1)
    partial = jnp.dot(cond_own, modulate_rows, preferred_element_type=jnp.float32)
    partial = partial.reshape(micros, latents, GROUP, -1).transpose(1, 2, 0, 3)
    partial = partial.reshape(planes, 2, 2, 2, -1, LANES)

    attend_shard = attend.reshape(rows, 3, 2, 2, OWN).transpose(2, 3, 0, 1, 4)
    gathered = gather_all(
        tokens,
        attend_shard.reshape(2, 2, rows, 3 * OWN),
        project.reshape(rows, D),
        expand.reshape(rows, FF),
        contract.reshape(FF // devices, D),
        partial,
        planes,
    )
    tokens_latent = gathered[0].reshape(micros, latent_rows, D)
    attend_own = gathered[1].reshape(D, 3 * OWN)
    project_full = gathered[2].reshape(D, D)
    expand_full = gathered[3].reshape(D, FF)
    contract_full = gathered[4].reshape(FF, D)
    modulation = gathered[5].reshape(GROUP, micros, -1).transpose(1, 0, 2)
    modulation = modulation.reshape(micros, 6 * D) + bias_modulate
    offsets_one, factors_one, gates_one, offsets_two, factors_two, gates_two = (
        modulation[:, None, part * D : (part + 1) * D] for part in range(6)
    )

    normed_latent, _ = normalize(tokens_latent.astype(jnp.float32))
    first = (normed_latent * (1.0 + factors_one) + offsets_one).astype(jnp.bfloat16)
    bias_row = jnp.concatenate(
        [
            lax.dynamic_slice_in_dim(bias_query, quarter * OWN, OWN),
            jnp.zeros((OWN,), jnp.float32),
            lax.dynamic_slice_in_dim(bias_value, quarter * OWN, OWN),
        ]
    )
    projected = (einsum("mrd,de->mre", first, attend_own) + bias_row).astype(jnp.bfloat16)
    blended_heads, logs = attention(projected)
    blended = heads_to_tokens(blended_heads)

    inputs = tokens.astype(jnp.float32)
    attended = einsum("mrd,de->mre", blended, project_full) + bias_project
    middle = inputs + gates_one * attended
    normed_two, scale_two = normalize(middle)
    second = (normed_two * (1.0 + factors_two) + offsets_two).astype(jnp.bfloat16)
    hidden = einsum("mrd,de->mre", second, expand_full) + bias_expand
    activated, gelu_pull = jax.vjp(lambda v: jax.nn.gelu(v, approximate=True), hidden)
    act_low = activated.astype(jnp.bfloat16)
    branch = einsum("mrd,de->mre", act_low, contract_full) + bias_contract
    output = (middle + gates_two * branch).astype(jnp.bfloat16)

    upstream = cotangent.astype(jnp.float32)
    grad_branch = (gates_two * upstream).astype(jnp.bfloat16)
    grad_gates_two = jnp.sum(upstream * branch, axis=1)
    grad_contract = einsum("mrd,mre->de", act_low, grad_branch)
    grad_act = einsum("mre,de->mrd", grad_branch, contract_full)
    grad_hidden = gelu_pull(grad_act)[0].astype(jnp.bfloat16)
    grad_expand = einsum("mrd,mre->de", second, grad_hidden)
    grad_second = einsum("mre,de->mrd", grad_hidden, expand_full)
    grad_middle = upstream + norm_back(grad_second, normed_two, scale_two, factors_two)
    grad_attended = (gates_one * grad_middle).astype(jnp.bfloat16)
    grad_gates_one = jnp.sum(grad_middle * attended, axis=1)
    grad_project = einsum("mrd,mre->de", blended, grad_attended)
    grad_blended = einsum("mre,de->mrd", grad_attended, project_full).astype(jnp.bfloat16)
    grad_heads = tokens_to_heads(grad_blended)
    grad_projected = attention_back(projected, blended_heads, grad_heads, logs)
    grad_attend = einsum("mrd,mre->de", first, grad_projected)
    grad_first = token_sums(
        einsum("mre,de->mrd", grad_projected, attend_own).astype(jnp.bfloat16)
    )
    normed_one, scale_one = normalize(inputs)
    grad_tokens = grad_middle + norm_back(grad_first, normed_one, scale_one, factors_one)

    grad_modulation = jnp.concatenate(
        [
            jnp.sum(grad_first, axis=1),
            jnp.sum(grad_first * normed_one, axis=1),
            grad_gates_one,
            jnp.sum(grad_second, axis=1),
            jnp.sum(grad_second * normed_two, axis=1),
            grad_gates_two,
        ],
        axis=1,
    )

    def token_sum(values):
        return jnp.sum(values, axis=(0, 1), dtype=jnp.float32)

    heads_sum = token_sum(grad_projected)
    bias_terms = jnp.concatenate(
        [
            lax.dynamic_update_slice(
                jnp.zeros((D,), jnp.float32), heads_sum[:OWN], (quarter * OWN,)
            ),
            lax.dynamic_update_slice(
                jnp.zeros((D,), jnp.float32), heads_sum[2 * OWN :], (quarter * OWN,)
            ),
            token_sum(grad_attended),
            token_sum(grad_hidden),
            token_sum(grad_branch),
        ]
    )
    to_sum = jnp.concatenate(
        [
            grad_modulation.reshape(micros, GROUP, -1).transpose(1, 0, 2).reshape(GROUP, -1),
            bias_terms.reshape(GROUP, -1),
        ],
        axis=1,
    )
    sums = small_sums(to_sum.reshape(2, 2, -1, LANES), planes).reshape(latents, GROUP, -1)
    split = micros * 6 * D // GROUP
    grad_modulations = sums[:, :, :split].reshape(latents, GROUP, micros, -1)
    grad_modulations = grad_modulations.transpose(2, 0, 1, 3).reshape(micros * latents, 6 * D)
    bias_sums = jnp.concatenate(
        [jnp.sum(sums[:, :, split:], axis=0).reshape(-1), jnp.sum(grad_modulations, axis=0)]
    )
    grad_biases = lax.dynamic_slice_in_dim(bias_sums, me * biases.size, biases.size)
    grad_modulate = lax.dot_general(
        cond_own.astype(jnp.float32),
        grad_modulations,
        (((0,), (0,)), ((), ())),
        precision=highest,
    )
    grad_cond_cols = lax.dot_general(
        grad_modulations,
        modulate_rows.astype(jnp.float32),
        (((1,), (1,)), ((), ())),
        precision=highest,
    )
    cols = grad_cond_cols.reshape(-1)
    cols = jnp.pad(cols, (0, -cols.size % (8 * LANES)))
    cols_all = small_gather(cols.reshape(-1, LANES), planes, 7).reshape(devices, -1)
    cols_all = cols_all[:, : micros * latents * rows].reshape(devices, micros, latents, rows)
    cols_own = lax.dynamic_index_in_dim(cols_all, latent, axis=2, keepdims=False)
    width = D // GROUP
    cols_own = lax.dynamic_slice_in_dim(
        cols_own, quarter * (devices // GROUP), devices // GROUP, axis=0
    )
    grad_silu = cols_own.transpose(1, 0, 2).reshape(micros, width)
    values = condition.astype(jnp.float32)
    gate = 1.0 / (1.0 + jnp.exp(-values))
    grad_condition = gate * (1.0 + values * (1.0 - gate)) * grad_silu

    weights = (
        grad_contract.astype(jnp.bfloat16).reshape(*grid, FF // devices, D),
        grad_expand.astype(jnp.bfloat16).reshape(*grid, rows, FF),
        grad_project.astype(jnp.bfloat16).reshape(*grid, rows, D),
    )
    attend_sum, contract_sum, expand_sum, project_sum = weight_sums(
        grad_attend.astype(jnp.bfloat16).reshape(*grid, rows, 3 * OWN), weights, (4, 4, 2), planes
    )
    attend_sum = attend_sum.reshape(2, 2, rows, 3, OWN).transpose(2, 3, 0, 1, 4)
    return (
        output,
        grad_tokens,
        grad_condition,
        attend_sum.reshape(-1),
        project_sum.reshape(-1),
        expand_sum.reshape(-1),
        contract_sum.reshape(-1),
        grad_modulate.reshape(-1),
        grad_biases,
    )


def solution(mesh):
    in_specs = (
        P(None, "fsdp", None),
        P(None, "fsdp"),
        P("fsdp"),
        P("fsdp"),
        P("fsdp"),
        P("fsdp"),
        P("fsdp"),
        P("fsdp"),
        P(None, "fsdp", None),
    )
    out_specs = (
        P(None, "fsdp", None),
        P(None, "fsdp", None),
        P(None, "fsdp"),
        P("fsdp"),
        P("fsdp"),
        P("fsdp"),
        P("fsdp"),
        P("fsdp"),
        P("fsdp"),
    )
    return jax.shard_map(
        per_device, mesh=mesh, in_specs=in_specs, out_specs=out_specs, check_vma=False
    )
```

```python
import functools

import jax
import jax.numpy as jnp
from jax import lax
from jax.experimental import pallas as pl
from jax.experimental.pallas import tpu as pltpu
from jax.sharding import PartitionSpec as P

D = 1024
HEADS = 16
HEAD = 64
FF = 4096
GROUP = 4
OWN = D // GROUP
SCALE = HEAD**-0.5
LANES = 128
MICROS = 2

epsilon = 1e-06
highest = lax.Precision.HIGHEST
MESH = pl.DeviceIdType.MESH
MIB = 1 << 20


def silu(values):
    return values / (1.0 + jnp.exp(-values))


class Links:
    def __init__(self, planes, send_sem, recv_sem, local_sem=None):
        me = lax.axis_index("fsdp")
        self.planes = planes
        self.c = me % 2
        self.x = (me // 2) % 2
        self.y = (me // 4) % 2
        self.z = me // 8
        self.core = me + 1 - 2 * self.c
        self.beside = me + 2 - 4 * self.x
        self.across = me + 4 - 8 * self.y
        self.place = me % 8
        self.send_sem, self.recv_sem, self.local_sem = send_sem, recv_sem, local_sem
        self.used = 0
        self.local_used = 0
        self.pending = []

    def plane(self, step):
        return (self.z + step) % self.planes

    def plane_device(self, step):
        return self.plane(step) * 8 + self.place

    def partners(self):
        return [self.core, self.beside, self.across] + [
            self.plane_device(step) for step in range(1, self.planes)
        ]

    def greet(self, partners):
        barrier = pltpu.get_barrier_semaphore()
        for partner in partners:
            pl.semaphore_signal(barrier, inc=1, device_id=(partner,), device_id_type=MESH)
        pl.semaphore_wait(barrier, len(partners))

    def send(self, source, target, device):
        assert self.used < self.send_sem.shape[0]
        copy = pltpu.make_async_remote_copy(
            src_ref=source,
            dst_ref=target,
            send_sem=self.send_sem.at[self.used],
            recv_sem=self.recv_sem.at[self.used],
            device_id=(device,),
            device_id_type=MESH,
        )
        self.used += 1
        copy.start()
        self.pending.append(copy)
        return copy

    def local(self, source, target):
        assert self.local_used < self.local_sem.shape[0]
        copy = pltpu.make_async_copy(source, target, self.local_sem.at[self.local_used])
        self.local_used += 1
        copy.start()
        return copy

    def finish_sends(self):
        for copy in self.pending:
            copy.wait_send()
        self.pending = []


def arrived(copies):
    for copy in copies:
        copy.wait_recv()


ANY = pl.BlockSpec(memory_space=pl.ANY)
VMEM = pl.BlockSpec(memory_space=pltpu.VMEM)


def remote_call(body, name, collective_id, outs, in_specs, out_specs, scratch, sems, local_sems, vmem):
    return pl.pallas_call(
        body,
        out_shape=outs,
        in_specs=in_specs,
        out_specs=out_specs,
        scratch_shapes=[
            pltpu.SemaphoreType.DMA((sems,)),
            pltpu.SemaphoreType.DMA((sems,)),
            pltpu.SemaphoreType.DMA((max(local_sems, 1),)),
            *scratch,
        ],
        compiler_params=pltpu.CompilerParams(
            collective_id=collective_id, has_side_effects=True, vmem_limit_bytes=vmem
        ),
        name=name,
    )


def small_gather_body(planes, own_ref, out_ref, send_sem, recv_sem, local_sem):
    links = Links(planes, send_sem, recv_sem)
    links.greet(links.partners())
    z, y, x, c = links.z, links.y, links.x, links.c
    out_ref[z, y, x, c] = own_ref[...]
    spread(links, out_ref)
    links.finish_sends()


def spread(links, out_ref):
    z, y, x, c = links.z, links.y, links.x, links.c
    block = out_ref.at[z, y, x, c]
    arrived([links.send(block, block, links.plane_device(s)) for s in range(1, links.planes)])
    block = out_ref.at[:, y, x, c]
    arrived([links.send(block, block, links.across)])
    block = out_ref.at[:, :, x, c]
    arrived([links.send(block, block, links.beside)])
    block = out_ref.at[:, :, :, c]
    arrived([links.send(block, block, links.core)])


def small_gather(own, planes, collective_id):
    return remote_call(
        functools.partial(small_gather_body, planes),
        "small_gather",
        collective_id,
        jax.ShapeDtypeStruct((planes, 2, 2, 2, *own.shape), own.dtype),
        [VMEM],
        VMEM,
        [],
        planes + 2,
        0,
        40 * MIB,
    )(own)


class WeightGather:
    def __init__(self, links, shard, full, parts):
        self.links, self.shard, self.full = links, shard, full
        width = shard.shape[-1] // parts
        self.columns = [pl.ds(part * width, width) for part in range(parts)]
        z, y, x, c = links.z, links.y, links.x, links.c
        self.own = links.local(shard, full.at[z, y, x, c])
        self.own_there = False


def gather_first(weight, part):
    links, columns = weight.links, weight.columns[part]
    source = weight.shard.at[:, columns]
    target = weight.full.at[links.z, links.y, links.x, links.c, :, columns]
    return [links.send(source, target, links.plane_device(s)) for s in range(1, links.planes)]


def gather_second(weight, part, late):
    links, columns = weight.links, weight.columns[part]
    if not weight.own_there:
        weight.own.wait()
        weight.own_there = True
    block = weight.full.at[:, links.y, links.x, links.c, :, columns]
    late.append(links.send(block, block, links.core))
    return [links.send(block, block, links.beside if part % 2 == 0 else links.across)]


def gather_third(weight, part, late):
    links, columns = weight.links, weight.columns[part]
    y, x, c = links.y, links.x, links.c
    if part % 2 == 0:
        fresh = weight.full.at[:, y, 1 - x, c, :, columns]
        block, device = weight.full.at[:, y, :, c, :, columns], links.across
    else:
        fresh = weight.full.at[:, 1 - y, x, c, :, columns]
        block, device = weight.full.at[:, :, x, c, :, columns], links.beside
    late.append(links.send(fresh, fresh, links.core))
    return [links.send(block, block, device)]


def gather_fourth(weight, part, late):
    links, columns = weight.links, weight.columns[part]
    y, x, c = links.y, links.x, links.c
    if part % 2 == 0:
        fresh = weight.full.at[:, 1 - y, :, c, :, columns]
    else:
        fresh = weight.full.at[:, :, 1 - x, c, :, columns]
    late.append(links.send(fresh, fresh, links.core))


def gather_steps(pieces):
    count = len(pieces)
    late = []
    first, second, third = {}, {}, {}
    for k in range(min(2, count)):
        first[k] = gather_first(*pieces[k])
    yield
    for k in range(count + 4):
        if k < count:
            if k + 2 < count:
                first[k + 2] = gather_first(*pieces[k + 2])
            arrived(first.pop(k))
            second[k] = gather_second(*pieces[k], late)
        if 0 <= k - 2 < count:
            arrived(second.pop(k - 2))
            third[k - 2] = gather_third(*pieces[k - 2], late)
        if 0 <= k - 4 < count:
            arrived(third.pop(k - 4))
            gather_fourth(*pieces[k - 4], late)
        yield
    arrived(late)


def gather_body(planes, fused, *refs):
    tokens, attend, project, expand, contract, partial = refs[:6]
    refs = refs[6:]
    if fused:
        shift_ref, bias_ref = refs[:2]
        refs = refs[2:]
    attend_out, project_out, expand_out, contract_out, modulation_out = refs[:5]
    refs = refs[5:]
    if fused:
        first_out, qkv_out, heads_out, log_out, blended_out = refs[:5]
        refs = refs[5:]
    else:
        tokens_out = refs[0]
        refs = refs[1:]
    send_sem, recv_sem, local_sem, attend_held = refs[:4]
    sum_core, sum_beside, sum_across, sum_planes, total = refs[4:9]
    if fused:
        tokens_out = refs[9]
    links = Links(planes, send_sem, recv_sem, local_sem)
    corner = links.beside + 1 - 2 * links.c
    links.greet(links.partners() + ([corner] if fused else []))
    z, y, x, c = links.z, links.y, links.x, links.c

    weights = [
        WeightGather(links, project, project_out, 2),
        WeightGather(links, expand, expand_out, 4),
        WeightGather(links, contract, contract_out, 4),
    ]
    pieces = [(w, part) for w in weights for part in range(len(w.columns))]

    own_slice = links.local(attend.at[x, c], attend_out.at[z, y, x, c])
    to_core = links.send(attend.at[x, 1 - c], attend_out.at[z, y, x, c], links.core)
    held = links.send(attend.at[1 - x, 1 - c], attend_held, links.core)
    to_beside = links.send(attend.at[1 - x, c], attend_out.at[z, y, x, c], links.beside)
    own_tokens = links.local(tokens, tokens_out.at[:, x, c])
    tokens_core = links.send(tokens, tokens_out.at[:, x, c], links.core)
    tokens_beside = links.send(tokens, tokens_out.at[:, x, c], links.beside)
    step = links.send(partial.at[:, :, :, 1 - c], sum_core, links.core)

    arrived([held])
    held_beside = links.send(attend_held, attend_out.at[z, y, x, 1 - c], links.beside)
    steps = gather_steps(pieces)
    next(steps)

    arrived([step])
    sum_core[...] = sum_core[...] + partial[:, :, :, c]
    step = links.send(sum_core.at[:, :, 1 - x], sum_beside, links.beside)

    own_slice.wait()
    arrived([to_core, to_beside, held_beside])
    half = attend_out.shape[-1] // 2
    over_planes = []
    for part in range(2):
        block = attend_out.at[z, y, :, :, :, pl.ds(part * half, half)]
        over_planes.append(
            [links.send(block, block, links.plane_device(s)) for s in range(1, planes)]
        )

    arrived([step])
    sum_beside[...] = sum_beside[...] + sum_core[:, :, x]
    step = links.send(sum_beside.at[:, 1 - y], sum_across, links.across)

    over_y = []
    for part in range(2):
        arrived(over_planes[part])
        block = attend_out.at[:, y, :, :, :, pl.ds(part * half, half)]
        over_y.append(links.send(block, block, links.across))

    arrived([step])
    sum_across[...] = sum_across[...] + sum_beside[:, y]
    step = [
        links.send(sum_across.at[links.plane(s)], sum_planes.at[s - 1], links.plane_device(s))
        for s in range(1, planes)
    ]
    next(steps)

    arrived(step)
    result = sum_across[z]
    for s in range(1, planes):
        result = result + sum_planes[s - 1]
    total[...] = result
    modulation_out[x, c] = result
    step = [
        links.send(total, modulation_out.at[x, c], links.core),
        links.send(total, modulation_out.at[x, c], links.beside),
    ]
    next(steps)
    arrived(step)
    step = links.send(modulation_out.at[1 - x, c], modulation_out.at[1 - x, c], links.core)

    arrived([tokens_beside])
    fresh = tokens_out.at[:, 1 - x, c]
    tokens_late = links.send(fresh, fresh, links.core)
    if fused:
        next(steps)
        arrived([step, tokens_core, tokens_late, *over_y])
        own_tokens.wait()
        exchanged = []
        own_heads = pl.ds(pl.multiple_of((2 * x + c) * OWN, OWN), OWN)
        own_rows = tokens.shape[1]
        for m in range(tokens.shape[0]):
            project_tokens(
                m, tokens_out, attend_out, modulation_out, shift_ref, bias_ref, first_out, qkv_out
            )
            next(steps, None)
            for head in range(OWN // HEAD):
                attention_unit(qkv_out.at[m], heads_out.at[m], log_out.at[m], head)
                next(steps, None)
            target = blended_out.at[m, :, own_heads]

            def part_of(to_x, to_c, m=m):
                start = pl.multiple_of((2 * to_x + to_c) * own_rows, own_rows)
                return heads_out.at[m, pl.ds(start, own_rows)]

            exchanged += [
                links.send(part_of(1 - x, 1 - c), target, corner),
                links.send(part_of(1 - x, c), target, links.beside),
                links.send(part_of(x, 1 - c), target, links.core),
            ]
            own_part = links.local(part_of(x, c), target)
            own_part.wait()
        for _ in steps:
            pass
        arrived(exchanged)
    else:
        for _ in steps:
            pass
        arrived([step, tokens_core, tokens_late, *over_y])
        own_tokens.wait()
    links.finish_sends()


def modulation_row(modulation, m, block):
    per_quarter = modulation.shape[2] // MICROS
    pieces = []
    for k in range(block * D // LANES, (block + 1) * D // LANES):
        quarter, row = k // per_quarter, m * per_quarter + k % per_quarter
        pieces.append(modulation[quarter // 2, quarter % 2, row : row + 1, :])
    return jnp.concatenate(pieces, axis=1)


def project_tokens(m, tokens, attend, modulation, shift, bias, first_out, qkv_out):
    offsets = modulation_row(modulation, m, 0) + shift[0:1, :]
    factors = 1.0 + modulation_row(modulation, m, 1) + shift[1:2, :]
    rows = tokens.shape[3]

    @pl.loop(0, GROUP)
    def _(block):
        values = tokens[m, block // 2, block % 2].astype(jnp.float32)
        normed, _ = normalize(values)
        first = (normed * factors + offsets).astype(jnp.bfloat16)
        here = pl.ds(pl.multiple_of(block * rows, rows), rows)
        first_out[m, here, :] = first
        weights = attend[...].reshape(D, 3 * OWN)
        product = jnp.dot(first, weights, preferred_element_type=jnp.float32)
        qkv_out[m, here, :] = (product + bias[...]).astype(jnp.bfloat16)


def gather_all(tokens, attend, project, expand, contract, partial, planes, shift=None, bias=None):
    grid = (planes, 2, 2, 2)
    rows = partial.shape[-2]
    micros, own_rows, _ = tokens.shape
    latent_rows = own_rows * GROUP
    fused = shift is not None

    def full(shard):
        return jax.ShapeDtypeStruct((*grid, *shard.shape[-2:]), shard.dtype)

    def low(*shape):
        return jax.ShapeDtypeStruct(shape, jnp.bfloat16)

    outs = [
        full(attend),
        full(project),
        full(expand),
        full(contract),
        jax.ShapeDtypeStruct((2, 2, rows, LANES), jnp.float32),
    ]
    tokens_shape = (micros, 2, 2, own_rows, D)
    scratch = [
        pltpu.VMEM((attend.shape[-2], attend.shape[-1]), attend.dtype),
        pltpu.VMEM((planes, 2, 2, rows, LANES), jnp.float32),
        pltpu.VMEM((planes, 2, rows, LANES), jnp.float32),
        pltpu.VMEM((planes, rows, LANES), jnp.float32),
        pltpu.VMEM((planes - 1, rows, LANES), jnp.float32),
        pltpu.VMEM((rows, LANES), jnp.float32),
    ]
    in_specs = [ANY] * 5 + [VMEM]
    sems = 32 + 13 * (planes - 1) + 10 * 5
    args = (tokens, attend, project, expand, contract, partial)
    if fused:
        blocks = latent_rows // QUERY_ROWS
        outs += [
            low(micros, latent_rows, D),
            low(micros, latent_rows, 3 * OWN),
            low(micros, latent_rows, OWN),
            jax.ShapeDtypeStruct((micros, OWN // HEAD, blocks, 1, QUERY_ROWS), jnp.float32),
            low(micros, own_rows, D),
        ]
        in_specs += [VMEM] * 2
        out_specs = [VMEM] + [ANY] * 3 + [VMEM] * 6
        scratch.append(pltpu.VMEM(tokens_shape, tokens.dtype))
        args += (shift, bias)
    else:
        outs.append(low(*tokens_shape))
        out_specs = [ANY] * 4 + [VMEM, ANY]
    return remote_call(
        functools.partial(gather_body, planes, fused),
        "gather_all",
        1,
        tuple(outs),
        in_specs,
        tuple(out_specs),
        scratch,
        sems,
        8,
        56 * MIB,
    )(*args)


QUERY_ROWS = 256


def attention_unit(qkv, out, log, head):
    at = head * HEAD
    keys = qkv[:, OWN + at : OWN + at + HEAD]
    values_t = qkv[:, 2 * OWN + at : 2 * OWN + at + HEAD].T

    @pl.loop(0, qkv.shape[0] // QUERY_ROWS)
    def _(block):
        here = pl.ds(pl.multiple_of(block * QUERY_ROWS, QUERY_ROWS), QUERY_ROWS)
        queries = qkv[here, at : at + HEAD] * SCALE
        scores = lax.dot_general(
            keys, queries, (((1,), (1,)), ((), ())), preferred_element_type=jnp.float32
        )
        top = jnp.max(scores, axis=0, keepdims=True)
        weights = jnp.exp(scores - top)
        totals = jnp.sum(weights, axis=0, keepdims=True)
        blended = jnp.dot(
            values_t, weights.astype(jnp.bfloat16), preferred_element_type=jnp.float32
        )
        out[here, at : at + HEAD] = (blended / totals).T.astype(jnp.bfloat16)
        log[head, block] = top + jnp.log(totals)


def attention_body(qkv_ref, out_ref, log_ref):
    for head in range(OWN // HEAD):
        attention_unit(qkv_ref.at[0], out_ref.at[0], log_ref.at[0], head)


def attention(qkv):
    micros, rows, _ = qkv.shape
    heads = OWN // HEAD
    blocks = rows // 256
    return pl.pallas_call(
        attention_body,
        grid=(micros,),
        out_shape=(
            jax.ShapeDtypeStruct((micros, rows, OWN), jnp.bfloat16),
            jax.ShapeDtypeStruct((micros, heads, blocks, 1, 256), jnp.float32),
        ),
        in_specs=[pl.BlockSpec((1, rows, 3 * OWN), lambda m: (m, 0, 0))],
        out_specs=(
            pl.BlockSpec((1, rows, OWN), lambda m: (m, 0, 0)),
            pl.BlockSpec((1, heads, blocks, 1, 256), lambda m: (m, 0, 0, 0, 0)),
        ),
        compiler_params=pltpu.CompilerParams(vmem_limit_bytes=48 * MIB),
        name="attention",
    )(qkv)


def attention_back_unit(qkv, blended_all, grad_all, log, out, key_sum, value_sum, head):
    at = head * HEAD
    keys = qkv[:, OWN + at : OWN + at + HEAD]
    keys_t = keys.T
    values = qkv[:, 2 * OWN + at : 2 * OWN + at + HEAD]
    key_sum[...] = jnp.zeros_like(key_sum)
    value_sum[...] = jnp.zeros_like(value_sum)

    @pl.loop(0, qkv.shape[0] // QUERY_ROWS)
    def _(block):
        here = pl.ds(pl.multiple_of(block * QUERY_ROWS, QUERY_ROWS), QUERY_ROWS)
        queries = qkv[here, at : at + HEAD] * SCALE
        grads = grad_all[here, at : at + HEAD]
        blended = blended_all[here, at : at + HEAD]
        row_terms = jnp.sum(
            (grads.astype(jnp.float32) * blended.astype(jnp.float32)).T, axis=0, keepdims=True
        )
        scores = lax.dot_general(
            keys, queries, (((1,), (1,)), ((), ())), preferred_element_type=jnp.float32
        )
        chances = jnp.exp(scores - log[head, block])
        grad_chances = lax.dot_general(
            values, grads, (((1,), (1,)), ((), ())), preferred_element_type=jnp.float32
        )
        grad_scores = (chances * (grad_chances - row_terms)).astype(jnp.bfloat16)
        value_sum[...] += jnp.dot(
            chances.astype(jnp.bfloat16), grads, preferred_element_type=jnp.float32
        )
        key_sum[...] += jnp.dot(grad_scores, queries, preferred_element_type=jnp.float32)
        grad_queries = jnp.dot(keys_t, grad_scores, preferred_element_type=jnp.float32)
        out[here, at : at + HEAD] = (grad_queries.T * SCALE).astype(jnp.bfloat16)

    out[:, OWN + at : OWN + at + HEAD] = key_sum[...].astype(jnp.bfloat16)
    out[:, 2 * OWN + at : 2 * OWN + at + HEAD] = value_sum[...].astype(jnp.bfloat16)


def attention_back_body(qkv_ref, blended_ref, grad_ref, log_ref, out_ref, key_sum, value_sum):
    for head in range(OWN // HEAD):
        attention_back_unit(
            qkv_ref.at[0],
            blended_ref.at[0],
            grad_ref.at[0],
            log_ref.at[0],
            out_ref.at[0],
            key_sum,
            value_sum,
            head,
        )


def attention_back(qkv, blended, grads, logs):
    micros, rows, _ = qkv.shape
    heads = OWN // HEAD
    blocks = rows // 256
    wide = pl.BlockSpec((1, rows, 3 * OWN), lambda m: (m, 0, 0))
    narrow = pl.BlockSpec((1, rows, OWN), lambda m: (m, 0, 0))
    return pl.pallas_call(
        attention_back_body,
        grid=(micros,),
        out_shape=jax.ShapeDtypeStruct((micros, rows, 3 * OWN), jnp.bfloat16),
        in_specs=[
            wide,
            narrow,
            narrow,
            pl.BlockSpec((1, heads, blocks, 1, 256), lambda m: (m, 0, 0, 0, 0)),
        ],
        out_specs=wide,
        scratch_shapes=[pltpu.VMEM((rows, HEAD), jnp.float32)] * 2,
        compiler_params=pltpu.CompilerParams(vmem_limit_bytes=48 * MIB),
        name="attention_back",
    )(qkv, blended, grads, logs)


def heads_to_tokens_body(blended, out, send_sem, recv_sem, local_sem):
    links = Links(1, send_sem, recv_sem, local_sem)
    x, c = links.x, links.c
    corner = links.beside + 1 - 2 * c
    links.greet([links.core, links.beside, corner])
    target = out.at[:, :, pl.ds(pl.multiple_of((2 * x + c) * OWN, OWN), OWN)]
    own = links.local(blended.at[:, x, c], target)
    copies = [
        links.send(blended.at[:, 1 - x, 1 - c], target, corner),
        links.send(blended.at[:, 1 - x, c], target, links.beside),
        links.send(blended.at[:, x, 1 - c], target, links.core),
    ]
    arrived(copies)
    own.wait()
    links.finish_sends()


def heads_to_tokens(blended):
    micros, rows, _ = blended.shape
    own_rows = rows // GROUP
    return remote_call(
        heads_to_tokens_body,
        "heads_to_tokens",
        2,
        jax.ShapeDtypeStruct((micros, own_rows, D), blended.dtype),
        [ANY],
        ANY,
        [],
        3,
        1,
        40 * MIB,
    )(blended.reshape(micros, 2, 2, own_rows, OWN))


def tokens_to_heads_body(grads, out, send_sem, recv_sem, local_sem):
    links = Links(1, send_sem, recv_sem, local_sem)
    x, c = links.x, links.c
    corner = links.beside + 1 - 2 * c
    links.greet([links.core, links.beside, corner])

    def columns(to_x, to_c):
        return grads.at[:, :, pl.ds(pl.multiple_of((2 * to_x + to_c) * OWN, OWN), OWN)]

    target = out.at[:, x, c]
    own = links.local(columns(x, c), target)
    copies = [
        links.send(columns(1 - x, 1 - c), target, corner),
        links.send(columns(1 - x, c), target, links.beside),
        links.send(columns(x, 1 - c), target, links.core),
    ]
    arrived(copies)
    own.wait()
    links.finish_sends()


def tokens_to_heads(grads):
    micros, own_rows, _ = grads.shape
    return remote_call(
        tokens_to_heads_body,
        "tokens_to_heads",
        3,
        jax.ShapeDtypeStruct((micros, 2, 2, own_rows, OWN), grads.dtype),
        [ANY],
        ANY,
        [],
        3,
        1,
        40 * MIB,
    )(grads).reshape(micros, GROUP * own_rows, OWN)


def token_sums_body(partial, out, send_sem, recv_sem, local_sem, from_core, own, from_beside):
    links = Links(1, send_sem, recv_sem, local_sem)
    x, c = links.x, links.c
    links.greet([links.core, links.beside])
    far = links.send(partial.at[:, 1 - x, 1 - c], from_core.at[0], links.core)
    near = links.send(partial.at[:, x, 1 - c], from_core.at[1], links.core)
    loads = [
        links.local(partial.at[:, 1 - x, c], own.at[0]),
        links.local(partial.at[:, x, c], own.at[1]),
    ]
    micros = out.shape[0]
    loads[0].wait()
    arrived([far])
    passed = []
    for m in range(micros):
        own[0, m] = (
            own[0, m].astype(jnp.float32) + from_core[0, m].astype(jnp.float32)
        ).astype(jnp.bfloat16)
        passed.append(links.send(own.at[0, m], from_beside.at[m], links.beside))
    loads[1].wait()
    arrived([near])
    for m in range(micros):
        out[m] = own[1, m].astype(jnp.float32) + from_core[1, m].astype(jnp.float32)
    for m in range(micros):
        arrived([passed[m]])
        out[m] += from_beside[m].astype(jnp.float32)
    links.finish_sends()


def token_sums(partial):
    micros, rows, width = partial.shape
    own_rows = rows // GROUP
    held = pltpu.VMEM((2, micros, own_rows, width), partial.dtype)
    return remote_call(
        token_sums_body,
        "token_sums",
        4,
        jax.ShapeDtypeStruct((micros, own_rows, width), jnp.float32),
        [ANY],
        VMEM,
        [held, held, pltpu.VMEM((micros, own_rows, width), partial.dtype)],
        4,
        2,
        40 * MIB,
    )(partial.reshape(micros, 2, 2, own_rows, width))


def small_sums_body(planes, partial, out, send_sem, recv_sem, local_sem, from_core, from_beside):
    links = Links(planes, send_sem, recv_sem)
    links.greet(links.partners())
    z, y, x, c = links.z, links.y, links.x, links.c
    arrived([links.send(partial.at[:, 1 - c], from_core, links.core)])
    from_core[...] = from_core[...] + partial[:, c]
    arrived([links.send(from_core.at[1 - x], from_beside, links.beside)])
    out[z, y, x, c] = from_core[x] + from_beside[...]
    spread(links, out)
    links.finish_sends()


def small_sums(partial, planes):
    block = partial.shape[2:]
    return remote_call(
        functools.partial(small_sums_body, planes),
        "small_sums",
        5,
        jax.ShapeDtypeStruct((planes, 2, 2, 2, *block), jnp.float32),
        [VMEM],
        VMEM,
        [pltpu.VMEM((2, *block), jnp.float32), pltpu.VMEM(block, jnp.float32)],
        planes + 4,
        0,
        40 * MIB,
    )(partial)


class SumPiece:
    def __init__(self, links, grads, out, columns, part, scratch):
        self.links, self.grads, self.out = links, grads, out
        self.columns, self.part = columns, part
        self.own, self.first, self.second, self.third, self.fourth = scratch


def add_blocks(target, left, right, count):
    @pl.loop(0, count)
    def _(i):
        target(i)[...] = (
            left(i)[...].astype(jnp.float32) + right(i)[...].astype(jnp.float32)
        ).astype(jnp.bfloat16)


def sum_first(piece):
    links = piece.links
    c = links.c
    source = piece.grads.at[:, :, :, 1 - c, :, piece.columns]
    sent = links.send(source, piece.first, links.core)
    loaded = links.local(piece.grads.at[:, :, :, c, :, piece.columns], piece.own)
    return sent, loaded


def sum_second(piece, before):
    links = piece.links
    x, y, planes = links.x, links.y, links.planes
    sent, loaded = before
    loaded.wait()
    arrived([sent])
    own, first = piece.own, piece.first
    turn = piece.part % 2 == 0
    for order in range(2):

        def at(ref):
            def block(i):
                z, other = i // 2, i % 2
                if turn:
                    return ref.at[z, other, (1 - x) if order == 0 else x]
                return ref.at[z, (1 - y) if order == 0 else y, other]

            return block

        add_blocks(at(own), at(own), at(first), planes * 2)
        if order == 0:
            source = own.at[:, :, 1 - x] if turn else own.at[:, 1 - y]
            copy = links.send(source, piece.second, links.beside if turn else links.across)
    return copy


def sum_third(piece, before):
    links = piece.links
    x, y, planes = links.x, links.y, links.planes
    arrived([before])
    own, second = piece.own, piece.second
    turn = piece.part % 2 == 0
    for order in range(2):
        if turn:
            away = (1 - y) if order == 0 else y

            def kept(i):
                return own.at[i, away, x]

        else:
            away = (1 - x) if order == 0 else x

            def kept(i):
                return own.at[i, y, away]

        def came(i):
            return second.at[i, away]

        add_blocks(came, kept, came, planes)
        if order == 0:
            copy = links.send(
                second.at[:, away], piece.third, links.across if turn else links.beside
            )
    return copy


def sum_fourth(piece, before):
    links = piece.links
    x, y, z, planes = links.x, links.y, links.z, links.planes
    arrived([before])
    second, third = piece.second, piece.third
    stay = y if piece.part % 2 == 0 else x

    def kept(i):
        return second.at[i, stay]

    def came(i):
        return third.at[i]

    add_blocks(came, kept, came, planes)
    return [
        links.send(third.at[links.plane(s)], piece.fourth.at[s - 1], links.plane_device(s))
        for s in range(1, planes)
    ]


def sum_last(piece, before):
    links = piece.links
    arrived(before)
    result = piece.third[links.z].astype(jnp.float32)
    for s in range(1, links.planes):
        result = result + piece.fourth[s - 1].astype(jnp.float32)
    piece.out[:, piece.columns] = result


def sum_steps(pieces):
    count = len(pieces)
    stages = (sum_second, sum_third, sum_fourth, sum_last)
    state = {}
    for k in range(count + 5):
        if k < count:
            state[k] = sum_first(pieces[k])
        yield
        for stage, run in enumerate(stages):
            j = k - 1 - stage
            if 0 <= j < count:
                state[j] = run(pieces[j], state[j])
        yield


class AttendSums:
    def __init__(self, links, grads, out, scratch):
        self.links, self.grads, self.out = links, grads, out
        self.own, self.over_y, self.over_planes, self.sum, self.held = scratch

    def start(self):
        links = self.links
        self.step = links.send(self.grads.at[:, 1 - links.y], self.over_y, links.across)
        self.loaded = links.local(self.grads.at[:, links.y], self.own)

    def planes(self):
        links, own, over_y = self.links, self.own, self.over_y
        self.loaded.wait()
        arrived([self.step])
        for i in range(2):

            def block(ref, i=i):
                return lambda k: ref.at[k // 2, i, k % 2]

            add_blocks(block(own), block(own), block(over_y), links.planes * 2)
        self.step = [
            links.send(own.at[links.plane(s)], self.over_planes.at[s - 1], links.plane_device(s))
            for s in range(1, links.planes)
        ]

    def owners(self):
        links = self.links
        x, c = links.x, links.c
        arrived(self.step)
        for i in range(2):
            for j in range(2):
                result = self.own[links.z, i, j].astype(jnp.float32)
                for s in range(1, links.planes):
                    result = result + self.over_planes[s - 1, i, j].astype(jnp.float32)
                self.sum[i, j] = result
        self.beside = links.send(self.sum.at[1 - x], self.held, links.beside)
        self.near = links.send(self.sum.at[x, 1 - c], self.out.at[x, c], links.core)
        self.out[x, c] = self.sum[x, c]

    def last(self):
        links = self.links
        x, c = links.x, links.c
        arrived([self.beside])
        self.out[1 - x, c] = self.held[c]
        self.far = links.send(self.held.at[1 - c], self.out.at[1 - x, c], links.core)

    def finish(self):
        arrived([self.near, self.far])


class TokenSums:
    def __init__(self, links, partial, out, scratch):
        self.links, self.partial, self.out = links, partial, out
        self.from_core, self.from_beside = scratch
        self.state = {}

    def start(self, m):
        links, partial = self.links, self.partial
        x, c = links.x, links.c
        self.state[m] = [
            links.send(partial.at[m, 1 - x, 1 - c], self.from_core.at[0, m], links.core),
            links.send(partial.at[m, x, 1 - c], self.from_core.at[1, m], links.core),
        ]

    def middle(self, m):
        links, partial = self.links, self.partial
        x, c = links.x, links.c
        arrived(self.state[m])
        away = partial.at[m, 1 - x, c]
        away[...] = (
            away[...].astype(jnp.float32) + self.from_core[0, m].astype(jnp.float32)
        ).astype(jnp.bfloat16)
        self.state[m] = [links.send(away, self.from_beside.at[m], links.beside)]

    def finish(self, m):
        links = self.links
        arrived(self.state[m])
        self.out[m] = (
            self.partial[m, links.x, links.c].astype(jnp.float32)
            + self.from_core[1, m].astype(jnp.float32)
            + self.from_beside[m].astype(jnp.float32)
        )


def sums_body(planes, plan, *refs):
    attend, refs = refs[0], refs[1:]
    grads, attend_out, outs = refs[: len(plan)], refs[len(plan)], refs[len(plan) + 1 :][: len(plan)]
    refs = refs[2 * len(plan) + 1 :]
    links = Links(planes, *refs[:3])
    links.greet(links.partners())
    attend_sums = AttendSums(links, attend, attend_out, refs[3:8])
    attend_sums.start()
    steps = sum_steps(sum_pieces(links, plan, grads, outs, refs[8:]))
    next(steps)
    next(steps)
    attend_sums.planes()
    next(steps)
    next(steps)
    attend_sums.owners()
    next(steps)
    next(steps)
    attend_sums.last()
    for _ in steps:
        pass
    attend_sums.finish()
    links.finish_sends()


def sum_pieces(links, plan, grads, outs, scratch):
    pieces = []
    for parts, grad, out in zip(plan, grads, outs):
        width = grad.shape[-1] // parts
        for part in range(parts):
            columns = pl.ds(part * width, width)
            used = 5 * len(pieces)
            pieces.append(SumPiece(links, grad, out, columns, part, scratch[used : used + 5]))
    return pieces


def advance(steps, count):
    for _ in range(count):
        next(steps, None)


def back_body(planes, plan, *refs):
    kinds = len(plan)
    grads, refs = refs[:kinds], refs[kinds:]
    grad_blended, qkv, heads, logs, first, attend, refs = *refs[:6], refs[6:]
    attend_out, outs, refs = refs[0], refs[1 : 1 + kinds], refs[1 + kinds :]
    first_out, bias_out, refs = refs[0], refs[1], refs[2:]
    links = Links(planes, *refs[:3])
    refs = refs[3:]
    attend_scratch, refs = refs[:5], refs[5:]
    piece_scratch, refs = refs[: 5 * sum(plan)], refs[5 * sum(plan) :]
    grad_heads, grad_qkv, key_sum, value_sum, attend_grads, partial, *token_scratch = refs
    x, c = links.x, links.c
    corner = links.beside + 1 - 2 * c
    links.greet([*links.partners(), corner])
    micros, latent_rows, _ = qkv.shape
    own_rows = latent_rows // GROUP

    here = pl.ds(pl.multiple_of((2 * x + c) * own_rows, own_rows), own_rows)
    exchanged = []
    for m in range(micros):

        def columns(to_x, to_c, m=m):
            return grad_blended.at[m, :, pl.ds(pl.multiple_of((2 * to_x + to_c) * OWN, OWN), OWN)]

        target = grad_heads.at[m, here]
        copies = [
            links.send(columns(1 - x, 1 - c), target, corner),
            links.send(columns(1 - x, c), target, links.beside),
            links.send(columns(x, 1 - c), target, links.core),
        ]
        exchanged.append((copies, links.local(columns(x, c), target)))

    steps = sum_steps(sum_pieces(links, plan, grads, outs, piece_scratch))
    attend_sums = AttendSums(links, attend_grads, attend_out, attend_scratch)
    token_sum = TokenSums(links, partial, first_out, token_scratch)
    advance(steps, 3)
    for m in range(micros):
        copies, own = exchanged[m]
        arrived(copies)
        own.wait()
        for head in range(OWN // HEAD):
            attention_back_unit(
                qkv.at[m],
                heads.at[m],
                grad_heads.at[m],
                logs.at[m],
                grad_qkv.at[m],
                key_sum,
                value_sum,
                head,
            )
            advance(steps, 2)
        if m == micros - 1:
            attend_product(first, grad_qkv, attend_grads, planes)
            attend_sums.start()
            advance(steps, 1)
        first_product(m, grad_qkv, attend, partial)
        token_sum.start(m)
        advance(steps, 1)
        token_sum.middle(m)
    attend_sums.planes()
    total = jnp.zeros((1, grad_qkv.shape[-1]), jnp.float32)
    for m in range(micros):
        total = total + jnp.sum(grad_qkv[m].astype(jnp.float32), axis=0, keepdims=True)
    bias_out[...] = total
    advance(steps, 2)
    for m in range(micros):
        token_sum.finish(m)
    attend_sums.owners()
    advance(steps, 2)
    attend_sums.last()
    for _ in steps:
        pass
    attend_sums.finish()
    links.finish_sends()


def attend_product(first, grad_qkv, out, planes):
    width = D // planes

    @pl.loop(0, planes)
    def _(plane):
        columns = pl.ds(pl.multiple_of(plane * width, width), width)
        total = None
        for m in range(first.shape[0]):
            product = lax.dot_general(
                first[m, :, columns],
                grad_qkv[m],
                (((0,), (0,)), ((), ())),
                preferred_element_type=jnp.float32,
            )
            total = product if total is None else total + product
        out[plane] = total.astype(jnp.bfloat16).reshape(out.shape[1:])


def first_product(m, grad_qkv, attend, partial):
    rows = partial.shape[3]

    @pl.loop(0, GROUP)
    def _(block):
        here = pl.ds(pl.multiple_of(block * rows, rows), rows)
        product = lax.dot_general(
            grad_qkv[m, here, :],
            attend[...].reshape(D, 3 * OWN),
            (((1,), (1,)), ((), ())),
            preferred_element_type=jnp.float32,
        )
        partial[m, block // 2, block % 2] = product.astype(jnp.bfloat16)


def sums_scratch(rows, width, weights, plan, planes):
    scratch = [
        pltpu.VMEM((planes, 2, 2, rows, width), jnp.bfloat16),
        pltpu.VMEM((planes, 2, 2, rows, width), jnp.bfloat16),
        pltpu.VMEM((planes - 1, 2, 2, rows, width), jnp.bfloat16),
        pltpu.VMEM((2, 2, rows, width), jnp.float32),
        pltpu.VMEM((2, rows, width), jnp.float32),
    ]
    for grad, parts in zip(weights, plan):
        rows, width = grad.shape[-2], grad.shape[-1] // parts
        for _ in range(parts):
            scratch += [
                pltpu.VMEM((planes, 2, 2, rows, width), jnp.bfloat16),
                pltpu.VMEM((planes, 2, 2, rows, width), jnp.bfloat16),
                pltpu.VMEM((planes, 2, rows, width), jnp.bfloat16),
                pltpu.VMEM((planes, rows, width), jnp.bfloat16),
                pltpu.VMEM((planes - 1, rows, width), jnp.bfloat16),
            ]
    return scratch


def sums_outs(rows, width, weights):
    return (
        jax.ShapeDtypeStruct((2, 2, rows, width), jnp.float32),
        *(jax.ShapeDtypeStruct(grad.shape[-2:], jnp.float32) for grad in weights),
    )


def weight_sums(attend, weights, plan, planes):
    rows, width = attend.shape[-2:]
    return remote_call(
        functools.partial(sums_body, planes, plan),
        "weight_sums",
        6,
        sums_outs(rows, width, weights),
        [ANY] * (1 + len(weights)),
        (VMEM,) * (1 + len(weights)),
        sums_scratch(rows, width, weights, plan, planes),
        8 + planes + sum(plan) * (2 + planes),
        2 + sum(plan),
        60 * MIB,
    )(attend, *weights)


def back_and_sums(weights, grad_blended, qkv, heads, logs, first, attend, plan, planes):
    rows, width = attend.shape[-2:]
    micros, own_rows, _ = grad_blended.shape
    latent_rows = own_rows * GROUP

    def low(*shape):
        return pltpu.VMEM(shape, jnp.bfloat16)

    return remote_call(
        functools.partial(back_body, planes, plan),
        "back_and_sums",
        6,
        (
            *sums_outs(rows, width, weights),
            jax.ShapeDtypeStruct((micros, own_rows, D), jnp.float32),
            jax.ShapeDtypeStruct((1, width), jnp.float32),
        ),
        [ANY] * len(weights) + [VMEM] * 6,
        (VMEM,) * (3 + len(weights)),
        [
            *sums_scratch(rows, width, weights, plan, planes),
            low(micros, latent_rows, OWN),
            low(micros, latent_rows, width),
            pltpu.VMEM((latent_rows, HEAD), jnp.float32),
            pltpu.VMEM((latent_rows, HEAD), jnp.float32),
            low(*attend.shape),
            low(micros, 2, 2, own_rows, D),
            low(2, micros, own_rows, D),
            low(micros, own_rows, D),
        ],
        24 + planes + sum(plan) * (2 + planes),
        4 + sum(plan),
        63 * MIB,
    )(*weights, grad_blended, qkv, heads, logs, first, attend)


def normalize(values):
    center = values - jnp.mean(values, axis=-1, keepdims=True)
    spread_of = jnp.mean(center * center, axis=-1, keepdims=True)
    scale = lax.rsqrt(spread_of + epsilon)
    return center * scale, scale


def norm_back(grads, normed, scale, factors):
    inner = grads * (1.0 + factors)
    return scale * (
        inner
        - jnp.mean(inner, axis=-1, keepdims=True)
        - normed * jnp.mean(inner * normed, axis=-1, keepdims=True)
    )


def einsum(spec, left, right):
    return jnp.einsum(spec, left, right, preferred_element_type=jnp.float32)


def per_device(tokens, condition, attend, project, expand, contract, modulate, biases, cotangent):
    devices = lax.axis_size("fsdp")
    planes = devices // 8
    latents = devices // GROUP
    me = lax.axis_index("fsdp")
    quarter, latent = me % GROUP, me // GROUP
    micros, own_rows, _ = tokens.shape
    latent_rows = own_rows * GROUP
    rows = D // devices
    grid = (planes, 2, 2, 2)

    held = jnp.concatenate([condition.reshape(-1), biases]).astype(jnp.float32)
    held = jnp.pad(held, (0, -held.size % (8 * LANES)))
    small = small_gather(held.reshape(-1, LANES), planes, 0).reshape(devices, -1)
    conditions = small[:, : condition.size].reshape(latents, GROUP, micros, -1)
    conditions = conditions.transpose(2, 0, 1, 3).reshape(micros * latents, D)
    cond_act = silu(conditions).astype(jnp.bfloat16)
    bias_all = small[:, condition.size : condition.size + biases.size].reshape(-1)
    bias_query = bias_all[0:D]
    bias_value = bias_all[D : 2 * D]
    bias_project = bias_all[2 * D : 3 * D]
    bias_expand = bias_all[3 * D : 3 * D + FF]
    bias_contract = bias_all[3 * D + FF : 4 * D + FF]
    bias_modulate = bias_all[4 * D + FF :]

    modulate_rows = modulate.reshape(rows, 6 * D)
    cond_own = lax.dynamic_slice_in_dim(cond_act, me * rows, rows, axis=1)
    partial = jnp.dot(cond_own, modulate_rows, preferred_element_type=jnp.float32)
    partial = partial.reshape(micros, latents, GROUP, -1).transpose(1, 2, 0, 3)
    partial = partial.reshape(planes, 2, 2, 2, -1, LANES)

    attend_shard = attend.reshape(rows, 3, 2, 2, OWN).transpose(2, 3, 0, 1, 4)
    bias_row = jnp.concatenate(
        [
            lax.dynamic_slice_in_dim(bias_query, quarter * OWN, OWN),
            jnp.zeros((OWN,), jnp.float32),
            lax.dynamic_slice_in_dim(bias_value, quarter * OWN, OWN),
        ]
    )
    fused = rows % 16 == 0 and own_rows % QUERY_ROWS == 0
    extras = (bias_modulate.reshape(6, D)[:2], bias_row[None]) if fused else ()
    attend_all, project_all, expand_all, contract_all, modulation_all, *rest = gather_all(
        tokens,
        attend_shard.reshape(2, 2, rows, 3 * OWN),
        project.reshape(rows, D),
        expand.reshape(rows, FF),
        contract.reshape(FF // devices, D),
        partial,
        planes,
        *extras,
    )
    attend_own = attend_all.reshape(D, 3 * OWN)
    project_full = project_all.reshape(D, D)
    expand_full = expand_all.reshape(D, FF)
    contract_full = contract_all.reshape(FF, D)
    modulation = modulation_all.reshape(GROUP, micros, -1).transpose(1, 0, 2)
    modulation = modulation.reshape(micros, 6 * D) + bias_modulate
    offsets_one, factors_one, gates_one, offsets_two, factors_two, gates_two = (
        modulation[:, None, part * D : (part + 1) * D] for part in range(6)
    )

    if fused:
        first, projected, blended_heads, logs, blended = rest
    else:
        tokens_latent = rest[0].reshape(micros, latent_rows, D)
        normed_latent, _ = normalize(tokens_latent.astype(jnp.float32))
        first = (normed_latent * (1.0 + factors_one) + offsets_one).astype(jnp.bfloat16)
        projected = (einsum("mrd,de->mre", first, attend_own) + bias_row).astype(jnp.bfloat16)
        blended_heads, logs = attention(projected)
        blended = heads_to_tokens(blended_heads)

    inputs = tokens.astype(jnp.float32)
    attended = einsum("mrd,de->mre", blended, project_full) + bias_project
    middle = inputs + gates_one * attended
    normed_two, scale_two = normalize(middle)
    second = (normed_two * (1.0 + factors_two) + offsets_two).astype(jnp.bfloat16)
    hidden = einsum("mrd,de->mre", second, expand_full) + bias_expand
    activated, gelu_pull = jax.vjp(lambda v: jax.nn.gelu(v, approximate=True), hidden)
    act_low = activated.astype(jnp.bfloat16)
    branch = einsum("mrd,de->mre", act_low, contract_full) + bias_contract
    output = (middle + gates_two * branch).astype(jnp.bfloat16)

    upstream = cotangent.astype(jnp.float32)
    grad_branch = (gates_two * upstream).astype(jnp.bfloat16)
    grad_gates_two = jnp.sum(upstream * branch, axis=1)
    grad_contract = einsum("mrd,mre->de", act_low, grad_branch)
    grad_act = einsum("mre,de->mrd", grad_branch, contract_full)
    grad_hidden = gelu_pull(grad_act)[0].astype(jnp.bfloat16)
    grad_expand = einsum("mrd,mre->de", second, grad_hidden)
    grad_second = einsum("mre,de->mrd", grad_hidden, expand_full)
    grad_middle = upstream + norm_back(grad_second, normed_two, scale_two, factors_two)
    grad_attended = (gates_one * grad_middle).astype(jnp.bfloat16)
    grad_gates_one = jnp.sum(grad_middle * attended, axis=1)
    grad_project = einsum("mrd,mre->de", blended, grad_attended)
    grad_blended = einsum("mre,de->mrd", grad_attended, project_full).astype(jnp.bfloat16)
    weights = (
        grad_contract.astype(jnp.bfloat16).reshape(*grid, FF // devices, D),
        grad_expand.astype(jnp.bfloat16).reshape(*grid, rows, FF),
        grad_project.astype(jnp.bfloat16).reshape(*grid, rows, D),
    )
    plan = (4, 4, 2)
    if fused:
        attend_sum, contract_sum, expand_sum, project_sum, grad_first, heads_sum = back_and_sums(
            weights, grad_blended, projected, blended_heads, logs, first, attend_all, plan, planes
        )
        heads_sum = heads_sum[0]
    else:
        grad_heads = tokens_to_heads(grad_blended)
        grad_projected = attention_back(projected, blended_heads, grad_heads, logs)
        grad_attend = einsum("mrd,mre->de", first, grad_projected)
        grad_first = token_sums(
            einsum("mre,de->mrd", grad_projected, attend_own).astype(jnp.bfloat16)
        )
        heads_sum = jnp.sum(grad_projected, axis=(0, 1), dtype=jnp.float32)
        attend_sum, contract_sum, expand_sum, project_sum = weight_sums(
            grad_attend.astype(jnp.bfloat16).reshape(*grid, rows, 3 * OWN), weights, plan, planes
        )
    normed_one, scale_one = normalize(inputs)
    grad_tokens = grad_middle + norm_back(grad_first, normed_one, scale_one, factors_one)

    grad_modulation = jnp.concatenate(
        [
            jnp.sum(grad_first, axis=1),
            jnp.sum(grad_first * normed_one, axis=1),
            grad_gates_one,
            jnp.sum(grad_second, axis=1),
            jnp.sum(grad_second * normed_two, axis=1),
            grad_gates_two,
        ],
        axis=1,
    )

    def token_sum(values):
        return jnp.sum(values, axis=(0, 1), dtype=jnp.float32)

    bias_terms = jnp.concatenate(
        [
            lax.dynamic_update_slice(
                jnp.zeros((D,), jnp.float32), heads_sum[:OWN], (quarter * OWN,)
            ),
            lax.dynamic_update_slice(
                jnp.zeros((D,), jnp.float32), heads_sum[2 * OWN :], (quarter * OWN,)
            ),
            token_sum(grad_attended),
            token_sum(grad_hidden),
            token_sum(grad_branch),
        ]
    )
    to_sum = jnp.concatenate(
        [
            grad_modulation.reshape(micros, GROUP, -1).transpose(1, 0, 2).reshape(GROUP, -1),
            bias_terms.reshape(GROUP, -1),
        ],
        axis=1,
    )
    sums = small_sums(to_sum.reshape(2, 2, -1, LANES), planes).reshape(latents, GROUP, -1)
    split = micros * 6 * D // GROUP
    grad_modulations = sums[:, :, :split].reshape(latents, GROUP, micros, -1)
    grad_modulations = grad_modulations.transpose(2, 0, 1, 3).reshape(micros * latents, 6 * D)
    bias_sums = jnp.concatenate(
        [jnp.sum(sums[:, :, split:], axis=0).reshape(-1), jnp.sum(grad_modulations, axis=0)]
    )
    grad_biases = lax.dynamic_slice_in_dim(bias_sums, me * biases.size, biases.size)
    grad_modulate = lax.dot_general(
        cond_own.astype(jnp.float32),
        grad_modulations,
        (((0,), (0,)), ((), ())),
        precision=highest,
    )
    grad_cond_cols = lax.dot_general(
        grad_modulations,
        modulate_rows.astype(jnp.float32),
        (((1,), (1,)), ((), ())),
        precision=highest,
    )
    cols = grad_cond_cols.reshape(-1)
    cols = jnp.pad(cols, (0, -cols.size % (8 * LANES)))
    cols_all = small_gather(cols.reshape(-1, LANES), planes, 7).reshape(devices, -1)
    cols_all = cols_all[:, : micros * latents * rows].reshape(devices, micros, latents, rows)
    cols_own = lax.dynamic_index_in_dim(cols_all, latent, axis=2, keepdims=False)
    width = D // GROUP
    cols_own = lax.dynamic_slice_in_dim(
        cols_own, quarter * (devices // GROUP), devices // GROUP, axis=0
    )
    grad_silu = cols_own.transpose(1, 0, 2).reshape(micros, width)
    values = condition.astype(jnp.float32)
    gate = 1.0 / (1.0 + jnp.exp(-values))
    grad_condition = gate * (1.0 + values * (1.0 - gate)) * grad_silu

    attend_sum = attend_sum.reshape(2, 2, rows, 3, OWN).transpose(2, 3, 0, 1, 4)
    return (
        output,
        grad_tokens,
        grad_condition,
        attend_sum.reshape(-1),
        project_sum.reshape(-1),
        expand_sum.reshape(-1),
        contract_sum.reshape(-1),
        grad_modulate.reshape(-1),
        grad_biases,
    )


def solution(mesh):
    in_specs = (
        P(None, "fsdp", None),
        P(None, "fsdp"),
        P("fsdp"),
        P("fsdp"),
        P("fsdp"),
        P("fsdp"),
        P("fsdp"),
        P("fsdp"),
        P(None, "fsdp", None),
    )
    out_specs = (
        P(None, "fsdp", None),
        P(None, "fsdp", None),
        P(None, "fsdp"),
        P("fsdp"),
        P("fsdp"),
        P("fsdp"),
        P("fsdp"),
        P("fsdp"),
        P("fsdp"),
    )
    return jax.shard_map(
        per_device, mesh=mesh, in_specs=in_specs, out_specs=out_specs, check_vma=False
    )
```

```python
import functools

import jax
import jax.numpy as jnp
from jax import lax
from jax.experimental import pallas as pl
from jax.experimental.pallas import tpu as pltpu
from jax.sharding import PartitionSpec as P

D = 1024
HEADS = 16
HEAD = 64
FF = 4096
GROUP = 4
OWN = D // GROUP
SCALE = HEAD**-0.5
LANES = 128
MICROS = 2

epsilon = 1e-06
highest = lax.Precision.HIGHEST
MESH = pl.DeviceIdType.MESH
MIB = 1 << 20


def silu(values):
    return values / (1.0 + jnp.exp(-values))


class Links:
    def __init__(self, planes, send_sem, recv_sem, local_sem=None):
        me = lax.axis_index("fsdp")
        self.planes = planes
        self.c = me % 2
        self.x = (me // 2) % 2
        self.y = (me // 4) % 2
        self.z = me // 8
        self.core = me + 1 - 2 * self.c
        self.beside = me + 2 - 4 * self.x
        self.across = me + 4 - 8 * self.y
        self.place = me % 8
        self.send_sem, self.recv_sem, self.local_sem = send_sem, recv_sem, local_sem
        self.used = 0
        self.local_used = 0
        self.pending = []

    def plane(self, step):
        return (self.z + step) % self.planes

    def plane_device(self, step):
        return self.plane(step) * 8 + self.place

    def partners(self):
        return [self.core, self.beside, self.across] + [
            self.plane_device(step) for step in range(1, self.planes)
        ]

    def greet(self, partners):
        barrier = pltpu.get_barrier_semaphore()
        for partner in partners:
            pl.semaphore_signal(barrier, inc=1, device_id=(partner,), device_id_type=MESH)
        pl.semaphore_wait(barrier, len(partners))

    def send(self, source, target, device):
        assert self.used < self.send_sem.shape[0]
        copy = pltpu.make_async_remote_copy(
            src_ref=source,
            dst_ref=target,
            send_sem=self.send_sem.at[self.used],
            recv_sem=self.recv_sem.at[self.used],
            device_id=(device,),
            device_id_type=MESH,
        )
        self.used += 1
        copy.start()
        self.pending.append(copy)
        return copy

    def local(self, source, target):
        assert self.local_used < self.local_sem.shape[0]
        copy = pltpu.make_async_copy(source, target, self.local_sem.at[self.local_used])
        self.local_used += 1
        copy.start()
        return copy

    def finish_sends(self):
        for copy in self.pending:
            copy.wait_send()
        self.pending = []


def arrived(copies):
    for copy in copies:
        copy.wait_recv()


ANY = pl.BlockSpec(memory_space=pl.ANY)
VMEM = pl.BlockSpec(memory_space=pltpu.VMEM)


def remote_call(body, name, collective_id, outs, in_specs, out_specs, scratch, sems, local_sems, vmem):
    return pl.pallas_call(
        body,
        out_shape=outs,
        in_specs=in_specs,
        out_specs=out_specs,
        scratch_shapes=[
            pltpu.SemaphoreType.DMA((sems,)),
            pltpu.SemaphoreType.DMA((sems,)),
            pltpu.SemaphoreType.DMA((max(local_sems, 1),)),
            *scratch,
        ],
        compiler_params=pltpu.CompilerParams(
            collective_id=collective_id, has_side_effects=True, vmem_limit_bytes=vmem
        ),
        name=name,
    )


def small_gather_body(planes, own_ref, out_ref, send_sem, recv_sem, local_sem):
    links = Links(planes, send_sem, recv_sem)
    links.greet(links.partners())
    z, y, x, c = links.z, links.y, links.x, links.c
    out_ref[z, y, x, c] = own_ref[...]
    spread(links, out_ref)
    links.finish_sends()


def spread(links, out_ref):
    z, y, x, c = links.z, links.y, links.x, links.c
    block = out_ref.at[z, y, x, c]
    arrived([links.send(block, block, links.plane_device(s)) for s in range(1, links.planes)])
    block = out_ref.at[:, y, x, c]
    arrived([links.send(block, block, links.across)])
    block = out_ref.at[:, :, x, c]
    arrived([links.send(block, block, links.beside)])
    block = out_ref.at[:, :, :, c]
    arrived([links.send(block, block, links.core)])


def small_gather(own, planes, collective_id):
    return remote_call(
        functools.partial(small_gather_body, planes),
        "small_gather",
        collective_id,
        jax.ShapeDtypeStruct((planes, 2, 2, 2, *own.shape), own.dtype),
        [VMEM],
        VMEM,
        [],
        planes + 2,
        0,
        40 * MIB,
    )(own)


WIDTH = 1024
OVER_X = 640


class Pieces:
    def __init__(self, links, shards, fulls):
        self.links = links
        self.pieces, self.owns = [], []
        for shard, full in zip(shards, fulls):
            z, y, x, c = links.z, links.y, links.x, links.c
            self.owns.append([links.local(shard, full.at[z, y, x, c]), False])
            for rows, columns in cuts(shard.shape):
                self.pieces.append((len(self.owns) - 1, shard, full, rows, columns))
        count = len(self.pieces)
        self.first = [None] * count
        self.second = [None] * count
        self.third = [None] * count
        self.late = [[] for _ in range(count)]

    def block(self, k, part, *place):
        _, _, full, rows, start = self.pieces[k]
        columns = {
            "all": pl.ds(start, WIDTH),
            "T": pl.ds(start, OVER_X),
            "F": pl.ds(start + OVER_X, WIDTH - OVER_X),
        }[part]
        return full.at[(*place, rows, columns)]

    def across_planes(self, k):
        links = self.links
        _, shard, _, rows, start = self.pieces[k]
        source = shard.at[rows, pl.ds(start, WIDTH)]
        target = self.block(k, "all", links.z, links.y, links.x, links.c)
        self.first[k] = [
            links.send(source, target, links.plane_device(s)) for s in range(1, links.planes)
        ]

    def pass_to_core(self, k, part, *place):
        block = self.block(k, part, *place)
        self.late[k].append(self.links.send(block, block, self.links.core))

    def B(self, k):
        links = self.links
        own = self.owns[self.pieces[k][0]]
        if not own[1]:
            own[0].wait()
            own[1] = True
        arrived(self.first[k])
        place = (slice(None), links.y, links.x, links.c)
        over_x, over_y = self.block(k, "T", *place), self.block(k, "F", *place)
        self.second[k] = {
            "T": links.send(over_x, over_x, links.beside),
            "F": links.send(over_y, over_y, links.across),
        }
        self.pass_to_core(k, "all", *place)

    def CT(self, k):
        links = self.links
        y, x, c = links.y, links.x, links.c
        arrived([self.second[k]["T"]])
        block = self.block(k, "T", slice(None), y, slice(None), c)
        self.third[k] = {**(self.third[k] or {}), "T": links.send(block, block, links.across)}
        self.pass_to_core(k, "T", slice(None), y, 1 - x, c)

    def CF(self, k):
        links = self.links
        y, x, c = links.y, links.x, links.c
        arrived([self.second[k]["F"]])
        block = self.block(k, "F", slice(None), slice(None), x, c)
        self.third[k] = {**(self.third[k] or {}), "F": links.send(block, block, links.beside)}
        self.pass_to_core(k, "F", slice(None), 1 - y, x, c)

    def DT(self, k):
        links = self.links
        arrived([self.third[k]["T"]])
        self.pass_to_core(k, "T", slice(None), 1 - links.y, slice(None), links.c)

    def DF(self, k):
        links = self.links
        arrived([self.third[k]["F"]])
        self.pass_to_core(k, "F", slice(None), slice(None), 1 - links.x, links.c)

    def there(self, k):
        arrived(self.late[k])
        self.late[k] = []


def cuts(shape):
    rows, width = shape
    if width > WIDTH:
        return [(slice(None), start) for start in range(0, width, WIDTH)]
    count = 4 if rows % 128 == 0 else 1
    return [(pl.ds(part * (rows // count), rows // count), 0) for part in range(count)]


def gather_order(count):
    order = []
    for k in range(count + 2):
        for task, behind in (("B", 0), ("CT", 1), ("CF", 1), ("DT", 2), ("DF", 2)):
            if 0 <= k - behind < count:
                order.append((task, k - behind))
    return order


AHEAD = 2


class Opening:
    CUTS = 3

    def __init__(self, links, tokens, attend, partial, tokens_out, attend_out, modulation_out, scratch):
        self.links, self.partial = links, partial
        self.tokens_out, self.attend_out, self.modulation_out = tokens_out, attend_out, modulation_out
        held, self.from_core, self.from_beside, self.from_across, self.from_planes, self.total = scratch
        z, y, x, c = links.z, links.y, links.x, links.c
        own_slice = links.local(attend.at[x, c], attend_out.at[z, y, x, c])
        far = links.send(attend.at[1 - x, 1 - c], held, links.core)
        to_core = links.send(attend.at[x, 1 - c], attend_out.at[z, y, x, c], links.core)
        to_beside = links.send(attend.at[1 - x, c], attend_out.at[z, y, x, c], links.beside)
        step = links.send(partial.at[:, :, :, 1 - c], self.from_core, links.core)
        arrived([step])
        self.from_core[...] = self.from_core[...] + partial[:, :, :, c]
        step = links.send(self.from_core.at[:, :, 1 - x], self.from_beside, links.beside)
        arrived([far])
        far_beside = links.send(held, attend_out.at[z, y, x, 1 - c], links.beside)
        self.own_tokens = links.local(tokens, tokens_out.at[:, x, c])
        self.tokens_beside = [
            links.send(tokens.at[m], tokens_out.at[m, x, c], links.beside)
            for m in range(tokens.shape[0])
        ]
        self.rest = [links.send(tokens, tokens_out.at[:, x, c], links.core)]
        own_slice.wait()
        arrived([to_core, to_beside, far_beside])
        width = attend_out.shape[-1] // self.CUTS
        self.columns = [pl.ds(part * width, width) for part in range(self.CUTS)]
        self.over_planes = []
        for columns in self.columns:
            block = attend_out.at[z, y, :, :, :, columns]
            self.over_planes.append(
                [links.send(block, block, links.plane_device(s)) for s in range(1, links.planes)]
            )
        arrived([step])
        self.from_beside[...] = self.from_beside[...] + self.from_core[:, :, x]
        step = links.send(self.from_beside.at[:, 1 - y], self.from_across, links.across)
        self.attend_over_y(0)
        arrived([step])
        self.from_across[...] = self.from_across[...] + self.from_beside[:, y]
        self.step = [
            links.send(
                self.from_across.at[links.plane(s)],
                self.from_planes.at[s - 1],
                links.plane_device(s),
            )
            for s in range(1, links.planes)
        ]

    def attend_over_y(self, part):
        links = self.links
        arrived(self.over_planes[part])
        block = self.attend_out.at[:, links.y, :, :, :, self.columns[part]]
        self.rest.append(links.send(block, block, links.across))

    def modulation_quarter(self):
        links = self.links
        arrived(self.step)
        result = self.from_across[links.z]
        for s in range(1, links.planes):
            result = result + self.from_planes[s - 1]
        self.total[...] = result
        self.modulation_out[links.x, links.c] = result
        target = self.modulation_out.at[links.x, links.c]
        self.step = [
            links.send(self.total, target, links.core),
            links.send(self.total, target, links.beside),
        ]

    def tokens_to_core(self, m):
        links = self.links
        arrived([self.tokens_beside[m]])
        fresh = self.tokens_out.at[m, 1 - links.x, links.c]
        self.rest.append(links.send(fresh, fresh, links.core))

    def modulation_to_core(self):
        links = self.links
        arrived(self.step)
        fresh = self.modulation_out.at[1 - links.x, links.c]
        self.rest.append(links.send(fresh, fresh, links.core))

    def finish(self):
        arrived(self.rest)
        self.own_tokens.wait()


def gather_body(
    planes,
    tokens,
    attend,
    project,
    expand,
    contract,
    partial,
    attend_out,
    project_out,
    expand_out,
    contract_out,
    modulation_out,
    tokens_out,
    send_sem,
    recv_sem,
    local_sem,
    *scratch,
):
    links = Links(planes, send_sem, recv_sem, local_sem)
    links.greet(links.partners())
    opening = Opening(
        links, tokens, attend, partial, tokens_out, attend_out, modulation_out, scratch
    )
    pieces = Pieces(links, (project, expand, contract), (project_out, expand_out, contract_out))
    count = len(pieces.pieces)
    for part in range(1, Opening.CUTS):
        opening.attend_over_y(part)
    opening.modulation_quarter()
    for m in range(tokens.shape[0]):
        opening.tokens_to_core(m)
    opening.modulation_to_core()
    for k in range(min(AHEAD, count)):
        pieces.across_planes(k)
    for task, k in gather_order(count):
        getattr(pieces, task)(k)
        if task == "B" and k + AHEAD < count:
            pieces.across_planes(k + AHEAD)
    for k in range(count):
        pieces.there(k)
    opening.finish()
    links.finish_sends()


FRONT_ORDER = (
    ("az", 1), ("az", 2), ("m3", 0), ("tk", 0), ("tk", 1), ("m4", 0), ("B", 0), ("att", 0), ("unit", 0),
    ("CF", 0), ("CT", 0), ("B", 1), ("unit", 1), ("unit", 2), ("unit", 3), ("DF", 0), ("B", 2),
    ("unit", 4), ("DT", 0), ("CT", 1), ("unit", 5), ("CF", 1), ("B", 3), ("CT", 2), ("CF", 2), ("unit", 6),
    ("B", 4), ("unit", 7), ("DT", 1), ("unit", 8), ("CF", 3), ("DF", 1), ("unit", 9), ("unit", 10),
    ("CT", 3), ("unit", 11), ("DT", 2), ("unit", 12), ("DF", 2), ("B", 5), ("unit", 13), ("CT", 4),
    ("CF", 4), ("unit", 14), ("unit", 15), ("DF", 3), ("DT", 3), ("B", 6), ("unit", 16), ("unit", 17),
    ("B", 7), ("load", 0), ("own", 0), ("CF", 5), ("CT", 5), ("DT", 4), ("there", 1), ("mlp", 0), ("B", 8),
    ("DF", 4), ("CF", 6), ("CT", 6), ("there", 2), ("mlp", 1), ("CF", 7), ("CT", 7), ("DT", 5),
    ("there", 3), ("mlp", 2), ("CF", 8), ("DF", 5), ("CT", 8), ("there", 4), ("mlp", 3), ("DT", 6),
    ("DF", 6), ("DF", 7), ("DT", 7), ("DF", 8), ("DT", 8),
)


def front_body(planes, *refs):
    tokens, attend, project, expand, contract, partial, refs = *refs[:6], refs[6:]
    shift, bias_qkv, bias_project, bias_expand, cotangent, refs = *refs[:5], refs[5:]
    attend_out, project_out, expand_out, contract_out, modulation_out, refs = *refs[:5], refs[5:]
    first_out, qkv_out, heads_out, log_out, blended_out, refs = *refs[:5], refs[5:]
    middle_out, attended_out, second_out, act_out, slope_out, branch_out, grad_out = refs[:7]
    send_sem, recv_sem, local_sem = refs[7:10]
    opening_scratch, refs = refs[10:16], refs[16:]
    tokens_all, attend_all, first, qkv, heads, blended, project_all, expand_all = refs[:8]
    middle, attended, second, act, slope, grad_branch, grads, upstream = refs[8:]
    links = Links(planes, send_sem, recv_sem, local_sem)
    x, c = links.x, links.c
    corner = links.beside + 1 - 2 * c
    links.greet([*links.partners(), corner])
    opening = Opening(
        links, tokens, attend, partial, tokens_all, attend_all, modulation_out, opening_scratch
    )
    pieces = Pieces(links, (project, expand, contract), (project_out, expand_out, contract_out))
    count = len(pieces.pieces)
    for k in range(min(AHEAD, count)):
        pieces.across_planes(k)
    loaded_upstream = links.local(cotangent, upstream)
    micros, own_rows, _ = tokens.shape
    stored, stored_grads, exchanged, loading = [], [], [], []
    own_heads = pl.ds(pl.multiple_of((2 * x + c) * OWN, OWN), OWN)

    def part_of(m, to_x, to_c):
        start = pl.multiple_of((2 * to_x + to_c) * own_rows, own_rows)
        return heads.at[m, pl.ds(start, own_rows)]

    def project_micro(m):
        project_tokens(m, tokens_all, attend_all, modulation_out, shift, bias_qkv, first, qkv)
        stored.append(links.local(first.at[m], first_out.at[m]))
        stored.append(links.local(qkv.at[m], qkv_out.at[m]))

    def far_heads(m, head):
        attention_unit(qkv.at[m], heads.at[m], log_out.at[m], head, 1 - x)
        if head == OWN // HEAD - 1:
            target = blended.at[m, :, own_heads]
            exchanged.append(links.send(part_of(m, 1 - x, 1 - c), target, corner))
            exchanged.append(links.send(part_of(m, 1 - x, c), target, links.beside))

    def near_heads(m, head):
        attention_unit(qkv.at[m], heads.at[m], log_out.at[m], head, x)
        if head == OWN // HEAD - 1:
            target = blended.at[m, :, own_heads]
            exchanged.append(links.send(part_of(m, x, 1 - c), target, links.core))
            stored.append(links.local(heads.at[m], heads_out.at[m]))
            links.local(part_of(m, x, c), target).wait()

    units = []
    for m in range(micros):
        units.append(functools.partial(project_micro, m))
        units += [functools.partial(far_heads, m, head) for head in range(OWN // HEAD)]
    for m in range(micros):
        units += [functools.partial(near_heads, m, head) for head in range(OWN // HEAD)]

    def load_project():
        pieces.there(0)
        loading.append(links.local(project_out, project_all))
        loaded_upstream.wait()
        for m in range(micros):
            gate = modulation_row(modulation_out, m, 5) + shift[5:6, :]
            grad_branch[m] = (gate * upstream[m].astype(jnp.float32)).astype(jnp.bfloat16)
        stored.append(links.local(grad_branch, branch_out))

    def own_tokens():
        loading.pop().wait()
        for m in range(micros):
            stored.append(links.local(blended.at[m], blended_out.at[m]))
            product = jnp.dot(
                blended[m],
                project_all[...].reshape(D, D),
                preferred_element_type=jnp.float32,
            )
            attended[m] = product + bias_project[...]
            gate = modulation_row(modulation_out, m, 2) + shift[2:3, :]
            middle[m] = tokens_all[m, x, c].astype(jnp.float32) + gate * attended[m]
            normed, _ = normalize(middle[m])
            factors = 1.0 + modulation_row(modulation_out, m, 4) + shift[4:5, :]
            offsets = modulation_row(modulation_out, m, 3) + shift[3:4, :]
            second[m] = (normed * factors + offsets).astype(jnp.bfloat16)
        stored.append(links.local(middle, middle_out))
        stored.append(links.local(attended, attended_out))
        stored.append(links.local(second, second_out))

    parts = FF // WIDTH
    blocks = grads.shape[1]

    def expand_unit(part):
        columns = pl.ds(part * WIDTH, WIDTH)
        loaded = links.local(expand_out.at[:, :, :, :, :, columns], expand_all)
        if part >= 2:
            stored_grads[part - 2].wait()
        loaded.wait()
        expand_part(part, WIDTH, second, expand_all, bias_expand, act, slope, grad_branch, grads)
        stored.append(links.local(act.at[:, :, columns], act_out.at[:, :, columns]))
        stored.append(links.local(slope.at[:, :, columns], slope_out.at[:, :, columns]))
        stored_grads.append(
            links.local(grads.at[part % 2], grad_out.at[pl.ds(part * blocks, blocks)])
        )

    for task, k in FRONT_ORDER:
        if task == "az":
            opening.attend_over_y(k)
        elif task == "m3":
            opening.modulation_quarter()
        elif task == "tk":
            opening.tokens_to_core(k)
        elif task == "m4":
            opening.modulation_to_core()
        elif task == "att":
            opening.finish()
            stored.append(links.local(attend_all, attend_out))
        elif task == "unit":
            units[k]()
        elif task == "load":
            load_project()
        elif task == "own":
            arrived(exchanged)
            own_tokens()
        elif task == "there":
            pieces.there(k)
        elif task == "mlp":
            expand_unit(k)
        else:
            getattr(pieces, task)(k)
            if task == "B" and k + AHEAD < count:
                pieces.across_planes(k + AHEAD)
    for k in range(count):
        pieces.there(k)
    for copy in stored + stored_grads[-2:]:
        copy.wait()
    links.finish_sends()


ROOT = 0.7978845608028654
CUBE = 0.044715
CHUNK = 512


def expand_part(part, width, second, expand, bias, act, slope, grad_branch, grads):
    micros = second.shape[0]
    rows = grads.shape[2]

    @pl.loop(0, width // CHUNK)
    def _(chunk):
        inside = pl.ds(pl.multiple_of(chunk * CHUNK, CHUNK), CHUNK)
        columns = pl.ds(pl.multiple_of(part * width + chunk * CHUNK, CHUNK), CHUNK)
        weights = expand[:, :, :, :, :, inside].reshape(D, CHUNK)
        total = None
        for m in range(micros):
            hidden = jnp.dot(second[m], weights, preferred_element_type=jnp.float32)
            hidden = hidden + bias[:, columns]
            square = hidden * hidden
            bend = jnp.tanh(hidden * (ROOT + (ROOT * CUBE) * square))
            half = 0.5 + 0.5 * bend
            low = (hidden * half).astype(jnp.bfloat16)
            act[m, :, columns] = low
            steep = hidden * (0.5 * ROOT + (1.5 * ROOT * CUBE) * square)
            slope[m, :, columns] = (half + steep * (1.0 - bend * bend)).astype(jnp.bfloat16)
            product = lax.dot_general(
                low, grad_branch[m], (((0,), (0,)), ((), ())), preferred_element_type=jnp.float32
            )
            total = product if total is None else total + product
        count = CHUNK // rows
        here = pl.ds(chunk * count, count)
        grads[part % 2, here] = total.astype(jnp.bfloat16).reshape(count, rows, D)


def modulation_row(modulation, m, block):
    per_quarter = modulation.shape[2] // MICROS
    pieces = []
    for k in range(block * D // LANES, (block + 1) * D // LANES):
        quarter, row = k // per_quarter, m * per_quarter + k % per_quarter
        pieces.append(modulation[quarter // 2, quarter % 2, row : row + 1, :])
    return jnp.concatenate(pieces, axis=1)


def project_tokens(m, tokens, attend, modulation, shift, bias, first_out, qkv_out):
    offsets = modulation_row(modulation, m, 0) + shift[0:1, :]
    factors = 1.0 + modulation_row(modulation, m, 1) + shift[1:2, :]
    rows = tokens.shape[3]

    @pl.loop(0, GROUP)
    def _(block):
        values = tokens[m, block // 2, block % 2].astype(jnp.float32)
        normed, _ = normalize(values)
        first = (normed * factors + offsets).astype(jnp.bfloat16)
        here = pl.ds(pl.multiple_of(block * rows, rows), rows)
        first_out[m, here, :] = first
        weights = attend[...].reshape(D, 3 * OWN)
        product = jnp.dot(first, weights, preferred_element_type=jnp.float32)
        qkv_out[m, here, :] = (product + bias[...]).astype(jnp.bfloat16)


def gather_scratch(attend, partial, planes):
    rows = partial.shape[-2]
    return [
        pltpu.VMEM((attend.shape[-2], attend.shape[-1]), attend.dtype),
        pltpu.VMEM((planes, 2, 2, rows, LANES), jnp.float32),
        pltpu.VMEM((planes, 2, rows, LANES), jnp.float32),
        pltpu.VMEM((planes, rows, LANES), jnp.float32),
        pltpu.VMEM((planes - 1, rows, LANES), jnp.float32),
        pltpu.VMEM((rows, LANES), jnp.float32),
    ]


def gather_outs(attend, project, expand, contract, partial, planes):
    return [
        *(
            jax.ShapeDtypeStruct((planes, 2, 2, 2, *shard.shape[-2:]), shard.dtype)
            for shard in (attend, project, expand, contract)
        ),
        jax.ShapeDtypeStruct((2, 2, partial.shape[-2], LANES), jnp.float32),
    ]


def gather_sems(planes):
    return 40 + 14 * (planes - 1) + 9 * 10


def gather_all(tokens, attend, project, expand, contract, partial, planes):
    micros, own_rows, _ = tokens.shape
    return remote_call(
        functools.partial(gather_body, planes),
        "gather_all",
        1,
        (
            *gather_outs(attend, project, expand, contract, partial, planes),
            jax.ShapeDtypeStruct((micros, 2, 2, own_rows, D), tokens.dtype),
        ),
        [ANY] * 5 + [VMEM],
        (ANY,) * 4 + (VMEM, ANY),
        gather_scratch(attend, partial, planes),
        gather_sems(planes),
        8,
        56 * MIB,
    )(tokens, attend, project, expand, contract, partial)


def front(tokens, attend, project, expand, contract, partial, vectors, cotangent, planes):
    micros, own_rows, _ = tokens.shape
    latent_rows = own_rows * GROUP
    blocks = latent_rows // QUERY_ROWS
    grad_rows = contract.shape[0]

    def low(*shape):
        return jax.ShapeDtypeStruct(shape, jnp.bfloat16)

    def held(*shape, dtype=jnp.bfloat16):
        return pltpu.VMEM(shape, dtype)

    log_shape = (micros, OWN // HEAD, blocks, 1, QUERY_ROWS)
    own = (micros, own_rows, D)
    parts = FF // WIDTH
    return remote_call(
        functools.partial(front_body, planes),
        "front",
        1,
        (
            *gather_outs(attend, project, expand, contract, partial, planes),
            low(micros, latent_rows, D),
            low(micros, latent_rows, 3 * OWN),
            low(micros, latent_rows, OWN),
            jax.ShapeDtypeStruct(log_shape, jnp.float32),
            low(*own),
            jax.ShapeDtypeStruct(own, jnp.float32),
            jax.ShapeDtypeStruct(own, jnp.float32),
            low(*own),
            low(micros, own_rows, FF),
            low(micros, own_rows, FF),
            low(*own),
            low(FF // grad_rows, grad_rows, D),
        ),
        [ANY] * 5 + [VMEM] * 5 + [ANY],
        (ANY,) * 4 + (VMEM,) + (ANY,) * 3 + (VMEM,) + (ANY,) * 8,
        [
            *gather_scratch(attend, partial, planes),
            held(micros, 2, 2, own_rows, D),
            held(planes, 2, 2, 2, *attend.shape[-2:]),
            held(micros, latent_rows, D),
            held(micros, latent_rows, 3 * OWN),
            held(micros, latent_rows, OWN),
            held(*own),
            held(planes, 2, 2, 2, *project.shape),
            held(planes, 2, 2, 2, expand.shape[0], FF // parts),
            held(*own, dtype=jnp.float32),
            held(*own, dtype=jnp.float32),
            held(*own),
            held(micros, own_rows, FF),
            held(micros, own_rows, FF),
            held(*own),
            held(2, FF // parts // grad_rows, grad_rows, D),
            held(*own),
        ],
        gather_sems(planes),
        40,
        60 * MIB,
    )(tokens, attend, project, expand, contract, partial, *vectors, cotangent)


QUERY_ROWS = 256


def attention_unit(qkv, out, log, head, side=None):
    count = qkv.shape[0] // QUERY_ROWS
    start = 0
    if side is not None:
        count //= 2
        start = side * count
    at = head * HEAD
    keys = qkv[:, OWN + at : OWN + at + HEAD]
    values_t = qkv[:, 2 * OWN + at : 2 * OWN + at + HEAD].T

    @pl.loop(0, count)
    def _(index):
        block = start + index
        here = pl.ds(pl.multiple_of(block * QUERY_ROWS, QUERY_ROWS), QUERY_ROWS)
        queries = qkv[here, at : at + HEAD] * SCALE
        scores = lax.dot_general(
            keys, queries, (((1,), (1,)), ((), ())), preferred_element_type=jnp.float32
        )
        top = jnp.max(scores, axis=0, keepdims=True)
        weights = jnp.exp(scores - top)
        totals = jnp.sum(weights, axis=0, keepdims=True)
        blended = jnp.dot(
            values_t, weights.astype(jnp.bfloat16), preferred_element_type=jnp.float32
        )
        out[here, at : at + HEAD] = (blended / totals).T.astype(jnp.bfloat16)
        log[head, block] = top + jnp.log(totals)


def attention_body(qkv_ref, out_ref, log_ref):
    for head in range(OWN // HEAD):
        attention_unit(qkv_ref.at[0], out_ref.at[0], log_ref.at[0], head)


def attention(qkv):
    micros, rows, _ = qkv.shape
    heads = OWN // HEAD
    blocks = rows // 256
    return pl.pallas_call(
        attention_body,
        grid=(micros,),
        out_shape=(
            jax.ShapeDtypeStruct((micros, rows, OWN), jnp.bfloat16),
            jax.ShapeDtypeStruct((micros, heads, blocks, 1, 256), jnp.float32),
        ),
        in_specs=[pl.BlockSpec((1, rows, 3 * OWN), lambda m: (m, 0, 0))],
        out_specs=(
            pl.BlockSpec((1, rows, OWN), lambda m: (m, 0, 0)),
            pl.BlockSpec((1, heads, blocks, 1, 256), lambda m: (m, 0, 0, 0, 0)),
        ),
        compiler_params=pltpu.CompilerParams(vmem_limit_bytes=48 * MIB),
        name="attention",
    )(qkv)


def attention_back_unit(qkv, blended_all, grad_all, log, out, key_sum, value_sum, head):
    at = head * HEAD
    keys = qkv[:, OWN + at : OWN + at + HEAD]
    keys_t = keys.T
    values = qkv[:, 2 * OWN + at : 2 * OWN + at + HEAD]
    key_sum[...] = jnp.zeros_like(key_sum)
    value_sum[...] = jnp.zeros_like(value_sum)

    @pl.loop(0, qkv.shape[0] // QUERY_ROWS)
    def _(block):
        here = pl.ds(pl.multiple_of(block * QUERY_ROWS, QUERY_ROWS), QUERY_ROWS)
        queries = qkv[here, at : at + HEAD] * SCALE
        grads = grad_all[here, at : at + HEAD]
        blended = blended_all[here, at : at + HEAD]
        row_terms = jnp.sum(
            (grads.astype(jnp.float32) * blended.astype(jnp.float32)).T, axis=0, keepdims=True
        )
        scores = lax.dot_general(
            keys, queries, (((1,), (1,)), ((), ())), preferred_element_type=jnp.float32
        )
        chances = jnp.exp(scores - log[head, block])
        grad_chances = lax.dot_general(
            values, grads, (((1,), (1,)), ((), ())), preferred_element_type=jnp.float32
        )
        grad_scores = (chances * (grad_chances - row_terms)).astype(jnp.bfloat16)
        value_sum[...] += jnp.dot(
            chances.astype(jnp.bfloat16), grads, preferred_element_type=jnp.float32
        )
        key_sum[...] += jnp.dot(grad_scores, queries, preferred_element_type=jnp.float32)
        grad_queries = jnp.dot(keys_t, grad_scores, preferred_element_type=jnp.float32)
        out[here, at : at + HEAD] = (grad_queries.T * SCALE).astype(jnp.bfloat16)

    out[:, OWN + at : OWN + at + HEAD] = key_sum[...].astype(jnp.bfloat16)
    out[:, 2 * OWN + at : 2 * OWN + at + HEAD] = value_sum[...].astype(jnp.bfloat16)


def attention_back_body(qkv_ref, blended_ref, grad_ref, log_ref, out_ref, key_sum, value_sum):
    for head in range(OWN // HEAD):
        attention_back_unit(
            qkv_ref.at[0],
            blended_ref.at[0],
            grad_ref.at[0],
            log_ref.at[0],
            out_ref.at[0],
            key_sum,
            value_sum,
            head,
        )


def attention_back(qkv, blended, grads, logs):
    micros, rows, _ = qkv.shape
    heads = OWN // HEAD
    blocks = rows // 256
    wide = pl.BlockSpec((1, rows, 3 * OWN), lambda m: (m, 0, 0))
    narrow = pl.BlockSpec((1, rows, OWN), lambda m: (m, 0, 0))
    return pl.pallas_call(
        attention_back_body,
        grid=(micros,),
        out_shape=jax.ShapeDtypeStruct((micros, rows, 3 * OWN), jnp.bfloat16),
        in_specs=[
            wide,
            narrow,
            narrow,
            pl.BlockSpec((1, heads, blocks, 1, 256), lambda m: (m, 0, 0, 0, 0)),
        ],
        out_specs=wide,
        scratch_shapes=[pltpu.VMEM((rows, HEAD), jnp.float32)] * 2,
        compiler_params=pltpu.CompilerParams(vmem_limit_bytes=48 * MIB),
        name="attention_back",
    )(qkv, blended, grads, logs)


def heads_to_tokens_body(blended, out, send_sem, recv_sem, local_sem):
    links = Links(1, send_sem, recv_sem, local_sem)
    x, c = links.x, links.c
    corner = links.beside + 1 - 2 * c
    links.greet([links.core, links.beside, corner])
    target = out.at[:, :, pl.ds(pl.multiple_of((2 * x + c) * OWN, OWN), OWN)]
    own = links.local(blended.at[:, x, c], target)
    copies = [
        links.send(blended.at[:, 1 - x, 1 - c], target, corner),
        links.send(blended.at[:, 1 - x, c], target, links.beside),
        links.send(blended.at[:, x, 1 - c], target, links.core),
    ]
    arrived(copies)
    own.wait()
    links.finish_sends()


def heads_to_tokens(blended):
    micros, rows, _ = blended.shape
    own_rows = rows // GROUP
    return remote_call(
        heads_to_tokens_body,
        "heads_to_tokens",
        2,
        jax.ShapeDtypeStruct((micros, own_rows, D), blended.dtype),
        [ANY],
        ANY,
        [],
        3,
        1,
        40 * MIB,
    )(blended.reshape(micros, 2, 2, own_rows, OWN))


def tokens_to_heads_body(grads, out, send_sem, recv_sem, local_sem):
    links = Links(1, send_sem, recv_sem, local_sem)
    x, c = links.x, links.c
    corner = links.beside + 1 - 2 * c
    links.greet([links.core, links.beside, corner])

    def columns(to_x, to_c):
        return grads.at[:, :, pl.ds(pl.multiple_of((2 * to_x + to_c) * OWN, OWN), OWN)]

    target = out.at[:, x, c]
    own = links.local(columns(x, c), target)
    copies = [
        links.send(columns(1 - x, 1 - c), target, corner),
        links.send(columns(1 - x, c), target, links.beside),
        links.send(columns(x, 1 - c), target, links.core),
    ]
    arrived(copies)
    own.wait()
    links.finish_sends()


def tokens_to_heads(grads):
    micros, own_rows, _ = grads.shape
    return remote_call(
        tokens_to_heads_body,
        "tokens_to_heads",
        3,
        jax.ShapeDtypeStruct((micros, 2, 2, own_rows, OWN), grads.dtype),
        [ANY],
        ANY,
        [],
        3,
        1,
        40 * MIB,
    )(grads).reshape(micros, GROUP * own_rows, OWN)


def token_sums_body(partial, out, send_sem, recv_sem, local_sem, from_core, own, from_beside):
    links = Links(1, send_sem, recv_sem, local_sem)
    x, c = links.x, links.c
    links.greet([links.core, links.beside])
    far = links.send(partial.at[:, 1 - x, 1 - c], from_core.at[0], links.core)
    near = links.send(partial.at[:, x, 1 - c], from_core.at[1], links.core)
    loads = [
        links.local(partial.at[:, 1 - x, c], own.at[0]),
        links.local(partial.at[:, x, c], own.at[1]),
    ]
    micros = out.shape[0]
    loads[0].wait()
    arrived([far])
    passed = []
    for m in range(micros):
        own[0, m] = (
            own[0, m].astype(jnp.float32) + from_core[0, m].astype(jnp.float32)
        ).astype(jnp.bfloat16)
        passed.append(links.send(own.at[0, m], from_beside.at[m], links.beside))
    loads[1].wait()
    arrived([near])
    for m in range(micros):
        out[m] = own[1, m].astype(jnp.float32) + from_core[1, m].astype(jnp.float32)
    for m in range(micros):
        arrived([passed[m]])
        out[m] += from_beside[m].astype(jnp.float32)
    links.finish_sends()


def token_sums(partial):
    micros, rows, width = partial.shape
    own_rows = rows // GROUP
    held = pltpu.VMEM((2, micros, own_rows, width), partial.dtype)
    return remote_call(
        token_sums_body,
        "token_sums",
        4,
        jax.ShapeDtypeStruct((micros, own_rows, width), jnp.float32),
        [ANY],
        VMEM,
        [held, held, pltpu.VMEM((micros, own_rows, width), partial.dtype)],
        4,
        2,
        40 * MIB,
    )(partial.reshape(micros, 2, 2, own_rows, width))


def small_sums_body(planes, partial, out, send_sem, recv_sem, local_sem, from_core, from_beside):
    links = Links(planes, send_sem, recv_sem)
    links.greet(links.partners())
    z, y, x, c = links.z, links.y, links.x, links.c
    arrived([links.send(partial.at[:, 1 - c], from_core, links.core)])
    from_core[...] = from_core[...] + partial[:, c]
    arrived([links.send(from_core.at[1 - x], from_beside, links.beside)])
    out[z, y, x, c] = from_core[x] + from_beside[...]
    spread(links, out)
    links.finish_sends()


def small_sums(partial, planes):
    block = partial.shape[2:]
    return remote_call(
        functools.partial(small_sums_body, planes),
        "small_sums",
        5,
        jax.ShapeDtypeStruct((planes, 2, 2, 2, *block), jnp.float32),
        [VMEM],
        VMEM,
        [pltpu.VMEM((2, *block), jnp.float32), pltpu.VMEM(block, jnp.float32)],
        planes + 4,
        0,
        40 * MIB,
    )(partial)


SUMS_OVER_X = 384


def add_blocks(target, left, right, count):
    @pl.loop(0, count)
    def _(i):
        target(i)[...] = (
            left(i)[...].astype(jnp.float32) + right(i)[...].astype(jnp.float32)
        ).astype(jnp.bfloat16)


class Sums:
    def __init__(self, links, grads, outs, scratch):
        self.links = links
        self.pieces = []
        used = 0
        for grad, out in zip(grads, outs):
            own = scratch[used]
            used += 1
            for rows, start in cuts(grad.shape[-2:]):
                self.pieces.append((grad, out, rows, start, own, *scratch[used : used + 5]))
                used += 5
        self.state = [dict() for _ in self.pieces]
        self.loaded = {}

    def core(self, k):
        links = self.links
        grad, _, rows, start, _, first, *_ = self.pieces[k]
        columns = pl.ds(start, WIDTH)
        source = grad.at[:, :, :, 1 - links.c, rows, columns]
        self.state[k]["core"] = links.send(source, first, links.core)

    def load(self, k):
        links = self.links
        grad, _, rows, start, own, *_ = self.pieces[k]
        source = grad.at[:, :, :, links.c, rows, pl.ds(start, WIDTH)]
        self.state[k]["own"] = links.local(source, own)

    def S1(self, k):
        links = self.links
        x, y, planes = links.x, links.y, links.planes
        *_, own, first, over_x, over_y, _, _ = self.pieces[k]
        state = self.state[k]
        state["own"].wait()
        arrived([state["core"]])
        lead, rest = pl.ds(0, SUMS_OVER_X), pl.ds(SUMS_OVER_X, WIDTH - SUMS_OVER_X)

        def at(ref, columns, place):
            return lambda i: ref.at[(*place(i // 2, i % 2), slice(None), columns)]

        def add(columns, place):
            add_blocks(at(first, columns, place), at(own, columns, place), at(first, columns, place), planes * 2)

        add(lead, lambda z, other: (z, other, 1 - x))
        state["T"] = links.send(first.at[:, :, 1 - x, :, lead], over_x, links.beside)
        add(rest, lambda z, other: (z, 1 - y, other))
        state["F"] = links.send(first.at[:, 1 - y, :, :, rest], over_y, links.across)
        add(lead, lambda z, other: (z, other, x))
        add(rest, lambda z, other: (z, y, other))

    def S2T(self, k):
        links = self.links
        x, y = links.x, links.y
        *_, first, over_x, _, third, _ = self.pieces[k]
        lead = pl.ds(0, SUMS_OVER_X)
        arrived([self.state[k]["T"]])
        for here in (1 - y, y):
            add_blocks(
                lambda i, here=here: over_x.at[i, here],
                lambda i, here=here: first.at[i, here, x, :, lead],
                lambda i, here=here: over_x.at[i, here],
                links.planes,
            )
            if here is not y:
                self.state[k]["T"] = links.send(
                    over_x.at[:, here], third.at[:, :, lead], links.across
                )

    def S2F(self, k):
        links = self.links
        x, y = links.x, links.y
        *_, first, _, over_y, third, _ = self.pieces[k]
        rest = pl.ds(SUMS_OVER_X, WIDTH - SUMS_OVER_X)
        arrived([self.state[k]["F"]])
        for here in (1 - x, x):
            add_blocks(
                lambda i, here=here: over_y.at[i, here],
                lambda i, here=here: first.at[i, y, here, :, rest],
                lambda i, here=here: over_y.at[i, here],
                links.planes,
            )
            if here is not x:
                self.state[k]["F"] = links.send(
                    over_y.at[:, here], third.at[:, :, rest], links.beside
                )

    def S3(self, k):
        links = self.links
        x, y = links.x, links.y
        *_, over_x, over_y, third, fourth = self.pieces[k]
        arrived([self.state[k]["T"], self.state[k]["F"]])
        lead, rest = pl.ds(0, SUMS_OVER_X), pl.ds(SUMS_OVER_X, WIDTH - SUMS_OVER_X)
        for kept, here, columns in ((over_x, y, lead), (over_y, x, rest)):
            add_blocks(
                lambda i, columns=columns: third.at[i, :, columns],
                lambda i, kept=kept, here=here: kept.at[i, here],
                lambda i, columns=columns: third.at[i, :, columns],
                links.planes,
            )
        self.state[k]["planes"] = [
            links.send(third.at[links.plane(s)], fourth.at[s - 1], links.plane_device(s))
            for s in range(1, links.planes)
        ]

    def S4(self, k):
        links = self.links
        _, out, rows, start, *_, third, fourth = self.pieces[k]
        arrived(self.state[k]["planes"])
        result = third[links.z].astype(jnp.float32)
        for s in range(1, links.planes):
            result = result + fourth[s - 1].astype(jnp.float32)
        out[rows, pl.ds(start, WIDTH)] = result


def sums_order(count):
    order = []
    for k in range(count + 4):
        for task, behind in (("core", 0), ("S1", 1), ("load", 0), ("S2T", 2), ("S2F", 2), ("S3", 3), ("S4", 4)):
            if 0 <= k - behind < count:
                order.append((task, k - behind))
    return order


MIDDLE_ORDER = (
    ("mlp", 0), ("S1", 0), ("load", 1), ("mlp", 1), ("S2T", 0), ("S1", 1), ("load", 2), ("S2F", 0),
    ("S1", 2), ("load", 3), ("mlp", 2), ("S3", 0), ("S2T", 1), ("S2F", 1), ("S1", 3), ("mlp", 3),
    ("S3", 1), ("S2T", 2), ("S2F", 2), ("S2T", 3), ("S4", 0), ("own", 0), ("S2F", 3), ("own", 1),
    ("S3", 2), ("S4", 1), ("project", 0), ("S3", 3), ("S4", 2), ("S4", 3),
)
BACK_ORDER = (
    ("head", 0), ("S1", 0), ("load", 1), ("head", 1), ("S1", 1), ("load", 2), ("S2T", 0), ("head", 2),
    ("S2F", 0), ("S2T", 1), ("S1", 2), ("load", 3), ("head", 3), ("S3", 0), ("S2F", 1), ("S1", 3),
    ("load", 4), ("first", 0), ("S2T", 2), ("head", 4), ("t1", 0), ("S3", 1), ("S2T", 3), ("S4", 0),
    ("head", 5), ("S2F", 2), ("head", 6), ("S2F", 3), ("S4", 1), ("S1", 4), ("t2", 0), ("head", 7),
    ("S3", 2), ("attend", 0), ("S3", 3), ("S2F", 4), ("first", 1), ("S4", 2), ("bias", 0), ("t1", 1),
    ("S4", 3), ("S2T", 4), ("a1", 0), ("t2", 1), ("S3", 4), ("a2", 0), ("a3", 0), ("S4", 4),
)


class AttendSums:
    def __init__(self, links, grads, out, scratch):
        self.links, self.grads, self.out = links, grads, out
        self.own, self.over_y, self.over_planes, self.sum, self.held = scratch

    def start(self):
        links = self.links
        self.step = links.send(self.grads.at[:, 1 - links.y], self.over_y, links.across)
        self.loaded = links.local(self.grads.at[:, links.y], self.own)

    def planes(self):
        links, own, over_y = self.links, self.own, self.over_y
        self.loaded.wait()
        arrived([self.step])
        for i in range(2):

            def block(ref, i=i):
                return lambda k: ref.at[k // 2, i, k % 2]

            add_blocks(block(own), block(own), block(over_y), links.planes * 2)
        self.step = [
            links.send(own.at[links.plane(s)], self.over_planes.at[s - 1], links.plane_device(s))
            for s in range(1, links.planes)
        ]

    def owners(self):
        links = self.links
        x, c = links.x, links.c
        arrived(self.step)
        for i in range(2):
            for j in range(2):
                result = self.own[links.z, i, j].astype(jnp.float32)
                for s in range(1, links.planes):
                    result = result + self.over_planes[s - 1, i, j].astype(jnp.float32)
                self.sum[i, j] = result
        self.beside = links.send(self.sum.at[1 - x], self.held, links.beside)
        self.near = links.send(self.sum.at[x, 1 - c], self.out.at[x, c], links.core)
        self.out[x, c] = self.sum[x, c]

    def last(self):
        links = self.links
        x, c = links.x, links.c
        arrived([self.beside])
        self.out[1 - x, c] = self.held[c]
        self.far = links.send(self.held.at[1 - c], self.out.at[1 - x, c], links.core)

    def finish(self):
        arrived([self.near, self.far])


class TokenSums:
    def __init__(self, links, partial, out, scratch):
        self.links, self.partial, self.out = links, partial, out
        self.from_core, self.from_beside = scratch
        self.state = {}

    def start(self, m):
        links, partial = self.links, self.partial
        x, c = links.x, links.c
        self.state[m] = [
            links.send(partial.at[m, 1 - x, 1 - c], self.from_core.at[0, m], links.core),
            links.send(partial.at[m, x, 1 - c], self.from_core.at[1, m], links.core),
        ]

    def middle(self, m):
        links, partial = self.links, self.partial
        x, c = links.x, links.c
        arrived(self.state[m])
        away = partial.at[m, 1 - x, c]
        away[...] = (
            away[...].astype(jnp.float32) + self.from_core[0, m].astype(jnp.float32)
        ).astype(jnp.bfloat16)
        self.state[m] = [links.send(away, self.from_beside.at[m], links.beside)]

    def finish(self, m):
        links = self.links
        arrived(self.state[m])
        self.out[m] = (
            self.partial[m, links.x, links.c].astype(jnp.float32)
            + self.from_core[1, m].astype(jnp.float32)
            + self.from_beside[m].astype(jnp.float32)
        )


def sums_body(planes, kinds, *refs):
    attend, grads, refs = refs[0], refs[1 : 1 + kinds], refs[1 + kinds :]
    attend_out, outs, refs = refs[0], refs[1 : 1 + kinds], refs[1 + kinds :]
    links = Links(planes, *refs[:3])
    links.greet(links.partners())
    attend_sums = AttendSums(links, attend, attend_out, refs[3:8])
    attend_sums.start()
    attend_sums.planes()
    attend_sums.owners()
    attend_sums.last()
    sums = Sums(links, grads, outs, refs[8:])
    for task, k in sums_order(len(sums.pieces)):
        getattr(sums, task)(k)
    attend_sums.finish()
    links.finish_sends()


def middle_body(planes, *refs):
    grad_contract, expand, contract, project, act, slope, second, grad_branch, refs = *refs[:8], refs[8:]
    middle, attended, upstream, blended, modulation, shift, bias_contract, refs = *refs[:7], refs[7:]
    contract_out, output, middle_grad_out, rows_out, bias_out, hidden_out, refs = *refs[:6], refs[6:]
    grad_expand, grad_project, grad_heads, refs = *refs[:3], refs[3:]
    links = Links(planes, *refs[:3])
    refs = refs[3:]
    used = scratch_count([grad_contract.shape[-2:]])
    sum_scratch, refs = refs[:used], refs[used:]
    contract_held, expand_held, act_held, slope_held, second_held, second_t, refs = *refs[:6], refs[6:]
    branch_grad, grads, branch, grad_second, middle_held, attended_held, refs = *refs[:6], refs[6:]
    upstream_held, project_held, blended_held, attended_grad, project_grads, refs = *refs[:5], refs[5:]
    middle_grad, grad_blended = refs
    x, c = links.x, links.c
    corner = links.beside + 1 - 2 * c
    micros, own_rows, _ = second.shape
    parts = FF // WIDTH
    part_width = FF // parts
    contract_blocks = contract.shape[0] // parts

    def load(part):
        columns = pl.ds(part * part_width, part_width)
        slot = part % 2
        return [
            links.local(
                contract.at[pl.ds(part * contract_blocks, contract_blocks)], contract_held.at[slot]
            ),
            links.local(expand.at[:, :, :, :, :, columns], expand_held.at[slot]),
            links.local(act.at[:, :, columns], act_held.at[slot]),
            links.local(slope.at[:, :, columns], slope_held.at[slot]),
        ]

    loaded = links.local(second, second_held), links.local(grad_branch, branch_grad)
    loading = {0: load(0), 1: load(1)}
    links.greet([*links.partners(), corner])
    sums = Sums(links, (grad_contract,), (contract_out,), sum_scratch)
    for k in range(len(sums.pieces)):
        sums.core(k)
    sums.load(0)
    later = [
        links.local(middle, middle_held),
        links.local(attended, attended_held),
        links.local(upstream, upstream_held),
        links.local(project, project_held),
        links.local(blended, blended_held),
    ]
    for copy in loaded:
        copy.wait()
    for m in range(micros):
        second_t[:, m * own_rows : (m + 1) * own_rows] = second_held[m].T
    branch[...] = jnp.zeros_like(branch)
    grad_second[...] = jnp.zeros_like(grad_second)
    stored = []

    def mlp_unit(part):
        for copy in loading.pop(part):
            copy.wait()
        slot = part % 2
        if part >= 2:
            stored[part - 2].wait()
        contract_part(
            part * part_width,
            contract_held.at[slot],
            expand_held.at[slot],
            act_held.at[slot],
            slope_held.at[slot],
            second_t,
            branch_grad,
            grads.at[slot],
            branch,
            grad_second,
            hidden_out,
        )
        if part + 2 < parts:
            loading[part + 2] = load(part + 2)
        columns = pl.ds(part * part_width, part_width)
        stored.append(links.local(grads.at[slot], grad_expand.at[:, :, :, :, :, columns]))

    totals = [jnp.zeros((1, D), jnp.float32)] * 2

    def own_tokens(m):
        def vector(block):
            return modulation_row(modulation, m, block) + shift[block : block + 1, :]

        ahead = upstream_held[m].astype(jnp.float32)
        outward = branch[m] + bias_contract[...]
        output[m] = (middle_held[m] + vector(5) * outward).astype(jnp.bfloat16)
        rows_out[m, 5:6, :] = jnp.sum(ahead * outward, axis=0, keepdims=True)
        normed, scale = normalize(middle_held[m])
        values = grad_second[m]
        rows_out[m, 3:4, :] = jnp.sum(values, axis=0, keepdims=True)
        rows_out[m, 4:5, :] = jnp.sum(values * normed, axis=0, keepdims=True)
        back = ahead + norm_back(values, normed, scale, vector(4))
        middle_grad[m] = back
        rows_out[m, 2:3, :] = jnp.sum(back * attended_held[m], axis=0, keepdims=True)
        lowered = (vector(2) * back).astype(jnp.bfloat16)
        attended_grad[m] = lowered
        totals[0] += jnp.sum(lowered.astype(jnp.float32), axis=0, keepdims=True)
        totals[1] += jnp.sum(branch_grad[m].astype(jnp.float32), axis=0, keepdims=True)
        product = lax.dot_general(
            lowered,
            project_held[...].reshape(D, D),
            (((1,), (1,)), ((), ())),
            preferred_element_type=jnp.float32,
        )
        grad_blended[m] = product.astype(jnp.bfloat16)
        here = pl.ds(pl.multiple_of((2 * x + c) * own_rows, own_rows), own_rows)

        def columns_of(to_x, to_c):
            start = pl.multiple_of((2 * to_x + to_c) * OWN, OWN)
            return grad_blended.at[m, :, pl.ds(start, OWN)]

        target = grad_heads.at[m, here]
        exchanged.append(links.send(columns_of(1 - x, 1 - c), target, corner))
        exchanged.append(links.send(columns_of(1 - x, c), target, links.beside))
        exchanged.append(links.send(columns_of(x, 1 - c), target, links.core))
        stored.append(links.local(columns_of(x, c), target))

    exchanged = []

    def project_unit():
        total = None
        for m in range(micros):
            product = lax.dot_general(
                blended_held[m],
                attended_grad[m],
                (((0,), (0,)), ((), ())),
                preferred_element_type=jnp.float32,
            )
            total = product if total is None else total + product
        project_grads[...] = total.astype(jnp.bfloat16).reshape(project_grads.shape)
        stored.append(links.local(project_grads, grad_project))
        stored.append(links.local(middle_grad, middle_grad_out))

    for task, k in MIDDLE_ORDER:
        if task == "mlp":
            mlp_unit(k)
        elif task == "own":
            if k == 0:
                for copy in later:
                    copy.wait()
            own_tokens(k)
        elif task == "project":
            project_unit()
        else:
            getattr(sums, task)(k)
    bias_out[0:1, :] = totals[0]
    bias_out[1:2, :] = totals[1]
    arrived(exchanged)
    for copy in stored[parts - 2 :]:
        copy.wait()
    links.finish_sends()


def contract_part(
    start,
    contract,
    expand,
    act,
    slope,
    second_t,
    grad_branch,
    grads,
    branch,
    grad_second,
    hidden_sums,
):
    micros = grad_branch.shape[0]
    blocks = CHUNK // contract.shape[1]

    @pl.loop(0, act.shape[-1] // CHUNK)
    def _(chunk):
        inside = pl.ds(pl.multiple_of(chunk * CHUNK, CHUNK), CHUNK)
        columns = pl.ds(pl.multiple_of(start + chunk * CHUNK, CHUNK), CHUNK)
        outward = contract[pl.ds(chunk * blocks, blocks)].reshape(CHUNK, D)
        inward = expand[:, :, :, :, :, inside].reshape(D, CHUNK)
        lows = []
        for m in range(micros):
            branch[m] += jnp.dot(act[m, :, inside], outward, preferred_element_type=jnp.float32)
            grad_act = lax.dot_general(
                grad_branch[m], outward, (((1,), (1,)), ((), ())), preferred_element_type=jnp.float32
            )
            lows.append((grad_act * slope[m, :, inside].astype(jnp.float32)).astype(jnp.bfloat16))
            grad_second[m] += lax.dot_general(
                lows[m], inward, (((1,), (1,)), ((), ())), preferred_element_type=jnp.float32
            )
        grad_hidden = jnp.concatenate(lows, axis=0)
        product = jnp.dot(second_t[...], grad_hidden, preferred_element_type=jnp.float32)
        grads[:, :, :, :, :, inside] = product.astype(jnp.bfloat16).reshape(
            *grads.shape[:-1], CHUNK
        )
        hidden_sums[:, columns] = jnp.sum(
            grad_hidden.astype(jnp.float32), axis=0, keepdims=True
        )


def back_body(planes, *refs):
    grad_expand, grad_project, grad_heads, qkv, heads, logs, first, attend, refs = *refs[:8], refs[8:]
    attend_out, expand_out, project_out, first_out, bias_out, refs = *refs[:5], refs[5:]
    links = Links(planes, *refs[:3])
    attend_held_scratch, refs = refs[3:8], refs[8:]
    used = scratch_count([grad_expand.shape[-2:], grad_project.shape[-2:]])
    sum_scratch, refs = refs[:used], refs[used:]
    grads_held, qkv_held, heads_held, first_held, attend_held, grad_qkv, refs = *refs[:6], refs[6:]
    key_sum, value_sum, attend_grads, partial, *token_scratch = refs
    micros, latent_rows, _ = qkv.shape
    loads = [
        links.local(grad_heads, grads_held),
        links.local(qkv, qkv_held),
        links.local(heads, heads_held),
        links.local(attend, attend_held),
        links.local(first, first_held),
    ]
    links.greet(links.partners())
    sums = Sums(links, (grad_expand, grad_project), (expand_out, project_out), sum_scratch)
    for k in range(len(sums.pieces)):
        sums.core(k)
    sums.load(0)
    attend_sums = AttendSums(links, attend_grads, attend_out, attend_held_scratch)
    token_sum = TokenSums(links, partial, first_out, token_scratch)

    def head_unit(m, head):
        if m == 0 and head == 0:
            for copy in loads:
                copy.wait()
        attention_back_unit(
            qkv_held.at[m],
            heads_held.at[m],
            grads_held.at[m],
            logs.at[m],
            grad_qkv.at[m],
            key_sum,
            value_sum,
            head,
        )

    def first_unit(m):
        first_product(m, grad_qkv, attend_held, partial)
        token_sum.start(m)

    def attend_unit():
        attend_product(first_held, grad_qkv, attend_grads, planes)
        attend_sums.start()

    def bias_unit():
        total = jnp.zeros((1, grad_qkv.shape[-1]), jnp.float32)
        for m in range(micros):
            total = total + jnp.sum(grad_qkv[m].astype(jnp.float32), axis=0, keepdims=True)
        bias_out[...] = total

    heads_each = OWN // HEAD
    for task, k in BACK_ORDER:
        if task == "head":
            head_unit(k // heads_each, k % heads_each)
        elif task == "first":
            first_unit(k)
        elif task == "attend":
            attend_unit()
        elif task == "bias":
            bias_unit()
        elif task == "t1":
            token_sum.middle(k)
        elif task == "t2":
            token_sum.finish(k)
        elif task == "a1":
            attend_sums.planes()
        elif task == "a2":
            attend_sums.owners()
        elif task == "a3":
            attend_sums.last()
        else:
            getattr(sums, task)(k)
    attend_sums.finish()
    links.finish_sends()


def attend_product(first, grad_qkv, out, planes):
    width = D // planes

    @pl.loop(0, planes)
    def _(plane):
        columns = pl.ds(pl.multiple_of(plane * width, width), width)
        total = None
        for m in range(first.shape[0]):
            product = lax.dot_general(
                first[m, :, columns],
                grad_qkv[m],
                (((0,), (0,)), ((), ())),
                preferred_element_type=jnp.float32,
            )
            total = product if total is None else total + product
        out[plane] = total.astype(jnp.bfloat16).reshape(out.shape[1:])


def first_product(m, grad_qkv, attend, partial):
    rows = partial.shape[3]

    @pl.loop(0, GROUP)
    def _(block):
        here = pl.ds(pl.multiple_of(block * rows, rows), rows)
        product = lax.dot_general(
            grad_qkv[m, here, :],
            attend[...].reshape(D, 3 * OWN),
            (((1,), (1,)), ((), ())),
            preferred_element_type=jnp.float32,
        )
        partial[m, block // 2, block % 2] = product.astype(jnp.bfloat16)


def attend_scratch(attend, planes):
    rows, width = attend.shape[-2:]
    return [
        pltpu.VMEM((planes, 2, 2, rows, width), jnp.bfloat16),
        pltpu.VMEM((planes, 2, 2, rows, width), jnp.bfloat16),
        pltpu.VMEM((planes - 1, 2, 2, rows, width), jnp.bfloat16),
        pltpu.VMEM((2, 2, rows, width), jnp.float32),
        pltpu.VMEM((2, rows, width), jnp.float32),
    ]


def sum_scratch(shapes, planes):
    held = []
    for shape in shapes:
        pieces = cuts(shape)
        rows = shape[0] if shape[1] > WIDTH else shape[0] // len(pieces)
        held.append(low_held(planes, 2, 2, rows, WIDTH))
        for _ in pieces:
            held += [
                low_held(planes, 2, 2, rows, WIDTH),
                low_held(planes, 2, rows, SUMS_OVER_X),
                low_held(planes, 2, rows, WIDTH - SUMS_OVER_X),
                low_held(planes, rows, WIDTH),
                low_held(planes - 1, rows, WIDTH),
            ]
    return held


def count_pieces(shapes):
    return sum(len(cuts(shape)) for shape in shapes)


def scratch_count(shapes):
    return len(shapes) + 5 * count_pieces(shapes)


def full_shape(*shape):
    return jax.ShapeDtypeStruct(shape, jnp.float32)


def low_shape(*shape):
    return jax.ShapeDtypeStruct(shape, jnp.bfloat16)


def full_held(*shape):
    return pltpu.VMEM(shape, jnp.float32)


def low_held(*shape):
    return pltpu.VMEM(shape, jnp.bfloat16)


def sum_sems(shapes, planes):
    return count_pieces(shapes) * (4 + planes)


def weight_sums(attend, weights, planes):
    shapes = [grad.shape[-2:] for grad in weights]
    return remote_call(
        functools.partial(sums_body, planes, len(weights)),
        "weight_sums",
        6,
        (full_shape(2, 2, *attend.shape[-2:]), *(full_shape(*shape) for shape in shapes)),
        [ANY] * (1 + len(weights)),
        (VMEM,) * (1 + len(weights)),
        [*attend_scratch(attend, planes), *sum_scratch(shapes, planes)],
        8 + planes + sum_sems(shapes, planes),
        2 + count_pieces(shapes),
        60 * MIB,
    )(attend, *weights)


def middle_part(grad_contract, weights, held, vectors, planes):
    expand, contract, project = weights
    second = held[2]
    micros, own_rows, _ = second.shape
    own = second.shape
    shape = grad_contract.shape[-2:]
    width = WIDTH
    blocks = width // shape[0]
    return remote_call(
        functools.partial(middle_body, planes),
        "middle",
        6,
        (
            full_shape(*shape),
            low_shape(*own),
            full_shape(*own),
            full_shape(micros, 8, D),
            full_shape(8, D),
            full_shape(1, FF),
            low_shape(*expand.shape),
            low_shape(*project.shape),
            low_shape(micros, own_rows * GROUP, OWN),
        ),
        [ANY] * 12 + [VMEM] * 3,
        (VMEM, VMEM, ANY) + (VMEM,) * 3 + (ANY,) * 3,
        [
            *sum_scratch([shape], planes),
            low_held(2, blocks, *shape),
            low_held(2, *expand.shape[:-1], width),
            low_held(2, micros, own_rows, width),
            low_held(2, micros, own_rows, width),
            low_held(*own),
            low_held(D, micros * own_rows),
            low_held(*own),
            low_held(2, *expand.shape[:-1], width),
            full_held(*own),
            full_held(*own),
            full_held(*own),
            full_held(*own),
            low_held(*own),
            low_held(*project.shape),
            low_held(*own),
            low_held(*own),
            low_held(*project.shape),
            full_held(*own),
            low_held(*own),
        ],
        8 + sum_sems([shape], planes),
        48,
        63 * MIB,
    )(
        grad_contract,
        expand,
        contract.reshape(FF // shape[0], *shape),
        project,
        *held,
        *vectors,
    )


def back_part(grad_expand, grad_project, grad_heads, qkv, heads, logs, first, attend, planes):
    shapes = [grad_expand.shape[-2:], grad_project.shape[-2:]]
    micros, latent_rows, width = qkv.shape
    own_rows = latent_rows // GROUP
    return remote_call(
        functools.partial(back_body, planes),
        "back",
        7,
        (
            full_shape(2, 2, *attend.shape[-2:]),
            *(full_shape(*shape) for shape in shapes),
            full_shape(micros, own_rows, D),
            full_shape(1, width),
        ),
        [ANY] * 5 + [VMEM] + [ANY] * 2,
        (VMEM,) * 5,
        [
            *attend_scratch(attend, planes),
            *sum_scratch(shapes, planes),
            low_held(*grad_heads.shape),
            low_held(*qkv.shape),
            low_held(*heads.shape),
            low_held(*first.shape),
            low_held(*attend.shape),
            low_held(*qkv.shape),
            full_held(latent_rows, HEAD),
            full_held(latent_rows, HEAD),
            low_held(*attend.shape),
            low_held(micros, 2, 2, own_rows, D),
            low_held(2, micros, own_rows, D),
            low_held(micros, own_rows, D),
        ],
        20 + planes + sum_sems(shapes, planes),
        8 + count_pieces(shapes),
        63 * MIB,
    )(grad_expand, grad_project, grad_heads, qkv, heads, logs, first, attend)


def normalize(values):
    center = values - jnp.mean(values, axis=-1, keepdims=True)
    spread_of = jnp.mean(center * center, axis=-1, keepdims=True)
    scale = lax.rsqrt(spread_of + epsilon)
    return center * scale, scale


def norm_back(grads, normed, scale, factors):
    inner = grads * (1.0 + factors)
    return scale * (
        inner
        - jnp.mean(inner, axis=-1, keepdims=True)
        - normed * jnp.mean(inner * normed, axis=-1, keepdims=True)
    )


def einsum(spec, left, right):
    return jnp.einsum(spec, left, right, preferred_element_type=jnp.float32)


def per_device(tokens, condition, attend, project, expand, contract, modulate, biases, cotangent):
    devices = lax.axis_size("fsdp")
    planes = devices // 8
    latents = devices // GROUP
    me = lax.axis_index("fsdp")
    quarter, latent = me % GROUP, me // GROUP
    micros, own_rows, _ = tokens.shape
    latent_rows = own_rows * GROUP
    rows = D // devices
    grid = (planes, 2, 2, 2)

    held = jnp.concatenate([condition.reshape(-1), biases]).astype(jnp.float32)
    held = jnp.pad(held, (0, -held.size % (8 * LANES)))
    small = small_gather(held.reshape(-1, LANES), planes, 0).reshape(devices, -1)
    conditions = small[:, : condition.size].reshape(latents, GROUP, micros, -1)
    conditions = conditions.transpose(2, 0, 1, 3).reshape(micros * latents, D)
    cond_act = silu(conditions).astype(jnp.bfloat16)
    bias_all = small[:, condition.size : condition.size + biases.size].reshape(-1)
    bias_query = bias_all[0:D]
    bias_value = bias_all[D : 2 * D]
    bias_project = bias_all[2 * D : 3 * D]
    bias_expand = bias_all[3 * D : 3 * D + FF]
    bias_contract = bias_all[3 * D + FF : 4 * D + FF]
    bias_modulate = bias_all[4 * D + FF :]

    modulate_rows = modulate.reshape(rows, 6 * D)
    cond_own = lax.dynamic_slice_in_dim(cond_act, me * rows, rows, axis=1)
    partial = jnp.dot(cond_own, modulate_rows, preferred_element_type=jnp.float32)
    partial = partial.reshape(micros, latents, GROUP, -1).transpose(1, 2, 0, 3)
    partial = partial.reshape(planes, 2, 2, 2, -1, LANES)

    attend_shard = attend.reshape(rows, 3, 2, 2, OWN).transpose(2, 3, 0, 1, 4)
    bias_row = jnp.concatenate(
        [
            lax.dynamic_slice_in_dim(bias_query, quarter * OWN, OWN),
            jnp.zeros((OWN,), jnp.float32),
            lax.dynamic_slice_in_dim(bias_value, quarter * OWN, OWN),
        ]
    )
    shards = (
        tokens,
        attend_shard.reshape(2, 2, rows, 3 * OWN),
        project.reshape(rows, D),
        expand.reshape(rows, FF),
        contract.reshape(FF // devices, D),
        partial,
    )
    shift = bias_modulate.reshape(6, D)
    fused = rows % 16 == 0 and own_rows % QUERY_ROWS == 0 and planes * 2 <= 8
    if fused:
        vectors = (shift, bias_row[None], bias_project[None], bias_expand[None])
        attend_all, project_all, expand_all, contract_all, modulation_all, *rest = front(
            *shards, vectors, cotangent, planes
        )
    else:
        attend_all, project_all, expand_all, contract_all, modulation_all, *rest = gather_all(
            *shards, planes
        )
    modulation = modulation_all.reshape(GROUP, micros, -1).transpose(1, 0, 2)
    modulation = modulation.reshape(micros, 6 * D) + bias_modulate
    offsets_one, factors_one, gates_one, offsets_two, factors_two, gates_two = (
        modulation[:, None, part * D : (part + 1) * D] for part in range(6)
    )
    inputs = tokens.astype(jnp.float32)
    if fused:
        first, projected, heads, logs, blended, middle, attended, second, act, slope, low, grads = rest
        contract_sum, output, grad_middle, row_sums, bias_sums, hidden_sums, *onward = middle_part(
            grads.reshape(*grid, FF // devices, D),
            (expand_all, contract_all, project_all),
            (act, slope, second, low, middle, attended, cotangent, blended),
            (modulation_all, shift, bias_contract[None]),
            planes,
        )
        attend_sum, expand_sum, project_sum, grad_first, heads_sum = back_part(
            *onward, projected, heads, logs, first, attend_all, planes
        )
        heads_sum, attended_sum, branch_sum = heads_sum[0], bias_sums[0], bias_sums[1]
        hidden_sum = hidden_sums[0]
        later_sums = row_sums[:, 2:6].reshape(micros, 4 * D)
    else:
        attend_own = attend_all.reshape(D, 3 * OWN)
        project_full = project_all.reshape(D, D)
        expand_full = expand_all.reshape(D, FF)
        contract_full = contract_all.reshape(FF, D)
        tokens_latent = rest[0].reshape(micros, latent_rows, D)
        normed_latent, _ = normalize(tokens_latent.astype(jnp.float32))
        first = (normed_latent * (1.0 + factors_one) + offsets_one).astype(jnp.bfloat16)
        projected = (einsum("mrd,de->mre", first, attend_own) + bias_row).astype(jnp.bfloat16)
        blended_heads, logs = attention(projected)
        blended = heads_to_tokens(blended_heads)

        attended = einsum("mrd,de->mre", blended, project_full) + bias_project
        middle = inputs + gates_one * attended
        normed_two, scale_two = normalize(middle)
        second = (normed_two * (1.0 + factors_two) + offsets_two).astype(jnp.bfloat16)
        hidden = einsum("mrd,de->mre", second, expand_full) + bias_expand
        activated, gelu_pull = jax.vjp(lambda v: jax.nn.gelu(v, approximate=True), hidden)
        act_low = activated.astype(jnp.bfloat16)
        branch = einsum("mrd,de->mre", act_low, contract_full) + bias_contract
        output = (middle + gates_two * branch).astype(jnp.bfloat16)

        upstream = cotangent.astype(jnp.float32)
        grad_branch = (gates_two * upstream).astype(jnp.bfloat16)
        grad_contract = einsum("mrd,mre->de", act_low, grad_branch)
        grad_act = einsum("mre,de->mrd", grad_branch, contract_full)
        grad_hidden = gelu_pull(grad_act)[0].astype(jnp.bfloat16)
        grad_expand = einsum("mrd,mre->de", second, grad_hidden)
        grad_second = einsum("mre,de->mrd", grad_hidden, expand_full)
        grad_middle = upstream + norm_back(grad_second, normed_two, scale_two, factors_two)
        grad_attended = (gates_one * grad_middle).astype(jnp.bfloat16)
        grad_project = einsum("mrd,mre->de", blended, grad_attended)
        grad_blended = einsum("mre,de->mrd", grad_attended, project_full).astype(jnp.bfloat16)
        grad_heads = tokens_to_heads(grad_blended)
        grad_projected = attention_back(projected, blended_heads, grad_heads, logs)
        grad_attend = einsum("mrd,mre->de", first, grad_projected)
        grad_first = token_sums(
            einsum("mre,de->mrd", grad_projected, attend_own).astype(jnp.bfloat16)
        )
        weights = (
            grad_contract.astype(jnp.bfloat16).reshape(*grid, FF // devices, D),
            grad_expand.astype(jnp.bfloat16).reshape(*grid, rows, FF),
            grad_project.astype(jnp.bfloat16).reshape(*grid, rows, D),
        )
        attend_sum, contract_sum, expand_sum, project_sum = weight_sums(
            grad_attend.astype(jnp.bfloat16).reshape(*grid, rows, 3 * OWN), weights, planes
        )

        def token_sum(values):
            return jnp.sum(values, axis=(0, 1), dtype=jnp.float32)

        heads_sum, attended_sum = token_sum(grad_projected), token_sum(grad_attended)
        hidden_sum, branch_sum = token_sum(grad_hidden), token_sum(grad_branch)
        later_sums = jnp.concatenate(
            [
                jnp.sum(grad_middle * attended, axis=1),
                jnp.sum(grad_second, axis=1),
                jnp.sum(grad_second * normed_two, axis=1),
                jnp.sum(upstream * branch, axis=1),
            ],
            axis=1,
        )
    normed_one, scale_one = normalize(inputs)
    grad_tokens = grad_middle + norm_back(grad_first, normed_one, scale_one, factors_one)

    grad_modulation = jnp.concatenate(
        [jnp.sum(grad_first, axis=1), jnp.sum(grad_first * normed_one, axis=1), later_sums], axis=1
    )
    bias_terms = jnp.concatenate(
        [
            lax.dynamic_update_slice(
                jnp.zeros((D,), jnp.float32), heads_sum[:OWN], (quarter * OWN,)
            ),
            lax.dynamic_update_slice(
                jnp.zeros((D,), jnp.float32), heads_sum[2 * OWN :], (quarter * OWN,)
            ),
            attended_sum,
            hidden_sum,
            branch_sum,
        ]
    )
    to_sum = jnp.concatenate(
        [
            grad_modulation.reshape(micros, GROUP, -1).transpose(1, 0, 2).reshape(GROUP, -1),
            bias_terms.reshape(GROUP, -1),
        ],
        axis=1,
    )
    sums = small_sums(to_sum.reshape(2, 2, -1, LANES), planes).reshape(latents, GROUP, -1)
    split = micros * 6 * D // GROUP
    grad_modulations = sums[:, :, :split].reshape(latents, GROUP, micros, -1)
    grad_modulations = grad_modulations.transpose(2, 0, 1, 3).reshape(micros * latents, 6 * D)
    bias_sums = jnp.concatenate(
        [jnp.sum(sums[:, :, split:], axis=0).reshape(-1), jnp.sum(grad_modulations, axis=0)]
    )
    grad_biases = lax.dynamic_slice_in_dim(bias_sums, me * biases.size, biases.size)
    grad_modulate = lax.dot_general(
        cond_own.astype(jnp.float32),
        grad_modulations,
        (((0,), (0,)), ((), ())),
        precision=highest,
    )
    grad_cond_cols = lax.dot_general(
        grad_modulations,
        modulate_rows.astype(jnp.float32),
        (((1,), (1,)), ((), ())),
        precision=highest,
    )
    cols = grad_cond_cols.reshape(-1)
    cols = jnp.pad(cols, (0, -cols.size % (8 * LANES)))
    cols_all = small_gather(cols.reshape(-1, LANES), planes, 8).reshape(devices, -1)
    cols_all = cols_all[:, : micros * latents * rows].reshape(devices, micros, latents, rows)
    cols_own = lax.dynamic_index_in_dim(cols_all, latent, axis=2, keepdims=False)
    width = D // GROUP
    cols_own = lax.dynamic_slice_in_dim(
        cols_own, quarter * (devices // GROUP), devices // GROUP, axis=0
    )
    grad_silu = cols_own.transpose(1, 0, 2).reshape(micros, width)
    values = condition.astype(jnp.float32)
    gate = 1.0 / (1.0 + jnp.exp(-values))
    grad_condition = gate * (1.0 + values * (1.0 - gate)) * grad_silu

    attend_sum = attend_sum.reshape(2, 2, rows, 3, OWN).transpose(2, 3, 0, 1, 4)
    return (
        output,
        grad_tokens,
        grad_condition,
        attend_sum.reshape(-1),
        project_sum.reshape(-1),
        expand_sum.reshape(-1),
        contract_sum.reshape(-1),
        grad_modulate.reshape(-1),
        grad_biases,
    )


def solution(mesh):
    in_specs = (
        P(None, "fsdp", None),
        P(None, "fsdp"),
        P("fsdp"),
        P("fsdp"),
        P("fsdp"),
        P("fsdp"),
        P("fsdp"),
        P("fsdp"),
        P(None, "fsdp", None),
    )
    out_specs = (
        P(None, "fsdp", None),
        P(None, "fsdp", None),
        P(None, "fsdp"),
        P("fsdp"),
        P("fsdp"),
        P("fsdp"),
        P("fsdp"),
        P("fsdp"),
        P("fsdp"),
    )
    return jax.shard_map(
        per_device, mesh=mesh, in_specs=in_specs, out_specs=out_specs, check_vma=False
    )
```

```python
import functools

import jax
import jax.numpy as jnp
from jax import lax
from jax.experimental import pallas as pl
from jax.experimental.pallas import tpu as pltpu
from jax.sharding import PartitionSpec as P

D = 1024
HEADS = 16
HEAD = 64
FF = 4096
GROUP = 4
OWN = D // GROUP
SCALE = HEAD**-0.5
LANES = 128
MICROS = 2

epsilon = 1e-06
highest = lax.Precision.HIGHEST
MESH = pl.DeviceIdType.MESH
MIB = 1 << 20


def silu(values):
    return values / (1.0 + jnp.exp(-values))


class Links:
    def __init__(self, planes, send_sem, recv_sem, local_sem=None):
        me = lax.axis_index("fsdp")
        self.planes = planes
        self.c = me % 2
        self.x = (me // 2) % 2
        self.y = (me // 4) % 2
        self.z = me // 8
        self.core = me + 1 - 2 * self.c
        self.beside = me + 2 - 4 * self.x
        self.across = me + 4 - 8 * self.y
        self.place = me % 8
        self.send_sem, self.recv_sem, self.local_sem = send_sem, recv_sem, local_sem
        self.used = 0
        self.local_used = 0
        self.pending = []

    def plane(self, step):
        return (self.z + step) % self.planes

    def plane_device(self, step):
        return self.plane(step) * 8 + self.place

    def column(self):
        places = []
        for step in range(self.planes):
            for y in (self.y, 1 - self.y):
                if step > 0 or y is not self.y:
                    z = self.plane(step)
                    places.append((z, y, z * 8 + y * 4 + self.place % 4))
        return places

    def partners(self):
        return [self.core, self.beside] + [device for _, _, device in self.column()]

    def greet(self, partners):
        barrier = pltpu.get_barrier_semaphore()
        for partner in partners:
            pl.semaphore_signal(barrier, inc=1, device_id=(partner,), device_id_type=MESH)
        pl.semaphore_wait(barrier, len(partners))

    def send(self, source, target, device):
        assert self.used < self.send_sem.shape[0]
        copy = pltpu.make_async_remote_copy(
            src_ref=source,
            dst_ref=target,
            send_sem=self.send_sem.at[self.used],
            recv_sem=self.recv_sem.at[self.used],
            device_id=(device,),
            device_id_type=MESH,
        )
        self.used += 1
        copy.start()
        self.pending.append(copy)
        return copy

    def local(self, source, target):
        assert self.local_used < self.local_sem.shape[0]
        copy = pltpu.make_async_copy(source, target, self.local_sem.at[self.local_used])
        self.local_used += 1
        copy.start()
        return copy

    def finish_sends(self):
        for copy in self.pending:
            copy.wait_send()
        self.pending = []


def arrived(copies):
    for copy in copies:
        copy.wait_recv()


ANY = pl.BlockSpec(memory_space=pl.ANY)
VMEM = pl.BlockSpec(memory_space=pltpu.VMEM)


def remote_call(body, name, collective_id, outs, in_specs, out_specs, scratch, sems, local_sems, vmem):
    return pl.pallas_call(
        body,
        out_shape=outs,
        in_specs=in_specs,
        out_specs=out_specs,
        scratch_shapes=[
            pltpu.SemaphoreType.DMA((sems,)),
            pltpu.SemaphoreType.DMA((sems,)),
            pltpu.SemaphoreType.DMA((max(local_sems, 1),)),
            *scratch,
        ],
        compiler_params=pltpu.CompilerParams(
            collective_id=collective_id, has_side_effects=True, vmem_limit_bytes=vmem
        ),
        name=name,
    )


def small_gather_body(planes, own_ref, out_ref, send_sem, recv_sem, local_sem):
    links = Links(planes, send_sem, recv_sem)
    links.greet(links.partners())
    z, y, x, c = links.z, links.y, links.x, links.c
    out_ref[z, y, x, c] = own_ref[...]
    spread_all(links, out_ref)
    links.finish_sends()


def spread_all(links, out_ref):
    spread = Spread(links, out_ref)
    for k in range(4):
        spread.step(k)


def small_gather(own, planes, collective_id):
    return remote_call(
        functools.partial(small_gather_body, planes),
        "small_gather",
        collective_id,
        jax.ShapeDtypeStruct((planes, 2, 2, 2, *own.shape), own.dtype),
        [VMEM],
        VMEM,
        [],
        2 * planes + 4,
        0,
        40 * MIB,
    )(own)


WIDTH = 1024
HALF = WIDTH // 2
ALL = slice(None)


class Pieces:
    def __init__(self, links, shards, fulls):
        self.links = links
        self.pieces, self.owns = [], []
        for shard, full in zip(shards, fulls):
            z, y, x, c = links.z, links.y, links.x, links.c
            self.owns.append([links.local(shard, full.at[z, y, x, c]), False])
            for rows, start in cuts(shard.shape):
                self.pieces.append((len(self.owns) - 1, shard, full, rows, start))
        self.count = len(self.pieces)
        self.lead = [None] * self.count
        self.rest = [None] * self.count
        self.late = [[] for _ in range(self.count)]

    def columns(self, k, half):
        return pl.ds(self.pieces[k][4] + half * HALF, HALF)

    def block(self, k, half, *place):
        _, _, full, rows, _ = self.pieces[k]
        return full.at[(*place, rows, self.columns(k, half))]

    def own_block(self, k, half):
        _, shard, _, rows, _ = self.pieces[k]
        links = self.links
        return shard.at[rows, self.columns(k, half)], self.block(
            k, half, links.z, links.y, links.x, links.c
        )

    def own_there(self, k):
        own = self.owns[self.pieces[k][0]]
        if not own[1]:
            own[0].wait()
            own[1] = True

    def to_core(self, k, half, *place):
        block = self.block(k, half, *place)
        self.late[k].append(self.links.send(block, block, self.links.core))

    def to_planes(self, source, target):
        links = self.links
        return [links.send(source, target, links.plane_device(s)) for s in range(1, links.planes)]

    def T0(self, k):
        if k < self.count:
            self.lead[k] = [self.links.send(*self.own_block(k, 0), self.links.beside)]

    def T1(self, k):
        links = self.links
        self.own_there(k)
        arrived(self.lead[k])
        block = self.block(k, 0, links.z, links.y, ALL, links.c)
        self.lead[k] = self.to_planes(block, block)
        self.T0(k + AHEAD)

    def T2(self, k):
        links = self.links
        arrived(self.lead[k])
        place = (ALL, links.y, ALL, links.c)
        block = self.block(k, 0, *place)
        self.lead[k] = [links.send(block, block, links.across)]
        self.to_core(k, 0, *place)

    def T3(self, k):
        links = self.links
        arrived(self.lead[k])
        self.to_core(k, 0, ALL, 1 - links.y, ALL, links.c)

    def F0(self, k):
        if k < self.count:
            self.rest[k] = self.to_planes(*self.own_block(k, 1))

    def F1(self, k):
        links = self.links
        self.own_there(k)
        arrived(self.rest[k])
        place = (ALL, links.y, links.x, links.c)
        block = self.block(k, 1, *place)
        self.rest[k] = [links.send(block, block, links.across)]
        self.to_core(k, 1, *place)
        self.F0(k + AHEAD)

    def F2(self, k):
        links = self.links
        arrived(self.rest[k])
        block = self.block(k, 1, ALL, ALL, links.x, links.c)
        self.rest[k] = [links.send(block, block, links.beside)]
        self.to_core(k, 1, ALL, 1 - links.y, links.x, links.c)

    def F3(self, k):
        links = self.links
        arrived(self.rest[k])
        self.to_core(k, 1, ALL, ALL, 1 - links.x, links.c)

    def there(self, k):
        arrived(self.late[k])
        self.late[k] = []


def tasks_of(order):
    return [(TASKS[code // 32], code % 32) for code in order]


TASKS = (
    "fb", "az", "sp", "ay", "pm", "tk", "F1", "F2", "att", "unit", "T1", "F3", "T2", "T3", "load",
    "own", "there", "mlp", "S1", "F4", "T4", "project", "head", "first", "t1", "attend", "small",
    "a1", "t2", "a2", "sums", "a3", "modulate", "cond",
)


def cuts(shape):
    rows, width = shape
    if width > WIDTH:
        return [(slice(None), start) for start in range(0, width, WIDTH)]
    count = 4 if rows % 128 == 0 else 1
    return [(pl.ds(part * (rows // count), rows // count), 0) for part in range(count)]


AHEAD = 3


class Opening:
    TOKEN_CUTS = 8
    ATTEND_CUTS = 4

    def __init__(self, links, tokens, attend, partial, tokens_out, attend_out, modulation_out, scratch):
        self.links, self.partial, self.attend = links, partial, attend
        self.tokens, self.tokens_out = tokens, tokens_out
        self.attend_out, self.modulation_out = attend_out, modulation_out
        self.held, self.from_core, self.from_beside, self.from_column, self.total = scratch
        z, y, x, c = links.z, links.y, links.x, links.c
        target = attend_out.at[z, y, x, c]
        self.own_slice = links.local(attend.at[x, c], target)
        self.own_tokens = links.local(tokens, tokens_out.at[:, x, c])
        self.far = links.send(attend.at[1 - x, 1 - c], self.held, links.core)
        self.near = [
            links.send(attend.at[x, 1 - c], target, links.core),
            links.send(attend.at[1 - x, c], target, links.beside),
        ]
        self.over_planes, self.beside, self.rest = {}, {}, []

    def tokens_start(self):
        links = self.links
        target = self.tokens_out.at[:, links.x, links.c]
        self.rest.append(links.send(self.tokens, target, links.core))
        for k in range(2):
            self.tkx(k)

    def token_block(self, k):
        each = self.TOKEN_CUTS // self.tokens.shape[0]
        rows = self.tokens.shape[1] // each
        return k // each, pl.ds(k % each * rows, rows)

    def tkx(self, k):
        links = self.links
        m, rows = self.token_block(k)
        target = self.tokens_out.at[m, links.x, links.c, rows]
        self.beside[k] = links.send(self.tokens.at[m, rows], target, links.beside)

    def tk(self, k):
        links = self.links
        arrived([self.beside.pop(k)])
        m, rows = self.token_block(k)
        fresh = self.tokens_out.at[m, 1 - links.x, links.c, rows]
        self.rest.append(links.send(fresh, fresh, links.core))
        if k + 2 < self.TOKEN_CUTS:
            self.tkx(k + 2)

    def fb(self, k):
        links = self.links
        arrived([self.far])
        target = self.attend_out.at[links.z, links.y, links.x, 1 - links.c]
        self.near.append(links.send(self.held, target, links.beside))

    def attend_block(self, k, *place):
        pair = k // 2
        return self.attend_out.at[(*place, k % 2, ALL, ALL, pl.ds(pair * PAIR, PAIR))]

    def azx(self, k):
        links = self.links
        block = self.attend_block(k, links.z, links.y)
        self.over_planes[k] = [
            links.send(block, block, links.plane_device(s)) for s in range(1, links.planes)
        ]

    def az(self, k):
        self.own_slice.wait()
        arrived(self.near)
        self.azx(0)
        self.azx(1)

    def ay(self, k):
        links = self.links
        arrived(self.over_planes.pop(k))
        block = self.attend_block(k, ALL, links.y)
        self.rest.append(links.send(block, block, links.across))
        if k + 2 < self.ATTEND_CUTS:
            self.azx(k + 2)

    def pm(self, k):
        links = self.links
        z, y, x, c = links.z, links.y, links.x, links.c
        if k > 0:
            arrived(self.step)
        if k == 0:
            self.step = [links.send(self.partial.at[:, :, :, 1 - c], self.from_core, links.core)]
        elif k == 1:
            self.from_core[...] = self.from_core[...] + self.partial[:, :, :, c]
            self.step = [
                links.send(self.from_core.at[:, :, 1 - x], self.from_beside, links.beside)
            ]
        elif k == 2:
            self.from_beside[...] = self.from_beside[...] + self.from_core[:, :, x]
            self.step = [
                links.send(self.from_beside.at[to_z, to_y], self.from_column.at[place], device)
                for place, (to_z, to_y, device) in enumerate(links.column())
            ]
        elif k == 3:
            result = self.from_beside[z, y]
            for place in range(2 * links.planes - 1):
                result = result + self.from_column[place]
            self.total[...] = result
            target = self.modulation_out.at[x, c]
            target[...] = result
            self.step = [
                links.send(self.total, target, links.core),
                links.send(self.total, target, links.beside),
            ]
        else:
            fresh = self.modulation_out.at[1 - x, c]
            self.rest.append(links.send(fresh, fresh, links.core))

    def finish(self):
        arrived(self.rest)
        self.own_tokens.wait()


def gather_body(
    planes,
    tokens,
    attend,
    project,
    expand,
    contract,
    partial,
    attend_out,
    project_out,
    expand_out,
    contract_out,
    modulation_out,
    tokens_out,
    send_sem,
    recv_sem,
    local_sem,
    *scratch,
):
    links = Links(planes, send_sem, recv_sem, local_sem)
    links.greet(links.partners())
    opening = Opening(
        links, tokens, attend, partial, tokens_out, attend_out, modulation_out, scratch
    )
    pieces = Pieces(links, (project, expand, contract), (project_out, expand_out, contract_out))
    opening.tokens_start()
    for k in range(5):
        opening.pm(k)
    for k in range(Opening.TOKEN_CUTS):
        opening.tk(k)
    opening.fb(0)
    opening.az(0)
    for k in range(Opening.ATTEND_CUTS):
        opening.ay(k)
    for k in range(AHEAD):
        pieces.T0(k)
        pieces.F0(k)
    for k in range(pieces.count + 2):
        for behind, names in enumerate((("T1", "F1"), ("T2", "F2"), ("T3", "F3"))):
            if 0 <= k - behind < pieces.count:
                for name in names:
                    getattr(pieces, name)(k - behind)
    for k in range(pieces.count):
        pieces.there(k)
    opening.finish()
    links.finish_sends()


FRONT_ORDER = (
    0, 32, 65, 66, 96, 128, 160, 97, 161, 129, 98, 162, 163, 99, 130, 164, 192, 165, 193, 166, 131,
    194, 224, 167, 195, 132, 196, 256, 288, 225, 320, 197, 226, 289, 352, 198, 321, 199, 290, 227,
    291, 322, 353, 384, 292, 293, 200, 323, 354, 294, 416, 385, 228, 324, 295, 355, 296, 297, 386,
    298, 325, 417, 299, 387, 300, 301, 326, 229, 418, 302, 356, 388, 303, 327, 230, 304, 419, 305,
    389, 448, 328, 231, 480, 420, 390, 513, 544, 357, 232, 421, 391, 358, 514, 545, 422, 392, 515,
    546, 359, 423, 516, 547, 360, 424,
)


def front_body(planes, *refs):
    tokens, attend, project, expand, contract, payload, modulate, cotangent, refs = *refs[:8], refs[8:]
    attend_out, project_out, expand_out, contract_out, modulation_out, refs = *refs[:5], refs[5:]
    normed_out, qkv_out, heads_out, log_out, blended_out, refs = *refs[:5], refs[5:]
    middle_out, attended_out, second_out, act_out, slope_out, branch_out, grad_out = refs[:7]
    bias_rows, cond_out, refs = *refs[7:9], refs[9:]
    send_sem, recv_sem, local_sem = refs[:3]
    opening_scratch, refs = refs[3:8], refs[8:]
    payloads, partial, refs = *refs[:2], refs[2:]
    tokens_all, attend_all, normed, qkv, heads, blended, project_all, expand_all = refs[:8]
    middle, attended, second, act, slope, grad_branch, grads, upstream, bias_held = refs[8:]
    links = Links(planes, send_sem, recv_sem, local_sem)
    z, y, x, c = links.z, links.y, links.x, links.c
    corner = links.beside + 1 - 2 * c
    links.greet([*links.partners(), corner])
    payloads[z, y, x, c] = payload[...]
    spread = Spread(links, payloads)
    spread.step(0)
    opening = Opening(
        links, tokens, attend, partial, tokens_all, attend_all, modulation_out, opening_scratch
    )
    pieces = Pieces(links, (project, expand, contract), (project_out, expand_out, contract_out))
    count = pieces.count
    loaded_upstream = links.local(cotangent, upstream)
    micros, own_rows, _ = tokens.shape
    stored, stored_grads, exchanged, loading = [], [], [], []
    own_heads = pl.ds(pl.multiple_of((2 * x + c) * OWN, OWN), OWN)

    def partial_unit():
        latents, rows = 2 * planes, modulate.shape[0]
        each = latents
        source = (links.z * 8 + links.place) // each
        column = (links.z * 8 + links.place) % each
        conds = [
            payloads[:, :, source // 2, source % 2, pl.ds(micros * column + m, 1), :].reshape(
                latents, LANES
            )
            for m in range(micros)
        ]
        active = silu(jnp.concatenate(conds, axis=0)[:, :rows]).astype(jnp.bfloat16)
        cond_out[...] = active.astype(jnp.float32)
        product = jnp.dot(active, modulate[...], preferred_element_type=jnp.float32)
        per_quarter = 6 * D // LANES // GROUP
        for m in range(micros):
            for k in range(6 * D // LANES):
                quarter, row = k // per_quarter, m * per_quarter + k % per_quarter
                values = product[m * latents : (m + 1) * latents, k * LANES : (k + 1) * LANES]
                partial[:, :, quarter // 2, quarter % 2, row, :] = values.reshape(
                    planes, 2, LANES
                )
        opening.pm(0)
        start = micros * each
        long = bias_rows.shape[0] // (4 * planes)
        for pair in range(4 * planes):
            place = (pair // 4, pair // 2 % 2, pair % 2)
            even = payloads[(*place, 0, slice(start, start + 4), ALL)]
            odd = payloads[(*place, 1, slice(start, start + 4), ALL)]
            joint = even[3:4] + odd[0:1]
            bias_rows[pair * long : (pair + 1) * long, :] = jnp.concatenate(
                [even[:3], joint, odd[1:]], axis=0
            )

    def shift(block):
        return bias_vector(bias_rows, 4 * D + FF + block * D, D)

    def part_of(m, to_x, to_c):
        start = pl.multiple_of((2 * to_x + to_c) * own_rows, own_rows)
        return heads.at[m, pl.ds(start, own_rows)]

    def project_micro(m):
        own = (2 * x + c) * PAIRS
        bias_qkv = []
        for pair in range(PAIRS):
            bias_qkv += [
                bias_rows[pl.ds(own + pair, 1), :],
                jnp.zeros((1, LANES), jnp.float32),
                bias_rows[pl.ds(D // LANES + own + pair, 1), :],
            ]
        offsets = modulation_row(modulation_out, m, 0) + shift(0)
        factors = 1.0 + modulation_row(modulation_out, m, 1) + shift(1)
        bias = jnp.concatenate(bias_qkv, axis=1)
        project_tokens(m, tokens_all, attend_all, offsets, factors, bias, normed, qkv)
        stored.append(links.local(normed.at[m], normed_out.at[m]))
        stored.append(links.local(qkv.at[m], qkv_out.at[m]))

    def far_heads(m, head):
        attention_unit(qkv.at[m], heads.at[m], log_out.at[m], head, 1 - x)
        if head == OWN // HEAD - 1:
            target = blended.at[m, :, own_heads]
            exchanged.append(links.send(part_of(m, 1 - x, 1 - c), target, corner))
            exchanged.append(links.send(part_of(m, 1 - x, c), target, links.beside))

    def near_heads(m, head):
        attention_unit(qkv.at[m], heads.at[m], log_out.at[m], head, x)
        if head == OWN // HEAD - 1:
            target = blended.at[m, :, own_heads]
            exchanged.append(links.send(part_of(m, x, 1 - c), target, links.core))
            stored.append(links.local(heads.at[m], heads_out.at[m]))
            links.local(part_of(m, x, c), target).wait()

    units = []
    for m in range(micros):
        units.append(functools.partial(project_micro, m))
        units += [functools.partial(far_heads, m, head) for head in range(OWN // HEAD)]
    for m in range(micros):
        units += [functools.partial(near_heads, m, head) for head in range(OWN // HEAD)]

    def load_project():
        pieces.there(0)
        loading.append(links.local(project_out, project_all))
        loaded_upstream.wait()
        for m in range(micros):
            gate = modulation_row(modulation_out, m, 5) + shift(5)
            grad_branch[m] = (gate * upstream[m].astype(jnp.float32)).astype(jnp.bfloat16)
        stored.append(links.local(grad_branch, branch_out))

    def own_tokens():
        loading.pop().wait()
        for m in range(micros):
            stored.append(links.local(blended.at[m], blended_out.at[m]))
            product = jnp.dot(
                blended[m],
                project_all[...].reshape(D, D),
                preferred_element_type=jnp.float32,
            )
            attended[m] = product + bias_vector(bias_rows, 2 * D, D)
            gate = modulation_row(modulation_out, m, 2) + shift(2)
            middle[m] = tokens_all[m, x, c].astype(jnp.float32) + gate * attended[m]
            normed_two, _ = normalize(middle[m])
            factors = 1.0 + modulation_row(modulation_out, m, 4) + shift(4)
            offsets = modulation_row(modulation_out, m, 3) + shift(3)
            second[m] = (normed_two * factors + offsets).astype(jnp.bfloat16)
        stored.append(links.local(middle, middle_out))
        stored.append(links.local(attended, attended_out))
        stored.append(links.local(second, second_out))

    parts = FF // WIDTH
    blocks = grads.shape[1]

    def expand_unit(part):
        columns = pl.ds(part * WIDTH, WIDTH)
        loaded = links.local(expand_out.at[:, :, :, :, :, columns], expand_all)
        if part >= 2:
            stored_grads[part - 2].wait()
        loaded.wait()
        bias = bias_vector(bias_rows, 3 * D + part * WIDTH, WIDTH)
        bias_held[...] = bias
        expand_part(part, WIDTH, second, expand_all, bias_held, act, slope, grad_branch, grads)
        stored.append(links.local(act.at[:, :, columns], act_out.at[:, :, columns]))
        stored.append(links.local(slope.at[:, :, columns], slope_out.at[:, :, columns]))
        stored_grads.append(
            links.local(grads.at[part % 2], grad_out.at[pl.ds(part * blocks, blocks)])
        )

    for task, k in tasks_of(FRONT_ORDER):
        if task == "sp":
            spread.step(k)
            if k == 1:
                opening.tokens_start()
        elif task in ("fb", "az", "ay", "tk"):
            getattr(opening, task)(k)
            if task == "ay" and k == Opening.ATTEND_CUTS - 2:
                for piece in range(AHEAD):
                    pieces.F0(piece)
            if task == "tk" and k == Opening.TOKEN_CUTS - 2:
                for piece in range(AHEAD):
                    pieces.T0(piece)
        elif task == "pm":
            if k == 0:
                spread.step(3)
                partial_unit()
            else:
                opening.pm(k)
        elif task == "att":
            opening.finish()
            stored.append(links.local(attend_all, attend_out))
        elif task == "unit":
            units[k]()
        elif task == "load":
            load_project()
        elif task == "own":
            arrived(exchanged)
            own_tokens()
        elif task == "there":
            pieces.there(k)
        elif task == "mlp":
            expand_unit(k)
        else:
            getattr(pieces, task)(k)
    for k in range(count):
        pieces.there(k)
    for copy in stored + stored_grads[-2:]:
        copy.wait()
    links.finish_sends()


ROOT = 0.7978845608028654
CUBE = 0.044715
CHUNK = 512


def expand_part(part, width, second, expand, bias, act, slope, grad_branch, grads):
    micros = second.shape[0]
    rows = grads.shape[2]

    @pl.loop(0, width // CHUNK)
    def _(chunk):
        inside = pl.ds(pl.multiple_of(chunk * CHUNK, CHUNK), CHUNK)
        columns = pl.ds(pl.multiple_of(part * width + chunk * CHUNK, CHUNK), CHUNK)
        weights = expand[:, :, :, :, :, inside].reshape(D, CHUNK)
        total = None
        for m in range(micros):
            hidden = jnp.dot(second[m], weights, preferred_element_type=jnp.float32)
            hidden = hidden + bias[:, inside]
            square = hidden * hidden
            bend = jnp.tanh(hidden * (ROOT + (ROOT * CUBE) * square))
            half = 0.5 + 0.5 * bend
            low = (hidden * half).astype(jnp.bfloat16)
            act[m, :, columns] = low
            steep = hidden * (0.5 * ROOT + (1.5 * ROOT * CUBE) * square)
            slope[m, :, columns] = (half + steep * (1.0 - bend * bend)).astype(jnp.bfloat16)
            product = lax.dot_general(
                low, grad_branch[m], (((0,), (0,)), ((), ())), preferred_element_type=jnp.float32
            )
            total = product if total is None else total + product
        count = CHUNK // rows
        here = pl.ds(chunk * count, count)
        grads[part % 2, here] = total.astype(jnp.bfloat16).reshape(count, rows, D)


def modulation_row(modulation, m, block):
    per_quarter = modulation.shape[2] // MICROS
    pieces = []
    for k in range(block * D // LANES, (block + 1) * D // LANES):
        quarter, row = k // per_quarter, m * per_quarter + k % per_quarter
        pieces.append(modulation[quarter // 2, quarter % 2, row : row + 1, :])
    return jnp.concatenate(pieces, axis=1)


def bias_vector(bias_rows, start, count):
    rows = range(start // LANES, (start + count) // LANES)
    return jnp.concatenate([bias_rows[row : row + 1, :] for row in rows], axis=1)


def project_tokens(m, tokens, attend, offsets, factors, bias, normed_out, qkv_out):
    rows = tokens.shape[3]

    @pl.loop(0, GROUP)
    def _(block):
        values = tokens[m, block // 2, block % 2].astype(jnp.float32)
        normed, _ = normalize(values)
        first = (normed * factors + offsets).astype(jnp.bfloat16)
        here = pl.ds(pl.multiple_of(block * rows, rows), rows)
        normed_out[m, here, :] = normed.astype(jnp.bfloat16)
        weights = attend[...].reshape(D, 3 * OWN)
        product = jnp.dot(first, weights, preferred_element_type=jnp.float32)
        qkv_out[m, here, :] = (product + bias).astype(jnp.bfloat16)


def gather_scratch(attend, rows, planes):
    return [
        pltpu.VMEM((attend.shape[-2], attend.shape[-1]), attend.dtype),
        pltpu.VMEM((planes, 2, 2, rows, LANES), jnp.float32),
        pltpu.VMEM((planes, 2, rows, LANES), jnp.float32),
        pltpu.VMEM((2 * planes - 1, rows, LANES), jnp.float32),
        pltpu.VMEM((rows, LANES), jnp.float32),
    ]


def gather_outs(attend, project, expand, contract, rows, planes):
    return [
        *(
            jax.ShapeDtypeStruct((planes, 2, 2, 2, *shard.shape[-2:]), shard.dtype)
            for shard in (attend, project, expand, contract)
        ),
        jax.ShapeDtypeStruct((2, 2, rows, LANES), jnp.float32),
    ]


def gather_sems(planes):
    return 60 + 30 * planes + 9 * (8 + 2 * planes)


def gather_all(tokens, attend, project, expand, contract, partial, planes):
    micros, own_rows, _ = tokens.shape
    return remote_call(
        functools.partial(gather_body, planes),
        "gather_all",
        1,
        (
            *gather_outs(attend, project, expand, contract, partial.shape[-2], planes),
            jax.ShapeDtypeStruct((micros, 2, 2, own_rows, D), tokens.dtype),
        ),
        [ANY] * 5 + [VMEM],
        (ANY,) * 4 + (VMEM, ANY),
        gather_scratch(attend, partial.shape[-2], planes),
        gather_sems(planes),
        8,
        56 * MIB,
    )(tokens, attend, project, expand, contract, partial)


def front(tokens, attend, project, expand, contract, payload, modulate, cotangent, planes):
    micros, own_rows, _ = tokens.shape
    latent_rows = own_rows * GROUP
    blocks = latent_rows // QUERY_ROWS
    grad_rows = contract.shape[0]

    def low(*shape):
        return jax.ShapeDtypeStruct(shape, jnp.bfloat16)

    def held(*shape, dtype=jnp.bfloat16):
        return pltpu.VMEM(shape, dtype)

    log_shape = (micros, OWN // HEAD, blocks, 1, QUERY_ROWS)
    own = (micros, own_rows, D)
    parts = FF // WIDTH
    rows = micros * 6 * D // LANES // GROUP
    biases = (10 * D + FF) // LANES
    return remote_call(
        functools.partial(front_body, planes),
        "front",
        1,
        (
            *gather_outs(attend, project, expand, contract, rows, planes),
            low(micros, latent_rows, D),
            low(micros, latent_rows, 3 * OWN),
            low(micros, latent_rows, OWN),
            jax.ShapeDtypeStruct(log_shape, jnp.float32),
            low(*own),
            jax.ShapeDtypeStruct(own, jnp.float32),
            jax.ShapeDtypeStruct(own, jnp.float32),
            low(*own),
            low(micros, own_rows, FF),
            low(micros, own_rows, FF),
            low(*own),
            low(FF // grad_rows, grad_rows, D),
            jax.ShapeDtypeStruct((biases, LANES), jnp.float32),
            jax.ShapeDtypeStruct((micros * 2 * planes, modulate.shape[0]), jnp.float32),
        ),
        [ANY] * 5 + [VMEM] * 2 + [ANY],
        (ANY,) * 4 + (VMEM,) + (ANY,) * 3 + (VMEM,) + (ANY,) * 8 + (VMEM,) * 2,
        [
            *gather_scratch(attend, rows, planes),
            held(planes, 2, 2, 2, *payload.shape, dtype=jnp.float32),
            held(planes, 2, 2, 2, rows, LANES, dtype=jnp.float32),
            held(micros, 2, 2, own_rows, D),
            held(planes, 2, 2, 2, *attend.shape[-2:]),
            held(micros, latent_rows, D),
            held(micros, latent_rows, 3 * OWN),
            held(micros, latent_rows, OWN),
            held(*own),
            held(planes, 2, 2, 2, *project.shape),
            held(planes, 2, 2, 2, expand.shape[0], FF // parts),
            held(*own, dtype=jnp.float32),
            held(*own, dtype=jnp.float32),
            held(*own),
            held(micros, own_rows, FF),
            held(micros, own_rows, FF),
            held(*own),
            held(2, FF // parts // grad_rows, grad_rows, D),
            held(*own),
            held(1, WIDTH, dtype=jnp.float32),
        ],
        gather_sems(planes),
        40,
        60 * MIB,
    )(tokens, attend, project, expand, contract, payload, modulate, cotangent)


QUERY_ROWS = 256
PAIRS = OWN // LANES
PAIR = 3 * LANES


def head_columns(head):
    start = head // 2 * PAIR + head % 2 * HEAD
    return [slice(start + kind * LANES, start + kind * LANES + HEAD) for kind in range(3)]


def attention_unit(qkv, out, log, head, side=None):
    count = qkv.shape[0] // QUERY_ROWS
    start = 0
    if side is not None:
        count //= 2
        start = side * count
    at = head * HEAD
    query_at, key_at, value_at = head_columns(head)
    keys = qkv[:, key_at]
    values_t = qkv[:, value_at].T

    @pl.loop(0, count)
    def _(index):
        block = start + index
        here = pl.ds(pl.multiple_of(block * QUERY_ROWS, QUERY_ROWS), QUERY_ROWS)
        queries = qkv[here, query_at] * SCALE
        scores = lax.dot_general(
            keys, queries, (((1,), (1,)), ((), ())), preferred_element_type=jnp.float32
        )
        top = jnp.max(scores, axis=0, keepdims=True)
        weights = jnp.exp(scores - top)
        totals = jnp.sum(weights, axis=0, keepdims=True)
        blended = jnp.dot(
            values_t, weights.astype(jnp.bfloat16), preferred_element_type=jnp.float32
        )
        out[here, at : at + HEAD] = (blended / totals).T.astype(jnp.bfloat16)
        log[head, block] = top + jnp.log(totals)


def attention_body(qkv_ref, out_ref, log_ref):
    for head in range(OWN // HEAD):
        attention_unit(qkv_ref.at[0], out_ref.at[0], log_ref.at[0], head)


def attention(qkv):
    micros, rows, _ = qkv.shape
    heads = OWN // HEAD
    blocks = rows // 256
    return pl.pallas_call(
        attention_body,
        grid=(micros,),
        out_shape=(
            jax.ShapeDtypeStruct((micros, rows, OWN), jnp.bfloat16),
            jax.ShapeDtypeStruct((micros, heads, blocks, 1, 256), jnp.float32),
        ),
        in_specs=[pl.BlockSpec((1, rows, 3 * OWN), lambda m: (m, 0, 0))],
        out_specs=(
            pl.BlockSpec((1, rows, OWN), lambda m: (m, 0, 0)),
            pl.BlockSpec((1, heads, blocks, 1, 256), lambda m: (m, 0, 0, 0, 0)),
        ),
        compiler_params=pltpu.CompilerParams(vmem_limit_bytes=48 * MIB),
        name="attention",
    )(qkv)


def attention_back_unit(qkv, blended_all, grad_all, log, out, key_sum, value_sum, head):
    at = head * HEAD
    query_at, key_at, value_at = head_columns(head)
    keys = qkv[:, key_at]
    keys_t = keys.T
    values = qkv[:, value_at]
    key_sum[...] = jnp.zeros_like(key_sum)
    value_sum[...] = jnp.zeros_like(value_sum)

    @pl.loop(0, qkv.shape[0] // QUERY_ROWS)
    def _(block):
        here = pl.ds(pl.multiple_of(block * QUERY_ROWS, QUERY_ROWS), QUERY_ROWS)
        queries = qkv[here, query_at] * SCALE
        grads = grad_all[here, at : at + HEAD]
        blended = blended_all[here, at : at + HEAD]
        row_terms = jnp.sum(
            (grads.astype(jnp.float32) * blended.astype(jnp.float32)).T, axis=0, keepdims=True
        )
        scores = lax.dot_general(
            keys, queries, (((1,), (1,)), ((), ())), preferred_element_type=jnp.float32
        )
        chances = jnp.exp(scores - log[head, block])
        grad_chances = lax.dot_general(
            values, grads, (((1,), (1,)), ((), ())), preferred_element_type=jnp.float32
        )
        grad_scores = (chances * (grad_chances - row_terms)).astype(jnp.bfloat16)
        value_sum[...] += jnp.dot(
            chances.astype(jnp.bfloat16), grads, preferred_element_type=jnp.float32
        )
        key_sum[...] += jnp.dot(grad_scores, queries, preferred_element_type=jnp.float32)
        grad_queries = jnp.dot(keys_t, grad_scores, preferred_element_type=jnp.float32)
        out[here, query_at] = (grad_queries.T * SCALE).astype(jnp.bfloat16)

    out[:, key_at] = key_sum[...].astype(jnp.bfloat16)
    out[:, value_at] = value_sum[...].astype(jnp.bfloat16)


def attention_back_body(qkv_ref, blended_ref, grad_ref, log_ref, out_ref, key_sum, value_sum):
    for head in range(OWN // HEAD):
        attention_back_unit(
            qkv_ref.at[0],
            blended_ref.at[0],
            grad_ref.at[0],
            log_ref.at[0],
            out_ref.at[0],
            key_sum,
            value_sum,
            head,
        )


def attention_back(qkv, blended, grads, logs):
    micros, rows, _ = qkv.shape
    heads = OWN // HEAD
    blocks = rows // 256
    wide = pl.BlockSpec((1, rows, 3 * OWN), lambda m: (m, 0, 0))
    narrow = pl.BlockSpec((1, rows, OWN), lambda m: (m, 0, 0))
    return pl.pallas_call(
        attention_back_body,
        grid=(micros,),
        out_shape=jax.ShapeDtypeStruct((micros, rows, 3 * OWN), jnp.bfloat16),
        in_specs=[
            wide,
            narrow,
            narrow,
            pl.BlockSpec((1, heads, blocks, 1, 256), lambda m: (m, 0, 0, 0, 0)),
        ],
        out_specs=wide,
        scratch_shapes=[pltpu.VMEM((rows, HEAD), jnp.float32)] * 2,
        compiler_params=pltpu.CompilerParams(vmem_limit_bytes=48 * MIB),
        name="attention_back",
    )(qkv, blended, grads, logs)


def heads_to_tokens_body(blended, out, send_sem, recv_sem, local_sem):
    links = Links(1, send_sem, recv_sem, local_sem)
    x, c = links.x, links.c
    corner = links.beside + 1 - 2 * c
    links.greet([links.core, links.beside, corner])
    target = out.at[:, :, pl.ds(pl.multiple_of((2 * x + c) * OWN, OWN), OWN)]
    own = links.local(blended.at[:, x, c], target)
    copies = [
        links.send(blended.at[:, 1 - x, 1 - c], target, corner),
        links.send(blended.at[:, 1 - x, c], target, links.beside),
        links.send(blended.at[:, x, 1 - c], target, links.core),
    ]
    arrived(copies)
    own.wait()
    links.finish_sends()


def heads_to_tokens(blended):
    micros, rows, _ = blended.shape
    own_rows = rows // GROUP
    return remote_call(
        heads_to_tokens_body,
        "heads_to_tokens",
        2,
        jax.ShapeDtypeStruct((micros, own_rows, D), blended.dtype),
        [ANY],
        ANY,
        [],
        3,
        1,
        40 * MIB,
    )(blended.reshape(micros, 2, 2, own_rows, OWN))


def tokens_to_heads_body(grads, out, send_sem, recv_sem, local_sem):
    links = Links(1, send_sem, recv_sem, local_sem)
    x, c = links.x, links.c
    corner = links.beside + 1 - 2 * c
    links.greet([links.core, links.beside, corner])

    def columns(to_x, to_c):
        return grads.at[:, :, pl.ds(pl.multiple_of((2 * to_x + to_c) * OWN, OWN), OWN)]

    target = out.at[:, x, c]
    own = links.local(columns(x, c), target)
    copies = [
        links.send(columns(1 - x, 1 - c), target, corner),
        links.send(columns(1 - x, c), target, links.beside),
        links.send(columns(x, 1 - c), target, links.core),
    ]
    arrived(copies)
    own.wait()
    links.finish_sends()


def tokens_to_heads(grads):
    micros, own_rows, _ = grads.shape
    return remote_call(
        tokens_to_heads_body,
        "tokens_to_heads",
        3,
        jax.ShapeDtypeStruct((micros, 2, 2, own_rows, OWN), grads.dtype),
        [ANY],
        ANY,
        [],
        3,
        1,
        40 * MIB,
    )(grads).reshape(micros, GROUP * own_rows, OWN)


def token_sums_body(partial, out, send_sem, recv_sem, local_sem, from_core, own, from_beside):
    links = Links(1, send_sem, recv_sem, local_sem)
    x, c = links.x, links.c
    links.greet([links.core, links.beside])
    far = links.send(partial.at[:, 1 - x, 1 - c], from_core.at[0], links.core)
    near = links.send(partial.at[:, x, 1 - c], from_core.at[1], links.core)
    loads = [
        links.local(partial.at[:, 1 - x, c], own.at[0]),
        links.local(partial.at[:, x, c], own.at[1]),
    ]
    micros = out.shape[0]
    loads[0].wait()
    arrived([far])
    passed = []
    for m in range(micros):
        own[0, m] = (
            own[0, m].astype(jnp.float32) + from_core[0, m].astype(jnp.float32)
        ).astype(jnp.bfloat16)
        passed.append(links.send(own.at[0, m], from_beside.at[m], links.beside))
    loads[1].wait()
    arrived([near])
    for m in range(micros):
        out[m] = own[1, m].astype(jnp.float32) + from_core[1, m].astype(jnp.float32)
    for m in range(micros):
        arrived([passed[m]])
        out[m] += from_beside[m].astype(jnp.float32)
    links.finish_sends()


def token_sums(partial):
    micros, rows, width = partial.shape
    own_rows = rows // GROUP
    held = pltpu.VMEM((2, micros, own_rows, width), partial.dtype)
    return remote_call(
        token_sums_body,
        "token_sums",
        4,
        jax.ShapeDtypeStruct((micros, own_rows, width), jnp.float32),
        [ANY],
        VMEM,
        [held, held, pltpu.VMEM((micros, own_rows, width), partial.dtype)],
        4,
        2,
        40 * MIB,
    )(partial.reshape(micros, 2, 2, own_rows, width))


def small_sums_body(planes, partial, out, send_sem, recv_sem, local_sem, from_core, from_beside):
    links = Links(planes, send_sem, recv_sem)
    links.greet(links.partners())
    z, y, x, c = links.z, links.y, links.x, links.c
    arrived([links.send(partial.at[:, 1 - c], from_core, links.core)])
    from_core[...] = from_core[...] + partial[:, c]
    arrived([links.send(from_core.at[1 - x], from_beside, links.beside)])
    out[z, y, x, c] = from_core[x] + from_beside[...]
    spread_all(links, out)
    links.finish_sends()


def small_sums(partial, planes):
    block = partial.shape[2:]
    return remote_call(
        functools.partial(small_sums_body, planes),
        "small_sums",
        5,
        jax.ShapeDtypeStruct((planes, 2, 2, 2, *block), jnp.float32),
        [VMEM],
        VMEM,
        [pltpu.VMEM((2, *block), jnp.float32), pltpu.VMEM(block, jnp.float32)],
        2 * planes + 6,
        0,
        40 * MIB,
    )(partial)


def add_blocks(target, left, right, count):
    @pl.loop(0, count)
    def _(i):
        target(i)[...] = (
            left(i)[...].astype(jnp.float32) + right(i)[...].astype(jnp.float32)
        ).astype(jnp.bfloat16)


class Sums:
    def __init__(self, links, grads, outs, scratch):
        self.links = links
        self.pieces = []
        used = 0
        for grad, out in zip(grads, outs):
            own = scratch[used]
            used += 1
            for rows, start in cuts(grad.shape[-2:]):
                self.pieces.append((grad, out, rows, start, own, *scratch[used : used + 7]))
                used += 7
        self.state = [dict() for _ in self.pieces]

    def core(self, k):
        links = self.links
        grad, _, rows, start, _, first, *_ = self.pieces[k]
        source = grad.at[:, :, :, 1 - links.c, rows, pl.ds(start, WIDTH)]
        self.state[k]["core"] = links.send(source, first, links.core)

    def load(self, k):
        links = self.links
        grad, _, rows, start, own, *_ = self.pieces[k]
        source = grad.at[:, :, :, links.c, rows, pl.ds(start, WIDTH)]
        self.state[k]["own"] = links.local(source, own)

    def S1(self, k):
        links = self.links
        x, y, planes = links.x, links.y, links.planes
        _, _, _, _, own, first, over_y, _, _, over_x, _, _ = self.pieces[k]
        state = self.state[k]
        state["own"].wait()
        arrived([state["core"]])
        lead, rest = pl.ds(0, HALF), pl.ds(HALF, HALF)

        def add(columns, place):
            def block(ref):
                return lambda i: ref.at[(*place(i // 2, i % 2), ALL, columns)]

            add_blocks(block(first), block(own), block(first), planes * 2)

        add(lead, lambda z, other: (z, 1 - y, other))
        state["T"] = [links.send(first.at[:, 1 - y, :, :, lead], over_y, links.across)]
        add(rest, lambda z, other: (z, other, 1 - x))
        state["F"] = [links.send(first.at[:, :, 1 - x, :, rest], over_x, links.beside)]
        add(lead, lambda z, other: (z, y, other))
        add(rest, lambda z, other: (z, other, x))

    def T2(self, k):
        links = self.links
        _, _, _, _, _, first, over_y, over_planes, _, _, _, _ = self.pieces[k]
        arrived(self.state[k]["T"])

        def kept(i):
            return first.at[i // 2, links.y, i % 2, :, pl.ds(0, HALF)]

        def came(i):
            return over_y.at[i // 2, i % 2]

        add_blocks(came, kept, came, links.planes * 2)
        self.state[k]["T"] = [
            links.send(over_y.at[links.plane(s)], over_planes.at[s - 1], links.plane_device(s))
            for s in range(1, links.planes)
        ]

    def T3(self, k):
        links = self.links
        _, _, _, _, _, _, over_y, over_planes, last, _, _, _ = self.pieces[k]
        arrived(self.state[k]["T"])
        for i in (1 - links.x, links.x):
            result = over_y[links.z, i].astype(jnp.float32)
            for s in range(1, links.planes):
                result = result + over_planes[s - 1, i].astype(jnp.float32)
            over_y[links.z, i] = result.astype(jnp.bfloat16)
        source = over_y.at[links.z, 1 - links.x]
        self.state[k]["T"] = [links.send(source, last, links.beside)]

    def T4(self, k):
        links = self.links
        _, out, rows, start, _, _, over_y, _, last, _, _, _ = self.pieces[k]
        arrived(self.state[k]["T"])
        kept = over_y[links.z, links.x].astype(jnp.float32)
        out[rows, pl.ds(start, HALF)] = kept + last[...].astype(jnp.float32)

    def F2(self, k):
        links = self.links
        x, y = links.x, links.y
        _, _, _, _, _, first, _, _, _, over_x, third, _ = self.pieces[k]
        arrived(self.state[k]["F"])
        for here in (1 - y, y):

            def kept(i, here=here):
                return first.at[i, here, x, :, pl.ds(HALF, HALF)]

            def came(i, here=here):
                return over_x.at[i, here]

            add_blocks(came, kept, came, links.planes)
            if here is not y:
                self.state[k]["F"] = [links.send(over_x.at[:, here], third, links.across)]

    def F3(self, k):
        links = self.links
        _, _, _, _, _, _, _, _, _, over_x, third, fourth = self.pieces[k]
        arrived(self.state[k]["F"])

        def kept(i):
            return over_x.at[i, links.y]

        def came(i):
            return third.at[i]

        add_blocks(came, kept, came, links.planes)
        self.state[k]["F"] = [
            links.send(third.at[links.plane(s)], fourth.at[s - 1], links.plane_device(s))
            for s in range(1, links.planes)
        ]

    def F4(self, k):
        links = self.links
        _, out, rows, start, *_, third, fourth = self.pieces[k]
        arrived(self.state[k]["F"])
        result = third[links.z].astype(jnp.float32)
        for s in range(1, links.planes):
            result = result + fourth[s - 1].astype(jnp.float32)
        out[rows, pl.ds(start + HALF, HALF)] = result


def sums_order(count):
    order = []
    stages = (("core", 0), ("S1", 1), ("load", 0), ("T2", 2), ("F2", 2), ("T3", 3), ("F3", 3), ("T4", 4), ("F4", 4))
    for k in range(count + 4):
        for task, behind in stages:
            if 0 <= k - behind < count:
                order.append((task, k - behind))
    return order


MIDDLE_ORDER = (
    544, 576, 449, 577, 450, 545, 546, 384, 224, 578, 451, 547, 385, 225, 480, 352, 226, 416, 579,
    386, 481, 353, 354, 608, 640, 672, 417, 387, 418, 609, 227, 610, 355, 641, 642, 419, 643, 611,
)
BACK_ORDER = (
    704, 576, 449, 705, 577, 450, 706, 384, 224, 578, 451, 707, 385, 225, 579, 452, 736, 352, 416,
    580, 708, 768, 386, 226, 709, 800, 353, 417, 387, 710, 418, 227, 711, 388, 228, 354, 801, 832,
    419, 608, 640, 737, 833, 864, 420, 609, 896, 834, 769, 355, 356, 641, 642, 643, 610, 644, 928,
    865, 961, 611, 897, 992, 612, 962, 1024, 929, 1057, 993, 1058, 1059,
)


class AttendSums:
    def __init__(self, links, grads, out, scratch):
        self.links, self.grads, self.out = links, grads, out
        self.own, self.over_y, self.over_planes, self.sum, self.held = scratch
        self.state = [dict() for _ in range(PAIRS)]
        self.columns = [pl.ds(pair * PAIR, PAIR) for pair in range(PAIRS)]

    def a0(self, k):
        links, columns = self.links, self.columns[k]
        source = self.grads.at[:, 1 - links.y, :, :, :, columns]
        self.state[k]["y"] = links.send(source, self.over_y.at[..., columns], links.across)
        source = self.grads.at[:, links.y, :, :, :, columns]
        self.state[k]["own"] = links.local(source, self.own.at[..., columns])

    def a1(self, k):
        links, own, over_y, columns = self.links, self.own, self.over_y, self.columns[k]
        self.state[k]["own"].wait()
        arrived([self.state[k]["y"]])
        for i in range(2):

            def block(ref, i=i):
                return lambda j: ref.at[j // 2, i, j % 2, :, columns]

            add_blocks(block(own), block(own), block(over_y), links.planes * 2)
        self.state[k]["planes"] = [
            links.send(
                own.at[links.plane(s), :, :, :, columns],
                self.over_planes.at[s - 1, :, :, :, columns],
                links.plane_device(s),
            )
            for s in range(1, links.planes)
        ]

    def a2(self, k):
        links, columns = self.links, self.columns[k]
        x, c = links.x, links.c
        arrived(self.state[k]["planes"])
        for i in range(2):
            for j in range(2):
                result = self.own[links.z, i, j, :, columns].astype(jnp.float32)
                for s in range(1, links.planes):
                    result = result + self.over_planes[s - 1, i, j, :, columns].astype(jnp.float32)
                self.sum[i, j, :, columns] = result
        self.state[k]["beside"] = links.send(
            self.sum.at[1 - x, :, :, columns], self.held.at[:, :, columns], links.beside
        )
        self.state[k]["near"] = links.send(
            self.sum.at[x, 1 - c, :, columns], self.out.at[x, c, :, columns], links.core
        )
        self.out[x, c, :, columns] = self.sum[x, c, :, columns]

    def a3(self, k):
        links, columns = self.links, self.columns[k]
        x, c = links.x, links.c
        arrived([self.state[k]["beside"]])
        self.out[1 - x, c, :, columns] = self.held[c, :, columns]
        self.state[k]["far"] = links.send(
            self.held.at[1 - c, :, columns], self.out.at[1 - x, c, :, columns], links.core
        )

    def finish(self):
        for state in self.state:
            arrived([state["near"], state["far"]])


class Spread:
    def __init__(self, links, ref):
        self.links, self.ref = links, ref

    def step(self, k):
        links, ref = self.links, self.ref
        z, y, x, c = links.z, links.y, links.x, links.c
        if k > 0:
            arrived(self.sent)
        if k == 0:
            block = ref.at[z, y, x, c]
            devices = [device for _, _, device in links.column()]
        elif k == 1:
            block, devices = ref.at[:, :, x, c], [links.beside, links.core]
        elif k == 2:
            block, devices = ref.at[:, :, 1 - x, c], [links.core]
        else:
            return
        self.sent = [links.send(block, block, device) for device in devices]


class TokenSums:
    def __init__(self, links, partial, scratch):
        self.links, self.partial = links, partial
        self.from_core, self.from_beside = scratch
        self.state = {}

    def start(self, m):
        links, partial = self.links, self.partial
        x, c = links.x, links.c
        self.state[m] = [
            links.send(partial.at[m, 1 - x, 1 - c], self.from_core.at[0, m], links.core),
            links.send(partial.at[m, x, 1 - c], self.from_core.at[1, m], links.core),
        ]

    def middle(self, m):
        links, partial = self.links, self.partial
        x, c = links.x, links.c
        arrived(self.state[m])
        away = partial.at[m, 1 - x, c]
        away[...] = (
            away[...].astype(jnp.float32) + self.from_core[0, m].astype(jnp.float32)
        ).astype(jnp.bfloat16)
        self.state[m] = [links.send(away, self.from_beside.at[m], links.beside)]

    def finish(self, m):
        links = self.links
        arrived(self.state[m])
        return (
            self.partial[m, links.x, links.c].astype(jnp.float32)
            + self.from_core[1, m].astype(jnp.float32)
            + self.from_beside[m].astype(jnp.float32)
        )


def sums_body(planes, kinds, *refs):
    attend, grads, refs = refs[0], refs[1 : 1 + kinds], refs[1 + kinds :]
    attend_out, outs, refs = refs[0], refs[1 : 1 + kinds], refs[1 + kinds :]
    links = Links(planes, *refs[:3])
    links.greet(links.partners())
    attend_sums = AttendSums(links, attend, attend_out, refs[3:8])
    for pair in range(PAIRS):
        for task in (attend_sums.a0, attend_sums.a1, attend_sums.a2, attend_sums.a3):
            task(pair)
    sums = Sums(links, grads, outs, refs[8:])
    for task, k in sums_order(len(sums.pieces)):
        getattr(sums, task)(k)
    attend_sums.finish()
    links.finish_sends()


def middle_body(planes, *refs):
    grad_contract, expand, contract, project, act, slope, second, grad_branch, refs = *refs[:8], refs[8:]
    middle, attended, upstream, blended, modulation, bias_rows, refs = *refs[:6], refs[6:]
    contract_out, output, middle_grad_out, rows_out, bias_out, hidden_out, refs = *refs[:6], refs[6:]
    grad_expand, grad_project, grad_heads, refs = *refs[:3], refs[3:]
    links = Links(planes, *refs[:3])
    refs = refs[3:]
    used = scratch_count([grad_contract.shape[-2:]])
    sum_scratch, refs = refs[:used], refs[used:]
    contract_held, expand_held, act_held, slope_held, second_held, second_t, refs = *refs[:6], refs[6:]
    branch_grad, grads, branch, grad_second, middle_held, attended_held, refs = *refs[:6], refs[6:]
    upstream_held, project_held, blended_held, attended_grad, project_grads, refs = *refs[:5], refs[5:]
    middle_grad, grad_blended = refs
    x, c = links.x, links.c
    corner = links.beside + 1 - 2 * c
    micros, own_rows, _ = second.shape
    parts = FF // WIDTH
    part_width = FF // parts
    contract_blocks = contract.shape[0] // parts

    def load(part):
        columns = pl.ds(part * part_width, part_width)
        slot = part % 2
        return [
            links.local(
                contract.at[pl.ds(part * contract_blocks, contract_blocks)], contract_held.at[slot]
            ),
            links.local(expand.at[:, :, :, :, :, columns], expand_held.at[slot]),
            links.local(act.at[:, :, columns], act_held.at[slot]),
            links.local(slope.at[:, :, columns], slope_held.at[slot]),
        ]

    loaded = links.local(second, second_held), links.local(grad_branch, branch_grad)
    loading = {0: load(0), 1: load(1)}
    links.greet([*links.partners(), corner])
    sums = Sums(links, (grad_contract,), (contract_out,), sum_scratch)
    for k in range(len(sums.pieces)):
        sums.core(k)
    sums.load(0)
    later = [
        links.local(middle, middle_held),
        links.local(attended, attended_held),
        links.local(upstream, upstream_held),
        links.local(project, project_held),
        links.local(blended, blended_held),
    ]
    for copy in loaded:
        copy.wait()
    for m in range(micros):
        second_t[:, m * own_rows : (m + 1) * own_rows] = second_held[m].T
    branch[...] = jnp.zeros_like(branch)
    grad_second[...] = jnp.zeros_like(grad_second)
    stored = []

    def mlp_unit(part):
        for copy in loading.pop(part):
            copy.wait()
        slot = part % 2
        if part >= 2:
            stored[part - 2].wait()
        contract_part(
            part * part_width,
            contract_held.at[slot],
            expand_held.at[slot],
            act_held.at[slot],
            slope_held.at[slot],
            second_t,
            branch_grad,
            grads.at[slot],
            branch,
            grad_second,
            hidden_out,
        )
        if part + 2 < parts:
            loading[part + 2] = load(part + 2)
        columns = pl.ds(part * part_width, part_width)
        stored.append(links.local(grads.at[slot], grad_expand.at[:, :, :, :, :, columns]))

    totals = [jnp.zeros((1, D), jnp.float32)] * 2

    def own_tokens(m):
        def vector(block):
            shift = bias_vector(bias_rows, 4 * D + FF + block * D, D)
            return modulation_row(modulation, m, block) + shift

        ahead = upstream_held[m].astype(jnp.float32)
        outward = branch[m] + bias_vector(bias_rows, 3 * D + FF, D)
        output[m] = (middle_held[m] + vector(5) * outward).astype(jnp.bfloat16)
        rows_out[m, 5:6, :] = jnp.sum(ahead * outward, axis=0, keepdims=True)
        normed, scale = normalize(middle_held[m])
        values = grad_second[m]
        rows_out[m, 3:4, :] = jnp.sum(values, axis=0, keepdims=True)
        rows_out[m, 4:5, :] = jnp.sum(values * normed, axis=0, keepdims=True)
        back = ahead + norm_back(values, normed, scale, vector(4))
        middle_grad[m] = back
        rows_out[m, 2:3, :] = jnp.sum(back * attended_held[m], axis=0, keepdims=True)
        lowered = (vector(2) * back).astype(jnp.bfloat16)
        attended_grad[m] = lowered
        totals[0] += jnp.sum(lowered.astype(jnp.float32), axis=0, keepdims=True)
        totals[1] += jnp.sum(branch_grad[m].astype(jnp.float32), axis=0, keepdims=True)
        product = lax.dot_general(
            lowered,
            project_held[...].reshape(D, D),
            (((1,), (1,)), ((), ())),
            preferred_element_type=jnp.float32,
        )
        grad_blended[m] = product.astype(jnp.bfloat16)
        here = pl.ds(pl.multiple_of((2 * x + c) * own_rows, own_rows), own_rows)

        def columns_of(to_x, to_c):
            start = pl.multiple_of((2 * to_x + to_c) * OWN, OWN)
            return grad_blended.at[m, :, pl.ds(start, OWN)]

        target = grad_heads.at[m, here]
        exchanged.append(links.send(columns_of(1 - x, 1 - c), target, corner))
        exchanged.append(links.send(columns_of(1 - x, c), target, links.beside))
        exchanged.append(links.send(columns_of(x, 1 - c), target, links.core))
        stored.append(links.local(columns_of(x, c), target))

    exchanged = []

    def project_unit():
        total = None
        for m in range(micros):
            product = lax.dot_general(
                blended_held[m],
                attended_grad[m],
                (((0,), (0,)), ((), ())),
                preferred_element_type=jnp.float32,
            )
            total = product if total is None else total + product
        project_grads[...] = total.astype(jnp.bfloat16).reshape(project_grads.shape)
        stored.append(links.local(project_grads, grad_project))
        stored.append(links.local(middle_grad, middle_grad_out))

    for task, k in tasks_of(MIDDLE_ORDER):
        if task == "mlp":
            mlp_unit(k)
        elif task == "own":
            if k == 0:
                for copy in later:
                    copy.wait()
            own_tokens(k)
        elif task == "project":
            project_unit()
        else:
            getattr(sums, task)(k)
    bias_out[0:1, :] = totals[0]
    bias_out[1:2, :] = totals[1]
    arrived(exchanged)
    for copy in stored[parts - 2 :]:
        copy.wait()
    links.finish_sends()


def contract_part(
    start,
    contract,
    expand,
    act,
    slope,
    second_t,
    grad_branch,
    grads,
    branch,
    grad_second,
    hidden_sums,
):
    micros = grad_branch.shape[0]
    blocks = CHUNK // contract.shape[1]

    @pl.loop(0, act.shape[-1] // CHUNK)
    def _(chunk):
        inside = pl.ds(pl.multiple_of(chunk * CHUNK, CHUNK), CHUNK)
        columns = pl.ds(pl.multiple_of(start + chunk * CHUNK, CHUNK), CHUNK)
        outward = contract[pl.ds(chunk * blocks, blocks)].reshape(CHUNK, D)
        inward = expand[:, :, :, :, :, inside].reshape(D, CHUNK)
        lows = []
        for m in range(micros):
            branch[m] += jnp.dot(act[m, :, inside], outward, preferred_element_type=jnp.float32)
            grad_act = lax.dot_general(
                grad_branch[m], outward, (((1,), (1,)), ((), ())), preferred_element_type=jnp.float32
            )
            lows.append((grad_act * slope[m, :, inside].astype(jnp.float32)).astype(jnp.bfloat16))
            grad_second[m] += lax.dot_general(
                lows[m], inward, (((1,), (1,)), ((), ())), preferred_element_type=jnp.float32
            )
        grad_hidden = jnp.concatenate(lows, axis=0)
        product = jnp.dot(second_t[...], grad_hidden, preferred_element_type=jnp.float32)
        grads[:, :, :, :, :, inside] = product.astype(jnp.bfloat16).reshape(
            *grads.shape[:-1], CHUNK
        )
        hidden_sums[:, columns] = jnp.sum(
            grad_hidden.astype(jnp.float32), axis=0, keepdims=True
        )


def back_body(planes, *refs):
    grad_expand, grad_project, grad_heads, qkv, heads, logs, normed, attend, refs = *refs[:8], refs[8:]
    tokens, middle_grad, modulation, bias_rows, row_sums, bias_sums, hidden_sums, refs = *refs[:7], refs[7:]
    cond, modulate, refs = *refs[:2], refs[2:]
    attend_out, expand_out, project_out, tokens_out, sums_out, modulate_out, cond_out, refs = *refs[:7], refs[7:]
    links = Links(planes, *refs[:3])
    attend_held_scratch, refs = refs[3:8], refs[8:]
    used = scratch_count([grad_expand.shape[-2:], grad_project.shape[-2:]])
    sum_scratch, refs = refs[:used], refs[used:]
    grads_held, qkv_held, heads_held, normed_held, attend_held, grad_qkv, refs = *refs[:6], refs[6:]
    key_sum, value_sum, attend_grads, partial, from_core, from_beside, refs = *refs[:6], refs[6:]
    tokens_held, middle_held, scales, head_sums, row_held, small, refs = *refs[:6], refs[6:]
    small_core, small_beside, modulations = refs
    micros, latent_rows, _ = qkv.shape
    loads = [
        links.local(grad_heads, grads_held),
        links.local(qkv, qkv_held),
        links.local(heads, heads_held),
        links.local(attend, attend_held),
        links.local(normed, normed_held),
        links.local(tokens, tokens_held),
        links.local(middle_grad, middle_held),
    ]
    links.greet(links.partners())
    z, y, x, c = links.z, links.y, links.x, links.c
    sums = Sums(links, (grad_expand, grad_project), (expand_out, project_out), sum_scratch)
    for k in range(len(sums.pieces)):
        sums.core(k)
    sums.load(0)
    attend_sums = AttendSums(links, attend_grads, attend_out, attend_held_scratch)
    token_sum = TokenSums(links, partial, (from_core, from_beside))
    spread_sums, spread_cond = Spread(links, sums_out), Spread(links, cond_out)
    sent = {}

    def vector(m, block):
        shift = bias_vector(bias_rows, 4 * D + FF + block * D, D)
        return modulation_row(modulation, m, block) + shift

    scale_rows = []
    for m in range(micros):
        scale_rows += [1.0 + vector(m, 1), vector(m, 0)]
    scale_rows.append(jnp.zeros((8 - 2 * micros, D), jnp.float32))
    scales[...] = jnp.concatenate(scale_rows, axis=0).T

    def head_unit(m, head):
        if m == 0 and head == 0:
            for copy in loads:
                copy.wait()
        attention_back_unit(
            qkv_held.at[m],
            heads_held.at[m],
            grads_held.at[m],
            logs.at[m],
            grad_qkv.at[m],
            key_sum,
            value_sum,
            head,
        )

    def tokens_unit(m):
        grads = token_sum.finish(m)
        normed_own, scale = normalize(tokens_held[m].astype(jnp.float32))
        tokens_out[m] = middle_held[m] + norm_back(grads, normed_own, scale, vector(m, 1))

    def small_start():
        highs = head_sums[...].astype(jnp.bfloat16)
        lows = (head_sums[...] - highs.astype(jnp.float32)).astype(jnp.bfloat16)
        product = lax.dot_general(
            jnp.concatenate([highs, lows], axis=0),
            attend_held[...].reshape(D, 3 * OWN),
            (((1,), (1,)), ((), ())),
            preferred_element_type=jnp.float32,
        )
        each = D // LANES
        per_quarter = 6 * each // GROUP
        for m in range(micros):
            blocks = [product[m : m + 1] + product[8 + m : 9 + m], row_held[m : m + 1, :]]
            blocks += [row_sums[m, block : block + 1, :] for block in range(2, 6)]
            for k in range(6 * each):
                quarter, row = k // per_quarter, m * per_quarter + k % per_quarter
                lanes = slice(k % each * LANES, (k % each + 1) * LANES)
                small[quarter // 2, quarter % 2, row : row + 1, :] = blocks[k // each][:, lanes]
        start = micros * per_quarter
        biases = {2: bias_sums[0:1, :], 7: bias_sums[1:2, :]}
        for k in range(FF // D):
            biases[3 + k] = hidden_sums[:, k * D : (k + 1) * D]
        each_quarter = 8 * each // GROUP
        small[0, 0, start:, :] = jnp.zeros((small.shape[2] - start, LANES), jnp.float32)
        for k in range(2 * each, 8 * each):
            quarter, row = k // each_quarter, start + k % each_quarter
            lanes = slice(k % each * LANES, (k % each + 1) * LANES)
            small[quarter // 2, quarter % 2, row : row + 1, :] = biases[k // each][:, lanes]
        for m in range(1, micros):
            head_sums[0:1, :] += head_sums[m : m + 1, :]
        for pair in range(PAIRS):
            for kind, first_row in ((0, start), (2, start + each)):
                lanes = pl.ds(pair * PAIR + kind * LANES, LANES)
                row = first_row + (2 * x + c) * PAIRS + pair
                small[0, 0, pl.ds(row, 1), :] = head_sums[0:1, lanes]
        sent["small"] = links.send(small.at[:, 1 - c], small_core, links.core)

    def small_core_sum():
        arrived([sent["small"]])
        small_core[...] = small_core[...] + small[:, c]
        sent["small"] = links.send(small_core.at[1 - x], small_beside, links.beside)

    def small_beside_sum():
        arrived([sent["small"]])
        sums_out[z, y, x, c] = small_core[x] + small_beside[...]
        spread_sums.step(0)

    def modulate_unit():
        spread_sums.step(3)
        latents = planes * 2
        per_quarter = 6 * D // LANES // GROUP
        for m in range(micros):
            for k in range(6 * D // LANES):
                quarter, row = k // per_quarter, m * per_quarter + k % per_quarter
                values = sums_out[:, :, quarter // 2, quarter % 2, row, :].reshape(latents, LANES)
                here = slice(m * latents, (m + 1) * latents)
                modulations[here, k * LANES : (k + 1) * LANES] = values
        modulate_out[...] = lax.dot_general(
            cond[...],
            modulations[...],
            (((0,), (0,)), ((), ())),
            precision=highest,
            preferred_element_type=jnp.float32,
        )
        product = lax.dot_general(
            modulations[...],
            modulate[...].astype(jnp.float32),
            (((1,), (1,)), ((), ())),
            precision=highest,
            preferred_element_type=jnp.float32,
        )
        cond_out[z, y, x, c] = jnp.zeros(cond_out.shape[4:], jnp.float32)
        cond_out[z, y, x, c, :, : product.shape[1]] = product
        spread_cond.step(0)

    heads_each = OWN // HEAD
    for task, k in tasks_of(BACK_ORDER):
        if task == "head":
            head_unit(k // heads_each, k % heads_each)
        elif task == "first":
            first_product(k, grad_qkv, attend_held, partial)
            token_sum.start(k)
        elif task == "attend":
            attend_product(
                k, normed_held, grad_qkv, attend_held, scales, head_sums, row_held, attend_grads
            )
            attend_sums.a0(k)
        elif task == "t1":
            token_sum.middle(k)
        elif task == "t2":
            tokens_unit(k)
        elif task in ("a1", "a2", "a3"):
            getattr(attend_sums, task)(k)
        elif task == "small":
            (small_start, small_core_sum, small_beside_sum)[k]()
        elif task == "sums":
            spread_sums.step(k)
        elif task == "modulate":
            modulate_unit()
        elif task == "cond":
            spread_cond.step(k)
        else:
            getattr(sums, task)(k)
    attend_sums.finish()
    links.finish_sends()


def attend_product(pair, normed, grad_qkv, attend, scales, head_sums, row_held, out):
    planes = attend.shape[0]
    width = D // planes
    micros = normed.shape[0]
    columns = pl.ds(pair * PAIR, PAIR)
    totals = [
        jnp.sum(grad_qkv[m, :, columns].astype(jnp.float32), axis=0, keepdims=True)
        for m in range(micros)
    ]
    head_sums[:, columns] = jnp.concatenate(
        [*totals, jnp.zeros((8 - micros, PAIR), jnp.float32)], axis=0
    )

    @pl.loop(0, planes)
    def _(plane):
        here = pl.ds(pl.multiple_of(plane * width, width), width)
        weights = attend[plane, :, :, :, :, columns].reshape(width, PAIR).astype(jnp.float32)
        total = jnp.zeros((width, PAIR), jnp.float32)
        for m in range(micros):
            product = lax.dot_general(
                normed[m, :, here],
                grad_qkv[m, :, columns],
                (((0,), (0,)), ((), ())),
                preferred_element_type=jnp.float32,
            )
            total = total + product * scales[here, 2 * m : 2 * m + 1]
            total = total + scales[here, 2 * m + 1 : 2 * m + 2] * totals[m]
            row = jnp.sum((weights * product).T, axis=0, keepdims=True)
            if pair == 0:
                row_held[m : m + 1, here] = row
            else:
                row_held[m : m + 1, here] += row
        out[plane, :, :, :, :, columns] = total.astype(jnp.bfloat16).reshape(
            *out.shape[1:-1], PAIR
        )


def first_product(m, grad_qkv, attend, partial):
    rows = partial.shape[3]

    @pl.loop(0, GROUP)
    def _(block):
        here = pl.ds(pl.multiple_of(block * rows, rows), rows)
        product = lax.dot_general(
            grad_qkv[m, here, :],
            attend[...].reshape(D, 3 * OWN),
            (((1,), (1,)), ((), ())),
            preferred_element_type=jnp.float32,
        )
        partial[m, block // 2, block % 2] = product.astype(jnp.bfloat16)


def attend_scratch(attend, planes):
    rows, width = attend.shape[-2:]
    return [
        pltpu.VMEM((planes, 2, 2, rows, width), jnp.bfloat16),
        pltpu.VMEM((planes, 2, 2, rows, width), jnp.bfloat16),
        pltpu.VMEM((planes - 1, 2, 2, rows, width), jnp.bfloat16),
        pltpu.VMEM((2, 2, rows, width), jnp.float32),
        pltpu.VMEM((2, rows, width), jnp.float32),
    ]


def sum_scratch(shapes, planes):
    held = []
    for shape in shapes:
        pieces = cuts(shape)
        rows = shape[0] if shape[1] > WIDTH else shape[0] // len(pieces)
        held.append(low_held(planes, 2, 2, rows, WIDTH))
        for _ in pieces:
            held += [
                low_held(planes, 2, 2, rows, WIDTH),
                low_held(planes, 2, rows, HALF),
                low_held(planes - 1, 2, rows, HALF),
                low_held(rows, HALF),
                low_held(planes, 2, rows, HALF),
                low_held(planes, rows, HALF),
                low_held(planes - 1, rows, HALF),
            ]
    return held


def count_pieces(shapes):
    return sum(len(cuts(shape)) for shape in shapes)


def scratch_count(shapes):
    return len(shapes) + 7 * count_pieces(shapes)


def full_shape(*shape):
    return jax.ShapeDtypeStruct(shape, jnp.float32)


def low_shape(*shape):
    return jax.ShapeDtypeStruct(shape, jnp.bfloat16)


def full_held(*shape):
    return pltpu.VMEM(shape, jnp.float32)


def low_held(*shape):
    return pltpu.VMEM(shape, jnp.bfloat16)


def sum_sems(shapes, planes):
    return count_pieces(shapes) * (4 + 2 * planes)


def weight_sums(attend, weights, planes):
    shapes = [grad.shape[-2:] for grad in weights]
    return remote_call(
        functools.partial(sums_body, planes, len(weights)),
        "weight_sums",
        6,
        (full_shape(2, 2, *attend.shape[-2:]), *(full_shape(*shape) for shape in shapes)),
        [ANY] * (1 + len(weights)),
        (VMEM,) * (1 + len(weights)),
        [*attend_scratch(attend, planes), *sum_scratch(shapes, planes)],
        8 + 2 * planes + sum_sems(shapes, planes),
        4 + count_pieces(shapes),
        60 * MIB,
    )(attend, *weights)


def middle_part(grad_contract, weights, held, vectors, planes):
    expand, contract, project = weights
    second = held[2]
    micros, own_rows, _ = second.shape
    own = second.shape
    shape = grad_contract.shape[-2:]
    width = WIDTH
    blocks = width // shape[0]
    return remote_call(
        functools.partial(middle_body, planes),
        "middle",
        6,
        (
            full_shape(*shape),
            low_shape(*own),
            full_shape(*own),
            full_shape(micros, 8, D),
            full_shape(8, D),
            full_shape(1, FF),
            low_shape(*expand.shape),
            low_shape(*project.shape),
            low_shape(micros, own_rows * GROUP, OWN),
        ),
        [ANY] * 12 + [VMEM] * 2,
        (VMEM, VMEM, ANY) + (VMEM,) * 3 + (ANY,) * 3,
        [
            *sum_scratch([shape], planes),
            low_held(2, blocks, *shape),
            low_held(2, *expand.shape[:-1], width),
            low_held(2, micros, own_rows, width),
            low_held(2, micros, own_rows, width),
            low_held(*own),
            low_held(D, micros * own_rows),
            low_held(*own),
            low_held(2, *expand.shape[:-1], width),
            full_held(*own),
            full_held(*own),
            full_held(*own),
            full_held(*own),
            low_held(*own),
            low_held(*project.shape),
            low_held(*own),
            low_held(*own),
            low_held(*project.shape),
            full_held(*own),
            low_held(*own),
        ],
        8 + sum_sems([shape], planes),
        48,
        63 * MIB,
    )(
        grad_contract,
        expand,
        contract.reshape(FF // shape[0], *shape),
        project,
        *held,
        *vectors,
    )


def back_part(grad_expand, grad_project, grad_heads, held, vectors, planes):
    qkv, heads, logs, normed, attend, tokens, middle_grad = held
    shapes = [grad_expand.shape[-2:], grad_project.shape[-2:]]
    micros, latent_rows, width = qkv.shape
    own = tokens.shape
    small = (micros * 6 + 8) * D // LANES // GROUP
    cond, modulate = vectors[-2:]
    return remote_call(
        functools.partial(back_body, planes),
        "back",
        7,
        (
            full_shape(2, 2, *attend.shape[-2:]),
            *(full_shape(*shape) for shape in shapes),
            full_shape(*own),
            full_shape(planes, 2, 2, 2, small, LANES),
            full_shape(*modulate.shape),
            full_shape(planes, 2, 2, 2, cond.shape[0], LANES),
        ),
        [ANY] * 5 + [VMEM] + [ANY] * 4 + [VMEM] * 7,
        (VMEM,) * 7,
        [
            *attend_scratch(attend, planes),
            *sum_scratch(shapes, planes),
            low_held(*grad_heads.shape),
            low_held(*qkv.shape),
            low_held(*heads.shape),
            low_held(*normed.shape),
            low_held(*attend.shape),
            low_held(*qkv.shape),
            full_held(latent_rows, HEAD),
            full_held(latent_rows, HEAD),
            low_held(*attend.shape),
            low_held(micros, 2, 2, *own[1:]),
            low_held(2, *own),
            low_held(*own),
            low_held(*own),
            full_held(*own),
            full_held(D, 8),
            full_held(8, width),
            full_held(8, D),
            full_held(2, 2, small, LANES),
            full_held(2, small, LANES),
            full_held(small, LANES),
            full_held(cond.shape[0], modulate.shape[1]),
        ],
        40 + 8 * planes + sum_sems(shapes, planes),
        12 + count_pieces(shapes),
        63 * MIB,
    )(grad_expand, grad_project, grad_heads, *held, *vectors)


def normalize(values):
    center = values - jnp.mean(values, axis=-1, keepdims=True)
    spread_of = jnp.mean(center * center, axis=-1, keepdims=True)
    scale = lax.rsqrt(spread_of + epsilon)
    return center * scale, scale


def norm_back(grads, normed, scale, factors):
    inner = grads * (1.0 + factors)
    return scale * (
        inner
        - jnp.mean(inner, axis=-1, keepdims=True)
        - normed * jnp.mean(inner * normed, axis=-1, keepdims=True)
    )


def einsum(spec, left, right):
    return jnp.einsum(spec, left, right, preferred_element_type=jnp.float32)


def per_device(tokens, condition, attend, project, expand, contract, modulate, biases, cotangent):
    devices = lax.axis_size("fsdp")
    planes = devices // 8
    latents = devices // GROUP
    me = lax.axis_index("fsdp")
    quarter, latent = me % GROUP, me // GROUP
    micros, own_rows, _ = tokens.shape
    latent_rows = own_rows * GROUP
    rows = D // devices
    grid = (planes, 2, 2, 2)

    modulate_rows = modulate.reshape(rows, 6 * D)
    attend_shard = attend.reshape(rows, 3, 2, 2, PAIRS, LANES).transpose(2, 3, 0, 4, 1, 5)
    shards = (
        tokens,
        attend_shard.reshape(2, 2, rows, 3 * OWN),
        project.reshape(rows, D),
        expand.reshape(rows, FF),
        contract.reshape(FF // devices, D),
    )
    fused = rows % 16 == 0 and own_rows % QUERY_ROWS == 0 and biases.size == 7 * LANES // 2
    inputs = tokens.astype(jnp.float32)
    if fused:
        half = LANES // 2
        spread_cond = condition.astype(jnp.float32).reshape(micros, -1, rows).transpose(1, 0, 2)
        spread_cond = spread_cond.reshape(-1, rows)
        spread_cond = jnp.pad(spread_cond, ((0, 0), (0, LANES - rows)))
        own_biases = biases.astype(jnp.float32)
        own_biases = jnp.where(
            me % 2 == 0, jnp.pad(own_biases, (0, half)), jnp.pad(own_biases, (half, 0))
        )
        payload = jnp.concatenate([spread_cond, own_biases.reshape(-1, LANES)])
        payload = jnp.pad(payload, ((0, -payload.shape[0] % 8), (0, 0)))
        attend_all, project_all, expand_all, contract_all, modulation_all, *rest = front(
            *shards, payload, modulate_rows, cotangent, planes
        )
        *rest, bias_rows, cond_own = rest
        normed, projected, heads, logs, blended, middle, attended, second, act, slope, low, grads = rest
        contract_sum, output, grad_middle, row_sums, bias_sums, hidden_sums, *onward = middle_part(
            grads.reshape(*grid, FF // devices, D),
            (expand_all, contract_all, project_all),
            (act, slope, second, low, middle, attended, cotangent, blended),
            (modulation_all, bias_rows),
            planes,
        )
        attend_sum, expand_sum, project_sum, grad_tokens, sums, grad_modulate, cond_cols = back_part(
            *onward,
            (projected, heads, logs, normed, attend_all, tokens, grad_middle),
            (
                modulation_all,
                bias_rows,
                row_sums,
                bias_sums,
                hidden_sums,
                cond_own,
                modulate_rows,
            ),
            planes,
        )
        sums = sums.reshape(latents, GROUP, -1)
        split = micros * 6 * D // GROUP
        cond_cols = cond_cols[..., :rows].reshape(devices, micros, latents, rows)
    else:
        held = jnp.concatenate([condition.reshape(-1), biases]).astype(jnp.float32)
        held = jnp.pad(held, (0, -held.size % (8 * LANES)))
        small = small_gather(held.reshape(-1, LANES), planes, 0).reshape(devices, -1)
        conditions = small[:, : condition.size].reshape(latents, GROUP, micros, -1)
        conditions = conditions.transpose(2, 0, 1, 3).reshape(micros * latents, D)
        cond_act = silu(conditions).astype(jnp.bfloat16)
        bias_all = small[:, condition.size : condition.size + biases.size].reshape(-1)
        bias_query = bias_all[0:D]
        bias_value = bias_all[D : 2 * D]
        bias_project = bias_all[2 * D : 3 * D]
        bias_expand = bias_all[3 * D : 3 * D + FF]
        bias_contract = bias_all[3 * D + FF : 4 * D + FF]
        bias_modulate = bias_all[4 * D + FF :]

        cond_own = lax.dynamic_slice_in_dim(cond_act, me * rows, rows, axis=1)
        partial = jnp.dot(cond_own, modulate_rows, preferred_element_type=jnp.float32)
        partial = partial.reshape(micros, latents, GROUP, -1).transpose(1, 2, 0, 3)
        partial = partial.reshape(planes, 2, 2, 2, -1, LANES)

        bias_row = jnp.concatenate(
            [
                lax.dynamic_slice_in_dim(bias_query, quarter * OWN, OWN),
                jnp.zeros((OWN,), jnp.float32),
                lax.dynamic_slice_in_dim(bias_value, quarter * OWN, OWN),
            ]
        )
        bias_row = bias_row.reshape(3, PAIRS, LANES).transpose(1, 0, 2).reshape(-1)
        attend_all, project_all, expand_all, contract_all, modulation_all, *rest = gather_all(
            *shards, partial, planes
        )
        modulation = modulation_all.reshape(GROUP, micros, -1).transpose(1, 0, 2)
        modulation = modulation.reshape(micros, 6 * D) + bias_modulate
        offsets_one, factors_one, gates_one, offsets_two, factors_two, gates_two = (
            modulation[:, None, part * D : (part + 1) * D] for part in range(6)
        )
        attend_own = attend_all.reshape(D, 3 * OWN)
        project_full = project_all.reshape(D, D)
        expand_full = expand_all.reshape(D, FF)
        contract_full = contract_all.reshape(FF, D)
        tokens_latent = rest[0].reshape(micros, latent_rows, D)
        normed_latent, _ = normalize(tokens_latent.astype(jnp.float32))
        first = (normed_latent * (1.0 + factors_one) + offsets_one).astype(jnp.bfloat16)
        projected = (einsum("mrd,de->mre", first, attend_own) + bias_row).astype(jnp.bfloat16)
        blended_heads, logs = attention(projected)
        blended = heads_to_tokens(blended_heads)

        attended = einsum("mrd,de->mre", blended, project_full) + bias_project
        middle = inputs + gates_one * attended
        normed_two, scale_two = normalize(middle)
        second = (normed_two * (1.0 + factors_two) + offsets_two).astype(jnp.bfloat16)
        hidden = einsum("mrd,de->mre", second, expand_full) + bias_expand
        activated, gelu_pull = jax.vjp(lambda v: jax.nn.gelu(v, approximate=True), hidden)
        act_low = activated.astype(jnp.bfloat16)
        branch = einsum("mrd,de->mre", act_low, contract_full) + bias_contract
        output = (middle + gates_two * branch).astype(jnp.bfloat16)

        upstream = cotangent.astype(jnp.float32)
        grad_branch = (gates_two * upstream).astype(jnp.bfloat16)
        grad_contract = einsum("mrd,mre->de", act_low, grad_branch)
        grad_act = einsum("mre,de->mrd", grad_branch, contract_full)
        grad_hidden = gelu_pull(grad_act)[0].astype(jnp.bfloat16)
        grad_expand = einsum("mrd,mre->de", second, grad_hidden)
        grad_second = einsum("mre,de->mrd", grad_hidden, expand_full)
        grad_middle = upstream + norm_back(grad_second, normed_two, scale_two, factors_two)
        grad_attended = (gates_one * grad_middle).astype(jnp.bfloat16)
        grad_project = einsum("mrd,mre->de", blended, grad_attended)
        grad_blended = einsum("mre,de->mrd", grad_attended, project_full).astype(jnp.bfloat16)
        grad_heads = tokens_to_heads(grad_blended)
        grad_projected = attention_back(projected, blended_heads, grad_heads, logs)
        grad_attend = einsum("mrd,mre->de", first, grad_projected)
        grad_first = token_sums(
            einsum("mre,de->mrd", grad_projected, attend_own).astype(jnp.bfloat16)
        )
        weights = (
            grad_contract.astype(jnp.bfloat16).reshape(*grid, FF // devices, D),
            grad_expand.astype(jnp.bfloat16).reshape(*grid, rows, FF),
            grad_project.astype(jnp.bfloat16).reshape(*grid, rows, D),
        )
        attend_sum, contract_sum, expand_sum, project_sum = weight_sums(
            grad_attend.astype(jnp.bfloat16).reshape(*grid, rows, 3 * OWN), weights, planes
        )

        def token_sum(values):
            return jnp.sum(values, axis=(0, 1), dtype=jnp.float32)

        heads_sum, attended_sum = token_sum(grad_projected), token_sum(grad_attended)
        hidden_sum, branch_sum = token_sum(grad_hidden), token_sum(grad_branch)
        later_sums = jnp.concatenate(
            [
                jnp.sum(grad_middle * attended, axis=1),
                jnp.sum(grad_second, axis=1),
                jnp.sum(grad_second * normed_two, axis=1),
                jnp.sum(upstream * branch, axis=1),
            ],
            axis=1,
        )
        normed_one, scale_one = normalize(inputs)
        grad_tokens = grad_middle + norm_back(grad_first, normed_one, scale_one, factors_one)

        grad_modulation = jnp.concatenate(
            [jnp.sum(grad_first, axis=1), jnp.sum(grad_first * normed_one, axis=1), later_sums], axis=1
        )
        heads_sum = heads_sum.reshape(PAIRS, 3, LANES).transpose(1, 0, 2).reshape(3, OWN)
        bias_terms = jnp.concatenate(
            [
                lax.dynamic_update_slice(
                    jnp.zeros((D,), jnp.float32), heads_sum[0], (quarter * OWN,)
                ),
                lax.dynamic_update_slice(
                    jnp.zeros((D,), jnp.float32), heads_sum[2], (quarter * OWN,)
                ),
                attended_sum,
                hidden_sum,
                branch_sum,
            ]
        )
        to_sum = jnp.concatenate(
            [
                grad_modulation.reshape(micros, GROUP, -1).transpose(1, 0, 2).reshape(GROUP, -1),
                bias_terms.reshape(GROUP, -1),
            ],
            axis=1,
        )
        sums = small_sums(to_sum.reshape(2, 2, -1, LANES), planes).reshape(latents, GROUP, -1)
        split = micros * 6 * D // GROUP
        grad_modulations = sums[:, :, :split].reshape(latents, GROUP, micros, -1)
        grad_modulations = grad_modulations.transpose(2, 0, 1, 3).reshape(micros * latents, 6 * D)
        grad_modulate = lax.dot_general(
            cond_own.astype(jnp.float32),
            grad_modulations,
            (((0,), (0,)), ((), ())),
            precision=highest,
        )
        grad_cond_cols = lax.dot_general(
            grad_modulations,
            modulate_rows.astype(jnp.float32),
            (((1,), (1,)), ((), ())),
            precision=highest,
        )
        cols = grad_cond_cols.reshape(-1)
        cols = jnp.pad(cols, (0, -cols.size % (8 * LANES)))
        cond_cols = small_gather(cols.reshape(-1, LANES), planes, 8).reshape(devices, -1)
        cond_cols = cond_cols[:, : micros * latents * rows].reshape(devices, micros, latents, rows)
    grad_modulations = sums[:, :, :split].reshape(latents, GROUP, micros, -1)
    grad_modulations = grad_modulations.transpose(2, 0, 1, 3).reshape(micros * latents, 6 * D)
    bias_sums = jnp.concatenate(
        [jnp.sum(sums[:, :, split:], axis=0).reshape(-1), jnp.sum(grad_modulations, axis=0)]
    )
    grad_biases = lax.dynamic_slice_in_dim(bias_sums, me * biases.size, biases.size)
    cols_own = lax.dynamic_index_in_dim(cond_cols, latent, axis=2, keepdims=False)
    width = D // GROUP
    cols_own = lax.dynamic_slice_in_dim(
        cols_own, quarter * (devices // GROUP), devices // GROUP, axis=0
    )
    grad_silu = cols_own.transpose(1, 0, 2).reshape(micros, width)
    values = condition.astype(jnp.float32)
    gate = 1.0 / (1.0 + jnp.exp(-values))
    grad_condition = gate * (1.0 + values * (1.0 - gate)) * grad_silu

    attend_sum = attend_sum.reshape(2, 2, rows, PAIRS, 3, LANES).transpose(2, 4, 0, 1, 3, 5)
    return (
        output,
        grad_tokens,
        grad_condition,
        attend_sum.reshape(-1),
        project_sum.reshape(-1),
        expand_sum.reshape(-1),
        contract_sum.reshape(-1),
        grad_modulate.reshape(-1),
        grad_biases,
    )


def solution(mesh):
    in_specs = (
        P(None, "fsdp", None),
        P(None, "fsdp"),
        P("fsdp"),
        P("fsdp"),
        P("fsdp"),
        P("fsdp"),
        P("fsdp"),
        P("fsdp"),
        P(None, "fsdp", None),
    )
    out_specs = (
        P(None, "fsdp", None),
        P(None, "fsdp", None),
        P(None, "fsdp"),
        P("fsdp"),
        P("fsdp"),
        P("fsdp"),
        P("fsdp"),
        P("fsdp"),
        P("fsdp"),
    )
    return jax.shard_map(
        per_device, mesh=mesh, in_specs=in_specs, out_specs=out_specs, check_vma=False
    )
```

```python
import functools

import jax
import jax.numpy as jnp
from jax import lax
from jax.experimental import pallas as pl
from jax.experimental.pallas import tpu as pltpu
from jax.sharding import PartitionSpec as P

D = 1024
HEADS = 16
HEAD = 64
FF = 4096
GROUP = 4
OWN = D // GROUP
SCALE = HEAD**-0.5
LANES = 128
MICROS = 2

epsilon = 1e-06
highest = lax.Precision.HIGHEST
MESH = pl.DeviceIdType.MESH
MIB = 1 << 20


def silu(values):
    return values / (1.0 + jnp.exp(-values))


class Links:
    def __init__(self, planes, send_sem, recv_sem, local_sem=None):
        me = lax.axis_index("fsdp")
        self.planes = planes
        self.c = me % 2
        self.x = (me // 2) % 2
        self.y = (me // 4) % 2
        self.z = me // 8
        self.core = me + 1 - 2 * self.c
        self.beside = me + 2 - 4 * self.x
        self.across = me + 4 - 8 * self.y
        self.place = me % 8
        self.send_sem, self.recv_sem, self.local_sem = send_sem, recv_sem, local_sem
        self.used = 0
        self.local_used = 0
        self.pending = []

    def plane(self, step):
        return (self.z + step) % self.planes

    def plane_device(self, step):
        return self.plane(step) * 8 + self.place

    def column(self):
        places = []
        for step in range(self.planes):
            for y in (self.y, 1 - self.y):
                if step > 0 or y is not self.y:
                    z = self.plane(step)
                    places.append((z, y, z * 8 + y * 4 + self.place % 4))
        return places

    def partners(self):
        return [self.core, self.beside] + [device for _, _, device in self.column()]

    def greet(self, partners):
        barrier = pltpu.get_barrier_semaphore()
        for partner in partners:
            pl.semaphore_signal(barrier, inc=1, device_id=(partner,), device_id_type=MESH)
        pl.semaphore_wait(barrier, len(partners))

    def send(self, source, target, device):
        assert self.used < self.send_sem.shape[0]
        copy = pltpu.make_async_remote_copy(
            src_ref=source,
            dst_ref=target,
            send_sem=self.send_sem.at[self.used],
            recv_sem=self.recv_sem.at[self.used],
            device_id=(device,),
            device_id_type=MESH,
        )
        self.used += 1
        copy.start()
        self.pending.append(copy)
        return copy

    def local(self, source, target):
        assert self.local_used < self.local_sem.shape[0]
        copy = pltpu.make_async_copy(source, target, self.local_sem.at[self.local_used])
        self.local_used += 1
        copy.start()
        return copy

    def finish_sends(self):
        for copy in self.pending:
            copy.wait_send()
        self.pending = []


def arrived(copies):
    for copy in copies:
        copy.wait_recv()


ANY = pl.BlockSpec(memory_space=pl.ANY)
VMEM = pl.BlockSpec(memory_space=pltpu.VMEM)


def remote_call(body, name, collective_id, outs, in_specs, out_specs, scratch, sems, local_sems, vmem):
    return pl.pallas_call(
        body,
        out_shape=outs,
        in_specs=in_specs,
        out_specs=out_specs,
        scratch_shapes=[
            pltpu.SemaphoreType.DMA((sems,)),
            pltpu.SemaphoreType.DMA((sems,)),
            pltpu.SemaphoreType.DMA((max(local_sems, 1),)),
            *scratch,
        ],
        compiler_params=pltpu.CompilerParams(
            collective_id=collective_id, has_side_effects=True, vmem_limit_bytes=vmem
        ),
        name=name,
    )


def small_gather_body(planes, own_ref, out_ref, send_sem, recv_sem, local_sem):
    links = Links(planes, send_sem, recv_sem)
    links.greet(links.partners())
    z, y, x, c = links.z, links.y, links.x, links.c
    out_ref[z, y, x, c] = own_ref[...]
    spread_all(links, out_ref)
    links.finish_sends()


def spread_all(links, out_ref):
    spread = Spread(links, out_ref)
    for k in range(4):
        spread.step(k)


def small_gather(own, planes, collective_id):
    return remote_call(
        functools.partial(small_gather_body, planes),
        "small_gather",
        collective_id,
        jax.ShapeDtypeStruct((planes, 2, 2, 2, *own.shape), own.dtype),
        [VMEM],
        VMEM,
        [],
        2 * planes + 4,
        0,
        40 * MIB,
    )(own)


WIDTH = 1024
HALF = WIDTH // 2
ALL = slice(None)


class Pieces:
    def __init__(self, links, shards, fulls):
        self.links = links
        self.pieces, self.owns = [], []
        for shard, full in zip(shards, fulls):
            z, y, x, c = links.z, links.y, links.x, links.c
            self.owns.append([links.local(shard, full.at[z, y, x, c]), False])
            for first, count, start in cuts(shard.shape):
                rows = rows_of(shard.shape, first, count)
                self.pieces.append((len(self.owns) - 1, shard, full, rows, start))
        self.count = len(self.pieces)
        self.lead = [None] * self.count
        self.rest = [None] * self.count
        self.late = [[] for _ in range(self.count)]

    def columns(self, k, half):
        return pl.ds(self.pieces[k][4] + half * HALF, HALF)

    def block(self, k, half, *place):
        _, _, full, rows, _ = self.pieces[k]
        return full.at[(*place, rows, self.columns(k, half))]

    def own_block(self, k, half):
        _, shard, _, rows, _ = self.pieces[k]
        links = self.links
        return shard.at[rows, self.columns(k, half)], self.block(
            k, half, links.z, links.y, links.x, links.c
        )

    def own_there(self, k):
        own = self.owns[self.pieces[k][0]]
        if not own[1]:
            own[0].wait()
            own[1] = True

    def to_core(self, k, half, *place):
        block = self.block(k, half, *place)
        self.late[k].append(self.links.send(block, block, self.links.core))

    def to_planes(self, source, target):
        links = self.links
        return [links.send(source, target, links.plane_device(s)) for s in range(1, links.planes)]

    def T0(self, k):
        if k < self.count:
            self.lead[k] = [self.links.send(*self.own_block(k, 0), self.links.beside)]

    def T1(self, k):
        links = self.links
        self.own_there(k)
        arrived(self.lead[k])
        block = self.block(k, 0, links.z, links.y, ALL, links.c)
        self.lead[k] = self.to_planes(block, block)
        self.T0(k + AHEAD)

    def T2(self, k):
        links = self.links
        arrived(self.lead[k])
        place = (ALL, links.y, ALL, links.c)
        block = self.block(k, 0, *place)
        self.lead[k] = [links.send(block, block, links.across)]
        self.to_core(k, 0, *place)

    def T3(self, k):
        links = self.links
        arrived(self.lead[k])
        self.to_core(k, 0, ALL, 1 - links.y, ALL, links.c)

    def F0(self, k):
        if k < self.count:
            self.rest[k] = self.to_planes(*self.own_block(k, 1))

    def F1(self, k):
        links = self.links
        self.own_there(k)
        arrived(self.rest[k])
        place = (ALL, links.y, links.x, links.c)
        block = self.block(k, 1, *place)
        self.rest[k] = [links.send(block, block, links.across)]
        self.to_core(k, 1, *place)
        self.F0(k + AHEAD)

    def F2(self, k):
        links = self.links
        arrived(self.rest[k])
        block = self.block(k, 1, ALL, ALL, links.x, links.c)
        self.rest[k] = [links.send(block, block, links.beside)]
        self.to_core(k, 1, ALL, 1 - links.y, links.x, links.c)

    def F3(self, k):
        links = self.links
        arrived(self.rest[k])
        self.to_core(k, 1, ALL, ALL, 1 - links.x, links.c)

    def there(self, k):
        arrived(self.late[k])
        self.late[k] = []


def tasks_of(order):
    return [(TASKS[code // 32], code % 32) for code in order]


TASKS = (
    "fb", "az", "sp", "ay", "pm", "tk", "F1", "F2", "T1", "att", "unit", "F3", "T2", "T3", "load",
    "own", "there", "mlp", "S1", "project", "F4", "T4", "head", "first", "t1", "attend", "small",
    "t2", "a1", "sums", "modulate", "a2", "a3", "cond",
)


def cuts(shape):
    rows, width = shape
    if width > WIDTH:
        return [(0, rows, start) for start in range(0, width, WIDTH)]
    count = 4 if rows % 128 == 0 else 1
    return [(part * (rows // count), rows // count, 0) for part in range(count)]


def rows_of(shape, first, count):
    return ALL if count == shape[-2] else pl.ds(first, count)


AHEAD = 2
MIDDLE_PIECES = 3


class Opening:
    TOKEN_CUTS = 8
    ATTEND_CUTS = 4

    def __init__(self, links, tokens, attend, partial, tokens_out, attend_out, modulation_out, scratch):
        self.links, self.partial, self.attend = links, partial, attend
        self.tokens, self.tokens_out = tokens, tokens_out
        self.attend_out, self.modulation_out = attend_out, modulation_out
        self.held, self.from_core, self.from_beside, self.from_column, self.total = scratch
        z, y, x, c = links.z, links.y, links.x, links.c
        target = attend_out.at[z, y, x, c]
        self.own_slice = links.local(attend.at[x, c], target)
        self.own_tokens = links.local(tokens, tokens_out.at[:, x, c])
        self.far = links.send(attend.at[1 - x, 1 - c], self.held, links.core)
        self.near = [
            links.send(attend.at[x, 1 - c], target, links.core),
            links.send(attend.at[1 - x, c], target, links.beside),
        ]
        self.over_planes, self.beside, self.rest = {}, {}, []

    def tokens_start(self):
        links = self.links
        target = self.tokens_out.at[:, links.x, links.c]
        self.rest.append(links.send(self.tokens, target, links.core))
        for k in range(2):
            self.tkx(k)

    def token_block(self, k):
        each = self.TOKEN_CUTS // self.tokens.shape[0]
        rows = self.tokens.shape[1] // each
        return k // each, pl.ds(k % each * rows, rows)

    def tkx(self, k):
        links = self.links
        m, rows = self.token_block(k)
        target = self.tokens_out.at[m, links.x, links.c, rows]
        self.beside[k] = links.send(self.tokens.at[m, rows], target, links.beside)

    def tk(self, k):
        links = self.links
        arrived([self.beside.pop(k)])
        m, rows = self.token_block(k)
        fresh = self.tokens_out.at[m, 1 - links.x, links.c, rows]
        self.rest.append(links.send(fresh, fresh, links.core))
        if k + 2 < self.TOKEN_CUTS:
            self.tkx(k + 2)

    def fb(self, k):
        links = self.links
        arrived([self.far])
        target = self.attend_out.at[links.z, links.y, links.x, 1 - links.c]
        self.near.append(links.send(self.held, target, links.beside))

    def attend_block(self, k, *place):
        pair = k // 2
        return self.attend_out.at[(*place, k % 2, ALL, ALL, pl.ds(pair * PAIR, PAIR))]

    def azx(self, k):
        links = self.links
        block = self.attend_block(k, links.z, links.y)
        self.over_planes[k] = [
            links.send(block, block, links.plane_device(s)) for s in range(1, links.planes)
        ]

    def az(self, k):
        self.own_slice.wait()
        arrived(self.near)
        self.azx(0)
        self.azx(1)

    def ay(self, k):
        links = self.links
        arrived(self.over_planes.pop(k))
        block = self.attend_block(k, ALL, links.y)
        self.rest.append(links.send(block, block, links.across))
        if k + 2 < self.ATTEND_CUTS:
            self.azx(k + 2)

    def pm(self, k):
        links = self.links
        z, y, x, c = links.z, links.y, links.x, links.c
        if k > 0:
            arrived(self.step)
        if k == 0:
            self.step = [links.send(self.partial.at[:, :, :, 1 - c], self.from_core, links.core)]
        elif k == 1:
            self.from_core[...] = self.from_core[...] + self.partial[:, :, :, c]
            self.step = [
                links.send(self.from_core.at[:, :, 1 - x], self.from_beside, links.beside)
            ]
        elif k == 2:
            self.from_beside[...] = self.from_beside[...] + self.from_core[:, :, x]
            self.step = [
                links.send(self.from_beside.at[to_z, to_y], self.from_column.at[place], device)
                for place, (to_z, to_y, device) in enumerate(links.column())
            ]
        elif k == 3:
            result = self.from_beside[z, y]
            for place in range(2 * links.planes - 1):
                result = result + self.from_column[place]
            self.total[...] = result
            target = self.modulation_out.at[x, c]
            target[...] = result
            self.step = [
                links.send(self.total, target, links.core),
                links.send(self.total, target, links.beside),
            ]
        else:
            fresh = self.modulation_out.at[1 - x, c]
            self.rest.append(links.send(fresh, fresh, links.core))

    def finish(self):
        arrived(self.rest)
        self.own_tokens.wait()


def gather_body(
    planes,
    tokens,
    attend,
    project,
    expand,
    contract,
    partial,
    attend_out,
    project_out,
    expand_out,
    contract_out,
    modulation_out,
    tokens_out,
    send_sem,
    recv_sem,
    local_sem,
    *scratch,
):
    links = Links(planes, send_sem, recv_sem, local_sem)
    links.greet(links.partners())
    opening = Opening(
        links, tokens, attend, partial, tokens_out, attend_out, modulation_out, scratch
    )
    pieces = Pieces(links, (project, expand, contract), (project_out, expand_out, contract_out))
    opening.tokens_start()
    for k in range(5):
        opening.pm(k)
    for k in range(Opening.TOKEN_CUTS):
        opening.tk(k)
    opening.fb(0)
    opening.az(0)
    for k in range(Opening.ATTEND_CUTS):
        opening.ay(k)
    for k in range(AHEAD):
        pieces.T0(k)
        pieces.F0(k)
    for k in range(pieces.count + 2):
        for behind, names in enumerate((("T1", "F1"), ("T2", "F2"), ("T3", "F3"))):
            if 0 <= k - behind < pieces.count:
                for name in names:
                    getattr(pieces, name)(k - behind)
    for k in range(pieces.count):
        pieces.there(k)
    opening.finish()
    links.finish_sends()


FRONT_ORDER = (
    0, 32, 65, 66, 96, 128, 160, 97, 161, 129, 98, 162, 163, 99, 130, 192, 164, 193, 165, 131, 166,
    224, 194, 167, 132, 195, 256, 225, 288, 320, 196, 321, 257, 226, 197, 227, 322, 352, 323, 384,
    324, 353, 325, 198, 326, 327, 416, 354, 385, 328, 258, 199, 329, 355, 200, 259, 330, 417, 331,
    332, 386, 333, 260, 334, 228, 261, 387, 335, 336, 418, 337, 229, 388, 448, 262, 356, 419, 480,
    230, 389, 263, 513, 544, 231, 232, 357, 420, 264, 390, 514, 545, 421, 358, 515, 546, 391, 516,
    547, 422, 359, 392, 423, 360, 424,
)


def front_body(planes, *refs):
    tokens, attend_flat, project_flat, expand_flat, contract_flat, refs = *refs[:5], refs[5:]
    payload, modulate_flat, cotangent, refs = *refs[:3], refs[3:]
    attend_out, project_out, expand_out, contract_out, modulation_out, refs = *refs[:5], refs[5:]
    normed_out, qkv_out, heads_out, log_out, blended_out, refs = *refs[:5], refs[5:]
    middle_out, attended_out, second_out, act_out, slope_out, branch_out, grad_out = refs[:7]
    bias_rows, cond_out, modulate, refs = *refs[7:10], refs[10:]
    send_sem, recv_sem, local_sem = refs[:3]
    opening_scratch, refs = refs[3:8], refs[8:]
    payloads, partial, refs = *refs[:2], refs[2:]
    flat, attend, project, expand, contract, refs = *refs[:5], refs[5:]
    tokens_all, attend_all, normed, qkv, heads, blended, project_all, expand_all = refs[:8]
    middle, attended, second, act, slope, grad_branch, grads, upstream, bias_held = refs[8:]
    links = Links(planes, send_sem, recv_sem, local_sem)
    z, y, x, c = links.z, links.y, links.x, links.c
    corner = links.beside + 1 - 2 * c
    links.greet([*links.partners(), corner])
    payloads[z, y, x, c] = payload[...]
    spread = Spread(links, payloads)
    spread.step(0)

    def rows_apart(source, count):
        stride = source.shape[0] // count
        flat[: source.shape[0], :] = source[...].astype(jnp.float32)
        for k in range(stride):
            yield k, flat[pl.ds(k, count, stride=stride), :].astype(jnp.bfloat16)

    rows_own = project.shape[0]
    for k, values in rows_apart(attend_flat, rows_own):
        kind, quarter, pair = k // (GROUP * PAIRS), k // PAIRS % GROUP, k % PAIRS
        lanes = pl.ds((pair * 3 + kind) * LANES, LANES)
        attend[quarter // 2, quarter % 2, :, lanes] = values
    opening = Opening(
        links, tokens, attend, partial, tokens_all, attend_all, modulation_out, opening_scratch
    )
    for source, target in (
        (modulate_flat, modulate),
        (expand_flat, expand),
        (project_flat, project),
        (contract_flat, contract),
    ):
        for k, values in rows_apart(source, target.shape[0]):
            target[:, k * LANES : (k + 1) * LANES] = values
    pieces = Pieces(links, (project, expand, contract), (project_all, expand_all, contract_out))
    count = pieces.count
    loaded_upstream = links.local(cotangent, upstream)
    micros, own_rows, _ = tokens.shape
    stored, stored_grads, exchanged = [], [], []
    own_heads = pl.ds(pl.multiple_of((2 * x + c) * OWN, OWN), OWN)

    def partial_unit():
        latents, rows = 2 * planes, modulate.shape[0]
        each = latents
        source = (links.z * 8 + links.place) // each
        column = (links.z * 8 + links.place) % each
        conds = [
            payloads[:, :, source // 2, source % 2, pl.ds(micros * column + m, 1), :].reshape(
                latents, LANES
            )
            for m in range(micros)
        ]
        active = silu(jnp.concatenate(conds, axis=0)[:, :rows]).astype(jnp.bfloat16)
        cond_out[...] = active.astype(jnp.float32)
        product = jnp.dot(active, modulate[...], preferred_element_type=jnp.float32)
        per_quarter = 6 * D // LANES // GROUP
        for m in range(micros):
            for k in range(6 * D // LANES):
                quarter, row = k // per_quarter, m * per_quarter + k % per_quarter
                values = product[m * latents : (m + 1) * latents, k * LANES : (k + 1) * LANES]
                partial[:, :, quarter // 2, quarter % 2, row, :] = values.reshape(
                    planes, 2, LANES
                )
        opening.pm(0)
        start = micros * each
        long = bias_rows.shape[0] // (4 * planes)
        for pair in range(4 * planes):
            place = (pair // 4, pair // 2 % 2, pair % 2)
            even = payloads[(*place, 0, slice(start, start + 4), ALL)]
            odd = payloads[(*place, 1, slice(start, start + 4), ALL)]
            joint = even[3:4] + odd[0:1]
            bias_rows[pair * long : (pair + 1) * long, :] = jnp.concatenate(
                [even[:3], joint, odd[1:]], axis=0
            )

    def shift(block):
        return bias_vector(bias_rows, 4 * D + FF + block * D, D)

    def part_of(m, to_x, to_c):
        start = pl.multiple_of((2 * to_x + to_c) * own_rows, own_rows)
        return heads.at[m, pl.ds(start, own_rows)]

    def project_micro(m):
        own = (2 * x + c) * PAIRS
        bias_qkv = []
        for pair in range(PAIRS):
            bias_qkv += [
                bias_rows[pl.ds(own + pair, 1), :],
                jnp.zeros((1, LANES), jnp.float32),
                bias_rows[pl.ds(D // LANES + own + pair, 1), :],
            ]
        offsets = modulation_row(modulation_out, m, 0) + shift(0)
        factors = 1.0 + modulation_row(modulation_out, m, 1) + shift(1)
        bias = jnp.concatenate(bias_qkv, axis=1)
        project_tokens(m, tokens_all, attend_all, offsets, factors, bias, normed, qkv)
        stored.append(links.local(normed.at[m], normed_out.at[m]))
        stored.append(links.local(qkv.at[m], qkv_out.at[m]))

    def far_heads(m, head):
        attention_unit(qkv.at[m], heads.at[m], log_out.at[m], head, 1 - x)
        if head == OWN // HEAD - 1:
            target = blended.at[m, :, own_heads]
            exchanged.append(links.send(part_of(m, 1 - x, 1 - c), target, corner))
            exchanged.append(links.send(part_of(m, 1 - x, c), target, links.beside))

    def near_heads(m, head):
        attention_unit(qkv.at[m], heads.at[m], log_out.at[m], head, x)
        if head == OWN // HEAD - 1:
            target = blended.at[m, :, own_heads]
            exchanged.append(links.send(part_of(m, x, 1 - c), target, links.core))
            stored.append(links.local(heads.at[m], heads_out.at[m]))
            links.local(part_of(m, x, c), target).wait()

    units = []
    for m in range(micros):
        units.append(functools.partial(project_micro, m))
        units += [functools.partial(far_heads, m, head) for head in range(OWN // HEAD)]
    for m in range(micros):
        units += [functools.partial(near_heads, m, head) for head in range(OWN // HEAD)]

    def load_project():
        pieces.there(0)
        stored.append(links.local(project_all, project_out))
        loaded_upstream.wait()
        for m in range(micros):
            gate = modulation_row(modulation_out, m, 5) + shift(5)
            grad_branch[m] = (gate * upstream[m].astype(jnp.float32)).astype(jnp.bfloat16)
        stored.append(links.local(grad_branch, branch_out))

    def own_tokens():
        for m in range(micros):
            stored.append(links.local(blended.at[m], blended_out.at[m]))
            product = jnp.dot(
                blended[m],
                project_all[...].reshape(D, D),
                preferred_element_type=jnp.float32,
            )
            attended[m] = product + bias_vector(bias_rows, 2 * D, D)
            gate = modulation_row(modulation_out, m, 2) + shift(2)
            middle[m] = tokens_all[m, x, c].astype(jnp.float32) + gate * attended[m]
            normed_two, _ = normalize(middle[m])
            factors = 1.0 + modulation_row(modulation_out, m, 4) + shift(4)
            offsets = modulation_row(modulation_out, m, 3) + shift(3)
            second[m] = (normed_two * factors + offsets).astype(jnp.bfloat16)
        stored.append(links.local(middle, middle_out))
        stored.append(links.local(attended, attended_out))
        stored.append(links.local(second, second_out))

    parts = FF // WIDTH
    blocks = grads.shape[1]

    def expand_unit(part):
        columns = pl.ds(part * WIDTH, WIDTH)
        stored.append(
            links.local(
                expand_all.at[:, :, :, :, :, columns], expand_out.at[:, :, :, :, :, columns]
            )
        )
        if part >= 2:
            stored_grads[part - 2].wait()
        bias = bias_vector(bias_rows, 3 * D + part * WIDTH, WIDTH)
        bias_held[...] = bias
        expand_part(part, WIDTH, second, expand_all, bias_held, act, slope, grad_branch, grads)
        stored.append(links.local(act.at[:, :, columns], act_out.at[:, :, columns]))
        stored.append(links.local(slope.at[:, :, columns], slope_out.at[:, :, columns]))
        stored_grads.append(
            links.local(grads.at[part % 2], grad_out.at[pl.ds(part * blocks, blocks)])
        )

    for task, k in tasks_of(FRONT_ORDER):
        if task == "sp":
            spread.step(k)
            if k == 1:
                opening.tokens_start()
        elif task in ("fb", "az", "ay", "tk"):
            getattr(opening, task)(k)
            if task == "ay" and k == Opening.ATTEND_CUTS - 2:
                for piece in range(AHEAD):
                    pieces.F0(piece)
            if task == "tk" and k == Opening.TOKEN_CUTS - 2:
                for piece in range(AHEAD):
                    pieces.T0(piece)
        elif task == "pm":
            if k == 0:
                spread.step(3)
                partial_unit()
            else:
                opening.pm(k)
        elif task == "att":
            opening.finish()
            stored.append(links.local(attend_all, attend_out))
        elif task == "unit":
            units[k]()
        elif task == "load":
            load_project()
        elif task == "own":
            arrived(exchanged)
            own_tokens()
        elif task == "there":
            pieces.there(k)
        elif task == "mlp":
            expand_unit(k)
        else:
            getattr(pieces, task)(k)
    for k in range(count):
        pieces.there(k)
    for copy in stored + stored_grads[-2:]:
        copy.wait()
    links.finish_sends()


ROOT = 0.7978845608028654
CUBE = 0.044715
CHUNK = 512


def expand_part(part, width, second, expand, bias, act, slope, grad_branch, grads):
    micros = second.shape[0]
    rows = grads.shape[2]

    @pl.loop(0, width // CHUNK)
    def _(chunk):
        inside = pl.ds(pl.multiple_of(chunk * CHUNK, CHUNK), CHUNK)
        columns = pl.ds(pl.multiple_of(part * width + chunk * CHUNK, CHUNK), CHUNK)
        weights = expand[:, :, :, :, :, columns].reshape(D, CHUNK)
        total = None
        for m in range(micros):
            hidden = jnp.dot(second[m], weights, preferred_element_type=jnp.float32)
            hidden = hidden + bias[:, inside]
            square = hidden * hidden
            bend = jnp.tanh(hidden * (ROOT + (ROOT * CUBE) * square))
            half = 0.5 + 0.5 * bend
            low = (hidden * half).astype(jnp.bfloat16)
            act[m, :, columns] = low
            steep = hidden * (0.5 * ROOT + (1.5 * ROOT * CUBE) * square)
            slope[m, :, columns] = (half + steep * (1.0 - bend * bend)).astype(jnp.bfloat16)
            product = lax.dot_general(
                low, grad_branch[m], (((0,), (0,)), ((), ())), preferred_element_type=jnp.float32
            )
            total = product if total is None else total + product
        count = CHUNK // rows
        here = pl.ds(chunk * count, count)
        grads[part % 2, here] = total.astype(jnp.bfloat16).reshape(count, rows, D)


def modulation_row(modulation, m, block):
    per_quarter = modulation.shape[2] // MICROS
    pieces = []
    for k in range(block * D // LANES, (block + 1) * D // LANES):
        quarter, row = k // per_quarter, m * per_quarter + k % per_quarter
        pieces.append(modulation[quarter // 2, quarter % 2, row : row + 1, :])
    return jnp.concatenate(pieces, axis=1)


def bias_vector(bias_rows, start, count):
    rows = range(start // LANES, (start + count) // LANES)
    return jnp.concatenate([bias_rows[row : row + 1, :] for row in rows], axis=1)


def project_tokens(m, tokens, attend, offsets, factors, bias, normed_out, qkv_out):
    rows = tokens.shape[3]

    @pl.loop(0, GROUP)
    def _(block):
        values = tokens[m, block // 2, block % 2].astype(jnp.float32)
        normed, _ = normalize(values)
        first = (normed * factors + offsets).astype(jnp.bfloat16)
        here = pl.ds(pl.multiple_of(block * rows, rows), rows)
        normed_out[m, here, :] = normed.astype(jnp.bfloat16)
        weights = attend[...].reshape(D, 3 * OWN)
        product = jnp.dot(first, weights, preferred_element_type=jnp.float32)
        qkv_out[m, here, :] = (product + bias).astype(jnp.bfloat16)


def gather_scratch(attend, rows, planes):
    return [
        pltpu.VMEM((attend.shape[-2], attend.shape[-1]), attend.dtype),
        pltpu.VMEM((planes, 2, 2, rows, LANES), jnp.float32),
        pltpu.VMEM((planes, 2, rows, LANES), jnp.float32),
        pltpu.VMEM((2 * planes - 1, rows, LANES), jnp.float32),
        pltpu.VMEM((rows, LANES), jnp.float32),
    ]


def gather_outs(attend, project, expand, contract, rows, planes):
    return [
        *(
            jax.ShapeDtypeStruct((planes, 2, 2, 2, *shard.shape[-2:]), shard.dtype)
            for shard in (attend, project, expand, contract)
        ),
        jax.ShapeDtypeStruct((2, 2, rows, LANES), jnp.float32),
    ]


def gather_sems(planes):
    return 60 + 30 * planes + 9 * (8 + 2 * planes)


def gather_all(tokens, attend, project, expand, contract, partial, planes):
    micros, own_rows, _ = tokens.shape
    return remote_call(
        functools.partial(gather_body, planes),
        "gather_all",
        1,
        (
            *gather_outs(attend, project, expand, contract, partial.shape[-2], planes),
            jax.ShapeDtypeStruct((micros, 2, 2, own_rows, D), tokens.dtype),
        ),
        [ANY] * 5 + [VMEM],
        (ANY,) * 4 + (VMEM, ANY),
        gather_scratch(attend, partial.shape[-2], planes),
        gather_sems(planes),
        8,
        56 * MIB,
    )(tokens, attend, project, expand, contract, partial)


def front(tokens, attend, project, expand, contract, payload, modulate, cotangent, planes):
    micros, own_rows, _ = tokens.shape
    latent_rows = own_rows * GROUP
    blocks = latent_rows // QUERY_ROWS
    def low(*shape):
        return jax.ShapeDtypeStruct(shape, jnp.bfloat16)

    def held(*shape, dtype=jnp.bfloat16):
        return pltpu.VMEM(shape, dtype)

    log_shape = (micros, OWN // HEAD, blocks, 1, QUERY_ROWS)
    own = (micros, own_rows, D)
    parts = FF // WIDTH
    rows = micros * 6 * D // LANES // GROUP
    rows_own, grad_rows = D // (8 * planes), FF // (8 * planes)
    shapes = ((2, 2, rows_own, 3 * OWN), (rows_own, D), (rows_own, FF), (grad_rows, D))
    shards = [jax.ShapeDtypeStruct(shape, jnp.bfloat16) for shape in shapes]
    biases = (10 * D + FF) // LANES
    return remote_call(
        functools.partial(front_body, planes),
        "front",
        1,
        (
            *gather_outs(*shards, rows, planes),
            low(micros, latent_rows, D),
            low(micros, latent_rows, 3 * OWN),
            low(micros, latent_rows, OWN),
            jax.ShapeDtypeStruct(log_shape, jnp.float32),
            low(*own),
            jax.ShapeDtypeStruct(own, jnp.float32),
            jax.ShapeDtypeStruct(own, jnp.float32),
            low(*own),
            low(micros, own_rows, FF),
            low(micros, own_rows, FF),
            low(*own),
            low(FF // grad_rows, grad_rows, D),
            jax.ShapeDtypeStruct((biases, LANES), jnp.float32),
            jax.ShapeDtypeStruct((micros * 2 * planes, rows_own), jnp.float32),
            low(rows_own, 6 * D),
        ),
        [ANY] + [VMEM] * 6 + [ANY],
        (ANY,) * 4 + (VMEM,) + (ANY,) * 3 + (VMEM,) + (ANY,) * 8 + (VMEM,) * 3,
        [
            *gather_scratch(shards[0], rows, planes),
            held(planes, 2, 2, 2, *payload.shape, dtype=jnp.float32),
            held(planes, 2, 2, 2, rows, LANES, dtype=jnp.float32),
            held(*modulate.shape, dtype=jnp.float32),
            *(held(*shape) for shape in shapes),
            held(micros, 2, 2, own_rows, D),
            held(planes, 2, 2, 2, rows_own, 3 * OWN),
            held(micros, latent_rows, D),
            held(micros, latent_rows, 3 * OWN),
            held(micros, latent_rows, OWN),
            held(*own),
            held(planes, 2, 2, 2, rows_own, D),
            held(planes, 2, 2, 2, rows_own, FF),
            held(*own, dtype=jnp.float32),
            held(*own, dtype=jnp.float32),
            held(*own),
            held(micros, own_rows, FF),
            held(micros, own_rows, FF),
            held(*own),
            held(2, FF // parts // grad_rows, grad_rows, D),
            held(*own),
            held(1, WIDTH, dtype=jnp.float32),
        ],
        gather_sems(planes),
        40,
        60 * MIB,
    )(tokens, attend, project, expand, contract, payload, modulate, cotangent)


QUERY_ROWS = 256
PAIRS = OWN // LANES
PAIR = 3 * LANES


def head_columns(head):
    start = head // 2 * PAIR + head % 2 * HEAD
    return [slice(start + kind * LANES, start + kind * LANES + HEAD) for kind in range(3)]


def attention_unit(qkv, out, log, head, side=None):
    count = qkv.shape[0] // QUERY_ROWS
    start = 0
    if side is not None:
        count //= 2
        start = side * count
    at = head * HEAD
    query_at, key_at, value_at = head_columns(head)
    keys = qkv[:, key_at]
    values_t = qkv[:, value_at].T

    @pl.loop(0, count)
    def _(index):
        block = start + index
        here = pl.ds(pl.multiple_of(block * QUERY_ROWS, QUERY_ROWS), QUERY_ROWS)
        queries = qkv[here, query_at] * SCALE
        scores = lax.dot_general(
            keys, queries, (((1,), (1,)), ((), ())), preferred_element_type=jnp.float32
        )
        top = jnp.max(scores, axis=0, keepdims=True)
        weights = jnp.exp(scores - top)
        totals = jnp.sum(weights, axis=0, keepdims=True)
        blended = jnp.dot(
            values_t, weights.astype(jnp.bfloat16), preferred_element_type=jnp.float32
        )
        out[here, at : at + HEAD] = (blended / totals).T.astype(jnp.bfloat16)
        log[head, block] = top + jnp.log(totals)


def attention_body(qkv_ref, out_ref, log_ref):
    for head in range(OWN // HEAD):
        attention_unit(qkv_ref.at[0], out_ref.at[0], log_ref.at[0], head)


def attention(qkv):
    micros, rows, _ = qkv.shape
    heads = OWN // HEAD
    blocks = rows // 256
    return pl.pallas_call(
        attention_body,
        grid=(micros,),
        out_shape=(
            jax.ShapeDtypeStruct((micros, rows, OWN), jnp.bfloat16),
            jax.ShapeDtypeStruct((micros, heads, blocks, 1, 256), jnp.float32),
        ),
        in_specs=[pl.BlockSpec((1, rows, 3 * OWN), lambda m: (m, 0, 0))],
        out_specs=(
            pl.BlockSpec((1, rows, OWN), lambda m: (m, 0, 0)),
            pl.BlockSpec((1, heads, blocks, 1, 256), lambda m: (m, 0, 0, 0, 0)),
        ),
        compiler_params=pltpu.CompilerParams(vmem_limit_bytes=48 * MIB),
        name="attention",
    )(qkv)


def attention_back_unit(qkv, blended_all, grad_all, log, out, key_sum, value_sum, head):
    at = head * HEAD
    query_at, key_at, value_at = head_columns(head)
    keys = qkv[:, key_at]
    keys_t = keys.T
    values = qkv[:, value_at]
    key_sum[...] = jnp.zeros_like(key_sum)
    value_sum[...] = jnp.zeros_like(value_sum)

    @pl.loop(0, qkv.shape[0] // QUERY_ROWS)
    def _(block):
        here = pl.ds(pl.multiple_of(block * QUERY_ROWS, QUERY_ROWS), QUERY_ROWS)
        queries = qkv[here, query_at] * SCALE
        grads = grad_all[here, at : at + HEAD]
        blended = blended_all[here, at : at + HEAD]
        row_terms = jnp.sum(
            (grads.astype(jnp.float32) * blended.astype(jnp.float32)).T, axis=0, keepdims=True
        )
        scores = lax.dot_general(
            keys, queries, (((1,), (1,)), ((), ())), preferred_element_type=jnp.float32
        )
        chances = jnp.exp(scores - log[head, block])
        grad_chances = lax.dot_general(
            values, grads, (((1,), (1,)), ((), ())), preferred_element_type=jnp.float32
        )
        grad_scores = (chances * (grad_chances - row_terms)).astype(jnp.bfloat16)
        value_sum[...] += jnp.dot(
            chances.astype(jnp.bfloat16), grads, preferred_element_type=jnp.float32
        )
        key_sum[...] += jnp.dot(grad_scores, queries, preferred_element_type=jnp.float32)
        grad_queries = jnp.dot(keys_t, grad_scores, preferred_element_type=jnp.float32)
        out[here, query_at] = (grad_queries.T * SCALE).astype(jnp.bfloat16)

    out[:, key_at] = key_sum[...].astype(jnp.bfloat16)
    out[:, value_at] = value_sum[...].astype(jnp.bfloat16)


def attention_back_body(qkv_ref, blended_ref, grad_ref, log_ref, out_ref, key_sum, value_sum):
    for head in range(OWN // HEAD):
        attention_back_unit(
            qkv_ref.at[0],
            blended_ref.at[0],
            grad_ref.at[0],
            log_ref.at[0],
            out_ref.at[0],
            key_sum,
            value_sum,
            head,
        )


def attention_back(qkv, blended, grads, logs):
    micros, rows, _ = qkv.shape
    heads = OWN // HEAD
    blocks = rows // 256
    wide = pl.BlockSpec((1, rows, 3 * OWN), lambda m: (m, 0, 0))
    narrow = pl.BlockSpec((1, rows, OWN), lambda m: (m, 0, 0))
    return pl.pallas_call(
        attention_back_body,
        grid=(micros,),
        out_shape=jax.ShapeDtypeStruct((micros, rows, 3 * OWN), jnp.bfloat16),
        in_specs=[
            wide,
            narrow,
            narrow,
            pl.BlockSpec((1, heads, blocks, 1, 256), lambda m: (m, 0, 0, 0, 0)),
        ],
        out_specs=wide,
        scratch_shapes=[pltpu.VMEM((rows, HEAD), jnp.float32)] * 2,
        compiler_params=pltpu.CompilerParams(vmem_limit_bytes=48 * MIB),
        name="attention_back",
    )(qkv, blended, grads, logs)


def heads_to_tokens_body(blended, out, send_sem, recv_sem, local_sem):
    links = Links(1, send_sem, recv_sem, local_sem)
    x, c = links.x, links.c
    corner = links.beside + 1 - 2 * c
    links.greet([links.core, links.beside, corner])
    target = out.at[:, :, pl.ds(pl.multiple_of((2 * x + c) * OWN, OWN), OWN)]
    own = links.local(blended.at[:, x, c], target)
    copies = [
        links.send(blended.at[:, 1 - x, 1 - c], target, corner),
        links.send(blended.at[:, 1 - x, c], target, links.beside),
        links.send(blended.at[:, x, 1 - c], target, links.core),
    ]
    arrived(copies)
    own.wait()
    links.finish_sends()


def heads_to_tokens(blended):
    micros, rows, _ = blended.shape
    own_rows = rows // GROUP
    return remote_call(
        heads_to_tokens_body,
        "heads_to_tokens",
        2,
        jax.ShapeDtypeStruct((micros, own_rows, D), blended.dtype),
        [ANY],
        ANY,
        [],
        3,
        1,
        40 * MIB,
    )(blended.reshape(micros, 2, 2, own_rows, OWN))


def tokens_to_heads_body(grads, out, send_sem, recv_sem, local_sem):
    links = Links(1, send_sem, recv_sem, local_sem)
    x, c = links.x, links.c
    corner = links.beside + 1 - 2 * c
    links.greet([links.core, links.beside, corner])

    def columns(to_x, to_c):
        return grads.at[:, :, pl.ds(pl.multiple_of((2 * to_x + to_c) * OWN, OWN), OWN)]

    target = out.at[:, x, c]
    own = links.local(columns(x, c), target)
    copies = [
        links.send(columns(1 - x, 1 - c), target, corner),
        links.send(columns(1 - x, c), target, links.beside),
        links.send(columns(x, 1 - c), target, links.core),
    ]
    arrived(copies)
    own.wait()
    links.finish_sends()


def tokens_to_heads(grads):
    micros, own_rows, _ = grads.shape
    return remote_call(
        tokens_to_heads_body,
        "tokens_to_heads",
        3,
        jax.ShapeDtypeStruct((micros, 2, 2, own_rows, OWN), grads.dtype),
        [ANY],
        ANY,
        [],
        3,
        1,
        40 * MIB,
    )(grads).reshape(micros, GROUP * own_rows, OWN)


def token_sums_body(partial, out, send_sem, recv_sem, local_sem, from_core, own, from_beside):
    links = Links(1, send_sem, recv_sem, local_sem)
    x, c = links.x, links.c
    links.greet([links.core, links.beside])
    far = links.send(partial.at[:, 1 - x, 1 - c], from_core.at[0], links.core)
    near = links.send(partial.at[:, x, 1 - c], from_core.at[1], links.core)
    loads = [
        links.local(partial.at[:, 1 - x, c], own.at[0]),
        links.local(partial.at[:, x, c], own.at[1]),
    ]
    micros = out.shape[0]
    loads[0].wait()
    arrived([far])
    passed = []
    for m in range(micros):
        own[0, m] = (
            own[0, m].astype(jnp.float32) + from_core[0, m].astype(jnp.float32)
        ).astype(jnp.bfloat16)
        passed.append(links.send(own.at[0, m], from_beside.at[m], links.beside))
    loads[1].wait()
    arrived([near])
    for m in range(micros):
        out[m] = own[1, m].astype(jnp.float32) + from_core[1, m].astype(jnp.float32)
    for m in range(micros):
        arrived([passed[m]])
        out[m] += from_beside[m].astype(jnp.float32)
    links.finish_sends()


def token_sums(partial):
    micros, rows, width = partial.shape
    own_rows = rows // GROUP
    held = pltpu.VMEM((2, micros, own_rows, width), partial.dtype)
    return remote_call(
        token_sums_body,
        "token_sums",
        4,
        jax.ShapeDtypeStruct((micros, own_rows, width), jnp.float32),
        [ANY],
        VMEM,
        [held, held, pltpu.VMEM((micros, own_rows, width), partial.dtype)],
        4,
        2,
        40 * MIB,
    )(partial.reshape(micros, 2, 2, own_rows, width))


def small_sums_body(planes, partial, out, send_sem, recv_sem, local_sem, from_core, from_beside):
    links = Links(planes, send_sem, recv_sem)
    links.greet(links.partners())
    z, y, x, c = links.z, links.y, links.x, links.c
    arrived([links.send(partial.at[:, 1 - c], from_core, links.core)])
    from_core[...] = from_core[...] + partial[:, c]
    arrived([links.send(from_core.at[1 - x], from_beside, links.beside)])
    out[z, y, x, c] = from_core[x] + from_beside[...]
    spread_all(links, out)
    links.finish_sends()


def small_sums(partial, planes):
    block = partial.shape[2:]
    return remote_call(
        functools.partial(small_sums_body, planes),
        "small_sums",
        5,
        jax.ShapeDtypeStruct((planes, 2, 2, 2, *block), jnp.float32),
        [VMEM],
        VMEM,
        [pltpu.VMEM((2, *block), jnp.float32), pltpu.VMEM(block, jnp.float32)],
        2 * planes + 6,
        0,
        40 * MIB,
    )(partial)


def add_blocks(target, left, right, count):
    @pl.loop(0, count)
    def _(i):
        target(i)[...] = (
            left(i)[...].astype(jnp.float32) + right(i)[...].astype(jnp.float32)
        ).astype(jnp.bfloat16)


class Sums:
    def __init__(self, links, grads, outs, plan, scratch):
        self.links = links
        self.pieces, self.rows = [], []
        used = 0
        for grad, out, pieces in zip(grads, outs, plan):
            own = scratch[used]
            used += 1
            for first, count, start in pieces:
                rows = rows_of(grad.shape, first, count)
                self.pieces.append((grad, out, rows, start, own, *scratch[used : used + 7]))
                self.rows.append((first - pieces[0][0], count, grad.shape[-1] // LANES))
                used += 7
        self.state = [dict() for _ in self.pieces]

    def put(self, k, start, values):
        first, count, stride = self.rows[k]
        out = self.pieces[k][1]
        for j in range(values.shape[1] // LANES):
            where = first * stride + start // LANES + j
            out[pl.ds(where, count, stride=stride), :] = values[:, j * LANES : (j + 1) * LANES]

    def core(self, k):
        links = self.links
        grad, _, rows, start, _, first, *_ = self.pieces[k]
        source = grad.at[:, :, :, 1 - links.c, rows, pl.ds(start, WIDTH)]
        self.state[k]["core"] = links.send(source, first, links.core)

    def load(self, k):
        links = self.links
        grad, _, rows, start, own, *_ = self.pieces[k]
        source = grad.at[:, :, :, links.c, rows, pl.ds(start, WIDTH)]
        self.state[k]["own"] = links.local(source, own)

    def S1(self, k):
        links = self.links
        x, y, planes = links.x, links.y, links.planes
        _, _, _, _, own, first, over_y, _, _, over_x, _, _ = self.pieces[k]
        state = self.state[k]
        state["own"].wait()
        arrived([state["core"]])
        lead, rest = pl.ds(0, HALF), pl.ds(HALF, HALF)

        def add(columns, place):
            def block(ref):
                return lambda i: ref.at[(*place(i // 2, i % 2), ALL, columns)]

            add_blocks(block(first), block(own), block(first), planes * 2)

        add(lead, lambda z, other: (z, 1 - y, other))
        state["T"] = [links.send(first.at[:, 1 - y, :, :, lead], over_y, links.across)]
        add(rest, lambda z, other: (z, other, 1 - x))
        state["F"] = [links.send(first.at[:, :, 1 - x, :, rest], over_x, links.beside)]
        add(lead, lambda z, other: (z, y, other))
        add(rest, lambda z, other: (z, other, x))

    def T2(self, k):
        links = self.links
        _, _, _, _, _, first, over_y, over_planes, _, _, _, _ = self.pieces[k]
        arrived(self.state[k]["T"])

        def kept(i):
            return first.at[i // 2, links.y, i % 2, :, pl.ds(0, HALF)]

        def came(i):
            return over_y.at[i // 2, i % 2]

        add_blocks(came, kept, came, links.planes * 2)
        self.state[k]["T"] = [
            links.send(over_y.at[links.plane(s)], over_planes.at[s - 1], links.plane_device(s))
            for s in range(1, links.planes)
        ]

    def T3(self, k):
        links = self.links
        _, _, _, _, _, _, over_y, over_planes, last, _, _, _ = self.pieces[k]
        arrived(self.state[k]["T"])
        for i in (1 - links.x, links.x):
            result = over_y[links.z, i].astype(jnp.float32)
            for s in range(1, links.planes):
                result = result + over_planes[s - 1, i].astype(jnp.float32)
            over_y[links.z, i] = result.astype(jnp.bfloat16)
        source = over_y.at[links.z, 1 - links.x]
        self.state[k]["T"] = [links.send(source, last, links.beside)]

    def T4(self, k):
        links = self.links
        _, _, _, start, _, _, over_y, _, last, _, _, _ = self.pieces[k]
        arrived(self.state[k]["T"])
        kept = over_y[links.z, links.x].astype(jnp.float32)
        self.put(k, start, kept + last[...].astype(jnp.float32))

    def F2(self, k):
        links = self.links
        x, y = links.x, links.y
        _, _, _, _, _, first, _, _, _, over_x, third, _ = self.pieces[k]
        arrived(self.state[k]["F"])
        for here in (1 - y, y):

            def kept(i, here=here):
                return first.at[i, here, x, :, pl.ds(HALF, HALF)]

            def came(i, here=here):
                return over_x.at[i, here]

            add_blocks(came, kept, came, links.planes)
            if here is not y:
                self.state[k]["F"] = [links.send(over_x.at[:, here], third, links.across)]

    def F3(self, k):
        links = self.links
        _, _, _, _, _, _, _, _, _, over_x, third, fourth = self.pieces[k]
        arrived(self.state[k]["F"])

        def kept(i):
            return over_x.at[i, links.y]

        def came(i):
            return third.at[i]

        add_blocks(came, kept, came, links.planes)
        self.state[k]["F"] = [
            links.send(third.at[links.plane(s)], fourth.at[s - 1], links.plane_device(s))
            for s in range(1, links.planes)
        ]

    def F4(self, k):
        links = self.links
        _, _, _, start, *_, third, fourth = self.pieces[k]
        arrived(self.state[k]["F"])
        result = third[links.z].astype(jnp.float32)
        for s in range(1, links.planes):
            result = result + fourth[s - 1].astype(jnp.float32)
        self.put(k, start + HALF, result)


def sums_order(count):
    order = []
    stages = (("core", 0), ("S1", 1), ("load", 0), ("T2", 2), ("F2", 2), ("T3", 3), ("F3", 3), ("T4", 4), ("F4", 4))
    for k in range(count + 4):
        for task, behind in stages:
            if 0 <= k - behind < count:
                order.append((task, k - behind))
    return order


MIDDLE_ORDER = (
    544, 576, 449, 545, 577, 450, 546, 384, 224, 547, 578, 385, 480, 481, 225, 352, 608, 226, 386,
    640, 353, 416, 417, 354, 418, 672, 641, 673, 674, 642,
)
BACK_ORDER = (
    704, 576, 449, 705, 577, 450, 706, 384, 224, 578, 451, 707, 385, 225, 579, 452, 352, 580, 453,
    416, 581, 226, 736, 386, 708, 768, 353, 640, 709, 387, 800, 672, 641, 710, 388, 711, 389, 801,
    832, 417, 418, 419, 354, 227, 420, 833, 228, 864, 229, 673, 421, 834, 896, 674, 675, 676, 677,
    642, 737, 929, 769, 897, 930, 960, 992, 355, 356, 865, 993, 1024, 1057, 357, 643, 1025, 1058,
    644, 1059, 645,
)


class AttendSums:
    def __init__(self, links, grads, out, scratch):
        self.links, self.grads, self.out = links, grads, out
        self.own, self.over_y, self.over_planes, self.sum, self.held = scratch
        self.state = [dict() for _ in range(PAIRS)]
        self.columns = [pl.ds(pair * PAIR, PAIR) for pair in range(PAIRS)]

    def a0(self, k):
        links, columns = self.links, self.columns[k]
        source = self.grads.at[:, 1 - links.y, :, :, :, columns]
        self.state[k]["y"] = links.send(source, self.over_y.at[..., columns], links.across)
        source = self.grads.at[:, links.y, :, :, :, columns]
        self.state[k]["own"] = links.local(source, self.own.at[..., columns])

    def a1(self, k):
        links, own, over_y, columns = self.links, self.own, self.over_y, self.columns[k]
        self.state[k]["own"].wait()
        arrived([self.state[k]["y"]])
        for i in range(2):

            def block(ref, i=i):
                return lambda j: ref.at[j // 2, i, j % 2, :, columns]

            add_blocks(block(own), block(own), block(over_y), links.planes * 2)
        self.state[k]["planes"] = [
            links.send(
                own.at[links.plane(s), :, :, :, columns],
                self.over_planes.at[s - 1, :, :, :, columns],
                links.plane_device(s),
            )
            for s in range(1, links.planes)
        ]

    def a2(self, k):
        links, columns = self.links, self.columns[k]
        x, c = links.x, links.c
        arrived(self.state[k]["planes"])
        for i in range(2):
            for j in range(2):
                result = self.own[links.z, i, j, :, columns].astype(jnp.float32)
                for s in range(1, links.planes):
                    result = result + self.over_planes[s - 1, i, j, :, columns].astype(jnp.float32)
                self.sum[i, j, :, columns] = result
        self.state[k]["beside"] = links.send(
            self.sum.at[1 - x, :, :, columns], self.held.at[:, :, columns], links.beside
        )
        self.state[k]["near"] = links.send(
            self.sum.at[x, 1 - c, :, columns], self.out.at[x, c, :, columns], links.core
        )
        self.out[x, c, :, columns] = self.sum[x, c, :, columns]

    def a3(self, k):
        links, columns = self.links, self.columns[k]
        x, c = links.x, links.c
        arrived([self.state[k]["beside"]])
        self.out[1 - x, c, :, columns] = self.held[c, :, columns]
        self.state[k]["far"] = links.send(
            self.held.at[1 - c, :, columns], self.out.at[1 - x, c, :, columns], links.core
        )

    def finish(self):
        for state in self.state:
            arrived([state["near"], state["far"]])


class Spread:
    def __init__(self, links, ref):
        self.links, self.ref = links, ref

    def step(self, k):
        links, ref = self.links, self.ref
        z, y, x, c = links.z, links.y, links.x, links.c
        if k > 0:
            arrived(self.sent)
        if k == 0:
            block = ref.at[z, y, x, c]
            devices = [device for _, _, device in links.column()]
        elif k == 1:
            block, devices = ref.at[:, :, x, c], [links.beside, links.core]
        elif k == 2:
            block, devices = ref.at[:, :, 1 - x, c], [links.core]
        else:
            return
        self.sent = [links.send(block, block, device) for device in devices]


class TokenSums:
    def __init__(self, links, partial, scratch):
        self.links, self.partial = links, partial
        self.from_core, self.from_beside = scratch
        self.state = {}

    def start(self, m):
        links, partial = self.links, self.partial
        x, c = links.x, links.c
        self.state[m] = [
            links.send(partial.at[m, 1 - x, 1 - c], self.from_core.at[0, m], links.core),
            links.send(partial.at[m, x, 1 - c], self.from_core.at[1, m], links.core),
        ]

    def middle(self, m):
        links, partial = self.links, self.partial
        x, c = links.x, links.c
        arrived(self.state[m])
        away = partial.at[m, 1 - x, c]
        away[...] = (
            away[...].astype(jnp.float32) + self.from_core[0, m].astype(jnp.float32)
        ).astype(jnp.bfloat16)
        self.state[m] = [links.send(away, self.from_beside.at[m], links.beside)]

    def finish(self, m):
        links = self.links
        arrived(self.state[m])
        return (
            self.partial[m, links.x, links.c].astype(jnp.float32)
            + self.from_core[1, m].astype(jnp.float32)
            + self.from_beside[m].astype(jnp.float32)
        )


def sums_body(planes, kinds, *refs):
    attend, grads, refs = refs[0], refs[1 : 1 + kinds], refs[1 + kinds :]
    attend_out, outs, refs = refs[0], refs[1 : 1 + kinds], refs[1 + kinds :]
    links = Links(planes, *refs[:3])
    links.greet(links.partners())
    attend_sums = AttendSums(links, attend, attend_out, refs[3:8])
    for pair in range(PAIRS):
        for task in (attend_sums.a0, attend_sums.a1, attend_sums.a2, attend_sums.a3):
            task(pair)
    plan = [cuts(grad.shape[-2:]) for grad in grads]
    sums = Sums(links, grads, outs, plan, refs[8:])
    for task, k in sums_order(len(sums.pieces)):
        getattr(sums, task)(k)
    attend_sums.finish()
    links.finish_sends()


def middle_body(planes, *refs):
    grad_contract, expand, contract, project, act, slope, second, grad_branch, refs = *refs[:8], refs[8:]
    middle, attended, upstream, blended, modulation, bias_rows, refs = *refs[:6], refs[6:]
    contract_out, output, middle_grad_out, rows_out, bias_out, hidden_out, refs = *refs[:6], refs[6:]
    grad_expand, grad_project, grad_heads, refs = *refs[:3], refs[3:]
    links = Links(planes, *refs[:3])
    refs = refs[3:]
    plan = [cuts(grad_contract.shape[-2:])[:MIDDLE_PIECES]]
    used = scratch_count(plan)
    sum_scratch, refs = refs[:used], refs[used:]
    contract_held, expand_held, act_held, slope_held, second_held, second_t, refs = *refs[:6], refs[6:]
    branch_grad, grads, branch, grad_second, middle_held, attended_held, refs = *refs[:6], refs[6:]
    upstream_held, project_held, blended_held, attended_grad, project_grads, refs = *refs[:5], refs[5:]
    middle_grad, grad_blended = refs
    x, c = links.x, links.c
    corner = links.beside + 1 - 2 * c
    micros, own_rows, _ = second.shape
    parts = FF // WIDTH
    part_width = FF // parts
    contract_blocks = contract.shape[0] // parts

    def load(part):
        columns = pl.ds(part * part_width, part_width)
        slot = part % 2
        return [
            links.local(
                contract.at[pl.ds(part * contract_blocks, contract_blocks)], contract_held.at[slot]
            ),
            links.local(expand.at[:, :, :, :, :, columns], expand_held.at[slot]),
            links.local(act.at[:, :, columns], act_held.at[slot]),
            links.local(slope.at[:, :, columns], slope_held.at[slot]),
        ]

    loaded = links.local(second, second_held), links.local(grad_branch, branch_grad)
    loading = {0: load(0), 1: load(1)}
    links.greet([*links.partners(), corner])
    sums = Sums(links, (grad_contract,), (contract_out,), plan, sum_scratch)
    for k in range(len(sums.pieces)):
        sums.core(k)
    sums.load(0)
    later = [
        links.local(middle, middle_held),
        links.local(attended, attended_held),
        links.local(upstream, upstream_held),
        links.local(project, project_held),
        links.local(blended, blended_held),
    ]
    for copy in loaded:
        copy.wait()
    for m in range(micros):
        second_t[:, m * own_rows : (m + 1) * own_rows] = second_held[m].T
    branch[...] = jnp.zeros_like(branch)
    grad_second[...] = jnp.zeros_like(grad_second)
    stored = []

    def mlp_unit(part):
        for copy in loading.pop(part):
            copy.wait()
        slot = part % 2
        if part >= 2:
            stored[part - 2].wait()
        contract_part(
            part * part_width,
            contract_held.at[slot],
            expand_held.at[slot],
            act_held.at[slot],
            slope_held.at[slot],
            second_t,
            branch_grad,
            grads.at[slot],
            branch,
            grad_second,
            hidden_out,
        )
        if part + 2 < parts:
            loading[part + 2] = load(part + 2)
        columns = pl.ds(part * part_width, part_width)
        stored.append(links.local(grads.at[slot], grad_expand.at[:, :, :, :, :, columns]))

    totals = [jnp.zeros((1, D), jnp.float32)] * 2

    def own_tokens(m):
        def vector(block):
            shift = bias_vector(bias_rows, 4 * D + FF + block * D, D)
            return modulation_row(modulation, m, block) + shift

        ahead = upstream_held[m].astype(jnp.float32)
        outward = branch[m] + bias_vector(bias_rows, 3 * D + FF, D)
        output[m] = (middle_held[m] + vector(5) * outward).astype(jnp.bfloat16)
        rows_out[m, 5:6, :] = jnp.sum(ahead * outward, axis=0, keepdims=True)
        normed, scale = normalize(middle_held[m])
        values = grad_second[m]
        rows_out[m, 3:4, :] = jnp.sum(values, axis=0, keepdims=True)
        rows_out[m, 4:5, :] = jnp.sum(values * normed, axis=0, keepdims=True)
        back = ahead + norm_back(values, normed, scale, vector(4))
        middle_grad[m] = back
        rows_out[m, 2:3, :] = jnp.sum(back * attended_held[m], axis=0, keepdims=True)
        lowered = (vector(2) * back).astype(jnp.bfloat16)
        attended_grad[m] = lowered
        totals[0] += jnp.sum(lowered.astype(jnp.float32), axis=0, keepdims=True)
        totals[1] += jnp.sum(branch_grad[m].astype(jnp.float32), axis=0, keepdims=True)
        product = lax.dot_general(
            lowered,
            project_held[...].reshape(D, D),
            (((1,), (1,)), ((), ())),
            preferred_element_type=jnp.float32,
        )
        grad_blended[m] = product.astype(jnp.bfloat16)
        here = pl.ds(pl.multiple_of((2 * x + c) * own_rows, own_rows), own_rows)

        def columns_of(to_x, to_c):
            start = pl.multiple_of((2 * to_x + to_c) * OWN, OWN)
            return grad_blended.at[m, :, pl.ds(start, OWN)]

        target = grad_heads.at[m, here]
        exchanged.append(links.send(columns_of(1 - x, 1 - c), target, corner))
        exchanged.append(links.send(columns_of(1 - x, c), target, links.beside))
        exchanged.append(links.send(columns_of(x, 1 - c), target, links.core))
        stored.append(links.local(columns_of(x, c), target))

    exchanged = []

    def project_unit():
        total = None
        for m in range(micros):
            product = lax.dot_general(
                blended_held[m],
                attended_grad[m],
                (((0,), (0,)), ((), ())),
                preferred_element_type=jnp.float32,
            )
            total = product if total is None else total + product
        project_grads[...] = total.astype(jnp.bfloat16).reshape(project_grads.shape)
        stored.append(links.local(project_grads, grad_project))
        stored.append(links.local(middle_grad, middle_grad_out))

    for task, k in tasks_of(MIDDLE_ORDER):
        if task == "mlp":
            mlp_unit(k)
        elif task == "own":
            if k == 0:
                for copy in later:
                    copy.wait()
            own_tokens(k)
        elif task == "project":
            project_unit()
        else:
            getattr(sums, task)(k)
    bias_out[0:1, :] = totals[0]
    bias_out[1:2, :] = totals[1]
    arrived(exchanged)
    for copy in stored[parts - 2 :]:
        copy.wait()
    links.finish_sends()


def contract_part(
    start,
    contract,
    expand,
    act,
    slope,
    second_t,
    grad_branch,
    grads,
    branch,
    grad_second,
    hidden_sums,
):
    micros = grad_branch.shape[0]
    blocks = CHUNK // contract.shape[1]

    @pl.loop(0, act.shape[-1] // CHUNK)
    def _(chunk):
        inside = pl.ds(pl.multiple_of(chunk * CHUNK, CHUNK), CHUNK)
        columns = pl.ds(pl.multiple_of(start + chunk * CHUNK, CHUNK), CHUNK)
        outward = contract[pl.ds(chunk * blocks, blocks)].reshape(CHUNK, D)
        inward = expand[:, :, :, :, :, inside].reshape(D, CHUNK)
        lows = []
        for m in range(micros):
            branch[m] += jnp.dot(act[m, :, inside], outward, preferred_element_type=jnp.float32)
            grad_act = lax.dot_general(
                grad_branch[m], outward, (((1,), (1,)), ((), ())), preferred_element_type=jnp.float32
            )
            lows.append((grad_act * slope[m, :, inside].astype(jnp.float32)).astype(jnp.bfloat16))
            grad_second[m] += lax.dot_general(
                lows[m], inward, (((1,), (1,)), ((), ())), preferred_element_type=jnp.float32
            )
        grad_hidden = jnp.concatenate(lows, axis=0)
        product = jnp.dot(second_t[...], grad_hidden, preferred_element_type=jnp.float32)
        grads[:, :, :, :, :, inside] = product.astype(jnp.bfloat16).reshape(
            *grads.shape[:-1], CHUNK
        )
        hidden_sums[:, columns] = jnp.sum(
            grad_hidden.astype(jnp.float32), axis=0, keepdims=True
        )


def back_body(planes, *refs):
    grad_contract, grad_expand, grad_project, grad_heads, refs = *refs[:4], refs[4:]
    qkv, heads, logs, normed, attend, refs = *refs[:5], refs[5:]
    tokens, middle_grad, modulation, bias_rows, row_sums, bias_sums, hidden_sums, refs = *refs[:7], refs[7:]
    cond, modulate, refs = *refs[:2], refs[2:]
    attend_flat, contract_out, expand_out, project_out, tokens_out, refs = *refs[:5], refs[5:]
    sums_out, modulate_out, cond_out, refs = *refs[:3], refs[3:]
    links = Links(planes, *refs[:3])
    attend_held_scratch, refs = refs[3:8], refs[8:]
    all_grads = (grad_contract, grad_expand, grad_project)
    plan = back_plan(all_grads)
    used = scratch_count(plan)
    sum_scratch, refs = refs[:used], refs[used:]
    grads_held, qkv_held, heads_held, normed_held, attend_held, grad_qkv, refs = *refs[:6], refs[6:]
    key_sum, value_sum, attend_grads, partial, from_core, from_beside, refs = *refs[:6], refs[6:]
    tokens_held, middle_held, scales, head_sums, row_held, small, refs = *refs[:6], refs[6:]
    small_core, small_beside, modulations, attend_out = refs
    micros, latent_rows, _ = qkv.shape
    loads = {
        "heads": [
            links.local(qkv, qkv_held),
            links.local(grad_heads, grads_held),
            links.local(heads, heads_held),
        ],
        "attend": [links.local(attend, attend_held)],
        "normed": [links.local(normed, normed_held)],
        "tokens": [links.local(tokens, tokens_held), links.local(middle_grad, middle_held)],
    }

    def need(*names):
        for name in names:
            for copy in loads.pop(name, ()):
                copy.wait()

    links.greet(links.partners())
    z, y, x, c = links.z, links.y, links.x, links.c
    outs = (contract_out, expand_out, project_out)
    sums = Sums(links, all_grads, outs, plan, sum_scratch)
    for k in range(len(sums.pieces)):
        sums.core(k)
    sums.load(0)
    attend_sums = AttendSums(links, attend_grads, attend_out, attend_held_scratch)
    token_sum = TokenSums(links, partial, (from_core, from_beside))
    spread_sums, spread_cond = Spread(links, sums_out), Spread(links, cond_out)
    sent = {}

    def vector(m, block):
        shift = bias_vector(bias_rows, 4 * D + FF + block * D, D)
        return modulation_row(modulation, m, block) + shift

    scale_rows = []
    for m in range(micros):
        scale_rows += [1.0 + vector(m, 1), vector(m, 0)]
    scale_rows.append(jnp.zeros((8 - 2 * micros, D), jnp.float32))
    scales[...] = jnp.concatenate(scale_rows, axis=0).T

    def head_unit(m, head):
        need("heads")
        attention_back_unit(
            qkv_held.at[m],
            heads_held.at[m],
            grads_held.at[m],
            logs.at[m],
            grad_qkv.at[m],
            key_sum,
            value_sum,
            head,
        )

    def tokens_unit(m):
        grads = token_sum.finish(m)
        need("tokens")
        normed_own, scale = normalize(tokens_held[m].astype(jnp.float32))
        tokens_out[m] = middle_held[m] + norm_back(grads, normed_own, scale, vector(m, 1))

    def small_start():
        highs = head_sums[...].astype(jnp.bfloat16)
        lows = (head_sums[...] - highs.astype(jnp.float32)).astype(jnp.bfloat16)
        product = lax.dot_general(
            jnp.concatenate([highs, lows], axis=0),
            attend_held[...].reshape(D, 3 * OWN),
            (((1,), (1,)), ((), ())),
            preferred_element_type=jnp.float32,
        )
        each = D // LANES
        per_quarter = 6 * each // GROUP
        for m in range(micros):
            blocks = [product[m : m + 1] + product[8 + m : 9 + m], row_held[m : m + 1, :]]
            blocks += [row_sums[m, block : block + 1, :] for block in range(2, 6)]
            for k in range(6 * each):
                quarter, row = k // per_quarter, m * per_quarter + k % per_quarter
                lanes = slice(k % each * LANES, (k % each + 1) * LANES)
                small[quarter // 2, quarter % 2, row : row + 1, :] = blocks[k // each][:, lanes]
        start = micros * per_quarter
        biases = {2: bias_sums[0:1, :], 7: bias_sums[1:2, :]}
        for k in range(FF // D):
            biases[3 + k] = hidden_sums[:, k * D : (k + 1) * D]
        each_quarter = 8 * each // GROUP
        small[0, 0, start:, :] = jnp.zeros((small.shape[2] - start, LANES), jnp.float32)
        for k in range(2 * each, 8 * each):
            quarter, row = k // each_quarter, start + k % each_quarter
            lanes = slice(k % each * LANES, (k % each + 1) * LANES)
            small[quarter // 2, quarter % 2, row : row + 1, :] = biases[k // each][:, lanes]
        for m in range(1, micros):
            head_sums[0:1, :] += head_sums[m : m + 1, :]
        for pair in range(PAIRS):
            for kind, first_row in ((0, start), (2, start + each)):
                lanes = pl.ds(pair * PAIR + kind * LANES, LANES)
                row = first_row + (2 * x + c) * PAIRS + pair
                small[0, 0, pl.ds(row, 1), :] = head_sums[0:1, lanes]
        sent["small"] = links.send(small.at[:, 1 - c], small_core, links.core)

    def small_core_sum():
        arrived([sent["small"]])
        small_core[...] = small_core[...] + small[:, c]
        sent["small"] = links.send(small_core.at[1 - x], small_beside, links.beside)

    def small_beside_sum():
        arrived([sent["small"]])
        sums_out[z, y, x, c] = small_core[x] + small_beside[...]
        spread_sums.step(0)

    def modulate_unit():
        spread_sums.step(3)
        latents = planes * 2
        per_quarter = 6 * D // LANES // GROUP
        for m in range(micros):
            for k in range(6 * D // LANES):
                quarter, row = k // per_quarter, m * per_quarter + k % per_quarter
                values = sums_out[:, :, quarter // 2, quarter % 2, row, :].reshape(latents, LANES)
                here = slice(m * latents, (m + 1) * latents)
                modulations[here, k * LANES : (k + 1) * LANES] = values
        grads = lax.dot_general(
            cond[...],
            modulations[...],
            (((0,), (0,)), ((), ())),
            precision=highest,
            preferred_element_type=jnp.float32,
        )
        stride = 6 * D // LANES
        for k in range(stride):
            lanes = slice(k * LANES, (k + 1) * LANES)
            modulate_out[pl.ds(k, grads.shape[0], stride=stride), :] = grads[:, lanes]
        product = lax.dot_general(
            modulations[...],
            modulate[...].astype(jnp.float32),
            (((1,), (1,)), ((), ())),
            precision=highest,
            preferred_element_type=jnp.float32,
        )
        cond_out[z, y, x, c] = jnp.zeros(cond_out.shape[4:], jnp.float32)
        cond_out[z, y, x, c, :, : product.shape[1]] = product
        spread_cond.step(0)

    heads_each = OWN // HEAD
    for task, k in tasks_of(BACK_ORDER):
        if task == "head":
            head_unit(k // heads_each, k % heads_each)
        elif task == "first":
            need("attend")
            first_product(k, grad_qkv, attend_held, partial)
            token_sum.start(k)
        elif task == "attend":
            need("attend", "normed")
            attend_product(
                k, normed_held, grad_qkv, attend_held, scales, head_sums, row_held, attend_grads
            )
            attend_sums.a0(k)
        elif task == "t1":
            token_sum.middle(k)
        elif task == "t2":
            tokens_unit(k)
        elif task in ("a1", "a2", "a3"):
            getattr(attend_sums, task)(k)
        elif task == "small":
            (small_start, small_core_sum, small_beside_sum)[k]()
        elif task == "sums":
            spread_sums.step(k)
        elif task == "modulate":
            modulate_unit()
        elif task == "cond":
            spread_cond.step(k)
        else:
            getattr(sums, task)(k)
    attend_sums.finish()
    count, stride = attend_out.shape[2], 3 * D // LANES
    for quarter in range(GROUP):
        for kind in range(3):
            for pair in range(PAIRS):
                lanes = pl.ds((pair * 3 + kind) * LANES, LANES)
                where = (kind * GROUP + quarter) * PAIRS + pair
                attend_flat[pl.ds(where, count, stride=stride), :] = attend_out[
                    quarter // 2, quarter % 2, :, lanes
                ]
    links.finish_sends()


def back_plan(grads):
    plan = [cuts(grad.shape[-2:]) for grad in grads]
    plan[0] = plan[0][MIDDLE_PIECES:]
    return plan


def attend_product(pair, normed, grad_qkv, attend, scales, head_sums, row_held, out):
    planes = attend.shape[0]
    width = D // planes
    micros = normed.shape[0]
    columns = pl.ds(pair * PAIR, PAIR)
    totals = [
        jnp.sum(grad_qkv[m, :, columns].astype(jnp.float32), axis=0, keepdims=True)
        for m in range(micros)
    ]
    head_sums[:, columns] = jnp.concatenate(
        [*totals, jnp.zeros((8 - micros, PAIR), jnp.float32)], axis=0
    )

    @pl.loop(0, planes)
    def _(plane):
        here = pl.ds(pl.multiple_of(plane * width, width), width)
        weights = attend[plane, :, :, :, :, columns].reshape(width, PAIR).astype(jnp.float32)
        total = jnp.zeros((width, PAIR), jnp.float32)
        for m in range(micros):
            product = lax.dot_general(
                normed[m, :, here],
                grad_qkv[m, :, columns],
                (((0,), (0,)), ((), ())),
                preferred_element_type=jnp.float32,
            )
            total = total + product * scales[here, 2 * m : 2 * m + 1]
            total = total + scales[here, 2 * m + 1 : 2 * m + 2] * totals[m]
            row = jnp.sum((weights * product).T, axis=0, keepdims=True)
            if pair == 0:
                row_held[m : m + 1, here] = row
            else:
                row_held[m : m + 1, here] += row
        out[plane, :, :, :, :, columns] = total.astype(jnp.bfloat16).reshape(
            *out.shape[1:-1], PAIR
        )


def first_product(m, grad_qkv, attend, partial):
    rows = partial.shape[3]

    @pl.loop(0, GROUP)
    def _(block):
        here = pl.ds(pl.multiple_of(block * rows, rows), rows)
        product = lax.dot_general(
            grad_qkv[m, here, :],
            attend[...].reshape(D, 3 * OWN),
            (((1,), (1,)), ((), ())),
            preferred_element_type=jnp.float32,
        )
        partial[m, block // 2, block % 2] = product.astype(jnp.bfloat16)


def attend_scratch(attend, planes):
    rows, width = attend.shape[-2:]
    return [
        pltpu.VMEM((planes, 2, 2, rows, width), jnp.bfloat16),
        pltpu.VMEM((planes, 2, 2, rows, width), jnp.bfloat16),
        pltpu.VMEM((planes - 1, 2, 2, rows, width), jnp.bfloat16),
        pltpu.VMEM((2, 2, rows, width), jnp.float32),
        pltpu.VMEM((2, rows, width), jnp.float32),
    ]


def sum_scratch(plan, planes):
    held = []
    for pieces in plan:
        rows = pieces[0][1]
        held.append(low_held(planes, 2, 2, rows, WIDTH))
        for _ in pieces:
            held += [
                low_held(planes, 2, 2, rows, WIDTH),
                low_held(planes, 2, rows, HALF),
                low_held(planes - 1, 2, rows, HALF),
                low_held(rows, HALF),
                low_held(planes, 2, rows, HALF),
                low_held(planes, rows, HALF),
                low_held(planes - 1, rows, HALF),
            ]
    return held


def count_pieces(plan):
    return sum(len(pieces) for pieces in plan)


def scratch_count(plan):
    return len(plan) + 7 * count_pieces(plan)


def flat_shape(count):
    return full_shape(count // LANES, LANES)


def full_shape(*shape):
    return jax.ShapeDtypeStruct(shape, jnp.float32)


def low_shape(*shape):
    return jax.ShapeDtypeStruct(shape, jnp.bfloat16)


def full_held(*shape):
    return pltpu.VMEM(shape, jnp.float32)


def low_held(*shape):
    return pltpu.VMEM(shape, jnp.bfloat16)


def sum_sems(plan, planes):
    return count_pieces(plan) * (4 + 2 * planes)


def weight_sums(attend, weights, planes):
    plan = [cuts(grad.shape[-2:]) for grad in weights]
    flats = [flat_shape(grad.shape[-2] * grad.shape[-1]) for grad in weights]
    return remote_call(
        functools.partial(sums_body, planes, len(weights)),
        "weight_sums",
        6,
        (full_shape(2, 2, *attend.shape[-2:]), *flats),
        [ANY] * (1 + len(weights)),
        (VMEM,) * (1 + len(weights)),
        [*attend_scratch(attend, planes), *sum_scratch(plan, planes)],
        8 + 2 * planes + sum_sems(plan, planes),
        4 + count_pieces(plan),
        60 * MIB,
    )(attend, *weights)


def middle_part(grad_contract, weights, held, vectors, planes):
    expand, contract, project = weights
    second = held[2]
    micros, own_rows, _ = second.shape
    own = second.shape
    shape = grad_contract.shape[-2:]
    plan = [cuts(shape)[:MIDDLE_PIECES]]
    width = WIDTH
    blocks = width // shape[0]
    return remote_call(
        functools.partial(middle_body, planes),
        "middle",
        6,
        (
            flat_shape(len(plan[0]) * plan[0][0][1] * D),
            low_shape(*own),
            full_shape(*own),
            full_shape(micros, 8, D),
            full_shape(8, D),
            full_shape(1, FF),
            low_shape(*expand.shape),
            low_shape(*project.shape),
            low_shape(micros, own_rows * GROUP, OWN),
        ),
        [ANY] * 12 + [VMEM] * 2,
        (VMEM, VMEM, ANY) + (VMEM,) * 3 + (ANY,) * 3,
        [
            *sum_scratch(plan, planes),
            low_held(2, blocks, *shape),
            low_held(2, *expand.shape[:-1], width),
            low_held(2, micros, own_rows, width),
            low_held(2, micros, own_rows, width),
            low_held(*own),
            low_held(D, micros * own_rows),
            low_held(*own),
            low_held(2, *expand.shape[:-1], width),
            full_held(*own),
            full_held(*own),
            full_held(*own),
            full_held(*own),
            low_held(*own),
            low_held(*project.shape),
            low_held(*own),
            low_held(*own),
            low_held(*project.shape),
            full_held(*own),
            low_held(*own),
        ],
        8 + sum_sems(plan, planes),
        48,
        63 * MIB,
    )(
        grad_contract,
        expand,
        contract.reshape(FF // shape[0], *shape),
        project,
        *held,
        *vectors,
    )


def back_part(grads, grad_heads, held, vectors, planes):
    qkv, heads, logs, normed, attend, tokens, middle_grad = held
    plan = back_plan(grads)
    micros, latent_rows, width = qkv.shape
    own = tokens.shape
    small = (micros * 6 + 8) * D // LANES // GROUP
    cond, modulate = vectors[-2:]
    return remote_call(
        functools.partial(back_body, planes),
        "back",
        7,
        (
            flat_shape(GROUP * attend.shape[-2] * attend.shape[-1]),
            *(
                flat_shape(len(pieces) * pieces[0][1] * WIDTH)
                for pieces in plan
            ),
            full_shape(*own),
            full_shape(planes, 2, 2, 2, small, LANES),
            flat_shape(modulate.shape[0] * modulate.shape[1]),
            full_shape(planes, 2, 2, 2, cond.shape[0], LANES),
        ),
        [ANY] * 6 + [VMEM] + [ANY] * 4 + [VMEM] * 7,
        (VMEM,) * 8,
        [
            *attend_scratch(attend, planes),
            *sum_scratch(plan, planes),
            low_held(*grad_heads.shape),
            low_held(*qkv.shape),
            low_held(*heads.shape),
            low_held(*normed.shape),
            low_held(*attend.shape),
            low_held(*qkv.shape),
            full_held(latent_rows, HEAD),
            full_held(latent_rows, HEAD),
            low_held(*attend.shape),
            low_held(micros, 2, 2, *own[1:]),
            low_held(2, *own),
            low_held(*own),
            low_held(*own),
            full_held(*own),
            full_held(D, 8),
            full_held(8, width),
            full_held(8, D),
            full_held(2, 2, small, LANES),
            full_held(2, small, LANES),
            full_held(small, LANES),
            full_held(cond.shape[0], modulate.shape[1]),
            full_held(2, 2, *attend.shape[-2:]),
        ],
        40 + 8 * planes + sum_sems(plan, planes),
        12 + count_pieces(plan),
        63 * MIB,
    )(*grads, grad_heads, *held, *vectors)


def normalize(values):
    center = values - jnp.mean(values, axis=-1, keepdims=True)
    spread_of = jnp.mean(center * center, axis=-1, keepdims=True)
    scale = lax.rsqrt(spread_of + epsilon)
    return center * scale, scale


def norm_back(grads, normed, scale, factors):
    inner = grads * (1.0 + factors)
    return scale * (
        inner
        - jnp.mean(inner, axis=-1, keepdims=True)
        - normed * jnp.mean(inner * normed, axis=-1, keepdims=True)
    )


def einsum(spec, left, right):
    return jnp.einsum(spec, left, right, preferred_element_type=jnp.float32)


def per_device(tokens, condition, attend, project, expand, contract, modulate, biases, cotangent):
    devices = lax.axis_size("fsdp")
    planes = devices // 8
    latents = devices // GROUP
    me = lax.axis_index("fsdp")
    quarter, latent = me % GROUP, me // GROUP
    micros, own_rows, _ = tokens.shape
    latent_rows = own_rows * GROUP
    rows = D // devices
    grid = (planes, 2, 2, 2)

    fused = rows % 16 == 0 and own_rows % QUERY_ROWS == 0 and biases.size == 7 * LANES // 2
    inputs = tokens.astype(jnp.float32)
    if fused:
        half = LANES // 2
        spread_cond = condition.astype(jnp.float32).reshape(micros, -1, rows).transpose(1, 0, 2)
        spread_cond = spread_cond.reshape(-1, rows)
        spread_cond = jnp.pad(spread_cond, ((0, 0), (0, LANES - rows)))
        own_biases = biases.astype(jnp.float32)
        own_biases = jnp.where(
            me % 2 == 0, jnp.pad(own_biases, (0, half)), jnp.pad(own_biases, (half, 0))
        )
        payload = jnp.concatenate([spread_cond, own_biases.reshape(-1, LANES)])
        payload = jnp.pad(payload, ((0, -payload.shape[0] % 8), (0, 0)))
        flats = [shard.reshape(-1, LANES) for shard in (attend, project, expand, contract)]
        attend_all, project_all, expand_all, contract_all, modulation_all, *rest = front(
            tokens, *flats, payload, modulate.reshape(-1, LANES), cotangent, planes
        )
        *rest, bias_rows, cond_own, modulate_rows = rest
        normed, projected, heads, logs, blended, middle, attended, second, act, slope, low, grads = rest
        grad_contract = grads.reshape(*grid, FF // devices, D)
        contract_first, output, grad_middle, row_sums, bias_sums, hidden_sums, *onward = middle_part(
            grad_contract,
            (expand_all, contract_all, project_all),
            (act, slope, second, low, middle, attended, cotangent, blended),
            (modulation_all, bias_rows),
            planes,
        )
        grad_expand, grad_project, grad_heads = onward
        attend_sum, contract_rest, expand_sum, project_sum, grad_tokens, *onward = back_part(
            (grad_contract, grad_expand, grad_project),
            grad_heads,
            (projected, heads, logs, normed, attend_all, tokens, grad_middle),
            (
                modulation_all,
                bias_rows,
                row_sums,
                bias_sums,
                hidden_sums,
                cond_own,
                modulate_rows,
            ),
            planes,
        )
        contract_sum = jnp.concatenate([contract_first, contract_rest])
        sums, grad_modulate, cond_cols = onward
        sums = sums.reshape(latents, GROUP, -1)
        split = micros * 6 * D // GROUP
        cond_cols = cond_cols[..., :rows].reshape(devices, micros, latents, rows)
    else:
        modulate_rows = modulate.reshape(rows, 6 * D)
        attend_shard = attend.reshape(rows, 3, 2, 2, PAIRS, LANES).transpose(2, 3, 0, 4, 1, 5)
        shards = (
            tokens,
            attend_shard.reshape(2, 2, rows, 3 * OWN),
            project.reshape(rows, D),
            expand.reshape(rows, FF),
            contract.reshape(FF // devices, D),
        )
        held = jnp.concatenate([condition.reshape(-1), biases]).astype(jnp.float32)
        held = jnp.pad(held, (0, -held.size % (8 * LANES)))
        small = small_gather(held.reshape(-1, LANES), planes, 0).reshape(devices, -1)
        conditions = small[:, : condition.size].reshape(latents, GROUP, micros, -1)
        conditions = conditions.transpose(2, 0, 1, 3).reshape(micros * latents, D)
        cond_act = silu(conditions).astype(jnp.bfloat16)
        bias_all = small[:, condition.size : condition.size + biases.size].reshape(-1)
        bias_query = bias_all[0:D]
        bias_value = bias_all[D : 2 * D]
        bias_project = bias_all[2 * D : 3 * D]
        bias_expand = bias_all[3 * D : 3 * D + FF]
        bias_contract = bias_all[3 * D + FF : 4 * D + FF]
        bias_modulate = bias_all[4 * D + FF :]

        cond_own = lax.dynamic_slice_in_dim(cond_act, me * rows, rows, axis=1)
        partial = jnp.dot(cond_own, modulate_rows, preferred_element_type=jnp.float32)
        partial = partial.reshape(micros, latents, GROUP, -1).transpose(1, 2, 0, 3)
        partial = partial.reshape(planes, 2, 2, 2, -1, LANES)

        bias_row = jnp.concatenate(
            [
                lax.dynamic_slice_in_dim(bias_query, quarter * OWN, OWN),
                jnp.zeros((OWN,), jnp.float32),
                lax.dynamic_slice_in_dim(bias_value, quarter * OWN, OWN),
            ]
        )
        bias_row = bias_row.reshape(3, PAIRS, LANES).transpose(1, 0, 2).reshape(-1)
        attend_all, project_all, expand_all, contract_all, modulation_all, *rest = gather_all(
            *shards, partial, planes
        )
        modulation = modulation_all.reshape(GROUP, micros, -1).transpose(1, 0, 2)
        modulation = modulation.reshape(micros, 6 * D) + bias_modulate
        offsets_one, factors_one, gates_one, offsets_two, factors_two, gates_two = (
            modulation[:, None, part * D : (part + 1) * D] for part in range(6)
        )
        attend_own = attend_all.reshape(D, 3 * OWN)
        project_full = project_all.reshape(D, D)
        expand_full = expand_all.reshape(D, FF)
        contract_full = contract_all.reshape(FF, D)
        tokens_latent = rest[0].reshape(micros, latent_rows, D)
        normed_latent, _ = normalize(tokens_latent.astype(jnp.float32))
        first = (normed_latent * (1.0 + factors_one) + offsets_one).astype(jnp.bfloat16)
        projected = (einsum("mrd,de->mre", first, attend_own) + bias_row).astype(jnp.bfloat16)
        blended_heads, logs = attention(projected)
        blended = heads_to_tokens(blended_heads)

        attended = einsum("mrd,de->mre", blended, project_full) + bias_project
        middle = inputs + gates_one * attended
        normed_two, scale_two = normalize(middle)
        second = (normed_two * (1.0 + factors_two) + offsets_two).astype(jnp.bfloat16)
        hidden = einsum("mrd,de->mre", second, expand_full) + bias_expand
        activated, gelu_pull = jax.vjp(lambda v: jax.nn.gelu(v, approximate=True), hidden)
        act_low = activated.astype(jnp.bfloat16)
        branch = einsum("mrd,de->mre", act_low, contract_full) + bias_contract
        output = (middle + gates_two * branch).astype(jnp.bfloat16)

        upstream = cotangent.astype(jnp.float32)
        grad_branch = (gates_two * upstream).astype(jnp.bfloat16)
        grad_contract = einsum("mrd,mre->de", act_low, grad_branch)
        grad_act = einsum("mre,de->mrd", grad_branch, contract_full)
        grad_hidden = gelu_pull(grad_act)[0].astype(jnp.bfloat16)
        grad_expand = einsum("mrd,mre->de", second, grad_hidden)
        grad_second = einsum("mre,de->mrd", grad_hidden, expand_full)
        grad_middle = upstream + norm_back(grad_second, normed_two, scale_two, factors_two)
        grad_attended = (gates_one * grad_middle).astype(jnp.bfloat16)
        grad_project = einsum("mrd,mre->de", blended, grad_attended)
        grad_blended = einsum("mre,de->mrd", grad_attended, project_full).astype(jnp.bfloat16)
        grad_heads = tokens_to_heads(grad_blended)
        grad_projected = attention_back(projected, blended_heads, grad_heads, logs)
        grad_attend = einsum("mrd,mre->de", first, grad_projected)
        grad_first = token_sums(
            einsum("mre,de->mrd", grad_projected, attend_own).astype(jnp.bfloat16)
        )
        weights = (
            grad_contract.astype(jnp.bfloat16).reshape(*grid, FF // devices, D),
            grad_expand.astype(jnp.bfloat16).reshape(*grid, rows, FF),
            grad_project.astype(jnp.bfloat16).reshape(*grid, rows, D),
        )
        attend_sum, contract_sum, expand_sum, project_sum = weight_sums(
            grad_attend.astype(jnp.bfloat16).reshape(*grid, rows, 3 * OWN), weights, planes
        )
        attend_sum = attend_sum.reshape(2, 2, rows, PAIRS, 3, LANES).transpose(2, 4, 0, 1, 3, 5)

        def token_sum(values):
            return jnp.sum(values, axis=(0, 1), dtype=jnp.float32)

        heads_sum, attended_sum = token_sum(grad_projected), token_sum(grad_attended)
        hidden_sum, branch_sum = token_sum(grad_hidden), token_sum(grad_branch)
        later_sums = jnp.concatenate(
            [
                jnp.sum(grad_middle * attended, axis=1),
                jnp.sum(grad_second, axis=1),
                jnp.sum(grad_second * normed_two, axis=1),
                jnp.sum(upstream * branch, axis=1),
            ],
            axis=1,
        )
        normed_one, scale_one = normalize(inputs)
        grad_tokens = grad_middle + norm_back(grad_first, normed_one, scale_one, factors_one)

        grad_modulation = jnp.concatenate(
            [jnp.sum(grad_first, axis=1), jnp.sum(grad_first * normed_one, axis=1), later_sums], axis=1
        )
        heads_sum = heads_sum.reshape(PAIRS, 3, LANES).transpose(1, 0, 2).reshape(3, OWN)
        bias_terms = jnp.concatenate(
            [
                lax.dynamic_update_slice(
                    jnp.zeros((D,), jnp.float32), heads_sum[0], (quarter * OWN,)
                ),
                lax.dynamic_update_slice(
                    jnp.zeros((D,), jnp.float32), heads_sum[2], (quarter * OWN,)
                ),
                attended_sum,
                hidden_sum,
                branch_sum,
            ]
        )
        to_sum = jnp.concatenate(
            [
                grad_modulation.reshape(micros, GROUP, -1).transpose(1, 0, 2).reshape(GROUP, -1),
                bias_terms.reshape(GROUP, -1),
            ],
            axis=1,
        )
        sums = small_sums(to_sum.reshape(2, 2, -1, LANES), planes).reshape(latents, GROUP, -1)
        split = micros * 6 * D // GROUP
        grad_modulations = sums[:, :, :split].reshape(latents, GROUP, micros, -1)
        grad_modulations = grad_modulations.transpose(2, 0, 1, 3).reshape(micros * latents, 6 * D)
        grad_modulate = lax.dot_general(
            cond_own.astype(jnp.float32),
            grad_modulations,
            (((0,), (0,)), ((), ())),
            precision=highest,
        )
        grad_cond_cols = lax.dot_general(
            grad_modulations,
            modulate_rows.astype(jnp.float32),
            (((1,), (1,)), ((), ())),
            precision=highest,
        )
        cols = grad_cond_cols.reshape(-1)
        cols = jnp.pad(cols, (0, -cols.size % (8 * LANES)))
        cond_cols = small_gather(cols.reshape(-1, LANES), planes, 8).reshape(devices, -1)
        cond_cols = cond_cols[:, : micros * latents * rows].reshape(devices, micros, latents, rows)
    grad_modulations = sums[:, :, :split].reshape(latents, GROUP, micros, -1)
    grad_modulations = grad_modulations.transpose(2, 0, 1, 3).reshape(micros * latents, 6 * D)
    bias_sums = jnp.concatenate(
        [jnp.sum(sums[:, :, split:], axis=0).reshape(-1), jnp.sum(grad_modulations, axis=0)]
    )
    grad_biases = lax.dynamic_slice_in_dim(bias_sums, me * biases.size, biases.size)
    cols_own = lax.dynamic_index_in_dim(cond_cols, latent, axis=2, keepdims=False)
    width = D // GROUP
    cols_own = lax.dynamic_slice_in_dim(
        cols_own, quarter * (devices // GROUP), devices // GROUP, axis=0
    )
    grad_silu = cols_own.transpose(1, 0, 2).reshape(micros, width)
    values = condition.astype(jnp.float32)
    gate = 1.0 / (1.0 + jnp.exp(-values))
    grad_condition = gate * (1.0 + values * (1.0 - gate)) * grad_silu

    return (
        output,
        grad_tokens,
        grad_condition,
        attend_sum.reshape(-1),
        project_sum.reshape(-1),
        expand_sum.reshape(-1),
        contract_sum.reshape(-1),
        grad_modulate.reshape(-1),
        grad_biases,
    )


def solution(mesh):
    in_specs = (
        P(None, "fsdp", None),
        P(None, "fsdp"),
        P("fsdp"),
        P("fsdp"),
        P("fsdp"),
        P("fsdp"),
        P("fsdp"),
        P("fsdp"),
        P(None, "fsdp", None),
    )
    out_specs = (
        P(None, "fsdp", None),
        P(None, "fsdp", None),
        P(None, "fsdp"),
        P("fsdp"),
        P("fsdp"),
        P("fsdp"),
        P("fsdp"),
        P("fsdp"),
        P("fsdp"),
    )
    return jax.shard_map(
        per_device, mesh=mesh, in_specs=in_specs, out_specs=out_specs, check_vma=False
    )
```

```python
import functools

import jax
import jax.numpy as jnp
from jax import lax
from jax.experimental import pallas as pl
from jax.experimental.pallas import tpu as pltpu
from jax.sharding import PartitionSpec as P

D = 1024
HEADS = 16
HEAD = 64
FF = 4096
GROUP = 4
OWN = D // GROUP
SCALE = HEAD**-0.5
LANES = 128
MICROS = 2

epsilon = 1e-06
highest = lax.Precision.HIGHEST
MESH = pl.DeviceIdType.MESH
MIB = 1 << 20


def silu(values):
    return values / (1.0 + jnp.exp(-values))


class Links:
    def __init__(self, planes, send_sem, recv_sem, local_sem=None):
        me = lax.axis_index("fsdp")
        self.planes = planes
        self.c = me % 2
        self.x = (me // 2) % 2
        self.y = (me // 4) % 2
        self.z = me // 8
        self.core = me + 1 - 2 * self.c
        self.beside = me + 2 - 4 * self.x
        self.across = me + 4 - 8 * self.y
        self.place = me % 8
        self.send_sem, self.recv_sem, self.local_sem = send_sem, recv_sem, local_sem
        self.used = 0
        self.local_used = 0
        self.pending = []

    def plane(self, step):
        return (self.z + step) % self.planes

    def plane_device(self, step):
        return self.plane(step) * 8 + self.place

    def column(self):
        places = []
        for step in range(self.planes):
            for y in (self.y, 1 - self.y):
                if step > 0 or y is not self.y:
                    z = self.plane(step)
                    places.append((z, y, z * 8 + y * 4 + self.place % 4))
        return places

    def partners(self):
        return [self.core, self.beside] + [device for _, _, device in self.column()]

    def greet(self, partners, meanwhile=None):
        barrier = pltpu.get_barrier_semaphore()
        for partner in partners:
            pl.semaphore_signal(barrier, inc=1, device_id=(partner,), device_id_type=MESH)
        if meanwhile is not None:
            meanwhile()
        pl.semaphore_wait(barrier, len(partners))

    def send(self, source, target, device):
        assert self.used < self.send_sem.shape[0]
        copy = pltpu.make_async_remote_copy(
            src_ref=source,
            dst_ref=target,
            send_sem=self.send_sem.at[self.used],
            recv_sem=self.recv_sem.at[self.used],
            device_id=(device,),
            device_id_type=MESH,
        )
        self.used += 1
        copy.start()
        self.pending.append(copy)
        return copy

    def local(self, source, target):
        assert self.local_used < self.local_sem.shape[0]
        copy = pltpu.make_async_copy(source, target, self.local_sem.at[self.local_used])
        self.local_used += 1
        copy.start()
        return copy

    def finish_sends(self):
        for copy in self.pending:
            copy.wait_send()
        self.pending = []


def arrived(copies):
    for copy in copies:
        copy.wait_recv()


ANY = pl.BlockSpec(memory_space=pl.ANY)
VMEM = pl.BlockSpec(memory_space=pltpu.VMEM)


def remote_call(body, name, collective_id, outs, in_specs, out_specs, scratch, sems, local_sems, vmem):
    return pl.pallas_call(
        body,
        out_shape=outs,
        in_specs=in_specs,
        out_specs=out_specs,
        scratch_shapes=[
            pltpu.SemaphoreType.DMA((sems,)),
            pltpu.SemaphoreType.DMA((sems,)),
            pltpu.SemaphoreType.DMA((max(local_sems, 1),)),
            *scratch,
        ],
        compiler_params=pltpu.CompilerParams(
            collective_id=collective_id, has_side_effects=True, vmem_limit_bytes=vmem
        ),
        name=name,
    )


def small_gather_body(planes, own_ref, out_ref, send_sem, recv_sem, local_sem):
    links = Links(planes, send_sem, recv_sem)
    links.greet(links.partners())
    z, y, x, c = links.z, links.y, links.x, links.c
    out_ref[z, y, x, c] = own_ref[...]
    spread_all(links, out_ref)
    links.finish_sends()


def spread_all(links, out_ref):
    spread = Spread(links, out_ref)
    for k in range(4):
        spread.step(k)


def small_gather(own, planes, collective_id):
    return remote_call(
        functools.partial(small_gather_body, planes),
        "small_gather",
        collective_id,
        jax.ShapeDtypeStruct((planes, 2, 2, 2, *own.shape), own.dtype),
        [VMEM],
        VMEM,
        [],
        2 * planes + 4,
        0,
        40 * MIB,
    )(own)


WIDTH = 1024
HALF = WIDTH // 2
ALL = slice(None)


class Pieces:
    def __init__(self, links, shards, fulls):
        self.links = links
        self.pieces, self.owns = [], []
        for shard, full in zip(shards, fulls):
            z, y, x, c = links.z, links.y, links.x, links.c
            self.owns.append([links.local(shard, full.at[z, y, x, c]), False])
            for first, count, start in cuts(shard.shape):
                rows = rows_of(shard.shape, first, count)
                self.pieces.append((len(self.owns) - 1, shard, full, rows, start))
        self.count = len(self.pieces)
        self.lead = [None] * self.count
        self.rest = [None] * self.count
        self.late = [[] for _ in range(self.count)]

    def columns(self, k, half):
        return pl.ds(self.pieces[k][4] + half * HALF, HALF)

    def block(self, k, half, *place):
        _, _, full, rows, _ = self.pieces[k]
        return full.at[(*place, rows, self.columns(k, half))]

    def own_block(self, k, half):
        _, shard, _, rows, _ = self.pieces[k]
        links = self.links
        return shard.at[rows, self.columns(k, half)], self.block(
            k, half, links.z, links.y, links.x, links.c
        )

    def own_there(self, k):
        own = self.owns[self.pieces[k][0]]
        if not own[1]:
            own[0].wait()
            own[1] = True

    def to_core(self, k, half, *place):
        block = self.block(k, half, *place)
        self.late[k].append(self.links.send(block, block, self.links.core))

    def to_planes(self, source, target):
        links = self.links
        return [links.send(source, target, links.plane_device(s)) for s in range(1, links.planes)]

    def T0(self, k):
        if k < self.count:
            self.lead[k] = [self.links.send(*self.own_block(k, 0), self.links.beside)]

    def T1(self, k):
        links = self.links
        self.own_there(k)
        arrived(self.lead[k])
        block = self.block(k, 0, links.z, links.y, ALL, links.c)
        self.lead[k] = self.to_planes(block, block)
        self.T0(k + AHEAD)

    def T2(self, k):
        links = self.links
        arrived(self.lead[k])
        place = (ALL, links.y, ALL, links.c)
        block = self.block(k, 0, *place)
        self.lead[k] = [links.send(block, block, links.across)]
        self.to_core(k, 0, *place)

    def T3(self, k):
        links = self.links
        arrived(self.lead[k])
        self.to_core(k, 0, ALL, 1 - links.y, ALL, links.c)

    def F0(self, k):
        if k < self.count:
            self.rest[k] = self.to_planes(*self.own_block(k, 1))

    def F1(self, k):
        links = self.links
        self.own_there(k)
        arrived(self.rest[k])
        place = (ALL, links.y, links.x, links.c)
        block = self.block(k, 1, *place)
        self.rest[k] = [links.send(block, block, links.across)]
        self.to_core(k, 1, *place)
        self.F0(k + AHEAD)

    def F2(self, k):
        links = self.links
        arrived(self.rest[k])
        block = self.block(k, 1, ALL, ALL, links.x, links.c)
        self.rest[k] = [links.send(block, block, links.beside)]
        self.to_core(k, 1, ALL, 1 - links.y, links.x, links.c)

    def F3(self, k):
        links = self.links
        arrived(self.rest[k])
        self.to_core(k, 1, ALL, ALL, 1 - links.x, links.c)

    def there(self, k):
        arrived(self.late[k])
        self.late[k] = []


def tasks_of(order):
    return [(TASKS[code // 32], code % 32) for code in order]


TASKS = (
    "fb", "az", "sp", "ay", "pm", "tk", "F1", "F2", "T1", "att", "unit", "F3", "T2", "T3", "load",
    "own", "there", "mlp", "S1", "project", "T4", "F4", "head", "first", "t1", "attend", "small",
    "t2", "a1", "sums", "a2", "a3", "modulate", "cond",
)


def cuts(shape):
    rows, width = shape
    if width > WIDTH:
        return [(0, rows, start) for start in range(0, width, WIDTH)]
    count = 4 if rows % 128 == 0 else 1
    return [(part * (rows // count), rows // count, 0) for part in range(count)]


def rows_of(shape, first, count):
    return ALL if count == shape[-2] else pl.ds(first, count)


AHEAD = 2
MIDDLE_PIECES = 3


class Opening:
    TOKEN_CUTS = 8
    ATTEND_CUTS = 4

    def __init__(self, links, tokens, attend, partial, tokens_out, attend_out, modulation_out, scratch):
        self.links, self.partial, self.attend = links, partial, attend
        self.tokens, self.tokens_out = tokens, tokens_out
        self.attend_out, self.modulation_out = attend_out, modulation_out
        self.held, self.from_core, self.from_beside, self.from_column, self.total = scratch
        z, y, x, c = links.z, links.y, links.x, links.c
        target = attend_out.at[z, y, x, c]
        self.own_slice = links.local(attend.at[x, c], target)
        self.own_tokens = links.local(tokens, tokens_out.at[:, x, c])
        self.far = links.send(attend.at[1 - x, 1 - c], self.held, links.core)
        self.near = [
            links.send(attend.at[x, 1 - c], target, links.core),
            links.send(attend.at[1 - x, c], target, links.beside),
        ]
        self.over_planes, self.beside, self.rest = {}, {}, []

    def tokens_start(self):
        links = self.links
        target = self.tokens_out.at[:, links.x, links.c]
        self.rest.append(links.send(self.tokens, target, links.core))
        for k in range(2):
            self.tkx(k)

    def token_block(self, k):
        each = self.TOKEN_CUTS // self.tokens.shape[0]
        rows = self.tokens.shape[1] // each
        return k // each, pl.ds(k % each * rows, rows)

    def tkx(self, k):
        links = self.links
        m, rows = self.token_block(k)
        target = self.tokens_out.at[m, links.x, links.c, rows]
        self.beside[k] = links.send(self.tokens.at[m, rows], target, links.beside)

    def tk(self, k):
        links = self.links
        arrived([self.beside.pop(k)])
        m, rows = self.token_block(k)
        fresh = self.tokens_out.at[m, 1 - links.x, links.c, rows]
        self.rest.append(links.send(fresh, fresh, links.core))
        if k + 2 < self.TOKEN_CUTS:
            self.tkx(k + 2)

    def fb(self, k):
        links = self.links
        arrived([self.far])
        target = self.attend_out.at[links.z, links.y, links.x, 1 - links.c]
        self.near.append(links.send(self.held, target, links.beside))

    def attend_block(self, k, *place):
        pair = k // 2
        return self.attend_out.at[(*place, k % 2, ALL, ALL, pl.ds(pair * PAIR, PAIR))]

    def azx(self, k):
        links = self.links
        block = self.attend_block(k, links.z, links.y)
        self.over_planes[k] = [
            links.send(block, block, links.plane_device(s)) for s in range(1, links.planes)
        ]

    def az(self, k):
        self.own_slice.wait()
        arrived(self.near)
        self.azx(0)
        self.azx(1)

    def ay(self, k):
        links = self.links
        arrived(self.over_planes.pop(k))
        block = self.attend_block(k, ALL, links.y)
        self.rest.append(links.send(block, block, links.across))
        if k + 2 < self.ATTEND_CUTS:
            self.azx(k + 2)

    def pm(self, k):
        links = self.links
        z, y, x, c = links.z, links.y, links.x, links.c
        if k > 0:
            arrived(self.step)
        if k == 0:
            self.step = [links.send(self.partial.at[:, :, :, 1 - c], self.from_core, links.core)]
        elif k == 1:
            self.from_core[...] = self.from_core[...] + self.partial[:, :, :, c]
            self.step = [
                links.send(self.from_core.at[:, :, 1 - x], self.from_beside, links.beside)
            ]
        elif k == 2:
            self.from_beside[...] = self.from_beside[...] + self.from_core[:, :, x]
            self.step = [
                links.send(self.from_beside.at[to_z, to_y], self.from_column.at[place], device)
                for place, (to_z, to_y, device) in enumerate(links.column())
            ]
        elif k == 3:
            result = self.from_beside[z, y]
            for place in range(2 * links.planes - 1):
                result = result + self.from_column[place]
            self.total[...] = result
            target = self.modulation_out.at[x, c]
            target[...] = result
            self.step = [
                links.send(self.total, target, links.core),
                links.send(self.total, target, links.beside),
            ]
        else:
            fresh = self.modulation_out.at[1 - x, c]
            self.rest.append(links.send(fresh, fresh, links.core))

    def finish(self):
        arrived(self.rest)
        self.own_tokens.wait()


def gather_body(
    planes,
    tokens,
    attend,
    project,
    expand,
    contract,
    partial,
    attend_out,
    project_out,
    expand_out,
    contract_out,
    modulation_out,
    tokens_out,
    send_sem,
    recv_sem,
    local_sem,
    *scratch,
):
    links = Links(planes, send_sem, recv_sem, local_sem)
    links.greet(links.partners())
    opening = Opening(
        links, tokens, attend, partial, tokens_out, attend_out, modulation_out, scratch
    )
    pieces = Pieces(links, (project, expand, contract), (project_out, expand_out, contract_out))
    opening.tokens_start()
    for k in range(5):
        opening.pm(k)
    for k in range(Opening.TOKEN_CUTS):
        opening.tk(k)
    opening.fb(0)
    opening.az(0)
    for k in range(Opening.ATTEND_CUTS):
        opening.ay(k)
    for k in range(AHEAD):
        pieces.T0(k)
        pieces.F0(k)
    for k in range(pieces.count + 2):
        for behind, names in enumerate((("T1", "F1"), ("T2", "F2"), ("T3", "F3"))):
            if 0 <= k - behind < pieces.count:
                for name in names:
                    getattr(pieces, name)(k - behind)
    for k in range(pieces.count):
        pieces.there(k)
    opening.finish()
    links.finish_sends()


FRONT_ORDER = (
    0, 32, 65, 66, 96, 128, 160, 97, 161, 129, 98, 162, 163, 99, 130, 192, 164, 193, 165, 131, 166,
    224, 194, 167, 132, 195, 256, 225, 288, 320, 196, 321, 257, 226, 197, 227, 322, 352, 323, 384,
    324, 353, 325, 198, 326, 327, 416, 354, 385, 328, 258, 199, 329, 355, 200, 259, 330, 417, 331,
    332, 386, 333, 260, 334, 228, 261, 387, 335, 336, 418, 337, 229, 388, 448, 262, 356, 419, 480,
    230, 389, 263, 513, 544, 231, 232, 357, 420, 264, 390, 514, 545, 421, 358, 515, 546, 391, 516,
    547, 422, 359, 392, 423, 360, 424,
)


def front_body(planes, *refs):
    tokens, attend_flat, project_flat, expand_flat, contract_flat, refs = *refs[:5], refs[5:]
    payload, modulate_flat, cotangent, refs = *refs[:3], refs[3:]
    attend_out, project_out, expand_out, contract_out, modulation_out, refs = *refs[:5], refs[5:]
    normed_out, qkv_out, heads_out, log_out, blended_out, refs = *refs[:5], refs[5:]
    middle_out, attended_out, second_out, act_out, slope_out, branch_out, grad_out = refs[:7]
    bias_rows, cond_out, modulate, refs = *refs[7:10], refs[10:]
    send_sem, recv_sem, local_sem = refs[:3]
    opening_scratch, refs = refs[3:8], refs[8:]
    payloads, partial, refs = *refs[:2], refs[2:]
    flat, attend, project, expand, contract, refs = *refs[:5], refs[5:]
    tokens_all, attend_all, normed, qkv, heads, blended, project_all, expand_all = refs[:8]
    middle, attended, second, act, slope, grad_branch, grads, upstream, bias_held = refs[8:]
    links = Links(planes, send_sem, recv_sem, local_sem)
    z, y, x, c = links.z, links.y, links.x, links.c
    corner = links.beside + 1 - 2 * c
    spread = Spread(links, payloads)

    def rows_apart(source, count):
        stride = source.shape[0] // count
        flat[: source.shape[0], :] = source[...].astype(jnp.float32)
        for k in range(stride):
            yield k, flat[pl.ds(k, count, stride=stride), :].astype(jnp.bfloat16)

    rows_own = project.shape[0]

    def prepare():
        payloads[z, y, x, c] = payload[...]
        for k, values in rows_apart(attend_flat, rows_own):
            kind, quarter, pair = k // (GROUP * PAIRS), k // PAIRS % GROUP, k % PAIRS
            lanes = pl.ds((pair * 3 + kind) * LANES, LANES)
            attend[quarter // 2, quarter % 2, :, lanes] = values

    links.greet([*links.partners(), corner], prepare)
    spread.step(0)
    opening = Opening(
        links, tokens, attend, partial, tokens_all, attend_all, modulation_out, opening_scratch
    )
    for source, target in (
        (modulate_flat, modulate),
        (expand_flat, expand),
        (project_flat, project),
        (contract_flat, contract),
    ):
        for k, values in rows_apart(source, target.shape[0]):
            target[:, k * LANES : (k + 1) * LANES] = values
    pieces = Pieces(links, (project, expand, contract), (project_all, expand_all, contract_out))
    count = pieces.count
    loaded_upstream = links.local(cotangent, upstream)
    micros, own_rows, _ = tokens.shape
    stored, stored_grads, exchanged = [], [], []
    own_heads = pl.ds(pl.multiple_of((2 * x + c) * OWN, OWN), OWN)

    def partial_unit():
        latents, rows = 2 * planes, modulate.shape[0]
        each = latents
        source = (links.z * 8 + links.place) // each
        column = (links.z * 8 + links.place) % each
        conds = [
            payloads[:, :, source // 2, source % 2, pl.ds(micros * column + m, 1), :].reshape(
                latents, LANES
            )
            for m in range(micros)
        ]
        active = silu(jnp.concatenate(conds, axis=0)[:, :rows]).astype(jnp.bfloat16)
        cond_out[...] = active.astype(jnp.float32)
        product = jnp.dot(active, modulate[...], preferred_element_type=jnp.float32)
        per_quarter = 6 * D // LANES // GROUP
        for m in range(micros):
            for k in range(6 * D // LANES):
                quarter, row = k // per_quarter, m * per_quarter + k % per_quarter
                values = product[m * latents : (m + 1) * latents, k * LANES : (k + 1) * LANES]
                partial[:, :, quarter // 2, quarter % 2, row, :] = values.reshape(
                    planes, 2, LANES
                )
        opening.pm(0)
        start = micros * each
        long = bias_rows.shape[0] // (4 * planes)
        for pair in range(4 * planes):
            place = (pair // 4, pair // 2 % 2, pair % 2)
            even = payloads[(*place, 0, slice(start, start + 4), ALL)]
            odd = payloads[(*place, 1, slice(start, start + 4), ALL)]
            joint = even[3:4] + odd[0:1]
            bias_rows[pair * long : (pair + 1) * long, :] = jnp.concatenate(
                [even[:3], joint, odd[1:]], axis=0
            )

    def shift(block):
        return bias_vector(bias_rows, 4 * D + FF + block * D, D)

    def part_of(m, to_x, to_c):
        start = pl.multiple_of((2 * to_x + to_c) * own_rows, own_rows)
        return heads.at[m, pl.ds(start, own_rows)]

    def project_micro(m):
        own = (2 * x + c) * PAIRS
        bias_qkv = []
        for pair in range(PAIRS):
            bias_qkv += [
                bias_rows[pl.ds(own + pair, 1), :],
                jnp.zeros((1, LANES), jnp.float32),
                bias_rows[pl.ds(D // LANES + own + pair, 1), :],
            ]
        offsets = modulation_row(modulation_out, m, 0) + shift(0)
        factors = 1.0 + modulation_row(modulation_out, m, 1) + shift(1)
        bias = jnp.concatenate(bias_qkv, axis=1)
        project_tokens(m, tokens_all, attend_all, offsets, factors, bias, normed, qkv)
        stored.append(links.local(normed.at[m], normed_out.at[m]))
        stored.append(links.local(qkv.at[m], qkv_out.at[m]))

    def far_heads(m, head):
        attention_unit(qkv.at[m], heads.at[m], log_out.at[m], head, 1 - x)
        if head == OWN // HEAD - 1:
            target = blended.at[m, :, own_heads]
            exchanged.append(links.send(part_of(m, 1 - x, 1 - c), target, corner))
            exchanged.append(links.send(part_of(m, 1 - x, c), target, links.beside))

    def near_heads(m, head):
        attention_unit(qkv.at[m], heads.at[m], log_out.at[m], head, x)
        if head == OWN // HEAD - 1:
            target = blended.at[m, :, own_heads]
            exchanged.append(links.send(part_of(m, x, 1 - c), target, links.core))
            stored.append(links.local(heads.at[m], heads_out.at[m]))
            links.local(part_of(m, x, c), target).wait()

    units = []
    for m in range(micros):
        units.append(functools.partial(project_micro, m))
        units += [functools.partial(far_heads, m, head) for head in range(OWN // HEAD)]
    for m in range(micros):
        units += [functools.partial(near_heads, m, head) for head in range(OWN // HEAD)]

    def load_project():
        pieces.there(0)
        stored.append(links.local(project_all, project_out))
        loaded_upstream.wait()
        for m in range(micros):
            gate = modulation_row(modulation_out, m, 5) + shift(5)
            grad_branch[m] = (gate * upstream[m].astype(jnp.float32)).astype(jnp.bfloat16)
        stored.append(links.local(grad_branch, branch_out))

    def own_tokens():
        for m in range(micros):
            stored.append(links.local(blended.at[m], blended_out.at[m]))
            product = jnp.dot(
                blended[m],
                project_all[...].reshape(D, D),
                preferred_element_type=jnp.float32,
            )
            attended[m] = product + bias_vector(bias_rows, 2 * D, D)
            gate = modulation_row(modulation_out, m, 2) + shift(2)
            middle[m] = tokens_all[m, x, c].astype(jnp.float32) + gate * attended[m]
            normed_two, _ = normalize(middle[m])
            factors = 1.0 + modulation_row(modulation_out, m, 4) + shift(4)
            offsets = modulation_row(modulation_out, m, 3) + shift(3)
            second[m] = (normed_two * factors + offsets).astype(jnp.bfloat16)
        stored.append(links.local(middle, middle_out))
        stored.append(links.local(attended, attended_out))
        stored.append(links.local(second, second_out))

    parts = FF // WIDTH
    blocks = grads.shape[1]

    def expand_unit(part):
        columns = pl.ds(part * WIDTH, WIDTH)
        stored.append(
            links.local(
                expand_all.at[:, :, :, :, :, columns], expand_out.at[:, :, :, :, :, columns]
            )
        )
        if part >= 2:
            stored_grads[part - 2].wait()
        bias = bias_vector(bias_rows, 3 * D + part * WIDTH, WIDTH)
        bias_held[...] = bias
        expand_part(part, WIDTH, second, expand_all, bias_held, act, slope, grad_branch, grads)
        stored.append(links.local(act.at[:, :, columns], act_out.at[:, :, columns]))
        stored.append(links.local(slope.at[:, :, columns], slope_out.at[:, :, columns]))
        stored_grads.append(
            links.local(grads.at[part % 2], grad_out.at[pl.ds(part * blocks, blocks)])
        )

    for task, k in tasks_of(FRONT_ORDER):
        if task == "sp":
            spread.step(k)
            if k == 1:
                opening.tokens_start()
        elif task in ("fb", "az", "ay", "tk"):
            getattr(opening, task)(k)
            if task == "ay" and k == Opening.ATTEND_CUTS - 2:
                for piece in range(AHEAD):
                    pieces.F0(piece)
            if task == "tk" and k == Opening.TOKEN_CUTS - 2:
                for piece in range(AHEAD):
                    pieces.T0(piece)
        elif task == "pm":
            if k == 0:
                spread.step(3)
                partial_unit()
            else:
                opening.pm(k)
        elif task == "att":
            opening.finish()
            stored.append(links.local(attend_all, attend_out))
        elif task == "unit":
            units[k]()
        elif task == "load":
            load_project()
        elif task == "own":
            arrived(exchanged)
            own_tokens()
        elif task == "there":
            pieces.there(k)
        elif task == "mlp":
            expand_unit(k)
        else:
            getattr(pieces, task)(k)
    for k in range(count):
        pieces.there(k)
    for copy in stored + stored_grads[-2:]:
        copy.wait()
    links.finish_sends()


ROOT = 0.7978845608028654
CUBE = 0.044715
CHUNK = 512


def expand_part(part, width, second, expand, bias, act, slope, grad_branch, grads):
    micros = second.shape[0]
    rows = grads.shape[2]

    @pl.loop(0, width // CHUNK, unroll=True)
    def _(chunk):
        inside = pl.ds(pl.multiple_of(chunk * CHUNK, CHUNK), CHUNK)
        columns = pl.ds(pl.multiple_of(part * width + chunk * CHUNK, CHUNK), CHUNK)
        weights = expand[:, :, :, :, :, columns].reshape(D, CHUNK)
        total = None
        for m in range(micros):
            hidden = jnp.dot(second[m], weights, preferred_element_type=jnp.float32)
            hidden = hidden + bias[:, inside]
            square = hidden * hidden
            bend = jnp.tanh(hidden * (ROOT + (ROOT * CUBE) * square))
            half = 0.5 + 0.5 * bend
            low = (hidden * half).astype(jnp.bfloat16)
            act[m, :, columns] = low
            steep = hidden * (0.5 * ROOT + (1.5 * ROOT * CUBE) * square)
            slope[m, :, columns] = (half + steep * (1.0 - bend * bend)).astype(jnp.bfloat16)
            product = lax.dot_general(
                low, grad_branch[m], (((0,), (0,)), ((), ())), preferred_element_type=jnp.float32
            )
            total = product if total is None else total + product
        count = CHUNK // rows
        here = pl.ds(chunk * count, count)
        grads[part % 2, here] = total.astype(jnp.bfloat16).reshape(count, rows, D)


def modulation_row(modulation, m, block):
    per_quarter = modulation.shape[2] // MICROS
    pieces = []
    for k in range(block * D // LANES, (block + 1) * D // LANES):
        quarter, row = k // per_quarter, m * per_quarter + k % per_quarter
        pieces.append(modulation[quarter // 2, quarter % 2, row : row + 1, :])
    return jnp.concatenate(pieces, axis=1)


def bias_vector(bias_rows, start, count):
    rows = range(start // LANES, (start + count) // LANES)
    return jnp.concatenate([bias_rows[row : row + 1, :] for row in rows], axis=1)


def project_tokens(m, tokens, attend, offsets, factors, bias, normed_out, qkv_out):
    rows = tokens.shape[3]

    @pl.loop(0, GROUP, unroll=2)
    def _(block):
        values = tokens[m, block // 2, block % 2].astype(jnp.float32)
        normed, _ = normalize(values)
        first = (normed * factors + offsets).astype(jnp.bfloat16)
        here = pl.ds(pl.multiple_of(block * rows, rows), rows)
        normed_out[m, here, :] = normed.astype(jnp.bfloat16)
        weights = attend[...].reshape(D, 3 * OWN)
        product = jnp.dot(first, weights, preferred_element_type=jnp.float32)
        qkv_out[m, here, :] = (product + bias).astype(jnp.bfloat16)


def gather_scratch(attend, rows, planes):
    return [
        pltpu.VMEM((attend.shape[-2], attend.shape[-1]), attend.dtype),
        pltpu.VMEM((planes, 2, 2, rows, LANES), jnp.float32),
        pltpu.VMEM((planes, 2, rows, LANES), jnp.float32),
        pltpu.VMEM((2 * planes - 1, rows, LANES), jnp.float32),
        pltpu.VMEM((rows, LANES), jnp.float32),
    ]


def gather_outs(attend, project, expand, contract, rows, planes):
    return [
        *(
            jax.ShapeDtypeStruct((planes, 2, 2, 2, *shard.shape[-2:]), shard.dtype)
            for shard in (attend, project, expand, contract)
        ),
        jax.ShapeDtypeStruct((2, 2, rows, LANES), jnp.float32),
    ]


def gather_sems(planes):
    return 60 + 30 * planes + 9 * (8 + 2 * planes)


def gather_all(tokens, attend, project, expand, contract, partial, planes):
    micros, own_rows, _ = tokens.shape
    return remote_call(
        functools.partial(gather_body, planes),
        "gather_all",
        1,
        (
            *gather_outs(attend, project, expand, contract, partial.shape[-2], planes),
            jax.ShapeDtypeStruct((micros, 2, 2, own_rows, D), tokens.dtype),
        ),
        [ANY] * 5 + [VMEM],
        (ANY,) * 4 + (VMEM, ANY),
        gather_scratch(attend, partial.shape[-2], planes),
        gather_sems(planes),
        8,
        56 * MIB,
    )(tokens, attend, project, expand, contract, partial)


def front(tokens, attend, project, expand, contract, payload, modulate, cotangent, planes):
    micros, own_rows, _ = tokens.shape
    latent_rows = own_rows * GROUP
    blocks = latent_rows // QUERY_ROWS
    def low(*shape):
        return jax.ShapeDtypeStruct(shape, jnp.bfloat16)

    def held(*shape, dtype=jnp.bfloat16):
        return pltpu.VMEM(shape, dtype)

    log_shape = (micros, OWN // HEAD, blocks, 1, QUERY_ROWS)
    own = (micros, own_rows, D)
    parts = FF // WIDTH
    rows = micros * 6 * D // LANES // GROUP
    rows_own, grad_rows = D // (8 * planes), FF // (8 * planes)
    shapes = ((2, 2, rows_own, 3 * OWN), (rows_own, D), (rows_own, FF), (grad_rows, D))
    shards = [jax.ShapeDtypeStruct(shape, jnp.bfloat16) for shape in shapes]
    biases = (10 * D + FF) // LANES
    return remote_call(
        functools.partial(front_body, planes),
        "front",
        1,
        (
            *gather_outs(*shards, rows, planes),
            low(micros, latent_rows, D),
            low(micros, latent_rows, 3 * OWN),
            low(micros, latent_rows, OWN),
            jax.ShapeDtypeStruct(log_shape, jnp.float32),
            low(*own),
            jax.ShapeDtypeStruct(own, jnp.float32),
            jax.ShapeDtypeStruct(own, jnp.float32),
            low(*own),
            low(micros, own_rows, FF),
            low(micros, own_rows, FF),
            low(*own),
            low(FF // grad_rows, grad_rows, D),
            jax.ShapeDtypeStruct((biases, LANES), jnp.float32),
            jax.ShapeDtypeStruct((micros * 2 * planes, rows_own), jnp.float32),
            low(rows_own, 6 * D),
        ),
        [ANY] + [VMEM] * 6 + [ANY],
        (ANY,) * 4 + (VMEM,) + (ANY,) * 3 + (VMEM,) + (ANY,) * 8 + (VMEM,) * 3,
        [
            *gather_scratch(shards[0], rows, planes),
            held(planes, 2, 2, 2, *payload.shape, dtype=jnp.float32),
            held(planes, 2, 2, 2, rows, LANES, dtype=jnp.float32),
            held(*modulate.shape, dtype=jnp.float32),
            *(held(*shape) for shape in shapes),
            held(micros, 2, 2, own_rows, D),
            held(planes, 2, 2, 2, rows_own, 3 * OWN),
            held(micros, latent_rows, D),
            held(micros, latent_rows, 3 * OWN),
            held(micros, latent_rows, OWN),
            held(*own),
            held(planes, 2, 2, 2, rows_own, D),
            held(planes, 2, 2, 2, rows_own, FF),
            held(*own, dtype=jnp.float32),
            held(*own, dtype=jnp.float32),
            held(*own),
            held(micros, own_rows, FF),
            held(micros, own_rows, FF),
            held(*own),
            held(2, FF // parts // grad_rows, grad_rows, D),
            held(*own),
            held(1, WIDTH, dtype=jnp.float32),
        ],
        gather_sems(planes),
        40,
        60 * MIB,
    )(tokens, attend, project, expand, contract, payload, modulate, cotangent)


QUERY_ROWS = 256
PAIRS = OWN // LANES
PAIR = 3 * LANES


def head_columns(head):
    start = head // 2 * PAIR + head % 2 * HEAD
    return [slice(start + kind * LANES, start + kind * LANES + HEAD) for kind in range(3)]


def attention_unit(qkv, out, log, head, side=None):
    count = qkv.shape[0] // QUERY_ROWS
    start = 0
    if side is not None:
        count //= 2
        start = side * count
    at = head * HEAD
    query_at, key_at, value_at = head_columns(head)
    keys = qkv[:, key_at]
    values_t = qkv[:, value_at].T

    @pl.loop(0, count, unroll=True)
    def _(index):
        block = start + index
        here = pl.ds(pl.multiple_of(block * QUERY_ROWS, QUERY_ROWS), QUERY_ROWS)
        queries = qkv[here, query_at] * SCALE
        scores = lax.dot_general(
            keys, queries, (((1,), (1,)), ((), ())), preferred_element_type=jnp.float32
        )
        top = jnp.max(scores, axis=0, keepdims=True)
        weights = jnp.exp(scores - top)
        totals = jnp.sum(weights, axis=0, keepdims=True)
        blended = jnp.dot(
            values_t, weights.astype(jnp.bfloat16), preferred_element_type=jnp.float32
        )
        out[here, at : at + HEAD] = (blended / totals).T.astype(jnp.bfloat16)
        log[head, block] = top + jnp.log(totals)


def attention_body(qkv_ref, out_ref, log_ref):
    for head in range(OWN // HEAD):
        attention_unit(qkv_ref.at[0], out_ref.at[0], log_ref.at[0], head)


def attention(qkv):
    micros, rows, _ = qkv.shape
    heads = OWN // HEAD
    blocks = rows // 256
    return pl.pallas_call(
        attention_body,
        grid=(micros,),
        out_shape=(
            jax.ShapeDtypeStruct((micros, rows, OWN), jnp.bfloat16),
            jax.ShapeDtypeStruct((micros, heads, blocks, 1, 256), jnp.float32),
        ),
        in_specs=[pl.BlockSpec((1, rows, 3 * OWN), lambda m: (m, 0, 0))],
        out_specs=(
            pl.BlockSpec((1, rows, OWN), lambda m: (m, 0, 0)),
            pl.BlockSpec((1, heads, blocks, 1, 256), lambda m: (m, 0, 0, 0, 0)),
        ),
        compiler_params=pltpu.CompilerParams(vmem_limit_bytes=48 * MIB),
        name="attention",
    )(qkv)


def attention_back_unit(qkv, blended_all, grad_all, log, out, key_sum, value_sum, head):
    at = head * HEAD
    query_at, key_at, value_at = head_columns(head)
    keys = qkv[:, key_at]
    keys_t = keys.T
    values = qkv[:, value_at]
    key_sum[...] = jnp.zeros_like(key_sum)
    value_sum[...] = jnp.zeros_like(value_sum)

    @pl.loop(0, qkv.shape[0] // QUERY_ROWS, unroll=True)
    def _(block):
        here = pl.ds(pl.multiple_of(block * QUERY_ROWS, QUERY_ROWS), QUERY_ROWS)
        queries = qkv[here, query_at] * SCALE
        grads = grad_all[here, at : at + HEAD]
        blended = blended_all[here, at : at + HEAD]
        row_terms = jnp.sum(
            (grads.astype(jnp.float32) * blended.astype(jnp.float32)).T, axis=0, keepdims=True
        )
        scores = lax.dot_general(
            keys, queries, (((1,), (1,)), ((), ())), preferred_element_type=jnp.float32
        )
        chances = jnp.exp(scores - log[head, block])
        grad_chances = lax.dot_general(
            values, grads, (((1,), (1,)), ((), ())), preferred_element_type=jnp.float32
        )
        grad_scores = (chances * (grad_chances - row_terms)).astype(jnp.bfloat16)
        value_sum[...] += jnp.dot(
            chances.astype(jnp.bfloat16), grads, preferred_element_type=jnp.float32
        )
        key_sum[...] += jnp.dot(grad_scores, queries, preferred_element_type=jnp.float32)
        grad_queries = jnp.dot(keys_t, grad_scores, preferred_element_type=jnp.float32)
        out[here, query_at] = (grad_queries.T * SCALE).astype(jnp.bfloat16)

    out[:, key_at] = key_sum[...].astype(jnp.bfloat16)
    out[:, value_at] = value_sum[...].astype(jnp.bfloat16)


def attention_back_body(qkv_ref, blended_ref, grad_ref, log_ref, out_ref, key_sum, value_sum):
    for head in range(OWN // HEAD):
        attention_back_unit(
            qkv_ref.at[0],
            blended_ref.at[0],
            grad_ref.at[0],
            log_ref.at[0],
            out_ref.at[0],
            key_sum,
            value_sum,
            head,
        )


def attention_back(qkv, blended, grads, logs):
    micros, rows, _ = qkv.shape
    heads = OWN // HEAD
    blocks = rows // 256
    wide = pl.BlockSpec((1, rows, 3 * OWN), lambda m: (m, 0, 0))
    narrow = pl.BlockSpec((1, rows, OWN), lambda m: (m, 0, 0))
    return pl.pallas_call(
        attention_back_body,
        grid=(micros,),
        out_shape=jax.ShapeDtypeStruct((micros, rows, 3 * OWN), jnp.bfloat16),
        in_specs=[
            wide,
            narrow,
            narrow,
            pl.BlockSpec((1, heads, blocks, 1, 256), lambda m: (m, 0, 0, 0, 0)),
        ],
        out_specs=wide,
        scratch_shapes=[pltpu.VMEM((rows, HEAD), jnp.float32)] * 2,
        compiler_params=pltpu.CompilerParams(vmem_limit_bytes=48 * MIB),
        name="attention_back",
    )(qkv, blended, grads, logs)


def heads_to_tokens_body(blended, out, send_sem, recv_sem, local_sem):
    links = Links(1, send_sem, recv_sem, local_sem)
    x, c = links.x, links.c
    corner = links.beside + 1 - 2 * c
    links.greet([links.core, links.beside, corner])
    target = out.at[:, :, pl.ds(pl.multiple_of((2 * x + c) * OWN, OWN), OWN)]
    own = links.local(blended.at[:, x, c], target)
    copies = [
        links.send(blended.at[:, 1 - x, 1 - c], target, corner),
        links.send(blended.at[:, 1 - x, c], target, links.beside),
        links.send(blended.at[:, x, 1 - c], target, links.core),
    ]
    arrived(copies)
    own.wait()
    links.finish_sends()


def heads_to_tokens(blended):
    micros, rows, _ = blended.shape
    own_rows = rows // GROUP
    return remote_call(
        heads_to_tokens_body,
        "heads_to_tokens",
        2,
        jax.ShapeDtypeStruct((micros, own_rows, D), blended.dtype),
        [ANY],
        ANY,
        [],
        3,
        1,
        40 * MIB,
    )(blended.reshape(micros, 2, 2, own_rows, OWN))


def tokens_to_heads_body(grads, out, send_sem, recv_sem, local_sem):
    links = Links(1, send_sem, recv_sem, local_sem)
    x, c = links.x, links.c
    corner = links.beside + 1 - 2 * c
    links.greet([links.core, links.beside, corner])

    def columns(to_x, to_c):
        return grads.at[:, :, pl.ds(pl.multiple_of((2 * to_x + to_c) * OWN, OWN), OWN)]

    target = out.at[:, x, c]
    own = links.local(columns(x, c), target)
    copies = [
        links.send(columns(1 - x, 1 - c), target, corner),
        links.send(columns(1 - x, c), target, links.beside),
        links.send(columns(x, 1 - c), target, links.core),
    ]
    arrived(copies)
    own.wait()
    links.finish_sends()


def tokens_to_heads(grads):
    micros, own_rows, _ = grads.shape
    return remote_call(
        tokens_to_heads_body,
        "tokens_to_heads",
        3,
        jax.ShapeDtypeStruct((micros, 2, 2, own_rows, OWN), grads.dtype),
        [ANY],
        ANY,
        [],
        3,
        1,
        40 * MIB,
    )(grads).reshape(micros, GROUP * own_rows, OWN)


def token_sums_body(partial, out, send_sem, recv_sem, local_sem, from_core, own, from_beside):
    links = Links(1, send_sem, recv_sem, local_sem)
    x, c = links.x, links.c
    links.greet([links.core, links.beside])
    far = links.send(partial.at[:, 1 - x, 1 - c], from_core.at[0], links.core)
    near = links.send(partial.at[:, x, 1 - c], from_core.at[1], links.core)
    loads = [
        links.local(partial.at[:, 1 - x, c], own.at[0]),
        links.local(partial.at[:, x, c], own.at[1]),
    ]
    micros = out.shape[0]
    loads[0].wait()
    arrived([far])
    passed = []
    for m in range(micros):
        own[0, m] = (
            own[0, m].astype(jnp.float32) + from_core[0, m].astype(jnp.float32)
        ).astype(jnp.bfloat16)
        passed.append(links.send(own.at[0, m], from_beside.at[m], links.beside))
    loads[1].wait()
    arrived([near])
    for m in range(micros):
        out[m] = own[1, m].astype(jnp.float32) + from_core[1, m].astype(jnp.float32)
    for m in range(micros):
        arrived([passed[m]])
        out[m] += from_beside[m].astype(jnp.float32)
    links.finish_sends()


def token_sums(partial):
    micros, rows, width = partial.shape
    own_rows = rows // GROUP
    held = pltpu.VMEM((2, micros, own_rows, width), partial.dtype)
    return remote_call(
        token_sums_body,
        "token_sums",
        4,
        jax.ShapeDtypeStruct((micros, own_rows, width), jnp.float32),
        [ANY],
        VMEM,
        [held, held, pltpu.VMEM((micros, own_rows, width), partial.dtype)],
        4,
        2,
        40 * MIB,
    )(partial.reshape(micros, 2, 2, own_rows, width))


def small_sums_body(planes, partial, out, send_sem, recv_sem, local_sem, from_core, from_beside):
    links = Links(planes, send_sem, recv_sem)
    links.greet(links.partners())
    z, y, x, c = links.z, links.y, links.x, links.c
    arrived([links.send(partial.at[:, 1 - c], from_core, links.core)])
    from_core[...] = from_core[...] + partial[:, c]
    arrived([links.send(from_core.at[1 - x], from_beside, links.beside)])
    out[z, y, x, c] = from_core[x] + from_beside[...]
    spread_all(links, out)
    links.finish_sends()


def small_sums(partial, planes):
    block = partial.shape[2:]
    return remote_call(
        functools.partial(small_sums_body, planes),
        "small_sums",
        5,
        jax.ShapeDtypeStruct((planes, 2, 2, 2, *block), jnp.float32),
        [VMEM],
        VMEM,
        [pltpu.VMEM((2, *block), jnp.float32), pltpu.VMEM(block, jnp.float32)],
        2 * planes + 6,
        0,
        40 * MIB,
    )(partial)


def add_blocks(target, left, right, count):
    @pl.loop(0, count, unroll=2)
    def _(i):
        target(i)[...] = (
            left(i)[...].astype(jnp.float32) + right(i)[...].astype(jnp.float32)
        ).astype(jnp.bfloat16)


class Sums:
    def __init__(self, links, grads, outs, plan, scratch):
        self.links = links
        self.pieces, self.rows = [], []
        used = 0
        for grad, out, pieces in zip(grads, outs, plan):
            own = scratch[used]
            used += 1
            for first, count, start in pieces:
                rows = rows_of(grad.shape, first, count)
                self.pieces.append((grad, out, rows, start, own, *scratch[used : used + 7]))
                self.rows.append((first - pieces[0][0], count, grad.shape[-1] // LANES))
                used += 7
        self.state = [dict() for _ in self.pieces]

    def put(self, k, start, values):
        first, count, stride = self.rows[k]
        out = self.pieces[k][1]
        for j in range(values.shape[1] // LANES):
            where = first * stride + start // LANES + j
            out[pl.ds(where, count, stride=stride), :] = values[:, j * LANES : (j + 1) * LANES]

    def core(self, k):
        links = self.links
        grad, _, rows, start, _, first, *_ = self.pieces[k]
        source = grad.at[:, :, :, 1 - links.c, rows, pl.ds(start, WIDTH)]
        self.state[k]["core"] = links.send(source, first, links.core)

    def load(self, k):
        links = self.links
        grad, _, rows, start, own, *_ = self.pieces[k]
        source = grad.at[:, :, :, links.c, rows, pl.ds(start, WIDTH)]
        self.state[k]["own"] = links.local(source, own)

    def S1(self, k):
        links = self.links
        x, y, planes = links.x, links.y, links.planes
        _, _, _, _, own, first, over_y, _, _, over_x, _, _ = self.pieces[k]
        state = self.state[k]
        state["own"].wait()
        arrived([state["core"]])
        lead, rest = pl.ds(0, HALF), pl.ds(HALF, HALF)

        def add(columns, place):
            def block(ref):
                return lambda i: ref.at[(*place(i // 2, i % 2), ALL, columns)]

            add_blocks(block(first), block(own), block(first), planes * 2)

        add(lead, lambda z, other: (z, 1 - y, other))
        state["T"] = [links.send(first.at[:, 1 - y, :, :, lead], over_y, links.across)]
        add(rest, lambda z, other: (z, other, 1 - x))
        state["F"] = [links.send(first.at[:, :, 1 - x, :, rest], over_x, links.beside)]
        add(lead, lambda z, other: (z, y, other))
        add(rest, lambda z, other: (z, other, x))

    def T2(self, k):
        links = self.links
        _, _, _, _, _, first, over_y, over_planes, _, _, _, _ = self.pieces[k]
        arrived(self.state[k]["T"])

        def kept(i):
            return first.at[i // 2, links.y, i % 2, :, pl.ds(0, HALF)]

        def came(i):
            return over_y.at[i // 2, i % 2]

        add_blocks(came, kept, came, links.planes * 2)
        self.state[k]["T"] = [
            links.send(over_y.at[links.plane(s)], over_planes.at[s - 1], links.plane_device(s))
            for s in range(1, links.planes)
        ]

    def T3(self, k):
        links = self.links
        _, _, _, _, _, _, over_y, over_planes, last, _, _, _ = self.pieces[k]
        arrived(self.state[k]["T"])
        for i in (1 - links.x, links.x):
            result = over_y[links.z, i].astype(jnp.float32)
            for s in range(1, links.planes):
                result = result + over_planes[s - 1, i].astype(jnp.float32)
            over_y[links.z, i] = result.astype(jnp.bfloat16)
        source = over_y.at[links.z, 1 - links.x]
        self.state[k]["T"] = [links.send(source, last, links.beside)]

    def T4(self, k):
        links = self.links
        _, _, _, start, _, _, over_y, _, last, _, _, _ = self.pieces[k]
        arrived(self.state[k]["T"])
        kept = over_y[links.z, links.x].astype(jnp.float32)
        self.put(k, start, kept + last[...].astype(jnp.float32))

    def F2(self, k):
        links = self.links
        x, y = links.x, links.y
        _, _, _, _, _, first, _, _, _, over_x, third, _ = self.pieces[k]
        arrived(self.state[k]["F"])
        for here in (1 - y, y):

            def kept(i, here=here):
                return first.at[i, here, x, :, pl.ds(HALF, HALF)]

            def came(i, here=here):
                return over_x.at[i, here]

            add_blocks(came, kept, came, links.planes)
            if here is not y:
                self.state[k]["F"] = [links.send(over_x.at[:, here], third, links.across)]

    def F3(self, k):
        links = self.links
        _, _, _, _, _, _, _, _, _, over_x, third, fourth = self.pieces[k]
        arrived(self.state[k]["F"])

        def kept(i):
            return over_x.at[i, links.y]

        def came(i):
            return third.at[i]

        add_blocks(came, kept, came, links.planes)
        self.state[k]["F"] = [
            links.send(third.at[links.plane(s)], fourth.at[s - 1], links.plane_device(s))
            for s in range(1, links.planes)
        ]

    def F4(self, k):
        links = self.links
        _, _, _, start, *_, third, fourth = self.pieces[k]
        arrived(self.state[k]["F"])
        result = third[links.z].astype(jnp.float32)
        for s in range(1, links.planes):
            result = result + fourth[s - 1].astype(jnp.float32)
        self.put(k, start + HALF, result)


def sums_order(count):
    order = []
    stages = (("core", 0), ("S1", 1), ("load", 0), ("T2", 2), ("F2", 2), ("T3", 3), ("F3", 3), ("T4", 4), ("F4", 4))
    for k in range(count + 4):
        for task, behind in stages:
            if 0 <= k - behind < count:
                order.append((task, k - behind))
    return order


MIDDLE_ORDER = (
    544, 576, 449, 577, 450, 578, 545, 384, 546, 224, 385, 547, 225, 480, 386, 226, 416, 352, 417,
    481, 353, 608, 640, 641, 354, 418, 672, 673, 642, 674,
)
BACK_ORDER = (
    704, 576, 449, 705, 577, 450, 706, 384, 224, 578, 451, 707, 579, 452, 385, 225, 736, 352, 416,
    580, 453, 708, 768, 226, 386, 417, 581, 709, 387, 800, 672, 640, 710, 353, 711, 388, 354, 801,
    832, 418, 737, 419, 833, 389, 420, 673, 864, 641, 642, 769, 834, 896, 674, 643, 644, 227, 929,
    228, 897, 229, 421, 865, 960, 930, 645, 355, 992, 1024, 961, 356, 675, 357, 1057, 993, 676,
    1058, 677, 1059,
)


class AttendSums:
    def __init__(self, links, grads, out, scratch):
        self.links, self.grads, self.out = links, grads, out
        self.own, self.over_y, self.over_planes, self.sum, self.held = scratch
        self.state = [dict() for _ in range(PAIRS)]
        self.columns = [pl.ds(pair * PAIR, PAIR) for pair in range(PAIRS)]

    def a0(self, k):
        links, columns = self.links, self.columns[k]
        source = self.grads.at[:, 1 - links.y, :, :, :, columns]
        self.state[k]["y"] = links.send(source, self.over_y.at[..., columns], links.across)
        source = self.grads.at[:, links.y, :, :, :, columns]
        self.state[k]["own"] = links.local(source, self.own.at[..., columns])

    def a1(self, k):
        links, own, over_y, columns = self.links, self.own, self.over_y, self.columns[k]
        self.state[k]["own"].wait()
        arrived([self.state[k]["y"]])
        for i in range(2):

            def block(ref, i=i):
                return lambda j: ref.at[j // 2, i, j % 2, :, columns]

            add_blocks(block(own), block(own), block(over_y), links.planes * 2)
        self.state[k]["planes"] = [
            links.send(
                own.at[links.plane(s), :, :, :, columns],
                self.over_planes.at[s - 1, :, :, :, columns],
                links.plane_device(s),
            )
            for s in range(1, links.planes)
        ]

    def a2(self, k):
        links, columns = self.links, self.columns[k]
        x, c = links.x, links.c
        arrived(self.state[k]["planes"])
        for i in range(2):
            for j in range(2):
                result = self.own[links.z, i, j, :, columns].astype(jnp.float32)
                for s in range(1, links.planes):
                    result = result + self.over_planes[s - 1, i, j, :, columns].astype(jnp.float32)
                self.sum[i, j, :, columns] = result
        self.state[k]["beside"] = links.send(
            self.sum.at[1 - x, :, :, columns], self.held.at[:, :, columns], links.beside
        )
        self.state[k]["near"] = links.send(
            self.sum.at[x, 1 - c, :, columns], self.out.at[x, c, :, columns], links.core
        )
        self.out[x, c, :, columns] = self.sum[x, c, :, columns]

    def a3(self, k):
        links, columns = self.links, self.columns[k]
        x, c = links.x, links.c
        arrived([self.state[k]["beside"]])
        self.out[1 - x, c, :, columns] = self.held[c, :, columns]
        self.state[k]["far"] = links.send(
            self.held.at[1 - c, :, columns], self.out.at[1 - x, c, :, columns], links.core
        )

    def finish(self):
        for state in self.state:
            arrived([state["near"], state["far"]])


class Spread:
    def __init__(self, links, ref):
        self.links, self.ref = links, ref

    def step(self, k):
        links, ref = self.links, self.ref
        z, y, x, c = links.z, links.y, links.x, links.c
        if k > 0:
            arrived(self.sent)
        if k == 0:
            block = ref.at[z, y, x, c]
            devices = [device for _, _, device in links.column()]
        elif k == 1:
            block, devices = ref.at[:, :, x, c], [links.beside, links.core]
        elif k == 2:
            block, devices = ref.at[:, :, 1 - x, c], [links.core]
        else:
            return
        self.sent = [links.send(block, block, device) for device in devices]


class TokenSums:
    def __init__(self, links, partial, scratch):
        self.links, self.partial = links, partial
        self.from_core, self.from_beside = scratch
        self.state = {}

    def start(self, m):
        links, partial = self.links, self.partial
        x, c = links.x, links.c
        self.state[m] = [
            links.send(partial.at[m, 1 - x, 1 - c], self.from_core.at[0, m], links.core),
            links.send(partial.at[m, x, 1 - c], self.from_core.at[1, m], links.core),
        ]

    def middle(self, m):
        links, partial = self.links, self.partial
        x, c = links.x, links.c
        arrived(self.state[m])
        away = partial.at[m, 1 - x, c]
        away[...] = (
            away[...].astype(jnp.float32) + self.from_core[0, m].astype(jnp.float32)
        ).astype(jnp.bfloat16)
        self.state[m] = [links.send(away, self.from_beside.at[m], links.beside)]

    def finish(self, m):
        links = self.links
        arrived(self.state[m])
        return (
            self.partial[m, links.x, links.c].astype(jnp.float32)
            + self.from_core[1, m].astype(jnp.float32)
            + self.from_beside[m].astype(jnp.float32)
        )


def sums_body(planes, kinds, *refs):
    attend, grads, refs = refs[0], refs[1 : 1 + kinds], refs[1 + kinds :]
    attend_out, outs, refs = refs[0], refs[1 : 1 + kinds], refs[1 + kinds :]
    links = Links(planes, *refs[:3])
    links.greet(links.partners())
    attend_sums = AttendSums(links, attend, attend_out, refs[3:8])
    for pair in range(PAIRS):
        for task in (attend_sums.a0, attend_sums.a1, attend_sums.a2, attend_sums.a3):
            task(pair)
    plan = [cuts(grad.shape[-2:]) for grad in grads]
    sums = Sums(links, grads, outs, plan, refs[8:])
    for task, k in sums_order(len(sums.pieces)):
        getattr(sums, task)(k)
    attend_sums.finish()
    links.finish_sends()


def middle_body(planes, *refs):
    grad_contract, expand, contract, project, act, slope, second, grad_branch, refs = *refs[:8], refs[8:]
    middle, attended, upstream, blended, modulation, bias_rows, refs = *refs[:6], refs[6:]
    contract_out, output, middle_grad_out, rows_out, bias_out, hidden_out, refs = *refs[:6], refs[6:]
    grad_expand, grad_project, grad_heads, refs = *refs[:3], refs[3:]
    links = Links(planes, *refs[:3])
    refs = refs[3:]
    plan = [cuts(grad_contract.shape[-2:])[:MIDDLE_PIECES]]
    used = scratch_count(plan)
    sum_scratch, refs = refs[:used], refs[used:]
    contract_held, expand_held, act_held, slope_held, second_held, second_t, refs = *refs[:6], refs[6:]
    branch_grad, grads, branch, grad_second, middle_held, attended_held, refs = *refs[:6], refs[6:]
    upstream_held, project_held, blended_held, attended_grad, project_grads, refs = *refs[:5], refs[5:]
    middle_grad, grad_blended = refs
    x, c = links.x, links.c
    corner = links.beside + 1 - 2 * c
    micros, own_rows, _ = second.shape
    parts = FF // WIDTH
    part_width = FF // parts
    contract_blocks = contract.shape[0] // parts

    def load(part):
        columns = pl.ds(part * part_width, part_width)
        slot = part % 2
        return [
            links.local(
                contract.at[pl.ds(part * contract_blocks, contract_blocks)], contract_held.at[slot]
            ),
            links.local(expand.at[:, :, :, :, :, columns], expand_held.at[slot]),
            links.local(act.at[:, :, columns], act_held.at[slot]),
            links.local(slope.at[:, :, columns], slope_held.at[slot]),
        ]

    loaded = links.local(second, second_held), links.local(grad_branch, branch_grad)
    loading = {0: load(0)}
    links.greet([*links.partners(), corner])
    sums = Sums(links, (grad_contract,), (contract_out,), plan, sum_scratch)
    for k in range(len(sums.pieces)):
        sums.core(k)
    sums.load(0)
    later = []
    for copy in loaded:
        copy.wait()
    for m in range(micros):
        second_t[:, m * own_rows : (m + 1) * own_rows] = second_held[m].T
    branch[...] = jnp.zeros_like(branch)
    grad_second[...] = jnp.zeros_like(grad_second)
    stored = []

    def mlp_unit(part):
        for copy in loading.pop(part):
            copy.wait()
        slot = part % 2
        if part == 0:
            loading[1] = load(1)
        if part == 1:
            later.extend(
                [
                    links.local(middle, middle_held),
                    links.local(attended, attended_held),
                    links.local(upstream, upstream_held),
                    links.local(project, project_held),
                    links.local(blended, blended_held),
                ]
            )
        if part >= 2:
            stored[part - 2].wait()
        contract_part(
            part * part_width,
            contract_held.at[slot],
            expand_held.at[slot],
            act_held.at[slot],
            slope_held.at[slot],
            second_t,
            branch_grad,
            grads.at[slot],
            branch,
            grad_second,
            hidden_out,
        )
        if part + 2 < parts:
            loading[part + 2] = load(part + 2)
        columns = pl.ds(part * part_width, part_width)
        stored.append(links.local(grads.at[slot], grad_expand.at[:, :, :, :, :, columns]))

    totals = [jnp.zeros((1, D), jnp.float32)] * 2

    def own_tokens(m):
        def vector(block):
            shift = bias_vector(bias_rows, 4 * D + FF + block * D, D)
            return modulation_row(modulation, m, block) + shift

        ahead = upstream_held[m].astype(jnp.float32)
        outward = branch[m] + bias_vector(bias_rows, 3 * D + FF, D)
        output[m] = (middle_held[m] + vector(5) * outward).astype(jnp.bfloat16)
        rows_out[m, 5:6, :] = jnp.sum(ahead * outward, axis=0, keepdims=True)
        normed, scale = normalize(middle_held[m])
        values = grad_second[m]
        rows_out[m, 3:4, :] = jnp.sum(values, axis=0, keepdims=True)
        rows_out[m, 4:5, :] = jnp.sum(values * normed, axis=0, keepdims=True)
        back = ahead + norm_back(values, normed, scale, vector(4))
        middle_grad[m] = back
        rows_out[m, 2:3, :] = jnp.sum(back * attended_held[m], axis=0, keepdims=True)
        lowered = (vector(2) * back).astype(jnp.bfloat16)
        attended_grad[m] = lowered
        totals[0] += jnp.sum(lowered.astype(jnp.float32), axis=0, keepdims=True)
        totals[1] += jnp.sum(branch_grad[m].astype(jnp.float32), axis=0, keepdims=True)
        product = lax.dot_general(
            lowered,
            project_held[...].reshape(D, D),
            (((1,), (1,)), ((), ())),
            preferred_element_type=jnp.float32,
        )
        grad_blended[m] = product.astype(jnp.bfloat16)
        here = pl.ds(pl.multiple_of((2 * x + c) * own_rows, own_rows), own_rows)

        def columns_of(to_x, to_c):
            start = pl.multiple_of((2 * to_x + to_c) * OWN, OWN)
            return grad_blended.at[m, :, pl.ds(start, OWN)]

        target = grad_heads.at[m, here]
        exchanged.append(links.send(columns_of(1 - x, 1 - c), target, corner))
        exchanged.append(links.send(columns_of(1 - x, c), target, links.beside))
        exchanged.append(links.send(columns_of(x, 1 - c), target, links.core))
        stored.append(links.local(columns_of(x, c), target))

    exchanged = []

    def project_unit():
        total = None
        for m in range(micros):
            product = lax.dot_general(
                blended_held[m],
                attended_grad[m],
                (((0,), (0,)), ((), ())),
                preferred_element_type=jnp.float32,
            )
            total = product if total is None else total + product
        project_grads[...] = total.astype(jnp.bfloat16).reshape(project_grads.shape)
        stored.append(links.local(project_grads, grad_project))
        stored.append(links.local(middle_grad, middle_grad_out))

    for task, k in tasks_of(MIDDLE_ORDER):
        if task == "mlp":
            mlp_unit(k)
        elif task == "own":
            if k == 0:
                for copy in later:
                    copy.wait()
            own_tokens(k)
        elif task == "project":
            project_unit()
        else:
            getattr(sums, task)(k)
    bias_out[0:1, :] = totals[0]
    bias_out[1:2, :] = totals[1]
    arrived(exchanged)
    for copy in stored[parts - 2 :]:
        copy.wait()
    links.finish_sends()


def contract_part(
    start,
    contract,
    expand,
    act,
    slope,
    second_t,
    grad_branch,
    grads,
    branch,
    grad_second,
    hidden_sums,
):
    micros = grad_branch.shape[0]
    blocks = CHUNK // contract.shape[1]

    @pl.loop(0, act.shape[-1] // CHUNK, unroll=True)
    def _(chunk):
        inside = pl.ds(pl.multiple_of(chunk * CHUNK, CHUNK), CHUNK)
        columns = pl.ds(pl.multiple_of(start + chunk * CHUNK, CHUNK), CHUNK)
        outward = contract[pl.ds(chunk * blocks, blocks)].reshape(CHUNK, D)
        inward = expand[:, :, :, :, :, inside].reshape(D, CHUNK)
        lows = []
        for m in range(micros):
            branch[m] += jnp.dot(act[m, :, inside], outward, preferred_element_type=jnp.float32)
            grad_act = lax.dot_general(
                grad_branch[m], outward, (((1,), (1,)), ((), ())), preferred_element_type=jnp.float32
            )
            lows.append((grad_act * slope[m, :, inside].astype(jnp.float32)).astype(jnp.bfloat16))
            grad_second[m] += lax.dot_general(
                lows[m], inward, (((1,), (1,)), ((), ())), preferred_element_type=jnp.float32
            )
        grad_hidden = jnp.concatenate(lows, axis=0)
        product = jnp.dot(second_t[...], grad_hidden, preferred_element_type=jnp.float32)
        grads[:, :, :, :, :, inside] = product.astype(jnp.bfloat16).reshape(
            *grads.shape[:-1], CHUNK
        )
        hidden_sums[:, columns] = jnp.sum(
            grad_hidden.astype(jnp.float32), axis=0, keepdims=True
        )


def back_body(planes, *refs):
    grad_contract, grad_expand, grad_project, grad_heads, refs = *refs[:4], refs[4:]
    qkv, heads, logs, normed, attend, refs = *refs[:5], refs[5:]
    tokens, middle_grad, modulation, bias_rows, row_sums, bias_sums, hidden_sums, refs = *refs[:7], refs[7:]
    cond, modulate, refs = *refs[:2], refs[2:]
    attend_flat, contract_out, expand_out, project_out, tokens_out, refs = *refs[:5], refs[5:]
    sums_out, modulate_out, cond_out, refs = *refs[:3], refs[3:]
    links = Links(planes, *refs[:3])
    attend_held_scratch, refs = refs[3:8], refs[8:]
    all_grads = (grad_contract, grad_expand, grad_project)
    plan = back_plan(all_grads)
    used = scratch_count(plan)
    sum_scratch, refs = refs[:used], refs[used:]
    grads_held, qkv_held, heads_held, normed_held, attend_held, grad_qkv, refs = *refs[:6], refs[6:]
    key_sum, value_sum, attend_grads, partial, from_core, from_beside, refs = *refs[:6], refs[6:]
    tokens_held, middle_held, scales, head_sums, row_held, small, refs = *refs[:6], refs[6:]
    small_core, small_beside, modulations, attend_out = refs
    micros, latent_rows, _ = qkv.shape
    loads = {
        "heads": [
            links.local(qkv, qkv_held),
            links.local(grad_heads, grads_held),
            links.local(heads, heads_held),
        ],
    }

    def need(*names):
        for name in names:
            for copy in loads.pop(name, ()):
                copy.wait()

    links.greet(links.partners())
    z, y, x, c = links.z, links.y, links.x, links.c
    outs = (contract_out, expand_out, project_out)
    sums = Sums(links, all_grads, outs, plan, sum_scratch)
    for k in range(len(sums.pieces)):
        sums.core(k)
    sums.load(0)
    attend_sums = AttendSums(links, attend_grads, attend_out, attend_held_scratch)
    token_sum = TokenSums(links, partial, (from_core, from_beside))
    spread_sums, spread_cond = Spread(links, sums_out), Spread(links, cond_out)
    sent = {}

    def vector(m, block):
        shift = bias_vector(bias_rows, 4 * D + FF + block * D, D)
        return modulation_row(modulation, m, block) + shift

    scale_rows = []
    for m in range(micros):
        scale_rows += [1.0 + vector(m, 1), vector(m, 0)]
    scale_rows.append(jnp.zeros((8 - 2 * micros, D), jnp.float32))
    scales[...] = jnp.concatenate(scale_rows, axis=0).T

    def head_unit(m, head):
        if m == 0 and head == 0:
            need("heads")
            loads["attend"] = [links.local(attend, attend_held)]
            loads["normed"] = [links.local(normed, normed_held)]
            loads["tokens"] = [
                links.local(tokens, tokens_held),
                links.local(middle_grad, middle_held),
            ]
        attention_back_unit(
            qkv_held.at[m],
            heads_held.at[m],
            grads_held.at[m],
            logs.at[m],
            grad_qkv.at[m],
            key_sum,
            value_sum,
            head,
        )

    def tokens_unit(m):
        grads = token_sum.finish(m)
        need("tokens")
        normed_own, scale = normalize(tokens_held[m].astype(jnp.float32))
        tokens_out[m] = middle_held[m] + norm_back(grads, normed_own, scale, vector(m, 1))

    def small_start():
        highs = head_sums[...].astype(jnp.bfloat16)
        lows = (head_sums[...] - highs.astype(jnp.float32)).astype(jnp.bfloat16)
        product = lax.dot_general(
            jnp.concatenate([highs, lows], axis=0),
            attend_held[...].reshape(D, 3 * OWN),
            (((1,), (1,)), ((), ())),
            preferred_element_type=jnp.float32,
        )
        each = D // LANES
        per_quarter = 6 * each // GROUP
        for m in range(micros):
            blocks = [product[m : m + 1] + product[8 + m : 9 + m], row_held[m : m + 1, :]]
            blocks += [row_sums[m, block : block + 1, :] for block in range(2, 6)]
            for k in range(6 * each):
                quarter, row = k // per_quarter, m * per_quarter + k % per_quarter
                lanes = slice(k % each * LANES, (k % each + 1) * LANES)
                small[quarter // 2, quarter % 2, row : row + 1, :] = blocks[k // each][:, lanes]
        start = micros * per_quarter
        biases = {2: bias_sums[0:1, :], 7: bias_sums[1:2, :]}
        for k in range(FF // D):
            biases[3 + k] = hidden_sums[:, k * D : (k + 1) * D]
        each_quarter = 8 * each // GROUP
        small[0, 0, start:, :] = jnp.zeros((small.shape[2] - start, LANES), jnp.float32)
        for k in range(2 * each, 8 * each):
            quarter, row = k // each_quarter, start + k % each_quarter
            lanes = slice(k % each * LANES, (k % each + 1) * LANES)
            small[quarter // 2, quarter % 2, row : row + 1, :] = biases[k // each][:, lanes]
        for m in range(1, micros):
            head_sums[0:1, :] += head_sums[m : m + 1, :]
        for pair in range(PAIRS):
            for kind, first_row in ((0, start), (2, start + each)):
                lanes = pl.ds(pair * PAIR + kind * LANES, LANES)
                row = first_row + (2 * x + c) * PAIRS + pair
                small[0, 0, pl.ds(row, 1), :] = head_sums[0:1, lanes]
        sent["small"] = links.send(small.at[:, 1 - c], small_core, links.core)

    def small_core_sum():
        arrived([sent["small"]])
        small_core[...] = small_core[...] + small[:, c]
        sent["small"] = links.send(small_core.at[1 - x], small_beside, links.beside)

    def small_beside_sum():
        arrived([sent["small"]])
        sums_out[z, y, x, c] = small_core[x] + small_beside[...]
        spread_sums.step(0)

    def modulate_unit():
        spread_sums.step(3)
        latents = planes * 2
        per_quarter = 6 * D // LANES // GROUP
        for m in range(micros):
            for k in range(6 * D // LANES):
                quarter, row = k // per_quarter, m * per_quarter + k % per_quarter
                values = sums_out[:, :, quarter // 2, quarter % 2, row, :].reshape(latents, LANES)
                here = slice(m * latents, (m + 1) * latents)
                modulations[here, k * LANES : (k + 1) * LANES] = values
        grads = lax.dot_general(
            cond[...],
            modulations[...],
            (((0,), (0,)), ((), ())),
            precision=highest,
            preferred_element_type=jnp.float32,
        )
        stride = 6 * D // LANES
        for k in range(stride):
            lanes = slice(k * LANES, (k + 1) * LANES)
            modulate_out[pl.ds(k, grads.shape[0], stride=stride), :] = grads[:, lanes]
        product = lax.dot_general(
            modulations[...],
            modulate[...].astype(jnp.float32),
            (((1,), (1,)), ((), ())),
            precision=highest,
            preferred_element_type=jnp.float32,
        )
        cond_out[z, y, x, c] = jnp.zeros(cond_out.shape[4:], jnp.float32)
        cond_out[z, y, x, c, :, : product.shape[1]] = product
        spread_cond.step(0)

    heads_each = OWN // HEAD
    for task, k in tasks_of(BACK_ORDER):
        if task == "head":
            head_unit(k // heads_each, k % heads_each)
        elif task == "first":
            need("attend")
            first_product(k, grad_qkv, attend_held, partial)
            token_sum.start(k)
        elif task == "attend":
            need("attend", "normed")
            attend_product(
                k, normed_held, grad_qkv, attend_held, scales, head_sums, row_held, attend_grads
            )
            attend_sums.a0(k)
        elif task == "t1":
            token_sum.middle(k)
        elif task == "t2":
            tokens_unit(k)
        elif task in ("a1", "a2", "a3"):
            getattr(attend_sums, task)(k)
        elif task == "small":
            (small_start, small_core_sum, small_beside_sum)[k]()
        elif task == "sums":
            spread_sums.step(k)
        elif task == "modulate":
            modulate_unit()
        elif task == "cond":
            spread_cond.step(k)
        else:
            getattr(sums, task)(k)
    attend_sums.finish()
    count, stride = attend_out.shape[2], 3 * D // LANES
    for quarter in range(GROUP):
        for kind in range(3):
            for pair in range(PAIRS):
                lanes = pl.ds((pair * 3 + kind) * LANES, LANES)
                where = (kind * GROUP + quarter) * PAIRS + pair
                attend_flat[pl.ds(where, count, stride=stride), :] = attend_out[
                    quarter // 2, quarter % 2, :, lanes
                ]
    links.finish_sends()


def back_plan(grads):
    plan = [cuts(grad.shape[-2:]) for grad in grads]
    plan[0] = plan[0][MIDDLE_PIECES:]
    return plan


def attend_product(pair, normed, grad_qkv, attend, scales, head_sums, row_held, out):
    planes = attend.shape[0]
    width = D // planes
    micros = normed.shape[0]
    columns = pl.ds(pair * PAIR, PAIR)
    totals = [
        jnp.sum(grad_qkv[m, :, columns].astype(jnp.float32), axis=0, keepdims=True)
        for m in range(micros)
    ]
    head_sums[:, columns] = jnp.concatenate(
        [*totals, jnp.zeros((8 - micros, PAIR), jnp.float32)], axis=0
    )

    @pl.loop(0, planes)
    def _(plane):
        here = pl.ds(pl.multiple_of(plane * width, width), width)
        weights = attend[plane, :, :, :, :, columns].reshape(width, PAIR).astype(jnp.float32)
        total = jnp.zeros((width, PAIR), jnp.float32)
        for m in range(micros):
            product = lax.dot_general(
                normed[m, :, here],
                grad_qkv[m, :, columns],
                (((0,), (0,)), ((), ())),
                preferred_element_type=jnp.float32,
            )
            total = total + product * scales[here, 2 * m : 2 * m + 1]
            total = total + scales[here, 2 * m + 1 : 2 * m + 2] * totals[m]
            row = jnp.sum((weights * product).T, axis=0, keepdims=True)
            if pair == 0:
                row_held[m : m + 1, here] = row
            else:
                row_held[m : m + 1, here] += row
        out[plane, :, :, :, :, columns] = total.astype(jnp.bfloat16).reshape(
            *out.shape[1:-1], PAIR
        )


def first_product(m, grad_qkv, attend, partial):
    rows = partial.shape[3]

    @pl.loop(0, GROUP, unroll=2)
    def _(block):
        here = pl.ds(pl.multiple_of(block * rows, rows), rows)
        product = lax.dot_general(
            grad_qkv[m, here, :],
            attend[...].reshape(D, 3 * OWN),
            (((1,), (1,)), ((), ())),
            preferred_element_type=jnp.float32,
        )
        partial[m, block // 2, block % 2] = product.astype(jnp.bfloat16)


def attend_scratch(attend, planes):
    rows, width = attend.shape[-2:]
    return [
        pltpu.VMEM((planes, 2, 2, rows, width), jnp.bfloat16),
        pltpu.VMEM((planes, 2, 2, rows, width), jnp.bfloat16),
        pltpu.VMEM((planes - 1, 2, 2, rows, width), jnp.bfloat16),
        pltpu.VMEM((2, 2, rows, width), jnp.float32),
        pltpu.VMEM((2, rows, width), jnp.float32),
    ]


def sum_scratch(plan, planes):
    held = []
    for pieces in plan:
        rows = pieces[0][1]
        held.append(low_held(planes, 2, 2, rows, WIDTH))
        for _ in pieces:
            held += [
                low_held(planes, 2, 2, rows, WIDTH),
                low_held(planes, 2, rows, HALF),
                low_held(planes - 1, 2, rows, HALF),
                low_held(rows, HALF),
                low_held(planes, 2, rows, HALF),
                low_held(planes, rows, HALF),
                low_held(planes - 1, rows, HALF),
            ]
    return held


def count_pieces(plan):
    return sum(len(pieces) for pieces in plan)


def scratch_count(plan):
    return len(plan) + 7 * count_pieces(plan)


def flat_shape(count):
    return full_shape(count // LANES, LANES)


def full_shape(*shape):
    return jax.ShapeDtypeStruct(shape, jnp.float32)


def low_shape(*shape):
    return jax.ShapeDtypeStruct(shape, jnp.bfloat16)


def full_held(*shape):
    return pltpu.VMEM(shape, jnp.float32)


def low_held(*shape):
    return pltpu.VMEM(shape, jnp.bfloat16)


def sum_sems(plan, planes):
    return count_pieces(plan) * (4 + 2 * planes)


def weight_sums(attend, weights, planes):
    plan = [cuts(grad.shape[-2:]) for grad in weights]
    flats = [flat_shape(grad.shape[-2] * grad.shape[-1]) for grad in weights]
    return remote_call(
        functools.partial(sums_body, planes, len(weights)),
        "weight_sums",
        6,
        (full_shape(2, 2, *attend.shape[-2:]), *flats),
        [ANY] * (1 + len(weights)),
        (VMEM,) * (1 + len(weights)),
        [*attend_scratch(attend, planes), *sum_scratch(plan, planes)],
        8 + 2 * planes + sum_sems(plan, planes),
        4 + count_pieces(plan),
        60 * MIB,
    )(attend, *weights)


def middle_part(grad_contract, weights, held, vectors, planes):
    expand, contract, project = weights
    second = held[2]
    micros, own_rows, _ = second.shape
    own = second.shape
    shape = grad_contract.shape[-2:]
    plan = [cuts(shape)[:MIDDLE_PIECES]]
    width = WIDTH
    blocks = width // shape[0]
    return remote_call(
        functools.partial(middle_body, planes),
        "middle",
        6,
        (
            flat_shape(len(plan[0]) * plan[0][0][1] * D),
            low_shape(*own),
            full_shape(*own),
            full_shape(micros, 8, D),
            full_shape(8, D),
            full_shape(1, FF),
            low_shape(*expand.shape),
            low_shape(*project.shape),
            low_shape(micros, own_rows * GROUP, OWN),
        ),
        [ANY] * 12 + [VMEM] * 2,
        (VMEM, VMEM, ANY) + (VMEM,) * 3 + (ANY,) * 3,
        [
            *sum_scratch(plan, planes),
            low_held(2, blocks, *shape),
            low_held(2, *expand.shape[:-1], width),
            low_held(2, micros, own_rows, width),
            low_held(2, micros, own_rows, width),
            low_held(*own),
            low_held(D, micros * own_rows),
            low_held(*own),
            low_held(2, *expand.shape[:-1], width),
            full_held(*own),
            full_held(*own),
            full_held(*own),
            full_held(*own),
            low_held(*own),
            low_held(*project.shape),
            low_held(*own),
            low_held(*own),
            low_held(*project.shape),
            full_held(*own),
            low_held(*own),
        ],
        8 + sum_sems(plan, planes),
        48,
        63 * MIB,
    )(
        grad_contract,
        expand,
        contract.reshape(FF // shape[0], *shape),
        project,
        *held,
        *vectors,
    )


def back_part(grads, grad_heads, held, vectors, planes):
    qkv, heads, logs, normed, attend, tokens, middle_grad = held
    plan = back_plan(grads)
    micros, latent_rows, width = qkv.shape
    own = tokens.shape
    small = (micros * 6 + 8) * D // LANES // GROUP
    cond, modulate = vectors[-2:]
    return remote_call(
        functools.partial(back_body, planes),
        "back",
        7,
        (
            flat_shape(GROUP * attend.shape[-2] * attend.shape[-1]),
            *(
                flat_shape(len(pieces) * pieces[0][1] * WIDTH)
                for pieces in plan
            ),
            full_shape(*own),
            full_shape(planes, 2, 2, 2, small, LANES),
            flat_shape(modulate.shape[0] * modulate.shape[1]),
            full_shape(planes, 2, 2, 2, cond.shape[0], LANES),
        ),
        [ANY] * 6 + [VMEM] + [ANY] * 4 + [VMEM] * 7,
        (VMEM,) * 8,
        [
            *attend_scratch(attend, planes),
            *sum_scratch(plan, planes),
            low_held(*grad_heads.shape),
            low_held(*qkv.shape),
            low_held(*heads.shape),
            low_held(*normed.shape),
            low_held(*attend.shape),
            low_held(*qkv.shape),
            full_held(latent_rows, HEAD),
            full_held(latent_rows, HEAD),
            low_held(*attend.shape),
            low_held(micros, 2, 2, *own[1:]),
            low_held(2, *own),
            low_held(*own),
            low_held(*own),
            full_held(*own),
            full_held(D, 8),
            full_held(8, width),
            full_held(8, D),
            full_held(2, 2, small, LANES),
            full_held(2, small, LANES),
            full_held(small, LANES),
            full_held(cond.shape[0], modulate.shape[1]),
            full_held(2, 2, *attend.shape[-2:]),
        ],
        40 + 8 * planes + sum_sems(plan, planes),
        12 + count_pieces(plan),
        63 * MIB,
    )(*grads, grad_heads, *held, *vectors)


def normalize(values):
    center = values - jnp.mean(values, axis=-1, keepdims=True)
    spread_of = jnp.mean(center * center, axis=-1, keepdims=True)
    scale = lax.rsqrt(spread_of + epsilon)
    return center * scale, scale


def norm_back(grads, normed, scale, factors):
    inner = grads * (1.0 + factors)
    return scale * (
        inner
        - jnp.mean(inner, axis=-1, keepdims=True)
        - normed * jnp.mean(inner * normed, axis=-1, keepdims=True)
    )


def einsum(spec, left, right):
    return jnp.einsum(spec, left, right, preferred_element_type=jnp.float32)


def per_device(tokens, condition, attend, project, expand, contract, modulate, biases, cotangent):
    devices = lax.axis_size("fsdp")
    planes = devices // 8
    latents = devices // GROUP
    me = lax.axis_index("fsdp")
    quarter, latent = me % GROUP, me // GROUP
    micros, own_rows, _ = tokens.shape
    latent_rows = own_rows * GROUP
    rows = D // devices
    grid = (planes, 2, 2, 2)

    fused = rows % 16 == 0 and own_rows % QUERY_ROWS == 0 and biases.size == 7 * LANES // 2
    inputs = tokens.astype(jnp.float32)
    if fused:
        half = LANES // 2
        spread_cond = condition.astype(jnp.float32).reshape(micros, -1, rows).transpose(1, 0, 2)
        spread_cond = spread_cond.reshape(-1, rows)
        spread_cond = jnp.pad(spread_cond, ((0, 0), (0, LANES - rows)))
        own_biases = biases.astype(jnp.float32)
        own_biases = jnp.where(
            me % 2 == 0, jnp.pad(own_biases, (0, half)), jnp.pad(own_biases, (half, 0))
        )
        payload = jnp.concatenate([spread_cond, own_biases.reshape(-1, LANES)])
        payload = jnp.pad(payload, ((0, -payload.shape[0] % 8), (0, 0)))
        flats = [shard.reshape(-1, LANES) for shard in (attend, project, expand, contract)]
        attend_all, project_all, expand_all, contract_all, modulation_all, *rest = front(
            tokens, *flats, payload, modulate.reshape(-1, LANES), cotangent, planes
        )
        *rest, bias_rows, cond_own, modulate_rows = rest
        normed, projected, heads, logs, blended, middle, attended, second, act, slope, low, grads = rest
        grad_contract = grads.reshape(*grid, FF // devices, D)
        contract_first, output, grad_middle, row_sums, bias_sums, hidden_sums, *onward = middle_part(
            grad_contract,
            (expand_all, contract_all, project_all),
            (act, slope, second, low, middle, attended, cotangent, blended),
            (modulation_all, bias_rows),
            planes,
        )
        grad_expand, grad_project, grad_heads = onward
        attend_sum, contract_rest, expand_sum, project_sum, grad_tokens, *onward = back_part(
            (grad_contract, grad_expand, grad_project),
            grad_heads,
            (projected, heads, logs, normed, attend_all, tokens, grad_middle),
            (
                modulation_all,
                bias_rows,
                row_sums,
                bias_sums,
                hidden_sums,
                cond_own,
                modulate_rows,
            ),
            planes,
        )
        contract_sum = jnp.concatenate([contract_first, contract_rest])
        sums, grad_modulate, cond_cols = onward
        sums = sums.reshape(latents, GROUP, -1)
        split = micros * 6 * D // GROUP
        cond_cols = cond_cols[..., :rows].reshape(devices, micros, latents, rows)
    else:
        modulate_rows = modulate.reshape(rows, 6 * D)
        attend_shard = attend.reshape(rows, 3, 2, 2, PAIRS, LANES).transpose(2, 3, 0, 4, 1, 5)
        shards = (
            tokens,
            attend_shard.reshape(2, 2, rows, 3 * OWN),
            project.reshape(rows, D),
            expand.reshape(rows, FF),
            contract.reshape(FF // devices, D),
        )
        held = jnp.concatenate([condition.reshape(-1), biases]).astype(jnp.float32)
        held = jnp.pad(held, (0, -held.size % (8 * LANES)))
        small = small_gather(held.reshape(-1, LANES), planes, 0).reshape(devices, -1)
        conditions = small[:, : condition.size].reshape(latents, GROUP, micros, -1)
        conditions = conditions.transpose(2, 0, 1, 3).reshape(micros * latents, D)
        cond_act = silu(conditions).astype(jnp.bfloat16)
        bias_all = small[:, condition.size : condition.size + biases.size].reshape(-1)
        bias_query = bias_all[0:D]
        bias_value = bias_all[D : 2 * D]
        bias_project = bias_all[2 * D : 3 * D]
        bias_expand = bias_all[3 * D : 3 * D + FF]
        bias_contract = bias_all[3 * D + FF : 4 * D + FF]
        bias_modulate = bias_all[4 * D + FF :]

        cond_own = lax.dynamic_slice_in_dim(cond_act, me * rows, rows, axis=1)
        partial = jnp.dot(cond_own, modulate_rows, preferred_element_type=jnp.float32)
        partial = partial.reshape(micros, latents, GROUP, -1).transpose(1, 2, 0, 3)
        partial = partial.reshape(planes, 2, 2, 2, -1, LANES)

        bias_row = jnp.concatenate(
            [
                lax.dynamic_slice_in_dim(bias_query, quarter * OWN, OWN),
                jnp.zeros((OWN,), jnp.float32),
                lax.dynamic_slice_in_dim(bias_value, quarter * OWN, OWN),
            ]
        )
        bias_row = bias_row.reshape(3, PAIRS, LANES).transpose(1, 0, 2).reshape(-1)
        attend_all, project_all, expand_all, contract_all, modulation_all, *rest = gather_all(
            *shards, partial, planes
        )
        modulation = modulation_all.reshape(GROUP, micros, -1).transpose(1, 0, 2)
        modulation = modulation.reshape(micros, 6 * D) + bias_modulate
        offsets_one, factors_one, gates_one, offsets_two, factors_two, gates_two = (
            modulation[:, None, part * D : (part + 1) * D] for part in range(6)
        )
        attend_own = attend_all.reshape(D, 3 * OWN)
        project_full = project_all.reshape(D, D)
        expand_full = expand_all.reshape(D, FF)
        contract_full = contract_all.reshape(FF, D)
        tokens_latent = rest[0].reshape(micros, latent_rows, D)
        normed_latent, _ = normalize(tokens_latent.astype(jnp.float32))
        first = (normed_latent * (1.0 + factors_one) + offsets_one).astype(jnp.bfloat16)
        projected = (einsum("mrd,de->mre", first, attend_own) + bias_row).astype(jnp.bfloat16)
        blended_heads, logs = attention(projected)
        blended = heads_to_tokens(blended_heads)

        attended = einsum("mrd,de->mre", blended, project_full) + bias_project
        middle = inputs + gates_one * attended
        normed_two, scale_two = normalize(middle)
        second = (normed_two * (1.0 + factors_two) + offsets_two).astype(jnp.bfloat16)
        hidden = einsum("mrd,de->mre", second, expand_full) + bias_expand
        activated, gelu_pull = jax.vjp(lambda v: jax.nn.gelu(v, approximate=True), hidden)
        act_low = activated.astype(jnp.bfloat16)
        branch = einsum("mrd,de->mre", act_low, contract_full) + bias_contract
        output = (middle + gates_two * branch).astype(jnp.bfloat16)

        upstream = cotangent.astype(jnp.float32)
        grad_branch = (gates_two * upstream).astype(jnp.bfloat16)
        grad_contract = einsum("mrd,mre->de", act_low, grad_branch)
        grad_act = einsum("mre,de->mrd", grad_branch, contract_full)
        grad_hidden = gelu_pull(grad_act)[0].astype(jnp.bfloat16)
        grad_expand = einsum("mrd,mre->de", second, grad_hidden)
        grad_second = einsum("mre,de->mrd", grad_hidden, expand_full)
        grad_middle = upstream + norm_back(grad_second, normed_two, scale_two, factors_two)
        grad_attended = (gates_one * grad_middle).astype(jnp.bfloat16)
        grad_project = einsum("mrd,mre->de", blended, grad_attended)
        grad_blended = einsum("mre,de->mrd", grad_attended, project_full).astype(jnp.bfloat16)
        grad_heads = tokens_to_heads(grad_blended)
        grad_projected = attention_back(projected, blended_heads, grad_heads, logs)
        grad_attend = einsum("mrd,mre->de", first, grad_projected)
        grad_first = token_sums(
            einsum("mre,de->mrd", grad_projected, attend_own).astype(jnp.bfloat16)
        )
        weights = (
            grad_contract.astype(jnp.bfloat16).reshape(*grid, FF // devices, D),
            grad_expand.astype(jnp.bfloat16).reshape(*grid, rows, FF),
            grad_project.astype(jnp.bfloat16).reshape(*grid, rows, D),
        )
        attend_sum, contract_sum, expand_sum, project_sum = weight_sums(
            grad_attend.astype(jnp.bfloat16).reshape(*grid, rows, 3 * OWN), weights, planes
        )
        attend_sum = attend_sum.reshape(2, 2, rows, PAIRS, 3, LANES).transpose(2, 4, 0, 1, 3, 5)

        def token_sum(values):
            return jnp.sum(values, axis=(0, 1), dtype=jnp.float32)

        heads_sum, attended_sum = token_sum(grad_projected), token_sum(grad_attended)
        hidden_sum, branch_sum = token_sum(grad_hidden), token_sum(grad_branch)
        later_sums = jnp.concatenate(
            [
                jnp.sum(grad_middle * attended, axis=1),
                jnp.sum(grad_second, axis=1),
                jnp.sum(grad_second * normed_two, axis=1),
                jnp.sum(upstream * branch, axis=1),
            ],
            axis=1,
        )
        normed_one, scale_one = normalize(inputs)
        grad_tokens = grad_middle + norm_back(grad_first, normed_one, scale_one, factors_one)

        grad_modulation = jnp.concatenate(
            [jnp.sum(grad_first, axis=1), jnp.sum(grad_first * normed_one, axis=1), later_sums], axis=1
        )
        heads_sum = heads_sum.reshape(PAIRS, 3, LANES).transpose(1, 0, 2).reshape(3, OWN)
        bias_terms = jnp.concatenate(
            [
                lax.dynamic_update_slice(
                    jnp.zeros((D,), jnp.float32), heads_sum[0], (quarter * OWN,)
                ),
                lax.dynamic_update_slice(
                    jnp.zeros((D,), jnp.float32), heads_sum[2], (quarter * OWN,)
                ),
                attended_sum,
                hidden_sum,
                branch_sum,
            ]
        )
        to_sum = jnp.concatenate(
            [
                grad_modulation.reshape(micros, GROUP, -1).transpose(1, 0, 2).reshape(GROUP, -1),
                bias_terms.reshape(GROUP, -1),
            ],
            axis=1,
        )
        sums = small_sums(to_sum.reshape(2, 2, -1, LANES), planes).reshape(latents, GROUP, -1)
        split = micros * 6 * D // GROUP
        grad_modulations = sums[:, :, :split].reshape(latents, GROUP, micros, -1)
        grad_modulations = grad_modulations.transpose(2, 0, 1, 3).reshape(micros * latents, 6 * D)
        grad_modulate = lax.dot_general(
            cond_own.astype(jnp.float32),
            grad_modulations,
            (((0,), (0,)), ((), ())),
            precision=highest,
        )
        grad_cond_cols = lax.dot_general(
            grad_modulations,
            modulate_rows.astype(jnp.float32),
            (((1,), (1,)), ((), ())),
            precision=highest,
        )
        cols = grad_cond_cols.reshape(-1)
        cols = jnp.pad(cols, (0, -cols.size % (8 * LANES)))
        cond_cols = small_gather(cols.reshape(-1, LANES), planes, 8).reshape(devices, -1)
        cond_cols = cond_cols[:, : micros * latents * rows].reshape(devices, micros, latents, rows)
    grad_modulations = sums[:, :, :split].reshape(latents, GROUP, micros, -1)
    grad_modulations = grad_modulations.transpose(2, 0, 1, 3).reshape(micros * latents, 6 * D)
    bias_sums = jnp.concatenate(
        [jnp.sum(sums[:, :, split:], axis=0).reshape(-1), jnp.sum(grad_modulations, axis=0)]
    )
    grad_biases = lax.dynamic_slice_in_dim(bias_sums, me * biases.size, biases.size)
    cols_own = lax.dynamic_index_in_dim(cond_cols, latent, axis=2, keepdims=False)
    width = D // GROUP
    cols_own = lax.dynamic_slice_in_dim(
        cols_own, quarter * (devices // GROUP), devices // GROUP, axis=0
    )
    grad_silu = cols_own.transpose(1, 0, 2).reshape(micros, width)
    values = condition.astype(jnp.float32)
    gate = 1.0 / (1.0 + jnp.exp(-values))
    grad_condition = gate * (1.0 + values * (1.0 - gate)) * grad_silu

    return (
        output,
        grad_tokens,
        grad_condition,
        attend_sum.reshape(-1),
        project_sum.reshape(-1),
        expand_sum.reshape(-1),
        contract_sum.reshape(-1),
        grad_modulate.reshape(-1),
        grad_biases,
    )


def solution(mesh):
    in_specs = (
        P(None, "fsdp", None),
        P(None, "fsdp"),
        P("fsdp"),
        P("fsdp"),
        P("fsdp"),
        P("fsdp"),
        P("fsdp"),
        P("fsdp"),
        P(None, "fsdp", None),
    )
    out_specs = (
        P(None, "fsdp", None),
        P(None, "fsdp", None),
        P(None, "fsdp"),
        P("fsdp"),
        P("fsdp"),
        P("fsdp"),
        P("fsdp"),
        P("fsdp"),
        P("fsdp"),
    )
    return jax.shard_map(
        per_device, mesh=mesh, in_specs=in_specs, out_specs=out_specs, check_vma=False
    )
```

```python
import functools

import jax
import jax.numpy as jnp
from jax import lax
from jax.experimental import pallas as pl
from jax.experimental.pallas import tpu as pltpu
from jax.sharding import PartitionSpec as P

D = 1024
HEADS = 16
HEAD = 64
FF = 4096
GROUP = 4
OWN = D // GROUP
SCALE = HEAD**-0.5
LANES = 128
MICROS = 2

epsilon = 1e-06
highest = lax.Precision.HIGHEST
MESH = pl.DeviceIdType.MESH
MIB = 1 << 20


def silu(values):
    return values / (1.0 + jnp.exp(-values))


class Links:
    def __init__(self, planes, send_sem, recv_sem, local_sem=None):
        me = lax.axis_index("fsdp")
        self.planes = planes
        self.c = me % 2
        self.x = (me // 2) % 2
        self.y = (me // 4) % 2
        self.z = me // 8
        self.core = me + 1 - 2 * self.c
        self.beside = me + 2 - 4 * self.x
        self.across = me + 4 - 8 * self.y
        self.place = me % 8
        self.send_sem, self.recv_sem, self.local_sem = send_sem, recv_sem, local_sem
        self.used = 0
        self.local_used = 0
        self.pending = []

    def plane(self, step):
        return (self.z + step) % self.planes

    def plane_device(self, step):
        return self.plane(step) * 8 + self.place

    def column(self):
        places = []
        for step in range(self.planes):
            for y in (self.y, 1 - self.y):
                if step > 0 or y is not self.y:
                    z = self.plane(step)
                    places.append((z, y, z * 8 + y * 4 + self.place % 4))
        return places

    def partners(self):
        return [self.core, self.beside] + [device for _, _, device in self.column()]

    def greet(self, partners, meanwhile=None):
        barrier = pltpu.get_barrier_semaphore()
        for partner in partners:
            pl.semaphore_signal(barrier, inc=1, device_id=(partner,), device_id_type=MESH)
        if meanwhile is not None:
            meanwhile()
        pl.semaphore_wait(barrier, len(partners))

    def send(self, source, target, device):
        assert self.used < self.send_sem.shape[0]
        copy = pltpu.make_async_remote_copy(
            src_ref=source,
            dst_ref=target,
            send_sem=self.send_sem.at[self.used],
            recv_sem=self.recv_sem.at[self.used],
            device_id=(device,),
            device_id_type=MESH,
        )
        self.used += 1
        copy.start()
        self.pending.append(copy)
        return copy

    def local(self, source, target):
        assert self.local_used < self.local_sem.shape[0]
        copy = pltpu.make_async_copy(source, target, self.local_sem.at[self.local_used])
        self.local_used += 1
        copy.start()
        return copy

    def finish_sends(self):
        for copy in self.pending:
            copy.wait_send()
        self.pending = []


def arrived(copies):
    for copy in copies:
        copy.wait_recv()


ANY = pl.BlockSpec(memory_space=pl.ANY)
VMEM = pl.BlockSpec(memory_space=pltpu.VMEM)


def remote_call(body, name, collective_id, outs, in_specs, out_specs, scratch, sems, local_sems, vmem):
    return pl.pallas_call(
        body,
        out_shape=outs,
        in_specs=in_specs,
        out_specs=out_specs,
        scratch_shapes=[
            pltpu.SemaphoreType.DMA((sems,)),
            pltpu.SemaphoreType.DMA((sems,)),
            pltpu.SemaphoreType.DMA((max(local_sems, 1),)),
            *scratch,
        ],
        compiler_params=pltpu.CompilerParams(
            collective_id=collective_id, has_side_effects=True, vmem_limit_bytes=vmem
        ),
        name=name,
    )


def small_gather_body(planes, own_ref, out_ref, send_sem, recv_sem, local_sem):
    links = Links(planes, send_sem, recv_sem)
    links.greet(links.partners())
    z, y, x, c = links.z, links.y, links.x, links.c
    out_ref[z, y, x, c] = own_ref[...]
    spread_all(links, out_ref)
    links.finish_sends()


def spread_all(links, out_ref):
    spread = Spread(links, out_ref)
    for k in range(4):
        spread.step(k)


def small_gather(own, planes, collective_id):
    return remote_call(
        functools.partial(small_gather_body, planes),
        "small_gather",
        collective_id,
        jax.ShapeDtypeStruct((planes, 2, 2, 2, *own.shape), own.dtype),
        [VMEM],
        VMEM,
        [],
        2 * planes + 4,
        0,
        40 * MIB,
    )(own)


WIDTH = 1024
HALF = WIDTH // 2
ALL = slice(None)


class Pieces:
    def __init__(self, links, shards, fulls):
        self.links = links
        self.pieces, self.owns = [], []
        for shard, full in zip(shards, fulls):
            z, y, x, c = links.z, links.y, links.x, links.c
            self.owns.append([links.local(shard, full.at[z, y, x, c]), False])
            for first, count, start in cuts(shard.shape):
                rows = rows_of(shard.shape, first, count)
                self.pieces.append((len(self.owns) - 1, shard, full, rows, start))
        self.count = len(self.pieces)
        self.lead = [None] * self.count
        self.rest = [None] * self.count
        self.late = [[] for _ in range(self.count)]

    def columns(self, k, half):
        return pl.ds(self.pieces[k][4] + half * HALF, HALF)

    def block(self, k, half, *place):
        _, _, full, rows, _ = self.pieces[k]
        return full.at[(*place, rows, self.columns(k, half))]

    def own_block(self, k, half):
        _, shard, _, rows, _ = self.pieces[k]
        links = self.links
        return shard.at[rows, self.columns(k, half)], self.block(
            k, half, links.z, links.y, links.x, links.c
        )

    def own_there(self, k):
        own = self.owns[self.pieces[k][0]]
        if not own[1]:
            own[0].wait()
            own[1] = True

    def to_core(self, k, half, *place):
        block = self.block(k, half, *place)
        self.late[k].append(self.links.send(block, block, self.links.core))

    def to_planes(self, source, target):
        links = self.links
        return [links.send(source, target, links.plane_device(s)) for s in range(1, links.planes)]

    def T0(self, k):
        if k < self.count:
            self.lead[k] = [self.links.send(*self.own_block(k, 0), self.links.beside)]

    def T1(self, k):
        links = self.links
        self.own_there(k)
        arrived(self.lead[k])
        block = self.block(k, 0, links.z, links.y, ALL, links.c)
        self.lead[k] = self.to_planes(block, block)
        self.T0(k + AHEAD)

    def T2(self, k):
        links = self.links
        arrived(self.lead[k])
        place = (ALL, links.y, ALL, links.c)
        block = self.block(k, 0, *place)
        self.lead[k] = [links.send(block, block, links.across)]
        self.to_core(k, 0, *place)

    def T3(self, k):
        links = self.links
        arrived(self.lead[k])
        self.to_core(k, 0, ALL, 1 - links.y, ALL, links.c)

    def F0(self, k):
        if k < self.count:
            self.rest[k] = self.to_planes(*self.own_block(k, 1))

    def F1(self, k):
        links = self.links
        self.own_there(k)
        arrived(self.rest[k])
        place = (ALL, links.y, links.x, links.c)
        block = self.block(k, 1, *place)
        self.rest[k] = [links.send(block, block, links.across)]
        self.to_core(k, 1, *place)
        self.F0(k + AHEAD)

    def F2(self, k):
        links = self.links
        arrived(self.rest[k])
        block = self.block(k, 1, ALL, ALL, links.x, links.c)
        self.rest[k] = [links.send(block, block, links.beside)]
        self.to_core(k, 1, ALL, 1 - links.y, links.x, links.c)

    def F3(self, k):
        links = self.links
        arrived(self.rest[k])
        self.to_core(k, 1, ALL, ALL, 1 - links.x, links.c)

    def there(self, k):
        arrived(self.late[k])
        self.late[k] = []


def tasks_of(order):
    return [(TASKS[code // 32], code % 32) for code in order]


TASKS = (
    "fb", "az", "sp", "ay", "pm", "tk", "F1", "F2", "T1", "att", "unit", "F3", "T2", "T3", "load",
    "own", "there", "mlp", "S1", "project", "T4", "F4", "head", "first", "t1", "attend", "small",
    "t2", "a1", "sums", "a2", "a3", "modulate", "cond",
)


def cuts(shape):
    rows, width = shape
    if width > WIDTH:
        return [(0, rows, start) for start in range(0, width, WIDTH)]
    count = 4 if rows % 128 == 0 else 1
    return [(part * (rows // count), rows // count, 0) for part in range(count)]


def rows_of(shape, first, count):
    return ALL if count == shape[-2] else pl.ds(first, count)


AHEAD = 2
MIDDLE_PIECES = 3


class Opening:
    TOKEN_CUTS = 8
    ATTEND_CUTS = 4

    def __init__(self, links, tokens, attend, partial, tokens_out, attend_out, modulation_out, scratch):
        self.links, self.partial, self.attend = links, partial, attend
        self.tokens, self.tokens_out = tokens, tokens_out
        self.attend_out, self.modulation_out = attend_out, modulation_out
        self.held, self.from_core, self.from_beside, self.from_column, self.total = scratch
        z, y, x, c = links.z, links.y, links.x, links.c
        target = attend_out.at[z, y, x, c]
        self.own_slice = links.local(attend.at[x, c], target)
        self.own_tokens = links.local(tokens, tokens_out.at[:, x, c])
        self.far = links.send(attend.at[1 - x, 1 - c], self.held, links.core)
        self.near = [
            links.send(attend.at[x, 1 - c], target, links.core),
            links.send(attend.at[1 - x, c], target, links.beside),
        ]
        self.over_planes, self.beside, self.rest = {}, {}, []

    def tokens_start(self):
        links = self.links
        target = self.tokens_out.at[:, links.x, links.c]
        self.rest.append(links.send(self.tokens, target, links.core))
        for k in range(2):
            self.tkx(k)

    def token_block(self, k):
        each = self.TOKEN_CUTS // self.tokens.shape[0]
        rows = self.tokens.shape[1] // each
        return k // each, pl.ds(k % each * rows, rows)

    def tkx(self, k):
        links = self.links
        m, rows = self.token_block(k)
        target = self.tokens_out.at[m, links.x, links.c, rows]
        self.beside[k] = links.send(self.tokens.at[m, rows], target, links.beside)

    def tk(self, k):
        links = self.links
        arrived([self.beside.pop(k)])
        m, rows = self.token_block(k)
        fresh = self.tokens_out.at[m, 1 - links.x, links.c, rows]
        self.rest.append(links.send(fresh, fresh, links.core))
        if k + 2 < self.TOKEN_CUTS:
            self.tkx(k + 2)

    def fb(self, k):
        links = self.links
        arrived([self.far])
        target = self.attend_out.at[links.z, links.y, links.x, 1 - links.c]
        self.near.append(links.send(self.held, target, links.beside))

    def attend_block(self, k, *place):
        pair = k // 2
        return self.attend_out.at[(*place, k % 2, ALL, ALL, pl.ds(pair * PAIR, PAIR))]

    def azx(self, k):
        links = self.links
        block = self.attend_block(k, links.z, links.y)
        self.over_planes[k] = [
            links.send(block, block, links.plane_device(s)) for s in range(1, links.planes)
        ]

    def az(self, k):
        self.own_slice.wait()
        arrived(self.near)
        self.azx(0)
        self.azx(1)

    def ay(self, k):
        links = self.links
        arrived(self.over_planes.pop(k))
        block = self.attend_block(k, ALL, links.y)
        self.rest.append(links.send(block, block, links.across))
        if k + 2 < self.ATTEND_CUTS:
            self.azx(k + 2)

    def pm(self, k):
        links = self.links
        z, y, x, c = links.z, links.y, links.x, links.c
        if k > 0:
            arrived(self.step)
        if k == 0:
            self.step = [links.send(self.partial.at[:, :, :, 1 - c], self.from_core, links.core)]
        elif k == 1:
            self.from_core[...] = self.from_core[...] + self.partial[:, :, :, c]
            self.step = [
                links.send(self.from_core.at[:, :, 1 - x], self.from_beside, links.beside)
            ]
        elif k == 2:
            self.from_beside[...] = self.from_beside[...] + self.from_core[:, :, x]
            self.step = [
                links.send(self.from_beside.at[to_z, to_y], self.from_column.at[place], device)
                for place, (to_z, to_y, device) in enumerate(links.column())
            ]
        elif k == 3:
            result = self.from_beside[z, y]
            for place in range(2 * links.planes - 1):
                result = result + self.from_column[place]
            self.total[...] = result
            target = self.modulation_out.at[x, c]
            target[...] = result
            self.step = [
                links.send(self.total, target, links.core),
                links.send(self.total, target, links.beside),
            ]
        else:
            fresh = self.modulation_out.at[1 - x, c]
            self.rest.append(links.send(fresh, fresh, links.core))

    def finish(self):
        arrived(self.rest)
        self.own_tokens.wait()


def gather_body(
    planes,
    tokens,
    attend,
    project,
    expand,
    contract,
    partial,
    attend_out,
    project_out,
    expand_out,
    contract_out,
    modulation_out,
    tokens_out,
    send_sem,
    recv_sem,
    local_sem,
    *scratch,
):
    links = Links(planes, send_sem, recv_sem, local_sem)
    links.greet(links.partners())
    opening = Opening(
        links, tokens, attend, partial, tokens_out, attend_out, modulation_out, scratch
    )
    pieces = Pieces(links, (project, expand, contract), (project_out, expand_out, contract_out))
    opening.tokens_start()
    for k in range(5):
        opening.pm(k)
    for k in range(Opening.TOKEN_CUTS):
        opening.tk(k)
    opening.fb(0)
    opening.az(0)
    for k in range(Opening.ATTEND_CUTS):
        opening.ay(k)
    for k in range(AHEAD):
        pieces.T0(k)
        pieces.F0(k)
    for k in range(pieces.count + 2):
        for behind, names in enumerate((("T1", "F1"), ("T2", "F2"), ("T3", "F3"))):
            if 0 <= k - behind < pieces.count:
                for name in names:
                    getattr(pieces, name)(k - behind)
    for k in range(pieces.count):
        pieces.there(k)
    opening.finish()
    links.finish_sends()


FRONT_ORDER = (
    0, 32, 65, 66, 96, 128, 160, 97, 161, 129, 98, 162, 163, 99, 130, 192, 164, 193, 165, 131, 166,
    224, 194, 167, 132, 195, 256, 225, 288, 320, 196, 321, 257, 226, 197, 227, 322, 352, 323, 384,
    324, 353, 325, 198, 326, 327, 416, 354, 385, 328, 258, 199, 329, 355, 200, 259, 330, 417, 331,
    332, 386, 333, 260, 334, 228, 261, 387, 335, 336, 418, 337, 229, 388, 448, 262, 356, 419, 480,
    230, 389, 263, 513, 544, 231, 232, 357, 420, 264, 390, 514, 545, 421, 358, 515, 546, 391, 516,
    547, 422, 359, 392, 423, 360, 424,
)


def front_body(planes, *refs):
    tokens, attend_flat, project_flat, expand_flat, contract_flat, refs = *refs[:5], refs[5:]
    payload, modulate_flat, cotangent, refs = *refs[:3], refs[3:]
    attend_out, project_out, expand_out, contract_out, modulation_out, refs = *refs[:5], refs[5:]
    normed_out, qkv_out, heads_out, log_out, blended_out, refs = *refs[:5], refs[5:]
    middle_out, attended_out, second_out, act_out, slope_out, branch_out, grad_out = refs[:7]
    bias_rows, cond_out, modulate, refs = *refs[7:10], refs[10:]
    send_sem, recv_sem, local_sem = refs[:3]
    opening_scratch, refs = refs[3:8], refs[8:]
    payloads, partial, refs = *refs[:2], refs[2:]
    flat, attend, project, expand, contract, refs = *refs[:5], refs[5:]
    tokens_all, attend_all, normed, qkv, heads, blended, project_all, expand_all = refs[:8]
    middle, attended, second, act, slope, grad_branch, grads, upstream, bias_held = refs[8:]
    links = Links(planes, send_sem, recv_sem, local_sem)
    z, y, x, c = links.z, links.y, links.x, links.c
    corner = links.beside + 1 - 2 * c
    spread = Spread(links, payloads)

    def rows_apart(source, count):
        stride = source.shape[0] // count
        flat[: source.shape[0], :] = source[...].astype(jnp.float32)
        for k in range(stride):
            yield k, flat[pl.ds(k, count, stride=stride), :].astype(jnp.bfloat16)

    rows_own = project.shape[0]

    def prepare():
        payloads[z, y, x, c] = payload[...]
        for k, values in rows_apart(attend_flat, rows_own):
            kind, quarter, pair = k // (GROUP * PAIRS), k // PAIRS % GROUP, k % PAIRS
            lanes = pl.ds((pair * 3 + kind) * LANES, LANES)
            attend[quarter // 2, quarter % 2, :, lanes] = values

    links.greet([*links.partners(), corner], prepare)
    spread.step(0)
    opening = Opening(
        links, tokens, attend, partial, tokens_all, attend_all, modulation_out, opening_scratch
    )
    for source, target in (
        (modulate_flat, modulate),
        (expand_flat, expand),
        (project_flat, project),
        (contract_flat, contract),
    ):
        for k, values in rows_apart(source, target.shape[0]):
            target[:, k * LANES : (k + 1) * LANES] = values
    pieces = Pieces(links, (project, expand, contract), (project_all, expand_all, contract_out))
    count = pieces.count
    loaded_upstream = links.local(cotangent, upstream)
    micros, own_rows, _ = tokens.shape
    stored, stored_grads, exchanged = [], [], []
    own_heads = pl.ds(pl.multiple_of((2 * x + c) * OWN, OWN), OWN)

    def partial_unit():
        latents, rows = 2 * planes, modulate.shape[0]
        each = latents
        source = (links.z * 8 + links.place) // each
        column = (links.z * 8 + links.place) % each
        conds = [
            payloads[:, :, source // 2, source % 2, pl.ds(micros * column + m, 1), :].reshape(
                latents, LANES
            )
            for m in range(micros)
        ]
        active = silu(jnp.concatenate(conds, axis=0)[:, :rows]).astype(jnp.bfloat16)
        cond_out[...] = active.astype(jnp.float32)
        product = jnp.dot(active, modulate[...], preferred_element_type=jnp.float32)
        per_quarter = 6 * D // LANES // GROUP
        for m in range(micros):
            for k in range(6 * D // LANES):
                quarter, row = k // per_quarter, m * per_quarter + k % per_quarter
                values = product[m * latents : (m + 1) * latents, k * LANES : (k + 1) * LANES]
                partial[:, :, quarter // 2, quarter % 2, row, :] = values.reshape(
                    planes, 2, LANES
                )
        opening.pm(0)
        start = micros * each
        long = bias_rows.shape[0] // (4 * planes)
        for pair in range(4 * planes):
            place = (pair // 4, pair // 2 % 2, pair % 2)
            even = payloads[(*place, 0, slice(start, start + 4), ALL)]
            odd = payloads[(*place, 1, slice(start, start + 4), ALL)]
            joint = even[3:4] + odd[0:1]
            bias_rows[pair * long : (pair + 1) * long, :] = jnp.concatenate(
                [even[:3], joint, odd[1:]], axis=0
            )

    def shift(block):
        return bias_vector(bias_rows, 4 * D + FF + block * D, D)

    def part_of(m, to_x, to_c):
        start = pl.multiple_of((2 * to_x + to_c) * own_rows, own_rows)
        return heads.at[m, pl.ds(start, own_rows)]

    def project_micro(m):
        own = (2 * x + c) * PAIRS
        bias_qkv = []
        for pair in range(PAIRS):
            bias_qkv += [
                bias_rows[pl.ds(own + pair, 1), :],
                jnp.zeros((1, LANES), jnp.float32),
                bias_rows[pl.ds(D // LANES + own + pair, 1), :],
            ]
        offsets = modulation_row(modulation_out, m, 0) + shift(0)
        factors = 1.0 + modulation_row(modulation_out, m, 1) + shift(1)
        bias = jnp.concatenate(bias_qkv, axis=1)
        project_tokens(m, tokens_all, attend_all, offsets, factors, bias, normed, qkv)
        stored.append(links.local(normed.at[m], normed_out.at[m]))
        stored.append(links.local(qkv.at[m], qkv_out.at[m]))

    def far_heads(m, head):
        attention_unit(qkv.at[m], heads.at[m], log_out.at[m], head, 1 - x)
        if head == OWN // HEAD - 1:
            target = blended.at[m, :, own_heads]
            exchanged.append(links.send(part_of(m, 1 - x, 1 - c), target, corner))
            exchanged.append(links.send(part_of(m, 1 - x, c), target, links.beside))

    def near_heads(m, head):
        attention_unit(qkv.at[m], heads.at[m], log_out.at[m], head, x)
        if head == OWN // HEAD - 1:
            target = blended.at[m, :, own_heads]
            exchanged.append(links.send(part_of(m, x, 1 - c), target, links.core))
            stored.append(links.local(heads.at[m], heads_out.at[m]))
            links.local(part_of(m, x, c), target).wait()

    units = []
    for m in range(micros):
        units.append(functools.partial(project_micro, m))
        units += [functools.partial(far_heads, m, head) for head in range(OWN // HEAD)]
    for m in range(micros):
        units += [functools.partial(near_heads, m, head) for head in range(OWN // HEAD)]

    def load_project():
        pieces.there(0)
        stored.append(links.local(project_all, project_out))
        loaded_upstream.wait()
        for m in range(micros):
            gate = modulation_row(modulation_out, m, 5) + shift(5)
            grad_branch[m] = (gate * upstream[m].astype(jnp.float32)).astype(jnp.bfloat16)
        stored.append(links.local(grad_branch, branch_out))

    def own_tokens():
        for m in range(micros):
            stored.append(links.local(blended.at[m], blended_out.at[m]))
            product = jnp.dot(
                blended[m],
                project_all[...].reshape(D, D),
                preferred_element_type=jnp.float32,
            )
            attended[m] = product + bias_vector(bias_rows, 2 * D, D)
            gate = modulation_row(modulation_out, m, 2) + shift(2)
            middle[m] = tokens_all[m, x, c].astype(jnp.float32) + gate * attended[m]
            normed_two, _ = normalize(middle[m])
            factors = 1.0 + modulation_row(modulation_out, m, 4) + shift(4)
            offsets = modulation_row(modulation_out, m, 3) + shift(3)
            second[m] = (normed_two * factors + offsets).astype(jnp.bfloat16)
        stored.append(links.local(middle, middle_out))
        stored.append(links.local(attended, attended_out))
        stored.append(links.local(second, second_out))

    parts = FF // WIDTH
    blocks = grads.shape[1]

    def expand_unit(part):
        columns = pl.ds(part * WIDTH, WIDTH)
        stored.append(
            links.local(
                expand_all.at[:, :, :, :, :, columns], expand_out.at[:, :, :, :, :, columns]
            )
        )
        if part >= 2:
            stored_grads[part - 2].wait()
        bias = bias_vector(bias_rows, 3 * D + part * WIDTH, WIDTH)
        bias_held[...] = bias
        expand_part(part, WIDTH, second, expand_all, bias_held, act, slope, grad_branch, grads)
        stored.append(links.local(act.at[:, :, columns], act_out.at[:, :, columns]))
        stored.append(links.local(slope.at[:, :, columns], slope_out.at[:, :, columns]))
        stored_grads.append(
            links.local(grads.at[part % 2], grad_out.at[pl.ds(part * blocks, blocks)])
        )

    for task, k in tasks_of(FRONT_ORDER):
        if task == "sp":
            spread.step(k)
            if k == 1:
                opening.tokens_start()
        elif task in ("fb", "az", "ay", "tk"):
            getattr(opening, task)(k)
            if task == "ay" and k == Opening.ATTEND_CUTS - 2:
                for piece in range(AHEAD):
                    pieces.F0(piece)
            if task == "tk" and k == Opening.TOKEN_CUTS - 2:
                for piece in range(AHEAD):
                    pieces.T0(piece)
        elif task == "pm":
            if k == 0:
                spread.step(3)
                partial_unit()
            else:
                opening.pm(k)
        elif task == "att":
            opening.finish()
            stored.append(links.local(attend_all, attend_out))
        elif task == "unit":
            units[k]()
        elif task == "load":
            load_project()
        elif task == "own":
            arrived(exchanged)
            own_tokens()
        elif task == "there":
            pieces.there(k)
        elif task == "mlp":
            expand_unit(k)
        else:
            getattr(pieces, task)(k)
    for k in range(count):
        pieces.there(k)
    for copy in stored + stored_grads[-2:]:
        copy.wait()
    links.finish_sends()


ROOT = 0.7978845608028654
CUBE = 0.044715
CHUNK = 512


def expand_part(part, width, second, expand, bias, act, slope, grad_branch, grads):
    micros = second.shape[0]
    rows = grads.shape[2]

    @pl.loop(0, width // CHUNK, unroll=True)
    def _(chunk):
        inside = pl.ds(pl.multiple_of(chunk * CHUNK, CHUNK), CHUNK)
        columns = pl.ds(pl.multiple_of(part * width + chunk * CHUNK, CHUNK), CHUNK)
        weights = expand[:, :, :, :, :, columns].reshape(D, CHUNK)
        total = None
        for m in range(micros):
            hidden = jnp.dot(second[m], weights, preferred_element_type=jnp.float32)
            hidden = hidden + bias[:, inside]
            square = hidden * hidden
            bend = jnp.tanh(hidden * (ROOT + (ROOT * CUBE) * square))
            half = 0.5 + 0.5 * bend
            low = (hidden * half).astype(jnp.bfloat16)
            act[m, :, columns] = low
            steep = hidden * (0.5 * ROOT + (1.5 * ROOT * CUBE) * square)
            slope[m, :, columns] = (half + steep * (1.0 - bend * bend)).astype(jnp.bfloat16)
            product = lax.dot_general(
                low, grad_branch[m], (((0,), (0,)), ((), ())), preferred_element_type=jnp.float32
            )
            total = product if total is None else total + product
        count = CHUNK // rows
        here = pl.ds(chunk * count, count)
        grads[part % 2, here] = total.astype(jnp.bfloat16).reshape(count, rows, D)


def modulation_row(modulation, m, block):
    per_quarter = modulation.shape[2] // MICROS
    pieces = []
    for k in range(block * D // LANES, (block + 1) * D // LANES):
        quarter, row = k // per_quarter, m * per_quarter + k % per_quarter
        pieces.append(modulation[quarter // 2, quarter % 2, row : row + 1, :])
    return jnp.concatenate(pieces, axis=1)


def bias_vector(bias_rows, start, count):
    rows = range(start // LANES, (start + count) // LANES)
    return jnp.concatenate([bias_rows[row : row + 1, :] for row in rows], axis=1)


def project_tokens(m, tokens, attend, offsets, factors, bias, normed_out, qkv_out):
    rows = tokens.shape[3]

    @pl.loop(0, GROUP, unroll=2)
    def _(block):
        values = tokens[m, block // 2, block % 2].astype(jnp.float32)
        normed, _ = normalize(values)
        first = (normed * factors + offsets).astype(jnp.bfloat16)
        here = pl.ds(pl.multiple_of(block * rows, rows), rows)
        normed_out[m, here, :] = normed.astype(jnp.bfloat16)
        weights = attend[...].reshape(D, 3 * OWN)
        product = jnp.dot(first, weights, preferred_element_type=jnp.float32)
        qkv_out[m, here, :] = (product + bias).astype(jnp.bfloat16)


def gather_scratch(attend, rows, planes):
    return [
        pltpu.VMEM((attend.shape[-2], attend.shape[-1]), attend.dtype),
        pltpu.VMEM((planes, 2, 2, rows, LANES), jnp.float32),
        pltpu.VMEM((planes, 2, rows, LANES), jnp.float32),
        pltpu.VMEM((2 * planes - 1, rows, LANES), jnp.float32),
        pltpu.VMEM((rows, LANES), jnp.float32),
    ]


def gather_outs(attend, project, expand, contract, rows, planes):
    return [
        *(
            jax.ShapeDtypeStruct((planes, 2, 2, 2, *shard.shape[-2:]), shard.dtype)
            for shard in (attend, project, expand, contract)
        ),
        jax.ShapeDtypeStruct((2, 2, rows, LANES), jnp.float32),
    ]


def gather_sems(planes):
    return 60 + 30 * planes + 9 * (8 + 2 * planes)


def gather_all(tokens, attend, project, expand, contract, partial, planes):
    micros, own_rows, _ = tokens.shape
    return remote_call(
        functools.partial(gather_body, planes),
        "gather_all",
        1,
        (
            *gather_outs(attend, project, expand, contract, partial.shape[-2], planes),
            jax.ShapeDtypeStruct((micros, 2, 2, own_rows, D), tokens.dtype),
        ),
        [ANY] * 5 + [VMEM],
        (ANY,) * 4 + (VMEM, ANY),
        gather_scratch(attend, partial.shape[-2], planes),
        gather_sems(planes),
        8,
        56 * MIB,
    )(tokens, attend, project, expand, contract, partial)


def front(tokens, attend, project, expand, contract, payload, modulate, cotangent, planes):
    micros, own_rows, _ = tokens.shape
    latent_rows = own_rows * GROUP
    blocks = latent_rows // QUERY_ROWS
    def low(*shape):
        return jax.ShapeDtypeStruct(shape, jnp.bfloat16)

    def held(*shape, dtype=jnp.bfloat16):
        return pltpu.VMEM(shape, dtype)

    log_shape = (micros, OWN // HEAD, blocks, 1, QUERY_ROWS)
    own = (micros, own_rows, D)
    parts = FF // WIDTH
    rows = micros * 6 * D // LANES // GROUP
    rows_own, grad_rows = D // (8 * planes), FF // (8 * planes)
    shapes = ((2, 2, rows_own, 3 * OWN), (rows_own, D), (rows_own, FF), (grad_rows, D))
    shards = [jax.ShapeDtypeStruct(shape, jnp.bfloat16) for shape in shapes]
    biases = (10 * D + FF) // LANES
    return remote_call(
        functools.partial(front_body, planes),
        "front",
        1,
        (
            *gather_outs(*shards, rows, planes),
            low(micros, latent_rows, D),
            low(micros, latent_rows, 3 * OWN),
            low(micros, latent_rows, OWN),
            jax.ShapeDtypeStruct(log_shape, jnp.float32),
            low(*own),
            jax.ShapeDtypeStruct(own, jnp.float32),
            jax.ShapeDtypeStruct(own, jnp.float32),
            low(*own),
            low(micros, own_rows, FF),
            low(micros, own_rows, FF),
            low(*own),
            low(FF // grad_rows, grad_rows, D),
            jax.ShapeDtypeStruct((biases, LANES), jnp.float32),
            jax.ShapeDtypeStruct((micros * 2 * planes, rows_own), jnp.float32),
            low(rows_own, 6 * D),
        ),
        [ANY] + [VMEM] * 6 + [ANY],
        (ANY,) * 4 + (VMEM,) + (ANY,) * 3 + (VMEM,) + (ANY,) * 8 + (VMEM,) * 3,
        [
            *gather_scratch(shards[0], rows, planes),
            held(planes, 2, 2, 2, *payload.shape, dtype=jnp.float32),
            held(planes, 2, 2, 2, rows, LANES, dtype=jnp.float32),
            held(*modulate.shape, dtype=jnp.float32),
            *(held(*shape) for shape in shapes),
            held(micros, 2, 2, own_rows, D),
            held(planes, 2, 2, 2, rows_own, 3 * OWN),
            held(micros, latent_rows, D),
            held(micros, latent_rows, 3 * OWN),
            held(micros, latent_rows, OWN),
            held(*own),
            held(planes, 2, 2, 2, rows_own, D),
            held(planes, 2, 2, 2, rows_own, FF),
            held(*own, dtype=jnp.float32),
            held(*own, dtype=jnp.float32),
            held(*own),
            held(micros, own_rows, FF),
            held(micros, own_rows, FF),
            held(*own),
            held(2, FF // parts // grad_rows, grad_rows, D),
            held(*own),
            held(1, WIDTH, dtype=jnp.float32),
        ],
        gather_sems(planes),
        40,
        60 * MIB,
    )(tokens, attend, project, expand, contract, payload, modulate, cotangent)


QUERY_ROWS = 256
PAIRS = OWN // LANES
PAIR = 3 * LANES


def head_columns(head):
    start = head // 2 * PAIR + head % 2 * HEAD
    return [slice(start + kind * LANES, start + kind * LANES + HEAD) for kind in range(3)]


def attention_unit(qkv, out, log, head, side=None):
    count = qkv.shape[0] // QUERY_ROWS
    start = 0
    if side is not None:
        count //= 2
        start = side * count
    at = head * HEAD
    query_at, key_at, value_at = head_columns(head)
    keys = qkv[:, key_at]
    values_t = qkv[:, value_at].T

    @pl.loop(0, count, unroll=True)
    def _(index):
        block = start + index
        here = pl.ds(pl.multiple_of(block * QUERY_ROWS, QUERY_ROWS), QUERY_ROWS)
        queries = qkv[here, query_at] * SCALE
        scores = lax.dot_general(
            keys, queries, (((1,), (1,)), ((), ())), preferred_element_type=jnp.float32
        )
        top = jnp.max(scores, axis=0, keepdims=True)
        weights = jnp.exp(scores - top)
        totals = jnp.sum(weights, axis=0, keepdims=True)
        blended = jnp.dot(
            values_t, weights.astype(jnp.bfloat16), preferred_element_type=jnp.float32
        )
        out[here, at : at + HEAD] = (blended / totals).T.astype(jnp.bfloat16)
        log[head, block] = top + jnp.log(totals)


def attention_body(qkv_ref, out_ref, log_ref):
    for head in range(OWN // HEAD):
        attention_unit(qkv_ref.at[0], out_ref.at[0], log_ref.at[0], head)


def attention(qkv):
    micros, rows, _ = qkv.shape
    heads = OWN // HEAD
    blocks = rows // 256
    return pl.pallas_call(
        attention_body,
        grid=(micros,),
        out_shape=(
            jax.ShapeDtypeStruct((micros, rows, OWN), jnp.bfloat16),
            jax.ShapeDtypeStruct((micros, heads, blocks, 1, 256), jnp.float32),
        ),
        in_specs=[pl.BlockSpec((1, rows, 3 * OWN), lambda m: (m, 0, 0))],
        out_specs=(
            pl.BlockSpec((1, rows, OWN), lambda m: (m, 0, 0)),
            pl.BlockSpec((1, heads, blocks, 1, 256), lambda m: (m, 0, 0, 0, 0)),
        ),
        compiler_params=pltpu.CompilerParams(vmem_limit_bytes=48 * MIB),
        name="attention",
    )(qkv)


def attention_back_unit(qkv, blended_all, grad_all, log, out, key_sum, value_sum, head):
    at = head * HEAD
    query_at, key_at, value_at = head_columns(head)
    keys = qkv[:, key_at]
    keys_t = keys.T
    values = qkv[:, value_at]
    key_sum[...] = jnp.zeros_like(key_sum)
    value_sum[...] = jnp.zeros_like(value_sum)

    @pl.loop(0, qkv.shape[0] // QUERY_ROWS, unroll=True)
    def _(block):
        here = pl.ds(pl.multiple_of(block * QUERY_ROWS, QUERY_ROWS), QUERY_ROWS)
        queries = qkv[here, query_at] * SCALE
        grads = grad_all[here, at : at + HEAD]
        blended = blended_all[here, at : at + HEAD]
        row_terms = jnp.sum(
            (grads.astype(jnp.float32) * blended.astype(jnp.float32)).T, axis=0, keepdims=True
        )
        scores = lax.dot_general(
            keys, queries, (((1,), (1,)), ((), ())), preferred_element_type=jnp.float32
        )
        chances = jnp.exp(scores - log[head, block])
        grad_chances = lax.dot_general(
            values, grads, (((1,), (1,)), ((), ())), preferred_element_type=jnp.float32
        )
        grad_scores = (chances * (grad_chances - row_terms)).astype(jnp.bfloat16)
        value_sum[...] += jnp.dot(
            chances.astype(jnp.bfloat16), grads, preferred_element_type=jnp.float32
        )
        key_sum[...] += jnp.dot(grad_scores, queries, preferred_element_type=jnp.float32)
        grad_queries = jnp.dot(keys_t, grad_scores, preferred_element_type=jnp.float32)
        out[here, query_at] = (grad_queries.T * SCALE).astype(jnp.bfloat16)

    out[:, key_at] = key_sum[...].astype(jnp.bfloat16)
    out[:, value_at] = value_sum[...].astype(jnp.bfloat16)


def attention_back_body(qkv_ref, blended_ref, grad_ref, log_ref, out_ref, key_sum, value_sum):
    for head in range(OWN // HEAD):
        attention_back_unit(
            qkv_ref.at[0],
            blended_ref.at[0],
            grad_ref.at[0],
            log_ref.at[0],
            out_ref.at[0],
            key_sum,
            value_sum,
            head,
        )


def attention_back(qkv, blended, grads, logs):
    micros, rows, _ = qkv.shape
    heads = OWN // HEAD
    blocks = rows // 256
    wide = pl.BlockSpec((1, rows, 3 * OWN), lambda m: (m, 0, 0))
    narrow = pl.BlockSpec((1, rows, OWN), lambda m: (m, 0, 0))
    return pl.pallas_call(
        attention_back_body,
        grid=(micros,),
        out_shape=jax.ShapeDtypeStruct((micros, rows, 3 * OWN), jnp.bfloat16),
        in_specs=[
            wide,
            narrow,
            narrow,
            pl.BlockSpec((1, heads, blocks, 1, 256), lambda m: (m, 0, 0, 0, 0)),
        ],
        out_specs=wide,
        scratch_shapes=[pltpu.VMEM((rows, HEAD), jnp.float32)] * 2,
        compiler_params=pltpu.CompilerParams(vmem_limit_bytes=48 * MIB),
        name="attention_back",
    )(qkv, blended, grads, logs)


def heads_to_tokens_body(blended, out, send_sem, recv_sem, local_sem):
    links = Links(1, send_sem, recv_sem, local_sem)
    x, c = links.x, links.c
    corner = links.beside + 1 - 2 * c
    links.greet([links.core, links.beside, corner])
    target = out.at[:, :, pl.ds(pl.multiple_of((2 * x + c) * OWN, OWN), OWN)]
    own = links.local(blended.at[:, x, c], target)
    copies = [
        links.send(blended.at[:, 1 - x, 1 - c], target, corner),
        links.send(blended.at[:, 1 - x, c], target, links.beside),
        links.send(blended.at[:, x, 1 - c], target, links.core),
    ]
    arrived(copies)
    own.wait()
    links.finish_sends()


def heads_to_tokens(blended):
    micros, rows, _ = blended.shape
    own_rows = rows // GROUP
    return remote_call(
        heads_to_tokens_body,
        "heads_to_tokens",
        2,
        jax.ShapeDtypeStruct((micros, own_rows, D), blended.dtype),
        [ANY],
        ANY,
        [],
        3,
        1,
        40 * MIB,
    )(blended.reshape(micros, 2, 2, own_rows, OWN))


def tokens_to_heads_body(grads, out, send_sem, recv_sem, local_sem):
    links = Links(1, send_sem, recv_sem, local_sem)
    x, c = links.x, links.c
    corner = links.beside + 1 - 2 * c
    links.greet([links.core, links.beside, corner])

    def columns(to_x, to_c):
        return grads.at[:, :, pl.ds(pl.multiple_of((2 * to_x + to_c) * OWN, OWN), OWN)]

    target = out.at[:, x, c]
    own = links.local(columns(x, c), target)
    copies = [
        links.send(columns(1 - x, 1 - c), target, corner),
        links.send(columns(1 - x, c), target, links.beside),
        links.send(columns(x, 1 - c), target, links.core),
    ]
    arrived(copies)
    own.wait()
    links.finish_sends()


def tokens_to_heads(grads):
    micros, own_rows, _ = grads.shape
    return remote_call(
        tokens_to_heads_body,
        "tokens_to_heads",
        3,
        jax.ShapeDtypeStruct((micros, 2, 2, own_rows, OWN), grads.dtype),
        [ANY],
        ANY,
        [],
        3,
        1,
        40 * MIB,
    )(grads).reshape(micros, GROUP * own_rows, OWN)


def token_sums_body(partial, out, send_sem, recv_sem, local_sem, from_core, own, from_beside):
    links = Links(1, send_sem, recv_sem, local_sem)
    x, c = links.x, links.c
    links.greet([links.core, links.beside])
    far = links.send(partial.at[:, 1 - x, 1 - c], from_core.at[0], links.core)
    near = links.send(partial.at[:, x, 1 - c], from_core.at[1], links.core)
    loads = [
        links.local(partial.at[:, 1 - x, c], own.at[0]),
        links.local(partial.at[:, x, c], own.at[1]),
    ]
    micros = out.shape[0]
    loads[0].wait()
    arrived([far])
    passed = []
    for m in range(micros):
        own[0, m] = (
            own[0, m].astype(jnp.float32) + from_core[0, m].astype(jnp.float32)
        ).astype(jnp.bfloat16)
        passed.append(links.send(own.at[0, m], from_beside.at[m], links.beside))
    loads[1].wait()
    arrived([near])
    for m in range(micros):
        out[m] = own[1, m].astype(jnp.float32) + from_core[1, m].astype(jnp.float32)
    for m in range(micros):
        arrived([passed[m]])
        out[m] += from_beside[m].astype(jnp.float32)
    links.finish_sends()


def token_sums(partial):
    micros, rows, width = partial.shape
    own_rows = rows // GROUP
    held = pltpu.VMEM((2, micros, own_rows, width), partial.dtype)
    return remote_call(
        token_sums_body,
        "token_sums",
        4,
        jax.ShapeDtypeStruct((micros, own_rows, width), jnp.float32),
        [ANY],
        VMEM,
        [held, held, pltpu.VMEM((micros, own_rows, width), partial.dtype)],
        4,
        2,
        40 * MIB,
    )(partial.reshape(micros, 2, 2, own_rows, width))


def small_sums_body(planes, partial, out, send_sem, recv_sem, local_sem, from_core, from_beside):
    links = Links(planes, send_sem, recv_sem)
    links.greet(links.partners())
    z, y, x, c = links.z, links.y, links.x, links.c
    arrived([links.send(partial.at[:, 1 - c], from_core, links.core)])
    from_core[...] = from_core[...] + partial[:, c]
    arrived([links.send(from_core.at[1 - x], from_beside, links.beside)])
    out[z, y, x, c] = from_core[x] + from_beside[...]
    spread_all(links, out)
    links.finish_sends()


def small_sums(partial, planes):
    block = partial.shape[2:]
    return remote_call(
        functools.partial(small_sums_body, planes),
        "small_sums",
        5,
        jax.ShapeDtypeStruct((planes, 2, 2, 2, *block), jnp.float32),
        [VMEM],
        VMEM,
        [pltpu.VMEM((2, *block), jnp.float32), pltpu.VMEM(block, jnp.float32)],
        2 * planes + 6,
        0,
        40 * MIB,
    )(partial)


def add_blocks(target, left, right, count):
    @pl.loop(0, count, unroll=2)
    def _(i):
        target(i)[...] = (
            left(i)[...].astype(jnp.float32) + right(i)[...].astype(jnp.float32)
        ).astype(jnp.bfloat16)


class Sums:
    def __init__(self, links, grads, outs, plan, scratch):
        self.links = links
        self.pieces, self.rows = [], []
        used = 0
        for grad, out, pieces in zip(grads, outs, plan):
            own = scratch[used]
            used += 1
            for first, count, start in pieces:
                rows = rows_of(grad.shape, first, count)
                self.pieces.append((grad, out, rows, start, own, *scratch[used : used + 7]))
                self.rows.append((first, count, grad.shape[-1] // LANES))
                used += 7
        self.state = [dict() for _ in self.pieces]

    def put(self, k, start, values):
        first, count, stride = self.rows[k]
        out = self.pieces[k][1]
        for j in range(values.shape[1] // LANES):
            where = first * stride + start // LANES + j
            out[pl.ds(where, count, stride=stride), :] = values[:, j * LANES : (j + 1) * LANES]

    def core(self, k):
        links = self.links
        grad, _, rows, start, _, first, *_ = self.pieces[k]
        source = grad.at[:, :, :, 1 - links.c, rows, pl.ds(start, WIDTH)]
        self.state[k]["core"] = links.send(source, first, links.core)

    def load(self, k):
        links = self.links
        grad, _, rows, start, own, *_ = self.pieces[k]
        source = grad.at[:, :, :, links.c, rows, pl.ds(start, WIDTH)]
        self.state[k]["own"] = links.local(source, own)

    def S1(self, k):
        links = self.links
        x, y, planes = links.x, links.y, links.planes
        _, _, _, _, own, first, over_y, _, _, over_x, _, _ = self.pieces[k]
        state = self.state[k]
        state["own"].wait()
        arrived([state["core"]])
        lead, rest = pl.ds(0, HALF), pl.ds(HALF, HALF)

        def add(columns, place):
            def block(ref):
                return lambda i: ref.at[(*place(i // 2, i % 2), ALL, columns)]

            add_blocks(block(first), block(own), block(first), planes * 2)

        add(lead, lambda z, other: (z, 1 - y, other))
        state["T"] = [links.send(first.at[:, 1 - y, :, :, lead], over_y, links.across)]
        add(rest, lambda z, other: (z, other, 1 - x))
        state["F"] = [links.send(first.at[:, :, 1 - x, :, rest], over_x, links.beside)]
        add(lead, lambda z, other: (z, y, other))
        add(rest, lambda z, other: (z, other, x))

    def T2(self, k):
        links = self.links
        _, _, _, _, _, first, over_y, over_planes, _, _, _, _ = self.pieces[k]
        arrived(self.state[k]["T"])

        def kept(i):
            return first.at[i // 2, links.y, i % 2, :, pl.ds(0, HALF)]

        def came(i):
            return over_y.at[i // 2, i % 2]

        add_blocks(came, kept, came, links.planes * 2)
        self.state[k]["T"] = [
            links.send(over_y.at[links.plane(s)], over_planes.at[s - 1], links.plane_device(s))
            for s in range(1, links.planes)
        ]

    def T3(self, k):
        links = self.links
        _, _, _, _, _, _, over_y, over_planes, last, _, _, _ = self.pieces[k]
        arrived(self.state[k]["T"])
        for i in (1 - links.x, links.x):
            result = over_y[links.z, i].astype(jnp.float32)
            for s in range(1, links.planes):
                result = result + over_planes[s - 1, i].astype(jnp.float32)
            over_y[links.z, i] = result.astype(jnp.bfloat16)
        source = over_y.at[links.z, 1 - links.x]
        self.state[k]["T"] = [links.send(source, last, links.beside)]

    def T4(self, k):
        links = self.links
        _, _, _, start, _, _, over_y, _, last, _, _, _ = self.pieces[k]
        arrived(self.state[k]["T"])
        kept = over_y[links.z, links.x].astype(jnp.float32)
        self.put(k, start, kept + last[...].astype(jnp.float32))

    def F2(self, k):
        links = self.links
        x, y = links.x, links.y
        _, _, _, _, _, first, _, _, _, over_x, third, _ = self.pieces[k]
        arrived(self.state[k]["F"])
        for here in (1 - y, y):

            def kept(i, here=here):
                return first.at[i, here, x, :, pl.ds(HALF, HALF)]

            def came(i, here=here):
                return over_x.at[i, here]

            add_blocks(came, kept, came, links.planes)
            if here is not y:
                self.state[k]["F"] = [links.send(over_x.at[:, here], third, links.across)]

    def F3(self, k):
        links = self.links
        _, _, _, _, _, _, _, _, _, over_x, third, fourth = self.pieces[k]
        arrived(self.state[k]["F"])

        def kept(i):
            return over_x.at[i, links.y]

        def came(i):
            return third.at[i]

        add_blocks(came, kept, came, links.planes)
        self.state[k]["F"] = [
            links.send(third.at[links.plane(s)], fourth.at[s - 1], links.plane_device(s))
            for s in range(1, links.planes)
        ]

    def F4(self, k):
        links = self.links
        _, _, _, start, *_, third, fourth = self.pieces[k]
        arrived(self.state[k]["F"])
        result = third[links.z].astype(jnp.float32)
        for s in range(1, links.planes):
            result = result + fourth[s - 1].astype(jnp.float32)
        self.put(k, start + HALF, result)


def sums_order(count):
    order = []
    stages = (("core", 0), ("S1", 1), ("load", 0), ("T2", 2), ("F2", 2), ("T3", 3), ("F3", 3), ("T4", 4), ("F4", 4))
    for k in range(count + 4):
        for task, behind in stages:
            if 0 <= k - behind < count:
                order.append((task, k - behind))
    return order


MIDDLE_ORDER = (
    544, 576, 449, 577, 450, 578, 545, 384, 546, 224, 385, 547, 225, 480, 386, 226, 416, 352, 417,
    481, 353, 608, 640, 641, 354, 418, 672, 673, 642, 674,
)
BACK_ORDER = (
    704, 576, 449, 705, 577, 450, 706, 384, 224, 578, 451, 707, 579, 452, 385, 225, 736, 352, 416,
    580, 453, 708, 768, 226, 386, 417, 581, 709, 387, 800, 672, 640, 710, 353, 711, 388, 354, 801,
    832, 418, 737, 419, 833, 389, 420, 673, 864, 641, 642, 769, 834, 896, 674, 643, 644, 227, 929,
    228, 897, 229, 421, 865, 960, 930, 645, 355, 992, 1024, 961, 356, 675, 357, 1057, 993, 676,
    1058, 677, 1059,
)


class AttendSums:
    def __init__(self, links, grads, out, scratch):
        self.links, self.grads, self.out = links, grads, out
        self.own, self.over_y, self.over_planes, self.sum, self.held = scratch
        self.state = [dict() for _ in range(PAIRS)]
        self.columns = [pl.ds(pair * PAIR, PAIR) for pair in range(PAIRS)]

    def a0(self, k):
        links, columns = self.links, self.columns[k]
        source = self.grads.at[:, 1 - links.y, :, :, :, columns]
        self.state[k]["y"] = links.send(source, self.over_y.at[..., columns], links.across)
        source = self.grads.at[:, links.y, :, :, :, columns]
        self.state[k]["own"] = links.local(source, self.own.at[..., columns])

    def a1(self, k):
        links, own, over_y, columns = self.links, self.own, self.over_y, self.columns[k]
        self.state[k]["own"].wait()
        arrived([self.state[k]["y"]])
        for i in range(2):

            def block(ref, i=i):
                return lambda j: ref.at[j // 2, i, j % 2, :, columns]

            add_blocks(block(own), block(own), block(over_y), links.planes * 2)
        self.state[k]["planes"] = [
            links.send(
                own.at[links.plane(s), :, :, :, columns],
                self.over_planes.at[s - 1, :, :, :, columns],
                links.plane_device(s),
            )
            for s in range(1, links.planes)
        ]

    def a2(self, k):
        links, columns = self.links, self.columns[k]
        x, c = links.x, links.c
        arrived(self.state[k]["planes"])
        for i in range(2):
            for j in range(2):
                result = self.own[links.z, i, j, :, columns].astype(jnp.float32)
                for s in range(1, links.planes):
                    result = result + self.over_planes[s - 1, i, j, :, columns].astype(jnp.float32)
                self.sum[i, j, :, columns] = result
        self.state[k]["beside"] = links.send(
            self.sum.at[1 - x, :, :, columns], self.held.at[:, :, columns], links.beside
        )
        self.state[k]["near"] = links.send(
            self.sum.at[x, 1 - c, :, columns], self.out.at[x, c, :, columns], links.core
        )
        self.out[x, c, :, columns] = self.sum[x, c, :, columns]

    def a3(self, k):
        links, columns = self.links, self.columns[k]
        x, c = links.x, links.c
        arrived([self.state[k]["beside"]])
        self.out[1 - x, c, :, columns] = self.held[c, :, columns]
        self.state[k]["far"] = links.send(
            self.held.at[1 - c, :, columns], self.out.at[1 - x, c, :, columns], links.core
        )

    def finish(self):
        for state in self.state:
            arrived([state["near"], state["far"]])


class Spread:
    def __init__(self, links, ref):
        self.links, self.ref = links, ref

    def step(self, k):
        links, ref = self.links, self.ref
        z, y, x, c = links.z, links.y, links.x, links.c
        if k > 0:
            arrived(self.sent)
        if k == 0:
            block = ref.at[z, y, x, c]
            devices = [device for _, _, device in links.column()]
        elif k == 1:
            block, devices = ref.at[:, :, x, c], [links.beside, links.core]
        elif k == 2:
            block, devices = ref.at[:, :, 1 - x, c], [links.core]
        else:
            return
        self.sent = [links.send(block, block, device) for device in devices]


class TokenSums:
    def __init__(self, links, partial, scratch):
        self.links, self.partial = links, partial
        self.from_core, self.from_beside = scratch
        self.state = {}

    def start(self, m):
        links, partial = self.links, self.partial
        x, c = links.x, links.c
        self.state[m] = [
            links.send(partial.at[m, 1 - x, 1 - c], self.from_core.at[0, m], links.core),
            links.send(partial.at[m, x, 1 - c], self.from_core.at[1, m], links.core),
        ]

    def middle(self, m):
        links, partial = self.links, self.partial
        x, c = links.x, links.c
        arrived(self.state[m])
        away = partial.at[m, 1 - x, c]
        away[...] = (
            away[...].astype(jnp.float32) + self.from_core[0, m].astype(jnp.float32)
        ).astype(jnp.bfloat16)
        self.state[m] = [links.send(away, self.from_beside.at[m], links.beside)]

    def finish(self, m):
        links = self.links
        arrived(self.state[m])
        return (
            self.partial[m, links.x, links.c].astype(jnp.float32)
            + self.from_core[1, m].astype(jnp.float32)
            + self.from_beside[m].astype(jnp.float32)
        )


def sums_body(planes, kinds, *refs):
    attend, grads, refs = refs[0], refs[1 : 1 + kinds], refs[1 + kinds :]
    attend_out, outs, refs = refs[0], refs[1 : 1 + kinds], refs[1 + kinds :]
    links = Links(planes, *refs[:3])
    links.greet(links.partners())
    attend_sums = AttendSums(links, attend, attend_out, refs[3:8])
    for pair in range(PAIRS):
        for task in (attend_sums.a0, attend_sums.a1, attend_sums.a2, attend_sums.a3):
            task(pair)
    plan = [cuts(grad.shape[-2:]) for grad in grads]
    sums = Sums(links, grads, outs, plan, refs[8:])
    for task, k in sums_order(len(sums.pieces)):
        getattr(sums, task)(k)
    attend_sums.finish()
    links.finish_sends()


def middle_body(planes, *refs):
    grad_contract, expand, contract, project, act, slope, second, grad_branch, refs = *refs[:8], refs[8:]
    middle, attended, upstream, blended, modulation, bias_rows, refs = *refs[:6], refs[6:]
    contract_out, output, middle_grad_out, rows_out, bias_out, hidden_out, refs = *refs[:6], refs[6:]
    grad_expand, grad_project, grad_heads, refs = *refs[:3], refs[3:]
    links = Links(planes, *refs[:3])
    refs = refs[3:]
    plan = [cuts(grad_contract.shape[-2:])[:MIDDLE_PIECES]]
    used = scratch_count(plan)
    sum_scratch, refs = refs[:used], refs[used:]
    contract_held, expand_held, act_held, slope_held, second_held, second_t, refs = *refs[:6], refs[6:]
    branch_grad, grads, branch, grad_second, middle_held, attended_held, refs = *refs[:6], refs[6:]
    upstream_held, project_held, blended_held, attended_grad, project_grads, refs = *refs[:5], refs[5:]
    middle_grad, grad_blended = refs
    x, c = links.x, links.c
    corner = links.beside + 1 - 2 * c
    micros, own_rows, _ = second.shape
    parts = FF // WIDTH
    part_width = FF // parts
    contract_blocks = contract.shape[0] // parts

    def load(part):
        columns = pl.ds(part * part_width, part_width)
        slot = part % 2
        return [
            links.local(
                contract.at[pl.ds(part * contract_blocks, contract_blocks)], contract_held.at[slot]
            ),
            links.local(expand.at[:, :, :, :, :, columns], expand_held.at[slot]),
            links.local(act.at[:, :, columns], act_held.at[slot]),
            links.local(slope.at[:, :, columns], slope_held.at[slot]),
        ]

    loaded = links.local(second, second_held), links.local(grad_branch, branch_grad)
    loading = {0: load(0)}
    links.greet([*links.partners(), corner])
    sums = Sums(links, (grad_contract,), (contract_out,), plan, sum_scratch)
    for k in range(len(sums.pieces)):
        sums.core(k)
    sums.load(0)
    later = []
    for copy in loaded:
        copy.wait()
    for m in range(micros):
        second_t[:, m * own_rows : (m + 1) * own_rows] = second_held[m].T
    branch[...] = jnp.zeros_like(branch)
    grad_second[...] = jnp.zeros_like(grad_second)
    stored = []

    def mlp_unit(part):
        for copy in loading.pop(part):
            copy.wait()
        slot = part % 2
        if part == 0:
            loading[1] = load(1)
        if part == 1:
            later.extend(
                [
                    links.local(middle, middle_held),
                    links.local(attended, attended_held),
                    links.local(upstream, upstream_held),
                    links.local(project, project_held),
                    links.local(blended, blended_held),
                ]
            )
        if part >= 2:
            stored[part - 2].wait()
        contract_part(
            part * part_width,
            contract_held.at[slot],
            expand_held.at[slot],
            act_held.at[slot],
            slope_held.at[slot],
            second_t,
            branch_grad,
            grads.at[slot],
            branch,
            grad_second,
            hidden_out,
        )
        if part + 2 < parts:
            loading[part + 2] = load(part + 2)
        columns = pl.ds(part * part_width, part_width)
        stored.append(links.local(grads.at[slot], grad_expand.at[:, :, :, :, :, columns]))

    totals = [jnp.zeros((1, D), jnp.float32)] * 2

    def own_tokens(m):
        def vector(block):
            shift = bias_vector(bias_rows, 4 * D + FF + block * D, D)
            return modulation_row(modulation, m, block) + shift

        ahead = upstream_held[m].astype(jnp.float32)
        outward = branch[m] + bias_vector(bias_rows, 3 * D + FF, D)
        output[m] = (middle_held[m] + vector(5) * outward).astype(jnp.bfloat16)
        rows_out[m, 5:6, :] = jnp.sum(ahead * outward, axis=0, keepdims=True)
        normed, scale = normalize(middle_held[m])
        values = grad_second[m]
        rows_out[m, 3:4, :] = jnp.sum(values, axis=0, keepdims=True)
        rows_out[m, 4:5, :] = jnp.sum(values * normed, axis=0, keepdims=True)
        back = ahead + norm_back(values, normed, scale, vector(4))
        middle_grad[m] = back
        rows_out[m, 2:3, :] = jnp.sum(back * attended_held[m], axis=0, keepdims=True)
        lowered = (vector(2) * back).astype(jnp.bfloat16)
        attended_grad[m] = lowered
        totals[0] += jnp.sum(lowered.astype(jnp.float32), axis=0, keepdims=True)
        totals[1] += jnp.sum(branch_grad[m].astype(jnp.float32), axis=0, keepdims=True)
        product = lax.dot_general(
            lowered,
            project_held[...].reshape(D, D),
            (((1,), (1,)), ((), ())),
            preferred_element_type=jnp.float32,
        )
        grad_blended[m] = product.astype(jnp.bfloat16)
        here = pl.ds(pl.multiple_of((2 * x + c) * own_rows, own_rows), own_rows)

        def columns_of(to_x, to_c):
            start = pl.multiple_of((2 * to_x + to_c) * OWN, OWN)
            return grad_blended.at[m, :, pl.ds(start, OWN)]

        target = grad_heads.at[m, here]
        exchanged.append(links.send(columns_of(1 - x, 1 - c), target, corner))
        exchanged.append(links.send(columns_of(1 - x, c), target, links.beside))
        exchanged.append(links.send(columns_of(x, 1 - c), target, links.core))
        stored.append(links.local(columns_of(x, c), target))

    exchanged = []

    def project_unit():
        total = None
        for m in range(micros):
            product = lax.dot_general(
                blended_held[m],
                attended_grad[m],
                (((0,), (0,)), ((), ())),
                preferred_element_type=jnp.float32,
            )
            total = product if total is None else total + product
        project_grads[...] = total.astype(jnp.bfloat16).reshape(project_grads.shape)
        stored.append(links.local(project_grads, grad_project))
        stored.append(links.local(middle_grad, middle_grad_out))

    for task, k in tasks_of(MIDDLE_ORDER):
        if task == "mlp":
            mlp_unit(k)
        elif task == "own":
            if k == 0:
                for copy in later:
                    copy.wait()
            own_tokens(k)
        elif task == "project":
            project_unit()
        else:
            getattr(sums, task)(k)
    bias_out[0:1, :] = totals[0]
    bias_out[1:2, :] = totals[1]
    arrived(exchanged)
    for copy in stored[parts - 2 :]:
        copy.wait()
    links.finish_sends()


def contract_part(
    start,
    contract,
    expand,
    act,
    slope,
    second_t,
    grad_branch,
    grads,
    branch,
    grad_second,
    hidden_sums,
):
    micros = grad_branch.shape[0]
    blocks = CHUNK // contract.shape[1]

    @pl.loop(0, act.shape[-1] // CHUNK, unroll=True)
    def _(chunk):
        inside = pl.ds(pl.multiple_of(chunk * CHUNK, CHUNK), CHUNK)
        columns = pl.ds(pl.multiple_of(start + chunk * CHUNK, CHUNK), CHUNK)
        outward = contract[pl.ds(chunk * blocks, blocks)].reshape(CHUNK, D)
        inward = expand[:, :, :, :, :, inside].reshape(D, CHUNK)
        lows = []
        for m in range(micros):
            branch[m] += jnp.dot(act[m, :, inside], outward, preferred_element_type=jnp.float32)
            grad_act = lax.dot_general(
                grad_branch[m], outward, (((1,), (1,)), ((), ())), preferred_element_type=jnp.float32
            )
            lows.append((grad_act * slope[m, :, inside].astype(jnp.float32)).astype(jnp.bfloat16))
            grad_second[m] += lax.dot_general(
                lows[m], inward, (((1,), (1,)), ((), ())), preferred_element_type=jnp.float32
            )
        grad_hidden = jnp.concatenate(lows, axis=0)
        product = jnp.dot(second_t[...], grad_hidden, preferred_element_type=jnp.float32)
        grads[:, :, :, :, :, inside] = product.astype(jnp.bfloat16).reshape(
            *grads.shape[:-1], CHUNK
        )
        hidden_sums[:, columns] = jnp.sum(
            grad_hidden.astype(jnp.float32), axis=0, keepdims=True
        )


def back_body(planes, *refs):
    contract_first, grad_contract, grad_expand, grad_project, refs = *refs[:4], refs[4:]
    grad_heads, refs = refs[0], refs[1:]
    qkv, heads, logs, normed, attend, refs = *refs[:5], refs[5:]
    tokens, middle_grad, modulation, bias_rows, row_sums, bias_sums, hidden_sums, refs = *refs[:7], refs[7:]
    cond, modulate, refs = *refs[:2], refs[2:]
    attend_flat, contract_out, expand_out, project_out, tokens_out, refs = *refs[:5], refs[5:]
    sums_out, modulate_out, cond_out, biases_out, refs = *refs[:4], refs[4:]
    links = Links(planes, *refs[:3])
    attend_held_scratch, refs = refs[3:8], refs[8:]
    all_grads = (grad_contract, grad_expand, grad_project)
    plan = back_plan(all_grads)
    used = scratch_count(plan)
    sum_scratch, refs = refs[:used], refs[used:]
    grads_held, qkv_held, heads_held, normed_held, attend_held, grad_qkv, refs = *refs[:6], refs[6:]
    key_sum, value_sum, attend_grads, partial, from_core, from_beside, refs = *refs[:6], refs[6:]
    tokens_held, middle_held, scales, head_sums, row_held, small, refs = *refs[:6], refs[6:]
    small_core, small_beside, modulations, attend_out = refs
    micros, latent_rows, _ = qkv.shape
    loads = {
        "heads": [
            links.local(qkv, qkv_held),
            links.local(grad_heads, grads_held),
            links.local(heads, heads_held),
        ],
    }

    def need(*names):
        for name in names:
            for copy in loads.pop(name, ()):
                copy.wait()

    links.greet(links.partners())
    z, y, x, c = links.z, links.y, links.x, links.c
    outs = (contract_out, expand_out, project_out)
    sums = Sums(links, all_grads, outs, plan, sum_scratch)
    kept = links.local(contract_first, contract_out.at[pl.ds(0, contract_first.shape[0])])
    for k in range(len(sums.pieces)):
        sums.core(k)
    sums.load(0)
    attend_sums = AttendSums(links, attend_grads, attend_out, attend_held_scratch)
    token_sum = TokenSums(links, partial, (from_core, from_beside))
    spread_sums, spread_cond = Spread(links, sums_out), Spread(links, cond_out)
    sent = {}

    def vector(m, block):
        shift = bias_vector(bias_rows, 4 * D + FF + block * D, D)
        return modulation_row(modulation, m, block) + shift

    scale_rows = []
    for m in range(micros):
        scale_rows += [1.0 + vector(m, 1), vector(m, 0)]
    scale_rows.append(jnp.zeros((8 - 2 * micros, D), jnp.float32))
    scales[...] = jnp.concatenate(scale_rows, axis=0).T

    def head_unit(m, head):
        if m == 0 and head == 0:
            need("heads")
            loads["attend"] = [links.local(attend, attend_held)]
            loads["normed"] = [links.local(normed, normed_held)]
            loads["tokens"] = [
                links.local(tokens, tokens_held),
                links.local(middle_grad, middle_held),
            ]
        attention_back_unit(
            qkv_held.at[m],
            heads_held.at[m],
            grads_held.at[m],
            logs.at[m],
            grad_qkv.at[m],
            key_sum,
            value_sum,
            head,
        )

    def tokens_unit(m):
        grads = token_sum.finish(m)
        need("tokens")
        normed_own, scale = normalize(tokens_held[m].astype(jnp.float32))
        tokens_out[m] = middle_held[m] + norm_back(grads, normed_own, scale, vector(m, 1))

    def small_start():
        highs = head_sums[...].astype(jnp.bfloat16)
        lows = (head_sums[...] - highs.astype(jnp.float32)).astype(jnp.bfloat16)
        product = lax.dot_general(
            jnp.concatenate([highs, lows], axis=0),
            attend_held[...].reshape(D, 3 * OWN),
            (((1,), (1,)), ((), ())),
            preferred_element_type=jnp.float32,
        )
        each = D // LANES
        per_quarter = 6 * each // GROUP
        for m in range(micros):
            blocks = [product[m : m + 1] + product[8 + m : 9 + m], row_held[m : m + 1, :]]
            blocks += [row_sums[m, block : block + 1, :] for block in range(2, 6)]
            for k in range(6 * each):
                quarter, row = k // per_quarter, m * per_quarter + k % per_quarter
                lanes = slice(k % each * LANES, (k % each + 1) * LANES)
                small[quarter // 2, quarter % 2, row : row + 1, :] = blocks[k // each][:, lanes]
        start = micros * per_quarter
        biases = {2: bias_sums[0:1, :], 7: bias_sums[1:2, :]}
        for k in range(FF // D):
            biases[3 + k] = hidden_sums[:, k * D : (k + 1) * D]
        each_quarter = 8 * each // GROUP
        small[0, 0, start:, :] = jnp.zeros((small.shape[2] - start, LANES), jnp.float32)
        for k in range(2 * each, 8 * each):
            quarter, row = k // each_quarter, start + k % each_quarter
            lanes = slice(k % each * LANES, (k % each + 1) * LANES)
            small[quarter // 2, quarter % 2, row : row + 1, :] = biases[k // each][:, lanes]
        for m in range(1, micros):
            head_sums[0:1, :] += head_sums[m : m + 1, :]
        for pair in range(PAIRS):
            for kind, first_row in ((0, start), (2, start + each)):
                lanes = pl.ds(pair * PAIR + kind * LANES, LANES)
                row = first_row + (2 * x + c) * PAIRS + pair
                small[0, 0, pl.ds(row, 1), :] = head_sums[0:1, lanes]
        sent["small"] = links.send(small.at[:, 1 - c], small_core, links.core)

    def small_core_sum():
        arrived([sent["small"]])
        small_core[...] = small_core[...] + small[:, c]
        sent["small"] = links.send(small_core.at[1 - x], small_beside, links.beside)

    def small_beside_sum():
        arrived([sent["small"]])
        sums_out[z, y, x, c] = small_core[x] + small_beside[...]
        spread_sums.step(0)

    def modulate_unit():
        spread_sums.step(3)
        latents = planes * 2
        per_quarter = 6 * D // LANES // GROUP
        for m in range(micros):
            for k in range(6 * D // LANES):
                quarter, row = k // per_quarter, m * per_quarter + k % per_quarter
                values = sums_out[:, :, quarter // 2, quarter % 2, row, :].reshape(latents, LANES)
                here = slice(m * latents, (m + 1) * latents)
                modulations[here, k * LANES : (k + 1) * LANES] = values
        grads = lax.dot_general(
            cond[...],
            modulations[...],
            (((0,), (0,)), ((), ())),
            precision=highest,
            preferred_element_type=jnp.float32,
        )
        stride = 6 * D // LANES
        for k in range(stride):
            lanes = slice(k * LANES, (k + 1) * LANES)
            modulate_out[pl.ds(k, grads.shape[0], stride=stride), :] = grads[:, lanes]
        product = lax.dot_general(
            modulations[...],
            modulate[...].astype(jnp.float32),
            (((1,), (1,)), ((), ())),
            precision=highest,
            preferred_element_type=jnp.float32,
        )
        start = micros * per_quarter
        long = sums_out.shape[4] - start
        for quarter in range(GROUP):
            block = sums_out[:, :, quarter // 2, quarter % 2, start:, :]
            biases_out[quarter * long : (quarter + 1) * long, :] = jnp.sum(block, axis=(0, 1))
        total = jnp.sum(modulations[...], axis=0, keepdims=True)
        for k in range(6 * D // LANES):
            row = GROUP * long + k
            biases_out[row : row + 1, :] = total[:, k * LANES : (k + 1) * LANES]
        cond_out[z, y, x, c] = jnp.zeros(cond_out.shape[4:], jnp.float32)
        cond_out[z, y, x, c, :, : product.shape[1]] = product
        spread_cond.step(0)

    heads_each = OWN // HEAD
    for task, k in tasks_of(BACK_ORDER):
        if task == "head":
            head_unit(k // heads_each, k % heads_each)
        elif task == "first":
            need("attend")
            first_product(k, grad_qkv, attend_held, partial)
            token_sum.start(k)
        elif task == "attend":
            need("attend", "normed")
            attend_product(
                k, normed_held, grad_qkv, attend_held, scales, head_sums, row_held, attend_grads
            )
            attend_sums.a0(k)
        elif task == "t1":
            token_sum.middle(k)
        elif task == "t2":
            tokens_unit(k)
        elif task in ("a1", "a2", "a3"):
            getattr(attend_sums, task)(k)
        elif task == "small":
            (small_start, small_core_sum, small_beside_sum)[k]()
        elif task == "sums":
            spread_sums.step(k)
        elif task == "modulate":
            modulate_unit()
        elif task == "cond":
            spread_cond.step(k)
        else:
            getattr(sums, task)(k)
    kept.wait()
    attend_sums.finish()
    count, stride = attend_out.shape[2], 3 * D // LANES
    for quarter in range(GROUP):
        for kind in range(3):
            for pair in range(PAIRS):
                lanes = pl.ds((pair * 3 + kind) * LANES, LANES)
                where = (kind * GROUP + quarter) * PAIRS + pair
                attend_flat[pl.ds(where, count, stride=stride), :] = attend_out[
                    quarter // 2, quarter % 2, :, lanes
                ]
    links.finish_sends()


def back_plan(grads):
    plan = [cuts(grad.shape[-2:]) for grad in grads]
    plan[0] = plan[0][MIDDLE_PIECES:]
    return plan


def attend_product(pair, normed, grad_qkv, attend, scales, head_sums, row_held, out):
    planes = attend.shape[0]
    width = D // planes
    micros = normed.shape[0]
    columns = pl.ds(pair * PAIR, PAIR)
    totals = [
        jnp.sum(grad_qkv[m, :, columns].astype(jnp.float32), axis=0, keepdims=True)
        for m in range(micros)
    ]
    head_sums[:, columns] = jnp.concatenate(
        [*totals, jnp.zeros((8 - micros, PAIR), jnp.float32)], axis=0
    )

    @pl.loop(0, planes)
    def _(plane):
        here = pl.ds(pl.multiple_of(plane * width, width), width)
        weights = attend[plane, :, :, :, :, columns].reshape(width, PAIR).astype(jnp.float32)
        total = jnp.zeros((width, PAIR), jnp.float32)
        for m in range(micros):
            product = lax.dot_general(
                normed[m, :, here],
                grad_qkv[m, :, columns],
                (((0,), (0,)), ((), ())),
                preferred_element_type=jnp.float32,
            )
            total = total + product * scales[here, 2 * m : 2 * m + 1]
            total = total + scales[here, 2 * m + 1 : 2 * m + 2] * totals[m]
            row = jnp.sum((weights * product).T, axis=0, keepdims=True)
            if pair == 0:
                row_held[m : m + 1, here] = row
            else:
                row_held[m : m + 1, here] += row
        out[plane, :, :, :, :, columns] = total.astype(jnp.bfloat16).reshape(
            *out.shape[1:-1], PAIR
        )


def first_product(m, grad_qkv, attend, partial):
    rows = partial.shape[3]

    @pl.loop(0, GROUP, unroll=2)
    def _(block):
        here = pl.ds(pl.multiple_of(block * rows, rows), rows)
        product = lax.dot_general(
            grad_qkv[m, here, :],
            attend[...].reshape(D, 3 * OWN),
            (((1,), (1,)), ((), ())),
            preferred_element_type=jnp.float32,
        )
        partial[m, block // 2, block % 2] = product.astype(jnp.bfloat16)


def attend_scratch(attend, planes):
    rows, width = attend.shape[-2:]
    return [
        pltpu.VMEM((planes, 2, 2, rows, width), jnp.bfloat16),
        pltpu.VMEM((planes, 2, 2, rows, width), jnp.bfloat16),
        pltpu.VMEM((planes - 1, 2, 2, rows, width), jnp.bfloat16),
        pltpu.VMEM((2, 2, rows, width), jnp.float32),
        pltpu.VMEM((2, rows, width), jnp.float32),
    ]


def sum_scratch(plan, planes):
    held = []
    for pieces in plan:
        rows = pieces[0][1]
        held.append(low_held(planes, 2, 2, rows, WIDTH))
        for _ in pieces:
            held += [
                low_held(planes, 2, 2, rows, WIDTH),
                low_held(planes, 2, rows, HALF),
                low_held(planes - 1, 2, rows, HALF),
                low_held(rows, HALF),
                low_held(planes, 2, rows, HALF),
                low_held(planes, rows, HALF),
                low_held(planes - 1, rows, HALF),
            ]
    return held


def count_pieces(plan):
    return sum(len(pieces) for pieces in plan)


def scratch_count(plan):
    return len(plan) + 7 * count_pieces(plan)


def flat_shape(count):
    return full_shape(count // LANES, LANES)


def full_shape(*shape):
    return jax.ShapeDtypeStruct(shape, jnp.float32)


def low_shape(*shape):
    return jax.ShapeDtypeStruct(shape, jnp.bfloat16)


def full_held(*shape):
    return pltpu.VMEM(shape, jnp.float32)


def low_held(*shape):
    return pltpu.VMEM(shape, jnp.bfloat16)


def sum_sems(plan, planes):
    return count_pieces(plan) * (4 + 2 * planes)


def weight_sums(attend, weights, planes):
    plan = [cuts(grad.shape[-2:]) for grad in weights]
    flats = [flat_shape(grad.shape[-2] * grad.shape[-1]) for grad in weights]
    return remote_call(
        functools.partial(sums_body, planes, len(weights)),
        "weight_sums",
        6,
        (full_shape(2, 2, *attend.shape[-2:]), *flats),
        [ANY] * (1 + len(weights)),
        (VMEM,) * (1 + len(weights)),
        [*attend_scratch(attend, planes), *sum_scratch(plan, planes)],
        8 + 2 * planes + sum_sems(plan, planes),
        4 + count_pieces(plan),
        60 * MIB,
    )(attend, *weights)


def middle_part(grad_contract, weights, held, vectors, planes):
    expand, contract, project = weights
    second = held[2]
    micros, own_rows, _ = second.shape
    own = second.shape
    shape = grad_contract.shape[-2:]
    plan = [cuts(shape)[:MIDDLE_PIECES]]
    width = WIDTH
    blocks = width // shape[0]
    return remote_call(
        functools.partial(middle_body, planes),
        "middle",
        6,
        (
            flat_shape(len(plan[0]) * plan[0][0][1] * D),
            low_shape(*own),
            full_shape(*own),
            full_shape(micros, 8, D),
            full_shape(8, D),
            full_shape(1, FF),
            low_shape(*expand.shape),
            low_shape(*project.shape),
            low_shape(micros, own_rows * GROUP, OWN),
        ),
        [ANY] * 12 + [VMEM] * 2,
        (VMEM, VMEM, ANY) + (VMEM,) * 3 + (ANY,) * 3,
        [
            *sum_scratch(plan, planes),
            low_held(2, blocks, *shape),
            low_held(2, *expand.shape[:-1], width),
            low_held(2, micros, own_rows, width),
            low_held(2, micros, own_rows, width),
            low_held(*own),
            low_held(D, micros * own_rows),
            low_held(*own),
            low_held(2, *expand.shape[:-1], width),
            full_held(*own),
            full_held(*own),
            full_held(*own),
            full_held(*own),
            low_held(*own),
            low_held(*project.shape),
            low_held(*own),
            low_held(*own),
            low_held(*project.shape),
            full_held(*own),
            low_held(*own),
        ],
        8 + sum_sems(plan, planes),
        48,
        63 * MIB,
    )(
        grad_contract,
        expand,
        contract.reshape(FF // shape[0], *shape),
        project,
        *held,
        *vectors,
    )


def back_part(contract_first, grads, grad_heads, held, vectors, planes):
    qkv, heads, logs, normed, attend, tokens, middle_grad = held
    plan = back_plan(grads)
    micros, latent_rows, width = qkv.shape
    own = tokens.shape
    small = (micros * 6 + 8) * D // LANES // GROUP
    cond, modulate = vectors[-2:]
    return remote_call(
        functools.partial(back_body, planes),
        "back",
        7,
        (
            flat_shape(GROUP * attend.shape[-2] * attend.shape[-1]),
            *(flat_shape(grad.shape[-2] * grad.shape[-1]) for grad in grads),
            full_shape(*own),
            full_shape(planes, 2, 2, 2, small, LANES),
            flat_shape(modulate.shape[0] * modulate.shape[1]),
            full_shape(planes, 2, 2, 2, cond.shape[0], LANES),
            flat_shape(10 * D + FF),
        ),
        [ANY] * 7 + [VMEM] + [ANY] * 4 + [VMEM] * 7,
        (VMEM,) * 9,
        [
            *attend_scratch(attend, planes),
            *sum_scratch(plan, planes),
            low_held(*grad_heads.shape),
            low_held(*qkv.shape),
            low_held(*heads.shape),
            low_held(*normed.shape),
            low_held(*attend.shape),
            low_held(*qkv.shape),
            full_held(latent_rows, HEAD),
            full_held(latent_rows, HEAD),
            low_held(*attend.shape),
            low_held(micros, 2, 2, *own[1:]),
            low_held(2, *own),
            low_held(*own),
            low_held(*own),
            full_held(*own),
            full_held(D, 8),
            full_held(8, width),
            full_held(8, D),
            full_held(2, 2, small, LANES),
            full_held(2, small, LANES),
            full_held(small, LANES),
            full_held(cond.shape[0], modulate.shape[1]),
            full_held(2, 2, *attend.shape[-2:]),
        ],
        40 + 8 * planes + sum_sems(plan, planes),
        12 + count_pieces(plan),
        63 * MIB,
    )(contract_first, *grads, grad_heads, *held, *vectors)


def normalize(values):
    center = values - jnp.mean(values, axis=-1, keepdims=True)
    spread_of = jnp.mean(center * center, axis=-1, keepdims=True)
    scale = lax.rsqrt(spread_of + epsilon)
    return center * scale, scale


def norm_back(grads, normed, scale, factors):
    inner = grads * (1.0 + factors)
    return scale * (
        inner
        - jnp.mean(inner, axis=-1, keepdims=True)
        - normed * jnp.mean(inner * normed, axis=-1, keepdims=True)
    )


def einsum(spec, left, right):
    return jnp.einsum(spec, left, right, preferred_element_type=jnp.float32)


def per_device(tokens, condition, attend, project, expand, contract, modulate, biases, cotangent):
    devices = lax.axis_size("fsdp")
    planes = devices // 8
    latents = devices // GROUP
    me = lax.axis_index("fsdp")
    quarter, latent = me % GROUP, me // GROUP
    micros, own_rows, _ = tokens.shape
    latent_rows = own_rows * GROUP
    rows = D // devices
    grid = (planes, 2, 2, 2)

    fused = rows % 16 == 0 and own_rows % QUERY_ROWS == 0 and biases.size == 7 * LANES // 2
    inputs = tokens.astype(jnp.float32)
    if fused:
        half = LANES // 2
        spread_cond = condition.astype(jnp.float32).reshape(micros, -1, rows).transpose(1, 0, 2)
        spread_cond = spread_cond.reshape(-1, rows)
        spread_cond = jnp.pad(spread_cond, ((0, 0), (0, LANES - rows)))
        own_biases = biases.astype(jnp.float32)
        own_biases = jnp.where(
            me % 2 == 0, jnp.pad(own_biases, (0, half)), jnp.pad(own_biases, (half, 0))
        )
        payload = jnp.concatenate([spread_cond, own_biases.reshape(-1, LANES)])
        payload = jnp.pad(payload, ((0, -payload.shape[0] % 8), (0, 0)))
        flats = [shard.reshape(-1, LANES) for shard in (attend, project, expand, contract)]
        attend_all, project_all, expand_all, contract_all, modulation_all, *rest = front(
            tokens, *flats, payload, modulate.reshape(-1, LANES), cotangent, planes
        )
        *rest, bias_rows, cond_own, modulate_rows = rest
        normed, projected, heads, logs, blended, middle, attended, second, act, slope, low, grads = rest
        grad_contract = grads.reshape(*grid, FF // devices, D)
        contract_first, output, grad_middle, row_sums, bias_sums, hidden_sums, *onward = middle_part(
            grad_contract,
            (expand_all, contract_all, project_all),
            (act, slope, second, low, middle, attended, cotangent, blended),
            (modulation_all, bias_rows),
            planes,
        )
        grad_expand, grad_project, grad_heads = onward
        attend_sum, contract_sum, expand_sum, project_sum, grad_tokens, *onward = back_part(
            contract_first,
            (grad_contract, grad_expand, grad_project),
            grad_heads,
            (projected, heads, logs, normed, attend_all, tokens, grad_middle),
            (
                modulation_all,
                bias_rows,
                row_sums,
                bias_sums,
                hidden_sums,
                cond_own,
                modulate_rows,
            ),
            planes,
        )
        _, grad_modulate, cond_cols, bias_sums = onward
        bias_sums = bias_sums.reshape(-1)
        cond_cols = cond_cols[..., :rows].reshape(devices, micros, latents, rows)
    else:
        modulate_rows = modulate.reshape(rows, 6 * D)
        attend_shard = attend.reshape(rows, 3, 2, 2, PAIRS, LANES).transpose(2, 3, 0, 4, 1, 5)
        shards = (
            tokens,
            attend_shard.reshape(2, 2, rows, 3 * OWN),
            project.reshape(rows, D),
            expand.reshape(rows, FF),
            contract.reshape(FF // devices, D),
        )
        held = jnp.concatenate([condition.reshape(-1), biases]).astype(jnp.float32)
        held = jnp.pad(held, (0, -held.size % (8 * LANES)))
        small = small_gather(held.reshape(-1, LANES), planes, 0).reshape(devices, -1)
        conditions = small[:, : condition.size].reshape(latents, GROUP, micros, -1)
        conditions = conditions.transpose(2, 0, 1, 3).reshape(micros * latents, D)
        cond_act = silu(conditions).astype(jnp.bfloat16)
        bias_all = small[:, condition.size : condition.size + biases.size].reshape(-1)
        bias_query = bias_all[0:D]
        bias_value = bias_all[D : 2 * D]
        bias_project = bias_all[2 * D : 3 * D]
        bias_expand = bias_all[3 * D : 3 * D + FF]
        bias_contract = bias_all[3 * D + FF : 4 * D + FF]
        bias_modulate = bias_all[4 * D + FF :]

        cond_own = lax.dynamic_slice_in_dim(cond_act, me * rows, rows, axis=1)
        partial = jnp.dot(cond_own, modulate_rows, preferred_element_type=jnp.float32)
        partial = partial.reshape(micros, latents, GROUP, -1).transpose(1, 2, 0, 3)
        partial = partial.reshape(planes, 2, 2, 2, -1, LANES)

        bias_row = jnp.concatenate(
            [
                lax.dynamic_slice_in_dim(bias_query, quarter * OWN, OWN),
                jnp.zeros((OWN,), jnp.float32),
                lax.dynamic_slice_in_dim(bias_value, quarter * OWN, OWN),
            ]
        )
        bias_row = bias_row.reshape(3, PAIRS, LANES).transpose(1, 0, 2).reshape(-1)
        attend_all, project_all, expand_all, contract_all, modulation_all, *rest = gather_all(
            *shards, partial, planes
        )
        modulation = modulation_all.reshape(GROUP, micros, -1).transpose(1, 0, 2)
        modulation = modulation.reshape(micros, 6 * D) + bias_modulate
        offsets_one, factors_one, gates_one, offsets_two, factors_two, gates_two = (
            modulation[:, None, part * D : (part + 1) * D] for part in range(6)
        )
        attend_own = attend_all.reshape(D, 3 * OWN)
        project_full = project_all.reshape(D, D)
        expand_full = expand_all.reshape(D, FF)
        contract_full = contract_all.reshape(FF, D)
        tokens_latent = rest[0].reshape(micros, latent_rows, D)
        normed_latent, _ = normalize(tokens_latent.astype(jnp.float32))
        first = (normed_latent * (1.0 + factors_one) + offsets_one).astype(jnp.bfloat16)
        projected = (einsum("mrd,de->mre", first, attend_own) + bias_row).astype(jnp.bfloat16)
        blended_heads, logs = attention(projected)
        blended = heads_to_tokens(blended_heads)

        attended = einsum("mrd,de->mre", blended, project_full) + bias_project
        middle = inputs + gates_one * attended
        normed_two, scale_two = normalize(middle)
        second = (normed_two * (1.0 + factors_two) + offsets_two).astype(jnp.bfloat16)
        hidden = einsum("mrd,de->mre", second, expand_full) + bias_expand
        activated, gelu_pull = jax.vjp(lambda v: jax.nn.gelu(v, approximate=True), hidden)
        act_low = activated.astype(jnp.bfloat16)
        branch = einsum("mrd,de->mre", act_low, contract_full) + bias_contract
        output = (middle + gates_two * branch).astype(jnp.bfloat16)

        upstream = cotangent.astype(jnp.float32)
        grad_branch = (gates_two * upstream).astype(jnp.bfloat16)
        grad_contract = einsum("mrd,mre->de", act_low, grad_branch)
        grad_act = einsum("mre,de->mrd", grad_branch, contract_full)
        grad_hidden = gelu_pull(grad_act)[0].astype(jnp.bfloat16)
        grad_expand = einsum("mrd,mre->de", second, grad_hidden)
        grad_second = einsum("mre,de->mrd", grad_hidden, expand_full)
        grad_middle = upstream + norm_back(grad_second, normed_two, scale_two, factors_two)
        grad_attended = (gates_one * grad_middle).astype(jnp.bfloat16)
        grad_project = einsum("mrd,mre->de", blended, grad_attended)
        grad_blended = einsum("mre,de->mrd", grad_attended, project_full).astype(jnp.bfloat16)
        grad_heads = tokens_to_heads(grad_blended)
        grad_projected = attention_back(projected, blended_heads, grad_heads, logs)
        grad_attend = einsum("mrd,mre->de", first, grad_projected)
        grad_first = token_sums(
            einsum("mre,de->mrd", grad_projected, attend_own).astype(jnp.bfloat16)
        )
        weights = (
            grad_contract.astype(jnp.bfloat16).reshape(*grid, FF // devices, D),
            grad_expand.astype(jnp.bfloat16).reshape(*grid, rows, FF),
            grad_project.astype(jnp.bfloat16).reshape(*grid, rows, D),
        )
        attend_sum, contract_sum, expand_sum, project_sum = weight_sums(
            grad_attend.astype(jnp.bfloat16).reshape(*grid, rows, 3 * OWN), weights, planes
        )
        attend_sum = attend_sum.reshape(2, 2, rows, PAIRS, 3, LANES).transpose(2, 4, 0, 1, 3, 5)

        def token_sum(values):
            return jnp.sum(values, axis=(0, 1), dtype=jnp.float32)

        heads_sum, attended_sum = token_sum(grad_projected), token_sum(grad_attended)
        hidden_sum, branch_sum = token_sum(grad_hidden), token_sum(grad_branch)
        later_sums = jnp.concatenate(
            [
                jnp.sum(grad_middle * attended, axis=1),
                jnp.sum(grad_second, axis=1),
                jnp.sum(grad_second * normed_two, axis=1),
                jnp.sum(upstream * branch, axis=1),
            ],
            axis=1,
        )
        normed_one, scale_one = normalize(inputs)
        grad_tokens = grad_middle + norm_back(grad_first, normed_one, scale_one, factors_one)

        grad_modulation = jnp.concatenate(
            [jnp.sum(grad_first, axis=1), jnp.sum(grad_first * normed_one, axis=1), later_sums], axis=1
        )
        heads_sum = heads_sum.reshape(PAIRS, 3, LANES).transpose(1, 0, 2).reshape(3, OWN)
        bias_terms = jnp.concatenate(
            [
                lax.dynamic_update_slice(
                    jnp.zeros((D,), jnp.float32), heads_sum[0], (quarter * OWN,)
                ),
                lax.dynamic_update_slice(
                    jnp.zeros((D,), jnp.float32), heads_sum[2], (quarter * OWN,)
                ),
                attended_sum,
                hidden_sum,
                branch_sum,
            ]
        )
        to_sum = jnp.concatenate(
            [
                grad_modulation.reshape(micros, GROUP, -1).transpose(1, 0, 2).reshape(GROUP, -1),
                bias_terms.reshape(GROUP, -1),
            ],
            axis=1,
        )
        sums = small_sums(to_sum.reshape(2, 2, -1, LANES), planes).reshape(latents, GROUP, -1)
        split = micros * 6 * D // GROUP
        grad_modulations = sums[:, :, :split].reshape(latents, GROUP, micros, -1)
        grad_modulations = grad_modulations.transpose(2, 0, 1, 3).reshape(micros * latents, 6 * D)
        grad_modulate = lax.dot_general(
            cond_own.astype(jnp.float32),
            grad_modulations,
            (((0,), (0,)), ((), ())),
            precision=highest,
        )
        grad_cond_cols = lax.dot_general(
            grad_modulations,
            modulate_rows.astype(jnp.float32),
            (((1,), (1,)), ((), ())),
            precision=highest,
        )
        cols = grad_cond_cols.reshape(-1)
        cols = jnp.pad(cols, (0, -cols.size % (8 * LANES)))
        cond_cols = small_gather(cols.reshape(-1, LANES), planes, 8).reshape(devices, -1)
        cond_cols = cond_cols[:, : micros * latents * rows].reshape(devices, micros, latents, rows)
        bias_sums = jnp.concatenate(
            [jnp.sum(sums[:, :, split:], axis=0).reshape(-1), jnp.sum(grad_modulations, axis=0)]
        )
    grad_biases = lax.dynamic_slice_in_dim(bias_sums, me * biases.size, biases.size)
    cols_own = lax.dynamic_index_in_dim(cond_cols, latent, axis=2, keepdims=False)
    width = D // GROUP
    cols_own = lax.dynamic_slice_in_dim(
        cols_own, quarter * (devices // GROUP), devices // GROUP, axis=0
    )
    grad_silu = cols_own.transpose(1, 0, 2).reshape(micros, width)
    values = condition.astype(jnp.float32)
    gate = 1.0 / (1.0 + jnp.exp(-values))
    grad_condition = gate * (1.0 + values * (1.0 - gate)) * grad_silu

    return (
        output,
        grad_tokens,
        grad_condition,
        attend_sum.reshape(-1),
        project_sum.reshape(-1),
        expand_sum.reshape(-1),
        contract_sum.reshape(-1),
        grad_modulate.reshape(-1),
        grad_biases,
    )


def solution(mesh):
    in_specs = (
        P(None, "fsdp", None),
        P(None, "fsdp"),
        P("fsdp"),
        P("fsdp"),
        P("fsdp"),
        P("fsdp"),
        P("fsdp"),
        P("fsdp"),
        P(None, "fsdp", None),
    )
    out_specs = (
        P(None, "fsdp", None),
        P(None, "fsdp", None),
        P(None, "fsdp"),
        P("fsdp"),
        P("fsdp"),
        P("fsdp"),
        P("fsdp"),
        P("fsdp"),
        P("fsdp"),
    )
    return jax.shard_map(
        per_device, mesh=mesh, in_specs=in_specs, out_specs=out_specs, check_vma=False
    )
```
